32 devices in a mesh: tok: 8 (over y, x, core), head: 4 (over z).
Axes of the slice: x: 2, y: 2, z: 4, core: 2. Of those that a mesh axis runs over, the one named last changes fastest.
Arguments:
- block_in: bfloat16 [16384, 1536], P(('tok', 'head')), may hold values from -6 to 6
- norm_gain: bfloat16 [1536], P('head'), may hold values from 0.5 to 1.5
- w_zx: bfloat16 [1536, 2, 3072], P('tok', None, 'head'), may hold values from -0.15625 to 0.15625
- w_bc: bfloat16 [1536, 256], P('tok'), may hold values from -0.15625 to 0.15625
- w_dt: bfloat16 [1536, 48], P('tok', 'head'), may hold values from -0.078125 to 0.078125
- conv_x_w: float32 [4, 3072], P(None, 'head'), may hold values from -3 to 3
- conv_x_b: float32 [3072], P('head'), may hold values from -3 to 3
- conv_bc_w: float32 [4, 256], replicated, may hold values from -3 to 3
- conv_bc_b: float32 [256], replicated, may hold values from -3 to 3
- dt_bias: float32 [48], P('head'), may hold values from -6 to -2
- a_log: float32 [48], P('head'), may hold values from 0 to 2.77
- d_skip: float32 [48], P('head'), may hold values from 0.5 to 1.5
- gate_gain: float32 [3072], P('head'), may hold values from 0.5 to 1.5
- w_out: bfloat16 [3072, 1536], P('head', 'tok'), may hold values from -0.109375 to 0.109375
- cotangent: bfloat16 [16384, 1536], P(('tok', 'head')), may hold values from -6 to 6
Outputs:
- block_out: float32 [16384, 1536], P(('tok', 'head'))
- d_block_in: float32 [16384, 1536], P(('tok', 'head'))
- d_norm_gain: float32 [1536], P('head')
- d_w_zx: float32 [1536, 2, 3072], P('tok', None, 'head')
- d_w_bc: float32 [1536, 256], P('tok')
- d_w_dt: float32 [1536, 48], P('tok', 'head')
- d_conv_x_w: float32 [4, 3072], P(None, 'head')
- d_conv_x_b: float32 [3072], P('head')
- d_conv_bc_w: float32 [4, 256], replicated
- d_conv_bc_b: float32 [256], replicated
- d_dt_bias: float32 [48], P('head')
- d_a_log: float32 [48], P('head')
- d_d_skip: float32 [48], P('head')
- d_gate_gain: float32 [3072], P('head')
- d_w_out: float32 [3072, 1536], P('head', 'tok')
The draws below stay inside these ranges and needn't reach their ends.
All inputs are finite; a program needn't handle non-finite values.
Results may differ from the reference program's by a relative error of at most 0.0066.
Values may be sent and summed in bfloat16 or wider, within the bound.
A program may use at most 192 MiB of HBM per device.

```python
import jax
import jax.numpy as jnp
from jax import lax

D = 1536
NHEADS = 48
HEADDIM = 64
STATE = 128
CONV = 4
STRETCH = 256
SEQLEN = 2048
SEQ_DEV = 1
INNER = 3072
TOKENS = 16384
N_TOK = 8


def steps_of(own_key, extent, cuts, smallest, top_value):
    def one(axis_at, blocks):
        heights = jax.random.uniform(jax.random.fold_in(jax.random.fold_in(own_key, 6), axis_at), (blocks,), jnp.float32, smallest / len(cuts), top_value / len(cuts))
        return jnp.repeat(jnp.exp(heights), extent[axis_at] // blocks).reshape((-1,) + (1,) * (len(extent) - axis_at - 1))

    loudness = one(*cuts[0])
    for cut in cuts[1:]:
        loudness = loudness * one(*cut)
    return loudness


def bell_draw(own_key, shape, width, reach, shards=(), held_as=jnp.bfloat16):
    drawn = jax.random.normal(own_key, shape, jnp.float32) * width
    if len(shards) > 0:
        drawn = steps_of(own_key, shape, shards, -0.22, 0.18) * drawn
    return jnp.clip(drawn, min=-reach, max=reach).astype(held_as)


def setup_inputs(seed: int = 0) -> dict:
    key_of = jax.random.split(jax.random.key(seed), 16)
    return {
        "block_in": bell_draw(key_of[0], (TOKENS, D), 1.0, 6.0, ((0, 32),)),
        "norm_gain": jnp.clip(1.0 + 0.1 * jax.random.normal(key_of[1], (D,), jnp.float32), 0.5, 1.5).astype(jnp.bfloat16),
        "w_zx": bell_draw(key_of[2], (D, 2, INNER), D ** -0.5, 0.15625, ((0, 8), (2, 4))),
        "w_bc": bell_draw(key_of[3], (D, 2 * STATE), D ** -0.5, 0.15625, ((0, 8),)),
        "w_dt": bell_draw(key_of[4], (D, NHEADS), (4 * D) ** -0.5, 0.078125, ((0, 8), (1, 4))),
        "conv_x_w": bell_draw(key_of[5], (CONV, INNER), CONV ** -0.5, 3.0, ((1, 4),), jnp.float32),
        "conv_x_b": bell_draw(key_of[6], (INNER,), 0.5, 3.0, ((0, 4),), jnp.float32),
        "conv_bc_w": bell_draw(key_of[7], (CONV, 2 * STATE), CONV ** -0.5, 3.0, (), jnp.float32),
        "conv_bc_b": bell_draw(key_of[8], (2 * STATE,), 0.5, 3.0, (), jnp.float32),
        "dt_bias": jnp.clip(-6.0 + 4.0 * jax.random.uniform(key_of[9], (NHEADS,), jnp.float32) ** steps_of(key_of[9], (NHEADS,), ((0, 4),), -0.2, 0.2), -6.0, -2.0),
        "a_log": jnp.clip(2.77 * jax.random.uniform(key_of[10], (NHEADS,), jnp.float32) ** steps_of(key_of[10], (NHEADS,), ((0, 4),), -0.2, 0.2), 0.0, 2.77),
        "d_skip": jnp.clip(0.5 + 1.0 * jax.random.uniform(key_of[11], (NHEADS,), jnp.float32) ** steps_of(key_of[11], (NHEADS,), ((0, 4),), -0.2, 0.2), 0.5, 1.5),
        "gate_gain": jnp.clip(1.0 + 0.1 * jax.random.normal(key_of[12], (INNER,), jnp.float32), 0.5, 1.5),
        "w_out": bell_draw(key_of[13], (INNER, D), INNER ** -0.5, 0.109375, ((0, 4), (1, 8))),
        "cotangent": bell_draw(key_of[14], (TOKENS, D), 1.0, 6.0, ((0, 32),)),
    }


epsilon = 1e-05
highest = lax.Precision.HIGHEST

@jax.custom_vjp
def low(v):
    return lax.optimization_barrier(v.astype(jnp.bfloat16)).astype(jnp.float32)

@jax.custom_vjp
def low_back(v):
    return v

def low_keep(v):
    return (low(v), None)

def low_pass(kept, grad):
    return (grad,)

def back_keep(v):
    return (v, None)

def back_low(kept, grad):
    return (low(grad),)
low.defvjp(low_keep, low_pass)
low_back.defvjp(back_keep, back_low)

def causal_conv(seq_in, weight, bias):
    seq_span = seq_in.shape[1]
    padded = jnp.pad(seq_in, ((0, 0), (CONV - 1, 0), (0, 0)))
    result = bias + weight[0] * padded[:, 0:seq_span]
    for offset in range(1, CONV):
        result = result + weight[offset] * padded[:, offset:offset + seq_span]
    return result

def ssd_one(x_heads, steps_dt, decay_rate, b_mat, c_mat):
    seq_span = x_heads.shape[0]
    head_count = x_heads.shape[1]
    blocks = seq_span // STRETCH
    x_blocks = x_heads.reshape(blocks, STRETCH, head_count, HEADDIM)
    dt_blocks = steps_dt.reshape(blocks, STRETCH, head_count)
    b_blocks = b_mat.reshape(blocks, STRETCH, STATE)
    c_blocks = c_mat.reshape(blocks, STRETCH, STATE)
    log_decay = dt_blocks * decay_rate
    positions = jnp.arange(STRETCH)
    lower_mask = positions[:, None] >= positions[None, :]
    cumulative = jnp.einsum('ij,kjh->kih', lower_mask.astype(jnp.float32), log_decay, precision=highest)
    log_gap = cumulative[:, :, None, :] - cumulative[:, None, :, :]
    mask_four = lower_mask[None, :, :, None]
    decay_pairs = jnp.where(mask_four, jnp.exp(jnp.where(mask_four, log_gap, 0.0)), 0.0)
    gram_mat = jnp.einsum('kin,kjn->kij', c_blocks, b_blocks, precision=highest)
    x_dt = x_blocks * dt_blocks[..., None]
    inside = jnp.einsum('kijh,kjhp->kihp', gram_mat[..., None] * decay_pairs, x_dt, precision=highest)
    to_end = jnp.exp(cumulative[:, -1:, :] - cumulative)
    block_states = jnp.einsum('kjhp,kjn->khpn', x_dt * to_end[..., None], b_blocks, precision=highest)
    block_decay = jnp.exp(cumulative[:, -1, :])

    def advance(state_now, scan_item):
        factor, fresh_state = scan_item
        return (state_now * factor[:, None, None] + fresh_state, state_now)
    start_state = jnp.zeros((head_count, HEADDIM, STATE), jnp.float32)
    unused, entering = lax.scan(advance, start_state, (block_decay, block_states))
    across = jnp.einsum('kin,khpn->kihp', c_blocks, entering, precision=highest) * jnp.exp(cumulative)[..., None]
    return (inside + across).reshape(seq_span, head_count, HEADDIM)

def mixer_part(zx_proj, bc_pre, dt_raw, conv_x_w, conv_x_b, conv_bc_w, conv_bc_b, dt_bias, a_log, d_skip):
    seq_count = zx_proj.shape[0] // SEQLEN
    part_width = zx_proj.shape[1] // 2
    head_count = part_width // HEADDIM
    gate_in = zx_proj[:, :part_width]
    x_pre = zx_proj[:, part_width:].reshape(seq_count, SEQLEN, part_width)
    x_conv = jax.nn.silu(causal_conv(x_pre, conv_x_w, conv_x_b))
    bc_conv = jax.nn.silu(causal_conv(bc_pre.reshape(seq_count, SEQLEN, 2 * STATE), conv_bc_w, conv_bc_b))
    steps_dt = jax.nn.softplus(dt_raw.reshape(seq_count, SEQLEN, head_count) + dt_bias)
    decay_rate = -jnp.exp(a_log)
    x_heads = x_conv.reshape(seq_count, SEQLEN, head_count, HEADDIM)

    def one_seq(seq_item):
        return ssd_one(seq_item[0], seq_item[1], decay_rate, seq_item[2], seq_item[3])
    y_heads = lax.map(jax.checkpoint(one_seq), (x_heads, steps_dt, bc_conv[..., :STATE], bc_conv[..., STATE:]))
    y_heads = y_heads + d_skip[:, None] * x_heads
    return y_heads.reshape(seq_count * SEQLEN, part_width) * jax.nn.silu(gate_in)

def layer(block_in, norm_gain, w_zx, w_bc, w_dt, conv_x_w, conv_x_b, conv_bc_w, conv_bc_b, dt_bias, a_log, d_skip, gate_gain, w_out):
    inv_rms = lax.rsqrt(lax.optimization_barrier(jnp.mean(block_in * block_in, axis=1, keepdims=True)) + epsilon)
    normed = low(block_in * inv_rms * norm_gain)
    zx_proj = low_back(jnp.dot(normed, w_zx.reshape(D, 2 * INNER), precision=highest))
    bc_pre = jnp.dot(normed, w_bc, precision=highest)
    dt_raw = low_back(jnp.dot(normed, w_dt, precision=highest))
    gated_out = mixer_part(zx_proj, bc_pre, dt_raw, conv_x_w, conv_x_b, conv_bc_w, conv_bc_b, dt_bias, a_log, d_skip)
    inv_gate = lax.rsqrt(lax.optimization_barrier(jnp.mean(gated_out * gated_out, axis=1, keepdims=True)) + epsilon)
    y_norm = low(gated_out * inv_gate * gate_gain)
    return block_in + jnp.dot(y_norm, w_out, precision=highest)

def reference(block_in, norm_gain, w_zx, w_bc, w_dt, conv_x_w, conv_x_b, conv_bc_w, conv_bc_b, dt_bias, a_log, d_skip, gate_gain, w_out, cotangent):
    params = (norm_gain.astype(jnp.float32), w_zx.astype(jnp.float32), w_bc.astype(jnp.float32), w_dt.astype(jnp.float32), conv_x_w.astype(jnp.float32), conv_x_b.astype(jnp.float32), conv_bc_w.astype(jnp.float32), conv_bc_b.astype(jnp.float32), dt_bias.astype(jnp.float32), a_log.astype(jnp.float32), d_skip.astype(jnp.float32), gate_gain.astype(jnp.float32), w_out.astype(jnp.float32))
    group_rows = SEQ_DEV * SEQLEN
    grouped_in = block_in.astype(jnp.float32).reshape(N_TOK, group_rows, D)
    grouped_cot = cotangent.astype(jnp.float32).reshape(N_TOK, group_rows, D)

    def one_group(totals, group_item):
        group_in, group_cot = group_item
        group_out, pull_back = jax.vjp(layer, group_in, *params)
        gradients = pull_back(group_cot)
        totals = tuple((a + b for a, b in zip(totals, gradients[1:])))
        return (totals, (group_out, gradients[0]))
    zeros_init = tuple((jnp.zeros_like(p) for p in params))
    totals, (block_outs, d_inputs) = lax.scan(one_group, zeros_init, (grouped_in, grouped_cot))
    return (block_outs.reshape(TOKENS, D), d_inputs.reshape(TOKENS, D), totals[0], totals[1], totals[2], totals[3], totals[4], totals[5], totals[6], totals[7], totals[8], totals[9], totals[10], totals[11], totals[12])
```

```python
import functools

import jax
import jax.numpy as jnp
from jax import lax
from jax.experimental import pallas as pl
from jax.experimental.pallas import tpu as pltpu
from jax.sharding import PartitionSpec as P

HEADDIM = 64
STATE = 128
CONV = 4
INNER = 3072
CHUNK = 256
HALVES = 2
LANES = 128
HALO = 16

EPS = 1e-05
HIGHEST = lax.Precision.HIGHEST
F32 = jnp.float32
BF16 = jnp.bfloat16


def dot_nn(a, b, precision=None):
    return lax.dot_general(
        a, b, (((1,), (0,)), ((), ())), preferred_element_type=F32, precision=precision
    )


def dot_nt(a, b, precision=None):
    return lax.dot_general(
        a, b, (((1,), (1,)), ((), ())), preferred_element_type=F32, precision=precision
    )


def dot_tn(a, b):
    return lax.dot_general(a, b, (((0,), (0,)), ((), ())), preferred_element_type=F32)


def iota(shape, dim):
    return lax.broadcasted_iota(jnp.int32, shape, dim)


def sigmoid(v):
    return 1.0 / (1.0 + jnp.exp(-v))


def softplus(v):
    return jnp.maximum(v, 0.0) + jnp.log1p(jnp.exp(-jnp.abs(v)))


def head_spread(width):
    return (iota((LANES, width), 1) // HEADDIM == iota((LANES, width), 0)).astype(F32)


def bit_of(axis, bit):
    return (lax.axis_index(axis) // (1 << bit)) % 2


def swap(value, axis, bit):
    size = lax.axis_size(axis)
    return lax.ppermute(value, axis, [(i, i ^ (1 << bit)) for i in range(size)])


def grow(value, axis, bit, dim):
    other = swap(value, axis, bit)
    low = bit_of(axis, bit) == 0
    return jnp.where(
        low,
        jnp.concatenate([value, other], dim),
        jnp.concatenate([other, value], dim),
    )


def halve(value, axis, bit, dim):
    mine = bit_of(axis, bit)
    if dim < value.ndim - 1:
        half = value.shape[dim] // 2
        keep = lax.dynamic_slice_in_dim(value, mine * half, half, dim)
        send = lax.dynamic_slice_in_dim(value, (1 - mine) * half, half, dim)
    else:
        low, high = jnp.split(value, 2, axis=dim)
        keep = jnp.where(mine == 0, low, high)
        send = jnp.where(mine == 0, high, low)
    return keep.astype(F32) + swap(send.astype(BF16), axis, bit).astype(F32)


def add_pairs(value, axis, bits):
    for bit in bits:
        value = value + swap(value, axis, bit)
    return value


def conv_rows(cur, tail, weight, bias):
    rows = cur.shape[0]
    ext = jnp.concatenate([tail, cur], axis=0)
    out = bias + weight[CONV - 1 : CONV] * cur
    for k in range(CONV - 1):
        start = 8 - (CONV - 1) + k
        out = out + weight[k : k + 1] * ext[start : start + rows]
    return out


def state_kernel(
    xm_ref, xt_ref, bm_ref, bt_ref, par_ref, bcpar_ref, hp_ref,
    xs_ref, u_ref, cume_ref, dte_ref, bc_ref, cumt_ref, sloc_ref, fin_ref, dec_ref,
    state, dsum, ue,
):
    c = pl.program_id(0)
    q, width = xm_ref.shape

    @pl.when(c == 0)
    def _():
        state[...] = jnp.zeros_like(state)
        dsum[...] = jnp.zeros_like(dsum)

    dt = softplus(bm_ref[:, 2 * STATE :] + hp_ref[0:1, :])
    tri = (iota((q, q), 0) >= iota((q, q), 1)).astype(F32)
    cum = dot_nn(tri, dt * hp_ref[1:2, :], HIGHEST)
    cumt_ref[...] = cum.T[: cumt_ref.shape[0], :]
    spread = head_spread(width)
    cume_ref[...] = dot_nn(cum, spread, HIGHEST)
    dte_ref[...] = dot_nn(dt, spread, HIGHEST)
    end = cume_ref[q - 1 : q, :]

    bpre = conv_rows(
        bm_ref[:, : 2 * STATE], bt_ref[:, : 2 * STATE], bcpar_ref[0:CONV, :], bcpar_ref[CONV : CONV + 1, :]
    )
    bc_ref[...] = bpre * sigmoid(bpre)

    block = 2 * LANES

    def body(i, carry):
        sl = pl.ds(pl.multiple_of(i * block, block), block)
        pre = conv_rows(
            xm_ref[:, sl], xt_ref[:, sl], par_ref[0:CONV, sl], par_ref[CONV : CONV + 1, sl]
        )
        xs = pre * sigmoid(pre)
        u = xs * dte_ref[:, sl]
        xs_ref[:, sl] = xs
        u_ref[:, sl] = u.astype(BF16)
        cume = cume_ref[:, sl]
        ue[:, sl] = (u * jnp.exp(cume[q - 1 : q, :] - cume)).astype(BF16)
        return carry

    lax.fori_loop(0, width // block, body, 0)
    sloc_ref[0] = state[...]
    dec_ref[0] = jnp.exp(dsum[...])
    state[...] = jnp.exp(end) * state[...] + dot_nn(bc_ref[:, :STATE].T.astype(BF16), ue[...])
    dsum[...] = dsum[...] + end
    fin_ref[...] = state[...].astype(BF16)


def main_kernel(
    xs_ref, u_ref, cume_ref, cumt_ref, bc_ref, sloc_ref, sin_ref, dec_ref, z_ref, gyn_ref, par_ref,
    y_ref, stat_ref,
    gram, ya, acc_sq, acc_in,
):
    q, width = xs_ref.shape
    bmat = bc_ref[:, :STATE].astype(BF16)
    cmat = bc_ref[:, STATE:].astype(BF16)
    lower = iota((q, q), 0) >= iota((q, q), 1)
    gram[...] = jnp.where(lower, dot_nt(cmat, bmat), 0.0)
    entering = sloc_ref[0] + dec_ref[0, 0:1, :] * sin_ref[...].astype(F32)
    ya[...] = dot_nn(cmat, entering.astype(BF16))
    acc_sq[...] = jnp.zeros_like(acc_sq)
    acc_in[...] = jnp.zeros_like(acc_in)
    first = iota((q, LANES), 1) < HEADDIM

    def body(p, carry):
        sl = pl.ds(pl.multiple_of(p * LANES, LANES), LANES)
        cume = cume_ref[:, sl]
        u = u_ref[:, sl]
        y = jnp.exp(cume) * ya[:, sl] + par_ref[CONV + 2 : CONV + 3, sl] * xs_ref[:, sl]
        for s in range(2):
            gap = cume[:, HEADDIM * s : HEADDIM * s + 1] - cumt_ref[pl.ds(2 * p + s, 1), :]
            pairs = (gram[...] * jnp.exp(jnp.minimum(gap, 0.0))).astype(BF16)
            y = y + dot_nn(pairs, jnp.where(first == (s == 0), u, jnp.zeros_like(u)))
        y_ref[:, sl] = y
        z = z_ref[:, sl]
        gated = y * z * sigmoid(z)
        acc_sq[...] += gated * gated
        acc_in[...] += gated * gyn_ref[:, sl] * par_ref[CONV + 1 : CONV + 2, sl]
        return carry

    lax.fori_loop(0, width // LANES, body, 0)
    ones = jnp.ones((8, LANES), F32)
    sums_sq = dot_nt(ones, acc_sq[...], HIGHEST)
    sums_in = dot_nt(ones, acc_in[...], HIGHEST)
    stat_ref[...] = jnp.where(iota(sums_sq.shape, 0) == 0, sums_sq, sums_in)


def gate_kernel(
    y_ref, z_ref, gyn_ref, xs_ref, cume_ref, bc_ref, stat_ref, par_ref,
    yn_ref, gy_ref, dz_ref, gloc_ref, gin_ref, dec_ref, acc_ref,
    adj, dsum, ge,
):
    q, width = y_ref.shape

    @pl.when(pl.program_id(0) == 0)
    def _():
        adj[...] = jnp.zeros_like(adj)
        dsum[...] = jnp.zeros_like(dsum)
        acc_ref[...] = jnp.zeros_like(acc_ref)

    end = cume_ref[q - 1 : q, :]
    inv = jnp.broadcast_to(stat_ref[:, 0:1], (q, LANES))
    back = jnp.broadcast_to(stat_ref[:, 1:2], (q, LANES))

    def body(p, carry):
        sl = pl.ds(pl.multiple_of(p * LANES, LANES), LANES)
        y, z, gyn = y_ref[:, sl], z_ref[:, sl], gyn_ref[:, sl]
        sig = sigmoid(z)
        sil = z * sig
        gated = y * sil
        gain = par_ref[CONV + 1 : CONV + 2, sl]
        unit = gated * inv
        yn_ref[:, sl] = (unit * gain).astype(BF16)
        d_gated = inv * gyn * gain - gated * back
        gy = d_gated * sil
        gy_ref[:, sl] = gy
        dz_ref[:, sl] = (d_gated * y * (sig * (1.0 + z * (1.0 - sig)))).astype(BF16)
        ge[:, sl] = (gy * jnp.exp(cume_ref[:, sl])).astype(BF16)
        acc_ref[0:1, sl] += jnp.sum(gyn * unit, axis=0, keepdims=True)
        acc_ref[1:2, sl] += jnp.sum(gy * xs_ref[:, sl], axis=0, keepdims=True)
        return carry

    lax.fori_loop(0, width // LANES, body, 0)
    gloc_ref[0] = adj[...]
    dec_ref[0] = jnp.exp(dsum[...])
    adj[...] = jnp.exp(end) * adj[...] + dot_nn(bc_ref[:, STATE:].T.astype(BF16), ge[...])
    dsum[...] = dsum[...] + end
    gin_ref[...] = adj[...].astype(BF16)


def back_kernel(
    xm_ref, xt_ref, bm_ref, bt_ref, par_ref, bcpar_ref, hp_ref,
    cume_ref, dte_ref, cumt_ref, gy_ref, sloc_ref, sin_ref, sdec_ref, gloc_ref, gout_ref, gdec_ref,
    dx_ref, ds_ref, accx_ref, accb_ref, acch_ref,
    xs, u, dsil, ue, ge, dus, ya, qx, qb, gram, dgram, da, acc_x, acc_w, acc_g,
):
    step = pl.program_id(0)
    q, width = xm_ref.shape
    tokens = dx_ref.shape[0] - HALO
    c = tokens // q - 1 - step
    block = 2 * LANES

    @pl.when(step == 0)
    def _():
        accx_ref[...] = jnp.zeros_like(accx_ref)
        accb_ref[...] = jnp.zeros_like(accb_ref)
        acch_ref[...] = jnp.zeros_like(acch_ref)
        qx[q:, :] = jnp.zeros((8, width), F32)
        qb[q:, :] = jnp.zeros((8, 2 * STATE), F32)
        da[...] = jnp.zeros_like(da)
        ds_ref[...] = jnp.zeros_like(ds_ref)

    bpre = conv_rows(
        bm_ref[:, : 2 * STATE], bt_ref[:, : 2 * STATE], bcpar_ref[0:CONV, :], bcpar_ref[CONV : CONV + 1, :]
    )
    bsig = sigmoid(bpre)
    bc = bpre * bsig
    qb[0:q, :] = bsig * (1.0 + bpre * (1.0 - bsig))
    bmat, cmat = bc[:, :STATE].astype(BF16), bc[:, STATE:].astype(BF16)

    def conv_body(i, carry):
        sl = pl.ds(pl.multiple_of(i * block, block), block)
        pre = conv_rows(
            xm_ref[:, sl], xt_ref[:, sl], par_ref[0:CONV, sl], par_ref[CONV : CONV + 1, sl]
        )
        sig = sigmoid(pre)
        x = pre * sig
        xs[:, sl] = x
        dsil[:, sl] = sig * (1.0 + pre * (1.0 - sig))
        uu = x * dte_ref[:, sl]
        u[:, sl] = uu.astype(BF16)
        cume = cume_ref[:, sl]
        ue[:, sl] = (uu * jnp.exp(cume[q - 1 : q, :] - cume)).astype(BF16)
        ge[:, sl] = (gy_ref[:, sl] * jnp.exp(cume)).astype(BF16)
        return carry

    lax.fori_loop(0, width // block, conv_body, 0)

    end = cume_ref[q - 1 : q, :]
    adj = gloc_ref[0] + gdec_ref[0, 0:1, :] * gout_ref[...].astype(F32)
    entering = sloc_ref[0] + sdec_ref[0, 0:1, :] * sin_ref[...].astype(F32)
    kept = jnp.exp(end) * jnp.sum(adj * entering, axis=0, keepdims=True)
    adj_low, ent_low = adj.astype(BF16), entering.astype(BF16)
    dus[...] = dot_nn(bmat, adj_low)
    ya[...] = dot_nn(cmat, ent_low)
    db = dot_nt(ue[...], adj_low)
    dc = dot_nt(ge[...], ent_low)
    upper = iota((q, q), 1) >= iota((q, q), 0)
    gram[...] = jnp.where(upper, dot_nt(bmat, cmat), 0.0)
    dgram[...] = jnp.zeros_like(dgram)
    acc_x[...] = jnp.zeros_like(acc_x)
    acc_w[...] = jnp.zeros_like(acc_w)
    acc_g[...] = jnp.zeros_like(acc_g)
    later = (iota((q, q), 0) >= iota((q, q), 1)).astype(BF16)
    first = iota((q, LANES), 1) < HEADDIM

    def pair_body(p, carry):
        sl = pl.ds(pl.multiple_of(p * LANES, LANES), LANES)
        cume = cume_ref[:, sl]
        ul = u[:, sl]
        gy = gy_ref[:, sl]
        gl = gy.astype(BF16)
        du = jnp.zeros((q, LANES), F32)
        for s in range(2):
            mine = first == (s == 0)
            row = pl.ds(2 * p + s, 1)
            gap = cumt_ref[row, :] - cume[:, HEADDIM * s : HEADDIM * s + 1]
            decay = jnp.exp(jnp.minimum(gap, 0.0))
            pairs = gram[...] * decay
            dpairs = dot_nt(jnp.where(mine, ul, jnp.zeros_like(ul)), gl)
            dgram[...] += dpairs * decay
            through = dot_nn((dpairs * pairs).astype(BF16), later)
            da[row, :] = jnp.sum(
                jnp.where(iota((q, q), 0) < iota((q, q), 1), through, 0.0), axis=0, keepdims=True
            )
            du = du + dot_nn(pairs.astype(BF16), jnp.where(mine, gl, jnp.zeros_like(gl)))
        x = xs[:, sl]
        wide = dus[:, sl] * jnp.exp(cume[q - 1 : q, :] - cume)
        du = du + wide
        to_head = (iota((LANES, LANES), 1) == 2 * p + iota((LANES, LANES), 0) // HEADDIM).astype(BF16)
        dte = dte_ref[:, sl]
        acc_x[...] += dot_nn((x * du).astype(BF16), to_head)
        acc_w[...] += dot_nn((x * dte * wide).astype(BF16), to_head)
        acc_g[...] += dot_nn((gy * jnp.exp(cume) * ya[:, sl]).astype(BF16), to_head)
        qx[0:q, sl] = (dte * du + par_ref[CONV + 2 : CONV + 3, sl] * gy) * dsil[:, sl]
        return carry

    lax.fori_loop(0, width // LANES, pair_body, 0)

    def unconv_body(i, carry):
        sl = pl.ds(pl.multiple_of(i * block, block), block)
        weight = par_ref[0:CONV, sl]
        ext = qx[:, sl]
        cur = ext[0:q]
        dpre = weight[CONV - 1 : CONV] * cur
        for k in range(CONV - 1):
            dpre = dpre + weight[k : k + 1] * ext[CONV - 1 - k : CONV - 1 - k + q]
        dx_ref[pl.ds(pl.multiple_of(c * q, q), q), sl] = dpre.astype(BF16)
        past = jnp.concatenate([xt_ref[:, sl], xm_ref[:, sl]], axis=0)
        for k in range(CONV):
            start = 8 - (CONV - 1) + k
            accx_ref[k : k + 1, sl] += jnp.sum(cur * past[start : start + q], axis=0, keepdims=True)
        accx_ref[CONV : CONV + 1, sl] += jnp.sum(cur, axis=0, keepdims=True)
        head_rows = jnp.concatenate([jnp.zeros((HALO, block), F32), cur[0:8]], axis=0)
        before = jnp.zeros((HALO, block), F32)
        for k in range(CONV - 1):
            before = before + weight[k : k + 1] * head_rows[CONV - 1 - k : CONV - 1 - k + HALO]
        dx_ref[pl.ds(tokens, HALO), sl] = before.astype(BF16)
        qx[q:, sl] = cur[0:8]
        return carry

    lax.fori_loop(0, width // block, unconv_body, 0)

    dg = jnp.where(upper, dgram[...], 0.0)
    db = db + dot_nn(dg.astype(BF16), cmat)
    dc = dc + dot_nn(dg.T.astype(BF16), bmat)
    qb[0:q, 0:STATE] = qb[0:q, 0:STATE] * db
    qb[0:q, STATE:] = qb[0:q, STATE:] * dc
    weight = bcpar_ref[0:CONV, :]
    ext = qb[...]
    cur = ext[0:q]
    dpre = weight[CONV - 1 : CONV] * cur
    for k in range(CONV - 1):
        dpre = dpre + weight[k : k + 1] * ext[CONV - 1 - k : CONV - 1 - k + q]
    ds_ref[pl.ds(pl.multiple_of(c * q, q), q), 0 : 2 * STATE] = dpre.astype(BF16)
    past = jnp.concatenate([bt_ref[:, 0 : 2 * STATE], bm_ref[:, 0 : 2 * STATE]], axis=0)
    for k in range(CONV):
        start = 8 - (CONV - 1) + k
        accb_ref[k : k + 1, :] += jnp.sum(cur * past[start : start + q], axis=0, keepdims=True)
    accb_ref[CONV : CONV + 1, :] += jnp.sum(cur, axis=0, keepdims=True)
    head_rows = jnp.concatenate([jnp.zeros((HALO, 2 * STATE), F32), cur[0:8]], axis=0)
    before = jnp.zeros((HALO, 2 * STATE), F32)
    for k in range(CONV - 1):
        before = before + weight[k : k + 1] * head_rows[CONV - 1 - k : CONV - 1 - k + HALO]
    ds_ref[pl.ds(tokens, HALO), 0 : 2 * STATE] = before.astype(BF16)
    qb[q:, :] = cur[0:8]

    raw = bm_ref[:, 2 * STATE :] + hp_ref[0:1, :]
    dt = softplus(raw)
    rate = hp_ref[1:2, :]
    from_here = (iota((q, q), 1) >= iota((q, q), 0)).astype(F32)
    up_to_here = (iota((q, q), 1) < iota((q, q), 0)).astype(F32)
    kept_heads = dot_nt(jnp.broadcast_to(kept, (8, width)), head_spread(width), HIGHEST)
    total = (
        da[...].T
        + dot_nn(from_here, acc_g[...], HIGHEST)
        + dot_nn(up_to_here, acc_w[...], HIGHEST)
        + kept_heads[0:1, :]
    )
    d_raw = (acc_x[...] + rate * total) * sigmoid(raw)
    ds_ref[pl.ds(pl.multiple_of(c * q, q), q), 2 * STATE :] = d_raw.astype(BF16)
    acch_ref[0:1, :] += jnp.sum(d_raw, axis=0, keepdims=True)
    acch_ref[1:2, :] += rate * jnp.sum(dt * total, axis=0, keepdims=True)


def shape(dims, dtype):
    return jax.ShapeDtypeStruct(dims, dtype)


def whole(dims):
    return pl.BlockSpec(dims, lambda c: (0,) * len(dims))


def run(kernel, name, grid, in_specs, out_specs, out_shape, scratch, args, flops):
    return pl.pallas_call(
        kernel,
        grid=(grid,),
        in_specs=in_specs,
        out_specs=out_specs,
        out_shape=out_shape,
        scratch_shapes=scratch,
        name=name,
        compiler_params=pltpu.CompilerParams(
            dimension_semantics=("arbitrary",), vmem_limit_bytes=60 * 1024 * 1024
        ),
        cost_estimate=pl.CostEstimate(
            flops=flops, bytes_accessed=sum(a.size * a.dtype.itemsize for a in args), transcendentals=0
        ),
    )(*args)


def mixer_forward_state(x_ext, s_ext, par, bcpar, hp, tokens):
    width = x_ext.shape[1]
    small = s_ext.shape[1]
    n = tokens // CHUNK
    q = CHUNK
    tail = q // 8
    last = (tokens + HALO) // 8 - 1
    tail_map = lambda c: (jnp.where(c == 0, last, c * tail - 1), 0)
    heads_pad = -(-(width // HEADDIM) // 8) * 8
    return run(
        state_kernel,
        "scan_states",
        n,
        [
            pl.BlockSpec((q, width), lambda c: (c, 0)),
            pl.BlockSpec((8, width), tail_map),
            pl.BlockSpec((q, small), lambda c: (c, 0)),
            pl.BlockSpec((8, small), tail_map),
            whole(par.shape),
            whole(bcpar.shape),
            whole(hp.shape),
        ],
        [
            pl.BlockSpec((q, width), lambda c: (c, 0)),
            pl.BlockSpec((q, width), lambda c: (c, 0)),
            pl.BlockSpec((q, width), lambda c: (c, 0)),
            pl.BlockSpec((q, width), lambda c: (c, 0)),
            pl.BlockSpec((q, 2 * STATE), lambda c: (c, 0)),
            pl.BlockSpec((heads_pad, q), lambda c: (0, c)),
            pl.BlockSpec((1, STATE, width), lambda c: (c, 0, 0)),
            whole((STATE, width)),
            pl.BlockSpec((1, 1, width), lambda c: (c, 0, 0)),
        ],
        [
            shape((tokens, width), F32),
            shape((tokens, width), BF16),
            shape((tokens, width), F32),
            shape((tokens, width), F32),
            shape((tokens, 2 * STATE), F32),
            shape((heads_pad, tokens), F32),
            shape((n, STATE, width), F32),
            shape((STATE, width), BF16),
            shape((n, 1, width), F32),
        ],
        [
            pltpu.VMEM((STATE, width), F32),
            pltpu.VMEM((1, width), F32),
            pltpu.VMEM((q, width), BF16),
        ],
        (x_ext, x_ext, s_ext, s_ext, par, bcpar, hp),
        int(3e9),
    )


def mixer_forward_main(xs, u, cume, cumt, bc, sloc, sin, dec, z, gyn, par):
    tokens, width = xs.shape
    q = CHUNK
    n = tokens // q
    rows = pl.BlockSpec((q, width), lambda c: (c, 0))
    return run(
        main_kernel,
        "scan_outputs",
        n,
        [
            rows,
            rows,
            rows,
            pl.BlockSpec((cumt.shape[0], q), lambda c: (0, c)),
            pl.BlockSpec((q, 2 * STATE), lambda c: (c, 0)),
            pl.BlockSpec((1, STATE, width), lambda c: (c, 0, 0)),
            whole(sin.shape),
            pl.BlockSpec((1, 1, width), lambda c: (c, 0, 0)),
            rows,
            rows,
            whole(par.shape),
        ],
        [rows, pl.BlockSpec((8, q), lambda c: (0, c))],
        [shape((tokens, width), F32), shape((8, tokens), F32)],
        [
            pltpu.VMEM((q, q), F32),
            pltpu.VMEM((q, width), F32),
            pltpu.VMEM((q, LANES), F32),
            pltpu.VMEM((q, LANES), F32),
        ],
        (xs, u, cume, cumt, bc, sloc, sin, dec, z, gyn, par),
        int(10e9),
    )


def mixer_backward_gate(y, z, gyn, xs, cume, bc, stat, par):
    tokens, width = y.shape
    q = CHUNK
    n = tokens // q
    rows = pl.BlockSpec((q, width), lambda c: (n - 1 - c, 0))
    return run(
        gate_kernel,
        "gate_back",
        n,
        [
            rows,
            rows,
            rows,
            rows,
            rows,
            pl.BlockSpec((q, 2 * STATE), lambda c: (n - 1 - c, 0)),
            pl.BlockSpec((q, 8), lambda c: (n - 1 - c, 0)),
            whole(par.shape),
        ],
        [
            rows,
            rows,
            rows,
            pl.BlockSpec((1, STATE, width), lambda c: (n - 1 - c, 0, 0)),
            whole((STATE, width)),
            pl.BlockSpec((1, 1, width), lambda c: (n - 1 - c, 0, 0)),
            whole((8, width)),
        ],
        [
            shape((tokens, width), BF16),
            shape((tokens, width), F32),
            shape((tokens, width), BF16),
            shape((n, STATE, width), F32),
            shape((STATE, width), BF16),
            shape((n, 1, width), F32),
            shape((8, width), F32),
        ],
        [
            pltpu.VMEM((STATE, width), F32),
            pltpu.VMEM((1, width), F32),
            pltpu.VMEM((q, width), BF16),
        ],
        (y, z, gyn, xs, cume, bc, stat, par),
        int(5e9),
    )


def mixer_backward_main(
    x_ext, s_ext, par, bcpar, hp, cume, dte, cumt, gy, sloc, sin, sdec, gloc, gout, gdec
):
    tokens, width = cume.shape
    small = s_ext.shape[1]
    q = CHUNK
    n = tokens // q
    tail = q // 8
    last = (tokens + HALO) // 8 - 1
    rows = pl.BlockSpec((q, width), lambda c: (n - 1 - c, 0))
    tail_map = lambda c: (jnp.where(c == n - 1, last, (n - 1 - c) * tail - 1), 0)
    states = pl.BlockSpec((1, STATE, width), lambda c: (n - 1 - c, 0, 0))
    decays = pl.BlockSpec((1, 1, width), lambda c: (n - 1 - c, 0, 0))
    return run(
        back_kernel,
        "scan_back",
        n,
        [
            rows,
            pl.BlockSpec((8, width), tail_map),
            pl.BlockSpec((q, small), lambda c: (n - 1 - c, 0)),
            pl.BlockSpec((8, small), tail_map),
            whole(par.shape),
            whole(bcpar.shape),
            whole(hp.shape),
            rows,
            rows,
            pl.BlockSpec((cumt.shape[0], q), lambda c: (0, n - 1 - c)),
            rows,
            states,
            whole(sin.shape),
            decays,
            states,
            whole(gout.shape),
            decays,
        ],
        [
            whole((tokens + HALO, width)),
            whole((tokens + HALO, small)),
            whole((8, width)),
            whole((8, 2 * STATE)),
            whole((8, LANES)),
        ],
        [
            shape((tokens + HALO, width), BF16),
            shape((tokens + HALO, small), BF16),
            shape((8, width), F32),
            shape((8, 2 * STATE), F32),
            shape((8, LANES), F32),
        ],
        [
            pltpu.VMEM((q, width), F32),
            pltpu.VMEM((q, width), BF16),
            pltpu.VMEM((q, width), F32),
            pltpu.VMEM((q, width), BF16),
            pltpu.VMEM((q, width), BF16),
            pltpu.VMEM((q, width), F32),
            pltpu.VMEM((q, width), F32),
            pltpu.VMEM((q + 8, width), F32),
            pltpu.VMEM((q + 8, 2 * STATE), F32),
            pltpu.VMEM((q, q), F32),
            pltpu.VMEM((q, q), F32),
            pltpu.VMEM((LANES, q), F32),
            pltpu.VMEM((q, LANES), F32),
            pltpu.VMEM((q, LANES), F32),
            pltpu.VMEM((q, LANES), F32),
        ],
        (x_ext, x_ext, s_ext, s_ext, par, bcpar, hp, cume, dte, cumt, gy, sloc, sin, sdec, gloc, gout, gdec),
        int(30e9),
    )


def per_device(
    block_in,
    norm_gain,
    w_zx,
    w_bc,
    w_dt,
    conv_x_w,
    conv_x_b,
    conv_bc_w,
    conv_bc_b,
    dt_bias,
    a_log,
    d_skip,
    gate_gain,
    w_out,
    cotangent,
):
    head_size = lax.axis_size("head")
    tok_size = lax.axis_size("tok")
    sets = head_size // HALVES
    row_bits = range(sets.bit_length() - 1)
    half_bit = sets.bit_length() - 1
    head_bits = range(head_size.bit_length() - 1)
    tok_bits = range(tok_size.bit_length() - 1)
    nbits = len(tok_bits)
    half = bit_of("head", half_bit)
    own_rows, model = block_in.shape
    share, _, own_width = w_zx.shape
    own_heads = w_dt.shape[1]
    tokens = own_rows * sets
    heads = own_heads * HALVES
    forward = list(tok_bits)[1:] + [0]
    other = list(tok_bits)[1:][::-1] + [0]

    gain = norm_gain[None, :]
    for bit in head_bits:
        gain = grow(gain, "head", bit, 1)
    gain = gain.astype(F32)

    tail = block_in[own_rows - HALO :]
    halo = jnp.zeros_like(tail)
    for o in range(sets):
        halo = halo + lax.ppermute(tail, "head", [(sets - 1, sets + o)])

    def all_rows(value):
        for bit in row_bits:
            value = grow(value, "head", bit, 0)
        return value

    def all_features(piece, order):
        piece = piece.reshape((1,) * nbits + piece.shape)
        for bit in order:
            piece = grow(piece, "tok", bit, nbits - 1 - bit)
        return piece.reshape(model, piece.shape[-1])

    rows = all_rows(block_in)
    wdt = grow(w_dt, "head", half_bit, 1)
    small_piece = jnp.concatenate([w_bc, jnp.pad(wdt, ((0, 0), (0, LANES - heads)))], axis=1)
    w_small = all_features(small_piece, forward)
    w_x = all_features(grow(w_zx[:, 1], "head", half_bit, 1), forward)
    cot = all_rows(cotangent)
    w_z = all_features(grow(w_zx[:, 0], "head", half_bit, 1), other)
    w_o = all_features(grow(w_out.T, "head", half_bit, 1), forward)

    def lane_pad(v):
        return jnp.pad(v, (0, LANES - v.shape[0]))

    heads_row = jnp.concatenate([lane_pad(dt_bias), lane_pad(a_log), lane_pad(d_skip)])
    own_par = jnp.concatenate(
        [
            conv_x_w,
            conv_x_b[None],
            gate_gain[None],
            jnp.repeat(d_skip, HEADDIM)[None],
            jnp.pad(heads_row, (0, own_width - heads_row.shape[0]))[None],
        ]
    )
    par = grow(own_par, "head", half_bit, 1)

    def of_heads(start):
        pieces = [
            par[CONV + 3, i * own_width + start : i * own_width + start + own_heads] for i in range(HALVES)
        ]
        return jnp.concatenate(pieces)

    rate = -jnp.exp(of_heads(LANES))
    hp = jnp.stack([lane_pad(of_heads(0)), lane_pad(rate)] + [jnp.zeros((LANES,), F32)] * 6)
    bcpar = jnp.concatenate([conv_bc_w, conv_bc_b[None], jnp.zeros((3, 2 * STATE), F32)])

    def norm(value):
        wide = value.astype(F32)
        inv = lax.rsqrt(jnp.mean(wide * wide, axis=1, keepdims=True) + EPS)
        return wide, inv, (wide * inv * gain).astype(BF16)

    rows_wide, inv_rms, normed = norm(rows)
    normed_ext = jnp.concatenate([normed, norm(halo)[2]], axis=0)
    s_ext = dot_nn(normed_ext, w_small)
    x_ext = dot_nn(normed_ext, w_x)
    xs, u, cume, dte, bc, cumt, sloc, fin, sdec = mixer_forward_state(x_ext, s_ext, par, bcpar, hp, tokens)
    to_next = [(i, i + sets) for i in range(sets)]
    to_prev = [(i + sets, i) for i in range(sets)]
    sin = lax.ppermute(fin, "head", to_next)
    z = dot_nn(normed, w_z)
    gyn = dot_nn(cot, w_o)
    y, stat = mixer_forward_main(xs, u, cume, cumt, bc, sloc, sin, sdec, z, gyn, par)
    stat = add_pairs(stat, "head", row_bits).T
    inv_gate = lax.rsqrt(stat[:, 0:1] / INNER + EPS)
    stat = jnp.concatenate(
        [inv_gate, inv_gate * inv_gate * inv_gate * stat[:, 1:2] / INNER, stat[:, 2:]], axis=1
    )
    yn, gy, dz, gloc, gin, gdec, acc_gate = mixer_backward_gate(y, z, gyn, xs, cume, bc, stat, par)
    gout = lax.ppermute(gin, "head", to_prev)

    def spread_rows(grad, order):
        grad = grad.reshape((2,) * nbits + (share, grad.shape[-1]))
        for bit in order[::-1]:
            grad = halve(grad, "tok", bit, nbits - 1 - bit)
        return grad.reshape(share, grad.shape[-1])

    def own_columns(grad):
        return halve(grad, "head", half_bit, 1)

    def own_row_sum(value):
        for bit in list(row_bits)[::-1]:
            value = halve(value, "head", bit, 0)
        return value

    branch = dot_nt(yn, w_o)
    block_out = block_in.astype(F32) + own_row_sum(branch)
    d_w_o = own_columns(spread_rows(dot_tn(cot, yn), forward)).T
    d_w_z = own_columns(spread_rows(dot_tn(normed, dz), other))
    d_normed_z = dot_nt(dz, w_z)

    dx, ds, acc_x, acc_b, acc_h = mixer_backward_main(
        x_ext, s_ext, par, bcpar, hp, cume, dte, cumt, gy, sloc, sin, sdec, gloc, gout, gdec
    )
    d_w_x = own_columns(spread_rows(dot_tn(normed_ext, dx), forward))
    d_small = spread_rows(dot_tn(normed_ext, ds), other)
    d_norm_ext = dot_nt(dx, w_x) + dot_nt(ds, w_small)
    d_w_bc = add_pairs(d_small[:, : 2 * STATE], "head", head_bits)
    d_w_dt = own_columns(
        jnp.concatenate(
            [
                jnp.pad(
                    d_small[:, 2 * STATE + i * own_heads : 2 * STATE + (i + 1) * own_heads],
                    ((0, 0), (0, LANES - own_heads)),
                )
                for i in range(HALVES)
            ],
            axis=1,
        )
    )[:, :own_heads]

    from_next = lax.ppermute(d_norm_ext[tokens:].astype(BF16), "head", to_prev).astype(F32)
    d_normed = d_normed_z + d_norm_ext[:tokens]
    d_normed = jnp.concatenate([d_normed[: tokens - HALO], d_normed[tokens - HALO :] + from_next])
    gain_part = jnp.sum(d_normed * rows_wide * inv_rms, axis=0)
    d_own = own_row_sum(d_normed)
    wide, inv, _ = norm(block_in)
    scaled = d_own * gain
    d_block_in = (
        cotangent.astype(F32)
        + inv * scaled
        - wide * (inv * inv * inv * jnp.sum(scaled * wide, axis=1, keepdims=True) / model)
    )

    per_channel = jnp.concatenate(
        [
            acc_x[: CONV + 1],
            acc_gate[0:1],
            jnp.concatenate(
                [
                    jnp.pad(
                        jnp.concatenate(
                            [
                                lane_pad(acc_h[0, i * own_heads : (i + 1) * own_heads]),
                                lane_pad(acc_h[1, i * own_heads : (i + 1) * own_heads]),
                                lane_pad(
                                    jnp.sum(
                                        acc_gate[1, i * own_width : (i + 1) * own_width].reshape(own_heads, HEADDIM),
                                        axis=1,
                                    )
                                ),
                            ]
                        ),
                        (0, own_width - 3 * LANES),
                    )
                    for i in range(HALVES)
                ]
            )[None],
        ]
    )

    def half_sum(value):
        low, high = jnp.split(value, 2, axis=1)
        keep = jnp.where(half == 0, low, high)
        return keep + swap(jnp.where(half == 0, high, low), "head", half_bit)

    own_sums = half_sum(per_channel)
    over_heads = jnp.concatenate([gain_part, acc_b[: CONV + 1].reshape(-1)])
    over_heads = add_pairs(over_heads, "head", head_bits)
    flat = jnp.concatenate([own_sums.reshape(-1), over_heads])
    flat = add_pairs(flat, "tok", tok_bits)
    own_size = own_sums.size
    own_sums = flat[:own_size].reshape(own_sums.shape)
    all_gain = flat[own_size : own_size + model]
    bc_sums = flat[own_size + model :].reshape(CONV + 1, 2 * STATE)
    gain_share = norm_gain.shape[0]
    d_norm_gain = lax.dynamic_slice_in_dim(all_gain, lax.axis_index("head") * gain_share, gain_share, 0)
    return (
        block_out,
        d_block_in,
        d_norm_gain,
        jnp.stack([d_w_z, d_w_x], axis=1),
        d_w_bc,
        d_w_dt,
        own_sums[:CONV],
        own_sums[CONV],
        bc_sums[:CONV],
        bc_sums[CONV],
        own_sums[CONV + 2, :own_heads],
        own_sums[CONV + 2, LANES : LANES + own_heads],
        own_sums[CONV + 2, 2 * LANES : 2 * LANES + own_heads],
        own_sums[CONV + 1],
        d_w_o,
    )


def solution(mesh):
    placed = (
        P(("tok", "head"), None),
        P("head"),
        P("tok", None, "head"),
        P("tok", None),
        P("tok", "head"),
        P(None, "head"),
        P("head"),
        P(),
        P(),
        P("head"),
        P("head"),
        P("head"),
        P("head"),
        P("head", "tok"),
        P(("tok", "head"), None),
    )
    return jax.shard_map(
        per_device,
        mesh=mesh,
        in_specs=placed,
        out_specs=(
            P(("tok", "head"), None),
            P(("tok", "head"), None),
            P("head"),
            P("tok", None, "head"),
            P("tok", None),
            P("tok", "head"),
            P(None, "head"),
            P("head"),
            P(),
            P(),
            P("head"),
            P("head"),
            P("head"),
            P("head"),
            P("head", "tok"),
        ),
        check_vma=False,
    )
```

```python
import functools

import jax
import jax.numpy as jnp
from jax import lax
from jax.experimental import pallas as pl
from jax.experimental.pallas import tpu as pltpu
from jax.sharding import PartitionSpec as P

HEADDIM = 64
STATE = 128
CONV = 4
INNER = 3072
CHUNK = 256
HALVES = 2
LANES = 128
HALO = 16

EPS = 1e-05
HIGHEST = lax.Precision.HIGHEST
F32 = jnp.float32
BF16 = jnp.bfloat16


def dot_nn(a, b, precision=None):
    return lax.dot_general(
        a, b, (((1,), (0,)), ((), ())), preferred_element_type=F32, precision=precision
    )


def dot_nt(a, b, precision=None):
    return lax.dot_general(
        a, b, (((1,), (1,)), ((), ())), preferred_element_type=F32, precision=precision
    )


def dot_tn(a, b):
    return lax.dot_general(a, b, (((0,), (0,)), ((), ())), preferred_element_type=F32)


def iota(shape, dim):
    return lax.broadcasted_iota(jnp.int32, shape, dim)


def sigmoid(v):
    return 1.0 / (1.0 + jnp.exp(-v))


def softplus(v):
    return jnp.maximum(v, 0.0) + jnp.log1p(jnp.exp(-jnp.abs(v)))


def head_spread(width):
    return (iota((LANES, width), 1) // HEADDIM == iota((LANES, width), 0)).astype(F32)


def bit_of(axis, bit):
    return (lax.axis_index(axis) // (1 << bit)) % 2


def swap(value, axis, bit):
    size = lax.axis_size(axis)
    return lax.ppermute(value, axis, [(i, i ^ (1 << bit)) for i in range(size)])


def grow(value, axis, bit, dim):
    other = swap(value, axis, bit)
    low = bit_of(axis, bit) == 0
    return jnp.where(
        low,
        jnp.concatenate([value, other], dim),
        jnp.concatenate([other, value], dim),
    )


def halve(value, axis, bit, dim):
    mine = bit_of(axis, bit)
    if dim < value.ndim - 1:
        half = value.shape[dim] // 2
        keep = lax.dynamic_slice_in_dim(value, mine * half, half, dim)
        send = lax.dynamic_slice_in_dim(value, (1 - mine) * half, half, dim)
    else:
        low, high = jnp.split(value, 2, axis=dim)
        keep = jnp.where(mine == 0, low, high)
        send = jnp.where(mine == 0, high, low)
    return keep.astype(F32) + swap(send.astype(BF16), axis, bit).astype(F32)


def add_pairs(value, axis, bits):
    for bit in bits:
        value = value + swap(value, axis, bit)
    return value


def conv_rows(cur, tail, weight, bias):
    rows = cur.shape[0]
    ext = jnp.concatenate([tail, cur], axis=0)
    out = bias + weight[CONV - 1 : CONV] * cur
    for k in range(CONV - 1):
        start = 8 - (CONV - 1) + k
        out = out + weight[k : k + 1] * ext[start : start + rows]
    return out


def step_lanes(ref, width):
    own_heads = width // (HALVES * HEADDIM)
    base = 2 * STATE
    return ref[:, base : base + LANES] + pltpu.roll(ref[:, base + LANES : base + 2 * LANES], own_heads, 1)


def state_kernel(
    xm_ref, xt_ref, bm_ref, bt_ref, par_ref, bcpar_ref, hp_ref,
    xs_ref, u_ref, cume_ref, dte_ref, bc_ref, cumt_ref, sloc_ref, fin_ref, dec_ref,
    state, dsum, ue,
):
    c = pl.program_id(0)
    q, width = xm_ref.shape

    @pl.when(c == 0)
    def _():
        state[...] = jnp.zeros_like(state)
        dsum[...] = jnp.zeros_like(dsum)

    dt = softplus(step_lanes(bm_ref, par_ref.shape[1]) + hp_ref[0:1, :])
    tri = (iota((q, q), 0) >= iota((q, q), 1)).astype(F32)
    cum = dot_nn(tri, dt * hp_ref[1:2, :], HIGHEST)
    cumt_ref[...] = cum.T[: cumt_ref.shape[0], :]
    spread = head_spread(width)
    cume_ref[...] = dot_nn(cum, spread, HIGHEST)
    dte_ref[...] = dot_nn(dt, spread, HIGHEST)
    end = cume_ref[q - 1 : q, :]

    bpre = conv_rows(
        bm_ref[:, : 2 * STATE], bt_ref[:, : 2 * STATE], bcpar_ref[0:CONV, :], bcpar_ref[CONV : CONV + 1, :]
    )
    bc_ref[...] = bpre * sigmoid(bpre)

    block = 2 * LANES

    def body(i, carry):
        sl = pl.ds(pl.multiple_of(i * block, block), block)
        pre = conv_rows(
            xm_ref[:, sl], xt_ref[:, sl], par_ref[0:CONV, sl], par_ref[CONV : CONV + 1, sl]
        )
        xs = pre * sigmoid(pre)
        u = xs * dte_ref[:, sl]
        xs_ref[:, sl] = xs
        u_ref[:, sl] = u.astype(BF16)
        cume = cume_ref[:, sl]
        ue[:, sl] = (u * jnp.exp(cume[q - 1 : q, :] - cume)).astype(BF16)
        return carry

    lax.fori_loop(0, width // block, body, 0)
    sloc_ref[0] = state[...]
    dec_ref[0] = jnp.exp(dsum[...])
    state[...] = jnp.exp(end) * state[...] + dot_nn(bc_ref[:, :STATE].T.astype(BF16), ue[...])
    dsum[...] = dsum[...] + end
    fin_ref[...] = state[...].astype(BF16)


def main_kernel(
    xs_ref, u_ref, cume_ref, cumt_ref, bc_ref, sloc_ref, sin_ref, dec_ref, z_ref, gyn_ref, par_ref,
    y_ref, stat_ref,
    gram, ya, acc_sq, acc_in,
):
    q, width = xs_ref.shape
    bmat = bc_ref[:, :STATE].astype(BF16)
    cmat = bc_ref[:, STATE:].astype(BF16)
    lower = iota((q, q), 0) >= iota((q, q), 1)
    gram[...] = jnp.where(lower, dot_nt(cmat, bmat), 0.0)
    entering = sloc_ref[0] + dec_ref[0, 0:1, :] * sin_ref[...].astype(F32)
    ya[...] = dot_nn(cmat, entering.astype(BF16))
    acc_sq[...] = jnp.zeros_like(acc_sq)
    acc_in[...] = jnp.zeros_like(acc_in)
    first = iota((q, LANES), 1) < HEADDIM

    def body(p, carry):
        sl = pl.ds(pl.multiple_of(p * LANES, LANES), LANES)
        cume = cume_ref[:, sl]
        u = u_ref[:, sl]
        y = jnp.exp(cume) * ya[:, sl] + par_ref[CONV + 2 : CONV + 3, sl] * xs_ref[:, sl]
        for s in range(2):
            gap = cume[:, HEADDIM * s : HEADDIM * s + 1] - cumt_ref[pl.ds(2 * p + s, 1), :]
            pairs = (gram[...] * jnp.exp(jnp.minimum(gap, 0.0))).astype(BF16)
            y = y + dot_nn(pairs, jnp.where(first == (s == 0), u, jnp.zeros_like(u)))
        y_ref[:, sl] = y
        z = z_ref[:, sl]
        gated = y * z * sigmoid(z)
        acc_sq[...] += gated * gated
        acc_in[...] += gated * gyn_ref[:, sl] * par_ref[CONV + 1 : CONV + 2, sl]
        return carry

    lax.fori_loop(0, width // LANES, body, 0)
    ones = jnp.ones((8, LANES), F32)
    sums_sq = dot_nt(ones, acc_sq[...], HIGHEST)
    sums_in = dot_nt(ones, acc_in[...], HIGHEST)
    stat_ref[...] = jnp.where(iota(sums_sq.shape, 0) == 0, sums_sq, sums_in)


def gate_kernel(
    y_ref, z_ref, gyn_ref, xs_ref, cume_ref, bc_ref, stat_ref, par_ref,
    yn_ref, gy_ref, dz_ref, gloc_ref, gin_ref, dec_ref, acc_ref,
    adj, dsum, ge,
):
    q, width = y_ref.shape

    @pl.when(pl.program_id(0) == 0)
    def _():
        adj[...] = jnp.zeros_like(adj)
        dsum[...] = jnp.zeros_like(dsum)
        acc_ref[...] = jnp.zeros_like(acc_ref)

    end = cume_ref[q - 1 : q, :]
    inv = jnp.broadcast_to(stat_ref[:, 0:1], (q, LANES))
    back = jnp.broadcast_to(stat_ref[:, 1:2], (q, LANES))

    def body(p, carry):
        sl = pl.ds(pl.multiple_of(p * LANES, LANES), LANES)
        y, z, gyn = y_ref[:, sl], z_ref[:, sl], gyn_ref[:, sl]
        sig = sigmoid(z)
        sil = z * sig
        gated = y * sil
        gain = par_ref[CONV + 1 : CONV + 2, sl]
        unit = gated * inv
        yn_ref[:, sl] = (unit * gain).astype(BF16)
        d_gated = inv * gyn * gain - gated * back
        gy = d_gated * sil
        gy_ref[:, sl] = gy
        dz_ref[:, sl] = (d_gated * y * (sig * (1.0 + z * (1.0 - sig)))).astype(BF16)
        ge[:, sl] = (gy * jnp.exp(cume_ref[:, sl])).astype(BF16)
        acc_ref[0:1, sl] += jnp.sum(gyn * unit, axis=0, keepdims=True)
        acc_ref[1:2, sl] += jnp.sum(gy * xs_ref[:, sl], axis=0, keepdims=True)
        return carry

    lax.fori_loop(0, width // LANES, body, 0)
    gloc_ref[0] = adj[...]
    dec_ref[0] = jnp.exp(dsum[...])
    adj[...] = jnp.exp(end) * adj[...] + dot_nn(bc_ref[:, STATE:].T.astype(BF16), ge[...])
    dsum[...] = dsum[...] + end
    gin_ref[...] = adj[...].astype(BF16)


def back_kernel(
    xm_ref, xt_ref, bm_ref, bt_ref, par_ref, bcpar_ref, hp_ref,
    cume_ref, dte_ref, cumt_ref, gy_ref, sloc_ref, sin_ref, sdec_ref, gloc_ref, gout_ref, gdec_ref,
    dx_ref, ds_ref, accx_ref, accb_ref, acch_ref,
    xs, u, dsil, ue, ge, dus, ya, qx, qb, gram, dgram, da, acc_x, acc_w, acc_g,
):
    step = pl.program_id(0)
    q, width = xm_ref.shape
    tokens = dx_ref.shape[0] - HALO
    c = tokens // q - 1 - step
    block = 2 * LANES

    @pl.when(step == 0)
    def _():
        accx_ref[...] = jnp.zeros_like(accx_ref)
        accb_ref[...] = jnp.zeros_like(accb_ref)
        acch_ref[...] = jnp.zeros_like(acch_ref)
        qx[q:, :] = jnp.zeros((8, width), F32)
        qb[q:, :] = jnp.zeros((8, 2 * STATE), F32)
        da[...] = jnp.zeros_like(da)
        ds_ref[...] = jnp.zeros_like(ds_ref)

    bpre = conv_rows(
        bm_ref[:, : 2 * STATE], bt_ref[:, : 2 * STATE], bcpar_ref[0:CONV, :], bcpar_ref[CONV : CONV + 1, :]
    )
    bsig = sigmoid(bpre)
    bc = bpre * bsig
    qb[0:q, :] = bsig * (1.0 + bpre * (1.0 - bsig))
    bmat, cmat = bc[:, :STATE].astype(BF16), bc[:, STATE:].astype(BF16)

    def conv_body(i, carry):
        sl = pl.ds(pl.multiple_of(i * block, block), block)
        pre = conv_rows(
            xm_ref[:, sl], xt_ref[:, sl], par_ref[0:CONV, sl], par_ref[CONV : CONV + 1, sl]
        )
        sig = sigmoid(pre)
        x = pre * sig
        xs[:, sl] = x
        dsil[:, sl] = sig * (1.0 + pre * (1.0 - sig))
        uu = x * dte_ref[:, sl]
        u[:, sl] = uu.astype(BF16)
        cume = cume_ref[:, sl]
        ue[:, sl] = (uu * jnp.exp(cume[q - 1 : q, :] - cume)).astype(BF16)
        ge[:, sl] = (gy_ref[:, sl] * jnp.exp(cume)).astype(BF16)
        return carry

    lax.fori_loop(0, width // block, conv_body, 0)

    end = cume_ref[q - 1 : q, :]
    adj = gloc_ref[0] + gdec_ref[0, 0:1, :] * gout_ref[...].astype(F32)
    entering = sloc_ref[0] + sdec_ref[0, 0:1, :] * sin_ref[...].astype(F32)
    kept = jnp.exp(end) * jnp.sum(adj * entering, axis=0, keepdims=True)
    adj_low, ent_low = adj.astype(BF16), entering.astype(BF16)
    dus[...] = dot_nn(bmat, adj_low)
    ya[...] = dot_nn(cmat, ent_low)
    db = dot_nt(ue[...], adj_low)
    dc = dot_nt(ge[...], ent_low)
    upper = iota((q, q), 1) >= iota((q, q), 0)
    gram[...] = jnp.where(upper, dot_nt(bmat, cmat), 0.0)
    dgram[...] = jnp.zeros_like(dgram)
    acc_x[...] = jnp.zeros_like(acc_x)
    acc_w[...] = jnp.zeros_like(acc_w)
    acc_g[...] = jnp.zeros_like(acc_g)
    later = (iota((q, q), 0) >= iota((q, q), 1)).astype(BF16)
    first = iota((q, LANES), 1) < HEADDIM

    def pair_body(p, carry):
        sl = pl.ds(pl.multiple_of(p * LANES, LANES), LANES)
        cume = cume_ref[:, sl]
        ul = u[:, sl]
        gy = gy_ref[:, sl]
        gl = gy.astype(BF16)
        du = jnp.zeros((q, LANES), F32)
        for s in range(2):
            mine = first == (s == 0)
            row = pl.ds(2 * p + s, 1)
            gap = cumt_ref[row, :] - cume[:, HEADDIM * s : HEADDIM * s + 1]
            decay = jnp.exp(jnp.minimum(gap, 0.0))
            pairs = gram[...] * decay
            dpairs = dot_nt(jnp.where(mine, ul, jnp.zeros_like(ul)), gl)
            dgram[...] += dpairs * decay
            through = dot_nn((dpairs * pairs).astype(BF16), later)
            da[row, :] = jnp.sum(
                jnp.where(iota((q, q), 0) < iota((q, q), 1), through, 0.0), axis=0, keepdims=True
            )
            du = du + dot_nn(pairs.astype(BF16), jnp.where(mine, gl, jnp.zeros_like(gl)))
        x = xs[:, sl]
        wide = dus[:, sl] * jnp.exp(cume[q - 1 : q, :] - cume)
        du = du + wide
        to_head = (iota((LANES, LANES), 1) == 2 * p + iota((LANES, LANES), 0) // HEADDIM).astype(BF16)
        dte = dte_ref[:, sl]
        acc_x[...] += dot_nn((x * du).astype(BF16), to_head)
        acc_w[...] += dot_nn((x * dte * wide).astype(BF16), to_head)
        acc_g[...] += dot_nn((gy * jnp.exp(cume) * ya[:, sl]).astype(BF16), to_head)
        qx[0:q, sl] = (dte * du + par_ref[CONV + 2 : CONV + 3, sl] * gy) * dsil[:, sl]
        return carry

    lax.fori_loop(0, width // LANES, pair_body, 0)

    def unconv_body(i, carry):
        sl = pl.ds(pl.multiple_of(i * block, block), block)
        weight = par_ref[0:CONV, sl]
        ext = qx[:, sl]
        cur = ext[0:q]
        dpre = weight[CONV - 1 : CONV] * cur
        for k in range(CONV - 1):
            dpre = dpre + weight[k : k + 1] * ext[CONV - 1 - k : CONV - 1 - k + q]
        dx_ref[pl.ds(pl.multiple_of(c * q, q), q), sl] = dpre.astype(BF16)
        past = jnp.concatenate([xt_ref[:, sl], xm_ref[:, sl]], axis=0)
        for k in range(CONV):
            start = 8 - (CONV - 1) + k
            accx_ref[k : k + 1, sl] += jnp.sum(cur * past[start : start + q], axis=0, keepdims=True)
        accx_ref[CONV : CONV + 1, sl] += jnp.sum(cur, axis=0, keepdims=True)
        head_rows = jnp.concatenate([jnp.zeros((HALO, block), F32), cur[0:8]], axis=0)
        before = jnp.zeros((HALO, block), F32)
        for k in range(CONV - 1):
            before = before + weight[k : k + 1] * head_rows[CONV - 1 - k : CONV - 1 - k + HALO]
        dx_ref[pl.ds(tokens, HALO), sl] = before.astype(BF16)
        qx[q:, sl] = cur[0:8]
        return carry

    lax.fori_loop(0, width // block, unconv_body, 0)

    dg = jnp.where(upper, dgram[...], 0.0)
    db = db + dot_nn(dg.astype(BF16), cmat)
    dc = dc + dot_nn(dg.T.astype(BF16), bmat)
    qb[0:q, 0:STATE] = qb[0:q, 0:STATE] * db
    qb[0:q, STATE:] = qb[0:q, STATE:] * dc
    weight = bcpar_ref[0:CONV, :]
    ext = qb[...]
    cur = ext[0:q]
    dpre = weight[CONV - 1 : CONV] * cur
    for k in range(CONV - 1):
        dpre = dpre + weight[k : k + 1] * ext[CONV - 1 - k : CONV - 1 - k + q]
    ds_ref[pl.ds(pl.multiple_of(c * q, q), q), 0 : 2 * STATE] = dpre.astype(BF16)
    past = jnp.concatenate([bt_ref[:, 0 : 2 * STATE], bm_ref[:, 0 : 2 * STATE]], axis=0)
    for k in range(CONV):
        start = 8 - (CONV - 1) + k
        accb_ref[k : k + 1, :] += jnp.sum(cur * past[start : start + q], axis=0, keepdims=True)
    accb_ref[CONV : CONV + 1, :] += jnp.sum(cur, axis=0, keepdims=True)
    head_rows = jnp.concatenate([jnp.zeros((HALO, 2 * STATE), F32), cur[0:8]], axis=0)
    before = jnp.zeros((HALO, 2 * STATE), F32)
    for k in range(CONV - 1):
        before = before + weight[k : k + 1] * head_rows[CONV - 1 - k : CONV - 1 - k + HALO]
    ds_ref[pl.ds(tokens, HALO), 0 : 2 * STATE] = before.astype(BF16)
    qb[q:, :] = cur[0:8]

    raw = step_lanes(bm_ref, width) + hp_ref[0:1, :]
    dt = softplus(raw)
    rate = hp_ref[1:2, :]
    from_here = (iota((q, q), 1) >= iota((q, q), 0)).astype(F32)
    up_to_here = (iota((q, q), 1) < iota((q, q), 0)).astype(F32)
    kept_heads = dot_nt(jnp.broadcast_to(kept, (8, width)), head_spread(width), HIGHEST)
    total = (
        da[...].T
        + dot_nn(from_here, acc_g[...], HIGHEST)
        + dot_nn(up_to_here, acc_w[...], HIGHEST)
        + kept_heads[0:1, :]
    )
    d_raw = (acc_x[...] + rate * total) * sigmoid(raw)
    own_heads = width // (HALVES * HEADDIM)
    here = pl.ds(pl.multiple_of(c * q, q), q)
    ds_ref[here, 2 * STATE : 2 * STATE + LANES] = d_raw.astype(BF16)
    ds_ref[here, 2 * STATE + LANES :] = pltpu.roll(d_raw, LANES - own_heads, 1).astype(BF16)
    acch_ref[0:1, :] += jnp.sum(d_raw, axis=0, keepdims=True)
    acch_ref[1:2, :] += rate * jnp.sum(dt * total, axis=0, keepdims=True)


def shape(dims, dtype):
    return jax.ShapeDtypeStruct(dims, dtype)


def whole(dims):
    return pl.BlockSpec(dims, lambda c: (0,) * len(dims))


def run(kernel, name, grid, in_specs, out_specs, out_shape, scratch, args, flops):
    return pl.pallas_call(
        kernel,
        grid=(grid,),
        in_specs=in_specs,
        out_specs=out_specs,
        out_shape=out_shape,
        scratch_shapes=scratch,
        name=name,
        compiler_params=pltpu.CompilerParams(
            dimension_semantics=("arbitrary",), vmem_limit_bytes=60 * 1024 * 1024
        ),
        cost_estimate=pl.CostEstimate(
            flops=flops, bytes_accessed=sum(a.size * a.dtype.itemsize for a in args), transcendentals=0
        ),
    )(*args)


def mixer_forward_state(x_ext, s_ext, par, bcpar, hp, tokens):
    width = x_ext.shape[1]
    small = s_ext.shape[1]
    n = tokens // CHUNK
    q = CHUNK
    tail = q // 8
    last = (tokens + HALO) // 8 - 1
    tail_map = lambda c: (jnp.where(c == 0, last, c * tail - 1), 0)
    heads_pad = -(-(width // HEADDIM) // 8) * 8
    return run(
        state_kernel,
        "scan_states",
        n,
        [
            pl.BlockSpec((q, width), lambda c: (c, 0)),
            pl.BlockSpec((8, width), tail_map),
            pl.BlockSpec((q, small), lambda c: (c, 0)),
            pl.BlockSpec((8, small), tail_map),
            whole(par.shape),
            whole(bcpar.shape),
            whole(hp.shape),
        ],
        [
            pl.BlockSpec((q, width), lambda c: (c, 0)),
            pl.BlockSpec((q, width), lambda c: (c, 0)),
            pl.BlockSpec((q, width), lambda c: (c, 0)),
            pl.BlockSpec((q, width), lambda c: (c, 0)),
            pl.BlockSpec((q, 2 * STATE), lambda c: (c, 0)),
            pl.BlockSpec((heads_pad, q), lambda c: (0, c)),
            pl.BlockSpec((1, STATE, width), lambda c: (c, 0, 0)),
            whole((STATE, width)),
            pl.BlockSpec((1, 1, width), lambda c: (c, 0, 0)),
        ],
        [
            shape((tokens, width), F32),
            shape((tokens, width), BF16),
            shape((tokens, width), F32),
            shape((tokens, width), F32),
            shape((tokens, 2 * STATE), F32),
            shape((heads_pad, tokens), F32),
            shape((n, STATE, width), F32),
            shape((STATE, width), BF16),
            shape((n, 1, width), F32),
        ],
        [
            pltpu.VMEM((STATE, width), F32),
            pltpu.VMEM((1, width), F32),
            pltpu.VMEM((q, width), BF16),
        ],
        (x_ext, x_ext, s_ext, s_ext, par, bcpar, hp),
        int(3e9),
    )


def mixer_forward_main(xs, u, cume, cumt, bc, sloc, sin, dec, z, gyn, par):
    tokens, width = xs.shape
    q = CHUNK
    n = tokens // q
    rows = pl.BlockSpec((q, width), lambda c: (c, 0))
    return run(
        main_kernel,
        "scan_outputs",
        n,
        [
            rows,
            rows,
            rows,
            pl.BlockSpec((cumt.shape[0], q), lambda c: (0, c)),
            pl.BlockSpec((q, 2 * STATE), lambda c: (c, 0)),
            pl.BlockSpec((1, STATE, width), lambda c: (c, 0, 0)),
            whole(sin.shape),
            pl.BlockSpec((1, 1, width), lambda c: (c, 0, 0)),
            rows,
            rows,
            whole(par.shape),
        ],
        [rows, pl.BlockSpec((8, q), lambda c: (0, c))],
        [shape((tokens, width), F32), shape((8, tokens), F32)],
        [
            pltpu.VMEM((q, q), F32),
            pltpu.VMEM((q, width), F32),
            pltpu.VMEM((q, LANES), F32),
            pltpu.VMEM((q, LANES), F32),
        ],
        (xs, u, cume, cumt, bc, sloc, sin, dec, z, gyn, par),
        int(10e9),
    )


def mixer_backward_gate(y, z, gyn, xs, cume, bc, stat, par):
    tokens, width = y.shape
    q = CHUNK
    n = tokens // q
    rows = pl.BlockSpec((q, width), lambda c: (n - 1 - c, 0))
    return run(
        gate_kernel,
        "gate_back",
        n,
        [
            rows,
            rows,
            rows,
            rows,
            rows,
            pl.BlockSpec((q, 2 * STATE), lambda c: (n - 1 - c, 0)),
            pl.BlockSpec((q, 8), lambda c: (n - 1 - c, 0)),
            whole(par.shape),
        ],
        [
            rows,
            rows,
            rows,
            pl.BlockSpec((1, STATE, width), lambda c: (n - 1 - c, 0, 0)),
            whole((STATE, width)),
            pl.BlockSpec((1, 1, width), lambda c: (n - 1 - c, 0, 0)),
            whole((8, width)),
        ],
        [
            shape((tokens, width), BF16),
            shape((tokens, width), F32),
            shape((tokens, width), BF16),
            shape((n, STATE, width), F32),
            shape((STATE, width), BF16),
            shape((n, 1, width), F32),
            shape((8, width), F32),
        ],
        [
            pltpu.VMEM((STATE, width), F32),
            pltpu.VMEM((1, width), F32),
            pltpu.VMEM((q, width), BF16),
        ],
        (y, z, gyn, xs, cume, bc, stat, par),
        int(5e9),
    )


def mixer_backward_main(
    x_ext, s_ext, par, bcpar, hp, cume, dte, cumt, gy, sloc, sin, sdec, gloc, gout, gdec
):
    tokens, width = cume.shape
    small = s_ext.shape[1]
    q = CHUNK
    n = tokens // q
    tail = q // 8
    last = (tokens + HALO) // 8 - 1
    rows = pl.BlockSpec((q, width), lambda c: (n - 1 - c, 0))
    tail_map = lambda c: (jnp.where(c == n - 1, last, (n - 1 - c) * tail - 1), 0)
    states = pl.BlockSpec((1, STATE, width), lambda c: (n - 1 - c, 0, 0))
    decays = pl.BlockSpec((1, 1, width), lambda c: (n - 1 - c, 0, 0))
    return run(
        back_kernel,
        "scan_back",
        n,
        [
            rows,
            pl.BlockSpec((8, width), tail_map),
            pl.BlockSpec((q, small), lambda c: (n - 1 - c, 0)),
            pl.BlockSpec((8, small), tail_map),
            whole(par.shape),
            whole(bcpar.shape),
            whole(hp.shape),
            rows,
            rows,
            pl.BlockSpec((cumt.shape[0], q), lambda c: (0, n - 1 - c)),
            rows,
            states,
            whole(sin.shape),
            decays,
            states,
            whole(gout.shape),
            decays,
        ],
        [
            whole((tokens + HALO, width)),
            whole((tokens + HALO, small)),
            whole((8, width)),
            whole((8, 2 * STATE)),
            whole((8, LANES)),
        ],
        [
            shape((tokens + HALO, width), BF16),
            shape((tokens + HALO, small), BF16),
            shape((8, width), F32),
            shape((8, 2 * STATE), F32),
            shape((8, LANES), F32),
        ],
        [
            pltpu.VMEM((q, width), F32),
            pltpu.VMEM((q, width), BF16),
            pltpu.VMEM((q, width), F32),
            pltpu.VMEM((q, width), BF16),
            pltpu.VMEM((q, width), BF16),
            pltpu.VMEM((q, width), F32),
            pltpu.VMEM((q, width), F32),
            pltpu.VMEM((q + 8, width), F32),
            pltpu.VMEM((q + 8, 2 * STATE), F32),
            pltpu.VMEM((q, q), F32),
            pltpu.VMEM((q, q), F32),
            pltpu.VMEM((LANES, q), F32),
            pltpu.VMEM((q, LANES), F32),
            pltpu.VMEM((q, LANES), F32),
            pltpu.VMEM((q, LANES), F32),
        ],
        (x_ext, x_ext, s_ext, s_ext, par, bcpar, hp, cume, dte, cumt, gy, sloc, sin, sdec, gloc, gout, gdec),
        int(30e9),
    )


MESH = pl.DeviceIdType.MESH


def flip(index, bit):
    return index + (1 - 2 * ((index // (1 << bit)) % 2)) * (1 << bit)


def flip_all(index, offset):
    bit = 0
    while offset >> bit:
        if (offset >> bit) & 1:
            index = flip(index, bit)
        bit += 1
    return index


def gather_kernel(
    tok_bits, row_bits, half_bit,
    in_ref, gain_ref, par_ref, small_ref, wx_ref, wz_ref, wo_ref,
    x_out, s_out, z_out, normed_out, rows_out, ws_out, wx_out, wz_out, wo_out, gains_out, pars_out,
    ws, wx, wz, wo, rows, halo, normed, gains, pars, stage,
    send_sem, recv_sem, local_sem, stage_sem,
):
    tok, head = lax.axis_index("tok"), lax.axis_index("head")
    sets = 1 << len(row_bits)
    heads = 2 * sets
    half, mine = head // sets, head % sets
    own_rows, model = in_ref.shape
    share, own_width = wx_ref.shape
    tokens = own_rows * sets
    partners = [{"tok": flip(tok, b)} for b in tok_bits]
    partners += [{"head": flip_all(head, p)} for p in range(1, heads)]

    barrier = pltpu.get_barrier_semaphore()
    for partner in partners:
        pl.semaphore_signal(barrier, inc=1, device_id=partner, device_id_type=MESH)
    pl.semaphore_wait(barrier, len(partners))

    sent, stored, open_local = [], [], []

    def send(src, dst, device):
        k = len(sent)
        copy = pltpu.make_async_remote_copy(
            src_ref=src, dst_ref=dst, send_sem=send_sem.at[k], recv_sem=recv_sem.at[k],
            device_id=device, device_id_type=MESH,
        )
        copy.start()
        sent.append(copy)
        return copy

    def local(src, dst):
        copy = pltpu.make_async_copy(src, dst, local_sem.at[len(stored)])
        copy.start()
        stored.append(copy)
        open_local.append(copy)
        return copy

    def settle(copy):
        if any(copy is other for other in open_local):
            open_local[:] = [other for other in open_local if other is not copy]
            copy.wait()

    def arrive(copies):
        for copy in copies:
            copy.wait_recv()

    other_half = {"head": flip(head, half_bit)}
    lanes = pl.ds(pl.multiple_of(half * own_width, LANES), own_width)

    class Piece:
        def __init__(self, src, dst, part, order):
            size = share // 2
            self.rows = pl.ds(part * size, size)
            self.dst, self.order, self.held = dst, list(order), [0]
            slot = dst.at[tok, self.rows, lanes]
            self.flight = [send(src.at[self.rows], slot, other_half)]
            self.kept = local(src.at[self.rows], slot)

        def advance(self):
            arrive(self.flight)
            settle(self.kept)
            self.flight = []
            if self.order:
                bit = self.order.pop(0)
                for offset in self.held:
                    slot = self.dst.at[flip_all(tok, offset), self.rows]
                    self.flight.append(send(slot, slot, {"tok": flip(tok, bit)}))
                self.held = self.held + [offset ^ (1 << bit) for offset in self.held]

        def finish(self):
            while self.flight:
                self.advance()

    class Small(Piece):
        def __init__(self, src, dst, order):
            self.rows = pl.ds(0, share)
            self.dst, self.order, self.held = dst, list(order), [0]
            wide = pl.ds(pl.multiple_of(2 * STATE + half * LANES, LANES), LANES)
            slot = dst.at[tok, :, wide]
            part = src.at[:, pl.ds(2 * STATE, LANES)]
            self.flight = [send(part, slot, other_half)]
            settle(local(part, slot))
            self.kept = local(src.at[:, pl.ds(0, 2 * STATE)], dst.at[tok, :, pl.ds(0, 2 * STATE)])

    class Rows:
        def __init__(self, src, dst):
            self.dst, self.order, self.held = dst, list(row_bits), [0]
            self.src = src
            self.kept = local(src, dst.at[mine])
            self.flight = []
            if self.order:
                bit = self.order.pop(0)
                self.flight.append(send(src, dst.at[mine], {"head": flip(head, bit)}))
                self.held = [0, 1 << bit]

        def advance(self):
            arrive(self.flight)
            settle(self.kept)
            self.flight = []
            if self.order:
                bit = self.order.pop(0)
                for offset in self.held:
                    slot = self.dst.at[flip_all(mine, offset)]
                    self.flight.append(send(slot, slot, {"head": flip(head, bit)}))
                self.held = self.held + [offset ^ (1 << bit) for offset in self.held]

        def finish(self):
            settle(self.kept)
            while self.flight:
                self.advance()

    up = list(tok_bits)[1:] + [0]
    down = list(tok_bits)[1:][::-1] + [0]
    gain_copies = [
        send(gain_ref, gains.at[p], {"head": flip_all(head, p)}) for p in range(1, heads)
    ]
    gain_kept = local(gain_ref, gains.at[0])
    par_slot = pars.at[:, lanes]
    par_copy = send(par_ref, par_slot, other_half)
    par_kept = local(par_ref, par_slot)
    p_small = Small(small_ref, ws, up)
    p_xa = Piece(wx_ref, wx, 0, up)
    p_xb = Piece(wx_ref, wx, 1, down)
    p_za = Piece(wz_ref, wz, 0, up)
    p_zb = Piece(wz_ref, wz, 1, down)
    r_in = Rows(in_ref, rows)
    p_oa = Piece(wo_ref, wo, 0, up)
    p_ob = Piece(wo_ref, wo, 1, down)
    first, second, third = (p_small, p_xa, p_xb), (p_za, p_zb), (p_oa, p_ob)

    def advance(pieces):
        for piece in pieces:
            piece.advance()

    def normalise(src, start, count, scale):
        def body(i, carry):
            at = pl.ds(pl.multiple_of(start + i * 16, 16), 16)
            wide = src[pl.ds(pl.multiple_of(i * 16, 16), 16), :].astype(F32)
            inv = lax.rsqrt(jnp.sum(wide * wide, axis=1, keepdims=True) / model + EPS)
            normed[at, :] = (wide * inv * scale).astype(BF16)
            return carry

        lax.fori_loop(0, count // 16, body, 0, unroll=4 if count >= 64 else 1)

    def project(lhs, count, weight, out, width):
        tile = 256 if width % 256 == 0 else LANES
        steps = width // tile

        def out_copy(i):
            at = pl.ds(pl.multiple_of(i * tile, tile), tile)
            return pltpu.make_async_copy(
                stage.at[i % 2, pl.ds(0, count), pl.ds(0, tile)], out.at[:, at], stage_sem.at[i % 2]
            )

        def body(i, carry):
            @pl.when(i >= 2)
            def _():
                out_copy(i - 2).wait()

            at = pl.ds(pl.multiple_of(i * tile, tile), tile)
            block = weight[:, :, at].reshape(model, tile)
            stage[i % 2, 0:count, 0:tile] = dot_nn(lhs[...].reshape(count, model), block)
            out_copy(i).start()
            return carry

        lax.fori_loop(0, steps, body, 0)
        for i in range(max(steps - 2, 0), steps):
            out_copy(i).wait()

    def finish(pieces):
        for piece in pieces:
            piece.finish()

    advance(first)
    advance(second)
    arrive(gain_copies)
    settle(gain_kept)
    scale = gains[0, 0:1, :]
    for p in range(1, heads):
        scale = scale + gains[p, 0:1, :]
    gains[0, 0:1, :] = scale
    advance(first)
    settle(r_in.kept)
    normalise(rows.at[mine], mine * own_rows, own_rows, scale)
    advance(second)
    advance(first)
    advance(third)
    advance(second)
    finish(first)
    local(ws, ws_out)
    local(wx, wx_out)
    r_in.finish()
    tail = rows.at[sets - 1, pl.ds(own_rows - HALO, HALO), :]
    tail_copy = send(tail, halo, other_half)
    advance(third)
    for i in range(1, sets):
        other = flip_all(mine, i)
        normalise(rows.at[other], other * own_rows, own_rows, scale)
    tail_copy.wait_recv()
    normalise(halo, tokens, HALO, scale * half.astype(F32))
    local(rows, rows_out)
    local(normed, normed_out)
    project(normed, tokens + HALO, ws, s_out, ws.shape[2])
    advance(third)
    project(normed, tokens + HALO, wx, x_out, wx.shape[2])
    finish(second)
    local(wz, wz_out)
    finish(third)
    local(wo, wo_out)
    project(normed.at[pl.ds(0, tokens)], tokens, wz, z_out, wz.shape[2])
    arrive([par_copy])
    settle(par_kept)
    local(pars, pars_out)
    local(gains.at[0], gains_out)
    for copy in list(open_local):
        settle(copy)
    for copy in sent:
        copy.wait_send()


def gather_and_project(block_in, gain, par, small, wx, wz, wo):
    tok_size, head_size = lax.axis_size("tok"), lax.axis_size("head")
    sets = head_size // HALVES
    tok_bits = range(tok_size.bit_length() - 1)
    row_bits = range(sets.bit_length() - 1)
    own_rows, model = block_in.shape
    share, own_width = wx.shape
    width = HALVES * own_width
    tokens = own_rows * sets
    lanes = 2 * STATE + HALVES * LANES
    anywhere = pl.BlockSpec(memory_space=pl.ANY)
    slots = (tok_size, share)
    copies = 128
    outs = [
        shape((tokens + HALO, width), F32),
        shape((tokens + HALO, lanes), F32),
        shape((tokens, width), F32),
        shape((tokens + HALO, model), BF16),
        shape((sets, own_rows, model), BF16),
        shape(slots + (lanes,), BF16),
        shape(slots + (width,), BF16),
        shape(slots + (width,), BF16),
        shape(slots + (width,), BF16),
        shape((8, model), F32),
        shape((8, width), F32),
    ]
    return pl.pallas_call(
        functools.partial(gather_kernel, tok_bits, row_bits, sets.bit_length() - 1),
        in_specs=[anywhere] * 7,
        out_specs=[anywhere] * len(outs),
        out_shape=outs,
        scratch_shapes=[
            pltpu.VMEM(slots + (lanes,), BF16),
            pltpu.VMEM(slots + (width,), BF16),
            pltpu.VMEM(slots + (width,), BF16),
            pltpu.VMEM(slots + (width,), BF16),
            pltpu.VMEM((sets, own_rows, model), BF16),
            pltpu.VMEM((HALO, model), BF16),
            pltpu.VMEM((tokens + HALO, model), BF16),
            pltpu.VMEM((head_size, 8, model), F32),
            pltpu.VMEM((8, width), F32),
            pltpu.VMEM((2, tokens + HALO, 256), F32),
            pltpu.SemaphoreType.DMA((copies,)),
            pltpu.SemaphoreType.DMA((copies,)),
            pltpu.SemaphoreType.DMA((32,)),
            pltpu.SemaphoreType.DMA((2,)),
        ],
        name="gather",
        compiler_params=pltpu.CompilerParams(
            collective_id=0, has_side_effects=True, vmem_limit_bytes=60 * 1024 * 1024
        ),
        cost_estimate=pl.CostEstimate(flops=int(12e9), bytes_accessed=int(60e6), transcendentals=0),
    )(block_in, gain, par, small, wx, wz, wo)


def per_device(
    block_in,
    norm_gain,
    w_zx,
    w_bc,
    w_dt,
    conv_x_w,
    conv_x_b,
    conv_bc_w,
    conv_bc_b,
    dt_bias,
    a_log,
    d_skip,
    gate_gain,
    w_out,
    cotangent,
):
    head_size = lax.axis_size("head")
    tok_size = lax.axis_size("tok")
    sets = head_size // HALVES
    row_bits = range(sets.bit_length() - 1)
    half_bit = sets.bit_length() - 1
    head_bits = range(head_size.bit_length() - 1)
    tok_bits = range(tok_size.bit_length() - 1)
    nbits = len(tok_bits)
    half = bit_of("head", half_bit)
    own_rows, model = block_in.shape
    share, _, own_width = w_zx.shape
    own_heads = w_dt.shape[1]
    tokens = own_rows * sets
    heads = own_heads * HALVES
    forward = list(tok_bits)[1:] + [0]
    other = list(tok_bits)[1:][::-1] + [0]

    def all_rows(value):
        for bit in row_bits:
            value = grow(value, "head", bit, 0)
        return value

    def lane_pad(v):
        return jnp.pad(v, (0, LANES - v.shape[0]))

    heads_row = jnp.concatenate([lane_pad(dt_bias), lane_pad(a_log), lane_pad(d_skip)])
    own_par = jnp.concatenate(
        [
            conv_x_w,
            conv_x_b[None],
            gate_gain[None],
            jnp.repeat(d_skip, HEADDIM)[None],
            jnp.pad(heads_row, (0, own_width - heads_row.shape[0]))[None],
        ]
    )
    gain_share = norm_gain.shape[0]
    own_gain = lax.dynamic_update_slice(
        jnp.zeros((8, model), F32),
        jnp.broadcast_to(norm_gain.astype(F32)[None], (8, gain_share)),
        (0, lax.axis_index("head") * gain_share),
    )
    small = jnp.concatenate([w_bc, jnp.pad(w_dt, ((0, 0), (0, LANES - own_heads)))], axis=1)
    x_ext, s_ext, z, normed_ext, rows, w_small, w_x, w_z, w_o, gain, par = gather_and_project(
        block_in, own_gain, own_par, small, w_zx[:, 1], w_zx[:, 0], w_out.T
    )
    later_cot, x_ext = lax.optimization_barrier((cotangent, x_ext))
    cot = all_rows(later_cot)
    gain = gain[0:1]
    normed = normed_ext[:tokens]
    w_small, w_x, w_z, w_o = (w.reshape(model, w.shape[2]) for w in (w_small, w_x, w_z, w_o))

    def of_heads(start):
        pieces = [
            par[CONV + 3, i * own_width + start : i * own_width + start + own_heads] for i in range(HALVES)
        ]
        return jnp.concatenate(pieces)

    rate = -jnp.exp(of_heads(LANES))
    hp = jnp.stack([lane_pad(of_heads(0)), lane_pad(rate)] + [jnp.zeros((LANES,), F32)] * 6)
    bcpar = jnp.concatenate([conv_bc_w, conv_bc_b[None], jnp.zeros((3, 2 * STATE), F32)])

    def norm(value):
        wide = value.astype(F32)
        inv = lax.rsqrt(jnp.mean(wide * wide, axis=1, keepdims=True) + EPS)
        return wide, inv, (wide * inv * gain).astype(BF16)

    rows_wide, inv_rms, _ = norm(rows.reshape(tokens, model))
    xs, u, cume, dte, bc, cumt, sloc, fin, sdec = mixer_forward_state(x_ext, s_ext, par, bcpar, hp, tokens)
    to_next = [(i, i + sets) for i in range(sets)]
    to_prev = [(i + sets, i) for i in range(sets)]
    sin = lax.ppermute(fin, "head", to_next)
    gyn = dot_nn(cot, w_o)
    y, stat = mixer_forward_main(xs, u, cume, cumt, bc, sloc, sin, sdec, z, gyn, par)
    stat = add_pairs(stat, "head", row_bits).T
    inv_gate = lax.rsqrt(stat[:, 0:1] / INNER + EPS)
    stat = jnp.concatenate(
        [inv_gate, inv_gate * inv_gate * inv_gate * stat[:, 1:2] / INNER, stat[:, 2:]], axis=1
    )
    yn, gy, dz, gloc, gin, gdec, acc_gate = mixer_backward_gate(y, z, gyn, xs, cume, bc, stat, par)
    gout = lax.ppermute(gin, "head", to_prev)

    def spread_rows(grad, order):
        grad = grad.reshape((2,) * nbits + (share, grad.shape[-1]))
        for bit in order[::-1]:
            grad = halve(grad, "tok", bit, nbits - 1 - bit)
        return grad.reshape(share, grad.shape[-1])

    def own_columns(grad):
        return halve(grad, "head", half_bit, 1)

    def own_row_sum(value):
        for bit in list(row_bits)[::-1]:
            value = halve(value, "head", bit, 0)
        return value

    branch = dot_nt(yn, w_o)
    block_out = block_in.astype(F32) + own_row_sum(branch)
    d_w_o = own_columns(spread_rows(dot_tn(cot, yn), forward)).T
    d_w_z = own_columns(spread_rows(dot_tn(normed, dz), other))
    d_normed_z = dot_nt(dz, w_z)

    dx, ds, acc_x, acc_b, acc_h = mixer_backward_main(
        x_ext, s_ext, par, bcpar, hp, cume, dte, cumt, gy, sloc, sin, sdec, gloc, gout, gdec
    )
    d_w_x = own_columns(spread_rows(dot_tn(normed_ext, dx), forward))
    d_small = spread_rows(dot_tn(normed_ext, ds), other)
    d_norm_ext = dot_nt(dx, w_x) + dot_nt(ds, w_small)
    d_w_bc = add_pairs(d_small[:, : 2 * STATE], "head", head_bits)
    d_w_dt = own_columns(d_small[:, 2 * STATE :])[:, :own_heads]

    from_next = lax.ppermute(d_norm_ext[tokens:].astype(BF16), "head", to_prev).astype(F32)
    d_normed = d_normed_z + d_norm_ext[:tokens]
    d_normed = jnp.concatenate([d_normed[: tokens - HALO], d_normed[tokens - HALO :] + from_next])
    gain_part = jnp.sum(d_normed * rows_wide * inv_rms, axis=0)
    d_own = own_row_sum(d_normed)
    wide, inv, _ = norm(block_in)
    scaled = d_own * gain
    d_block_in = (
        cotangent.astype(F32)
        + inv * scaled
        - wide * (inv * inv * inv * jnp.sum(scaled * wide, axis=1, keepdims=True) / model)
    )

    per_channel = jnp.concatenate(
        [
            acc_x[: CONV + 1],
            acc_gate[0:1],
            jnp.concatenate(
                [
                    jnp.pad(
                        jnp.concatenate(
                            [
                                lane_pad(acc_h[0, i * own_heads : (i + 1) * own_heads]),
                                lane_pad(acc_h[1, i * own_heads : (i + 1) * own_heads]),
                                lane_pad(
                                    jnp.sum(
                                        acc_gate[1, i * own_width : (i + 1) * own_width].reshape(own_heads, HEADDIM),
                                        axis=1,
                                    )
                                ),
                            ]
                        ),
                        (0, own_width - 3 * LANES),
                    )
                    for i in range(HALVES)
                ]
            )[None],
        ]
    )

    def half_sum(value):
        low, high = jnp.split(value, 2, axis=1)
        keep = jnp.where(half == 0, low, high)
        return keep + swap(jnp.where(half == 0, high, low), "head", half_bit)

    own_sums = half_sum(per_channel)
    over_heads = jnp.concatenate([gain_part, acc_b[: CONV + 1].reshape(-1)])
    over_heads = add_pairs(over_heads, "head", head_bits)
    flat = jnp.concatenate([own_sums.reshape(-1), over_heads])
    flat = add_pairs(flat, "tok", tok_bits)
    own_size = own_sums.size
    own_sums = flat[:own_size].reshape(own_sums.shape)
    all_gain = flat[own_size : own_size + model]
    bc_sums = flat[own_size + model :].reshape(CONV + 1, 2 * STATE)
    d_norm_gain = lax.dynamic_slice_in_dim(all_gain, lax.axis_index("head") * gain_share, gain_share, 0)
    return (
        block_out,
        d_block_in,
        d_norm_gain,
        jnp.stack([d_w_z, d_w_x], axis=1),
        d_w_bc,
        d_w_dt,
        own_sums[:CONV],
        own_sums[CONV],
        bc_sums[:CONV],
        bc_sums[CONV],
        own_sums[CONV + 2, :own_heads],
        own_sums[CONV + 2, LANES : LANES + own_heads],
        own_sums[CONV + 2, 2 * LANES : 2 * LANES + own_heads],
        own_sums[CONV + 1],
        d_w_o,
    )


def solution(mesh):
    placed = (
        P(("tok", "head"), None),
        P("head"),
        P("tok", None, "head"),
        P("tok", None),
        P("tok", "head"),
        P(None, "head"),
        P("head"),
        P(),
        P(),
        P("head"),
        P("head"),
        P("head"),
        P("head"),
        P("head", "tok"),
        P(("tok", "head"), None),
    )
    return jax.shard_map(
        per_device,
        mesh=mesh,
        in_specs=placed,
        out_specs=(
            P(("tok", "head"), None),
            P(("tok", "head"), None),
            P("head"),
            P("tok", None, "head"),
            P("tok", None),
            P("tok", "head"),
            P(None, "head"),
            P("head"),
            P(),
            P(),
            P("head"),
            P("head"),
            P("head"),
            P("head"),
            P("head", "tok"),
        ),
        check_vma=False,
    )
```

```python
import functools

import jax
import jax.numpy as jnp
from jax import lax
from jax.experimental import pallas as pl
from jax.experimental.pallas import tpu as pltpu
from jax.sharding import PartitionSpec as P

HEADDIM = 64
STATE = 128
CONV = 4
INNER = 3072
CHUNK = 256
HALVES = 2
LANES = 128
HALO = 16

EPS = 1e-05
HIGHEST = lax.Precision.HIGHEST
F32 = jnp.float32
BF16 = jnp.bfloat16


def dot_nn(a, b, precision=None):
    return lax.dot_general(
        a, b, (((1,), (0,)), ((), ())), preferred_element_type=F32, precision=precision
    )


def dot_nt(a, b, precision=None):
    return lax.dot_general(
        a, b, (((1,), (1,)), ((), ())), preferred_element_type=F32, precision=precision
    )


def dot_tn(a, b):
    return lax.dot_general(a, b, (((0,), (0,)), ((), ())), preferred_element_type=F32)


def dot_split(a, b):
    a_top, b_top = a.astype(BF16), b.astype(BF16)
    a_rest = (a - a_top.astype(F32)).astype(BF16)
    b_rest = (b - b_top.astype(F32)).astype(BF16)
    return dot_nn(a_top, b_top) + (dot_nn(a_rest, b_top) + dot_nn(a_top, b_rest))


def iota(shape, dim):
    return lax.broadcasted_iota(jnp.int32, shape, dim)


def sigmoid(v):
    return 1.0 / (1.0 + jnp.exp(-v))


def softplus(v):
    return jnp.maximum(v, 0.0) + jnp.log1p(jnp.exp(-jnp.abs(v)))


def head_spread(width):
    return (iota((LANES, width), 1) // HEADDIM == iota((LANES, width), 0)).astype(F32)


def bit_of(axis, bit):
    return (lax.axis_index(axis) // (1 << bit)) % 2


def swap(value, axis, bit):
    size = lax.axis_size(axis)
    return lax.ppermute(value, axis, [(i, i ^ (1 << bit)) for i in range(size)])


def grow(value, axis, bit, dim):
    other = swap(value, axis, bit)
    low = bit_of(axis, bit) == 0
    return jnp.where(
        low,
        jnp.concatenate([value, other], dim),
        jnp.concatenate([other, value], dim),
    )


def halve(value, axis, bit, dim):
    mine = bit_of(axis, bit)
    if dim < value.ndim - 1:
        half = value.shape[dim] // 2
        keep = lax.dynamic_slice_in_dim(value, mine * half, half, dim)
        send = lax.dynamic_slice_in_dim(value, (1 - mine) * half, half, dim)
    else:
        low, high = jnp.split(value, 2, axis=dim)
        keep = jnp.where(mine == 0, low, high)
        send = jnp.where(mine == 0, high, low)
    return keep.astype(F32) + swap(send.astype(BF16), axis, bit).astype(F32)


def add_pairs(value, axis, bits):
    for bit in bits:
        value = value + swap(value, axis, bit)
    return value


def conv_rows(cur, tail, weight, bias):
    rows = cur.shape[0]
    ext = jnp.concatenate([tail, cur], axis=0)
    out = bias + weight[CONV - 1 : CONV] * cur
    for k in range(CONV - 1):
        start = 8 - (CONV - 1) + k
        out = out + weight[k : k + 1] * ext[start : start + rows]
    return out


def state_kernel(
    xm_ref, xt_ref, bm_ref, bt_ref, par_ref, bcpar_ref, hp_ref,
    xs_ref, u_ref, cume_ref, dte_ref, bc_ref, cumt_ref, sloc_ref, fin_ref, dec_ref,
    state, dsum, ue,
):
    c = pl.program_id(0)
    q, width = xm_ref.shape

    @pl.when(c == 0)
    def _():
        state[...] = jnp.zeros_like(state)
        dsum[...] = jnp.zeros_like(dsum)

    dt = softplus(bm_ref[:, 2 * STATE :] + hp_ref[0:1, :])
    tri = (iota((q, q), 0) >= iota((q, q), 1)).astype(F32)
    cum = dot_nn(tri, dt * hp_ref[1:2, :], HIGHEST)
    cumt_ref[...] = cum.T[: cumt_ref.shape[0], :]
    spread = head_spread(width)
    cume_ref[...] = dot_nn(cum, spread, HIGHEST)
    dte_ref[...] = dot_nn(dt, spread, HIGHEST)
    end = cume_ref[q - 1 : q, :]

    bpre = conv_rows(
        bm_ref[:, : 2 * STATE], bt_ref[:, : 2 * STATE], bcpar_ref[0:CONV, :], bcpar_ref[CONV : CONV + 1, :]
    )
    bc_ref[...] = bpre * sigmoid(bpre)

    block = 2 * LANES

    def body(i, carry):
        sl = pl.ds(pl.multiple_of(i * block, block), block)
        pre = conv_rows(
            xm_ref[:, sl], xt_ref[:, sl], par_ref[0:CONV, sl], par_ref[CONV : CONV + 1, sl]
        )
        xs = pre * sigmoid(pre)
        u = xs * dte_ref[:, sl]
        xs_ref[:, sl] = xs
        u_ref[:, sl] = u.astype(BF16)
        cume = cume_ref[:, sl]
        ue[:, sl] = (u * jnp.exp(cume[q - 1 : q, :] - cume)).astype(BF16)
        return carry

    lax.fori_loop(0, width // block, body, 0)
    sloc_ref[0] = state[...]
    dec_ref[0] = jnp.exp(dsum[...])
    state[...] = jnp.exp(end) * state[...] + dot_nn(bc_ref[:, :STATE].T.astype(BF16), ue[...])
    dsum[...] = dsum[...] + end
    fin_ref[...] = state[...].astype(BF16)


def main_kernel(
    xs_ref, u_ref, cume_ref, cumt_ref, bc_ref, sloc_ref, sin_ref, dec_ref, z_ref, gyn_ref, par_ref,
    y_ref, stat_ref,
    gram, ya, acc_sq, acc_in,
):
    q, width = xs_ref.shape
    bmat = bc_ref[:, :STATE].astype(BF16)
    cmat = bc_ref[:, STATE:].astype(BF16)
    lower = iota((q, q), 0) >= iota((q, q), 1)
    gram[...] = jnp.where(lower, dot_nt(cmat, bmat), 0.0)
    entering = sloc_ref[0] + dec_ref[0, 0:1, :] * sin_ref[...].astype(F32)
    ya[...] = dot_nn(cmat, entering.astype(BF16))
    acc_sq[...] = jnp.zeros_like(acc_sq)
    acc_in[...] = jnp.zeros_like(acc_in)
    first = iota((q, LANES), 1) < HEADDIM

    def body(p, carry):
        sl = pl.ds(pl.multiple_of(p * LANES, LANES), LANES)
        cume = cume_ref[:, sl]
        u = u_ref[:, sl]
        y = jnp.exp(cume) * ya[:, sl] + par_ref[CONV + 2 : CONV + 3, sl] * xs_ref[:, sl]
        for s in range(2):
            gap = cume[:, HEADDIM * s : HEADDIM * s + 1] - cumt_ref[pl.ds(2 * p + s, 1), :]
            pairs = (gram[...] * jnp.exp(jnp.minimum(gap, 0.0))).astype(BF16)
            y = y + dot_nn(pairs, jnp.where(first == (s == 0), u, jnp.zeros_like(u)))
        y_ref[:, sl] = y
        z = z_ref[:, sl]
        gated = y * z * sigmoid(z)
        acc_sq[...] += gated * gated
        acc_in[...] += gated * gyn_ref[:, sl] * par_ref[CONV + 1 : CONV + 2, sl]
        return carry

    lax.fori_loop(0, width // LANES, body, 0)
    ones = jnp.ones((8, LANES), F32)
    sums_sq = dot_nt(ones, acc_sq[...], HIGHEST)
    sums_in = dot_nt(ones, acc_in[...], HIGHEST)
    stat_ref[...] = jnp.where(iota(sums_sq.shape, 0) == 0, sums_sq, sums_in)


def gate_kernel(
    y_ref, z_ref, gyn_ref, xs_ref, cume_ref, bc_ref, stat_ref, par_ref,
    yn_ref, gy_ref, dz_ref, gloc_ref, gin_ref, dec_ref, acc_ref,
    adj, dsum, ge,
):
    q, width = y_ref.shape

    @pl.when(pl.program_id(0) == 0)
    def _():
        adj[...] = jnp.zeros_like(adj)
        dsum[...] = jnp.zeros_like(dsum)
        acc_ref[...] = jnp.zeros_like(acc_ref)

    end = cume_ref[q - 1 : q, :]
    inv = jnp.broadcast_to(stat_ref[:, 0:1], (q, LANES))
    back = jnp.broadcast_to(stat_ref[:, 1:2], (q, LANES))

    def body(p, carry):
        sl = pl.ds(pl.multiple_of(p * LANES, LANES), LANES)
        y, z, gyn = y_ref[:, sl], z_ref[:, sl], gyn_ref[:, sl]
        sig = sigmoid(z)
        sil = z * sig
        gated = y * sil
        gain = par_ref[CONV + 1 : CONV + 2, sl]
        unit = gated * inv
        yn_ref[:, sl] = (unit * gain).astype(BF16)
        d_gated = inv * gyn * gain - gated * back
        gy = d_gated * sil
        gy_ref[:, sl] = gy
        dz_ref[:, sl] = (d_gated * y * (sig * (1.0 + z * (1.0 - sig)))).astype(BF16)
        ge[:, sl] = (gy * jnp.exp(cume_ref[:, sl])).astype(BF16)
        acc_ref[0:1, sl] += jnp.sum(gyn * unit, axis=0, keepdims=True)
        acc_ref[1:2, sl] += jnp.sum(gy * xs_ref[:, sl], axis=0, keepdims=True)
        return carry

    lax.fori_loop(0, width // LANES, body, 0)
    gloc_ref[0] = adj[...]
    dec_ref[0] = jnp.exp(dsum[...])
    adj[...] = jnp.exp(end) * adj[...] + dot_nn(bc_ref[:, STATE:].T.astype(BF16), ge[...])
    dsum[...] = dsum[...] + end
    gin_ref[...] = adj[...].astype(BF16)


def back_kernel(
    xm_ref, xt_ref, bm_ref, bt_ref, par_ref, bcpar_ref, hp_ref,
    cume_ref, dte_ref, cumt_ref, gy_ref, sloc_ref, sin_ref, sdec_ref, gloc_ref, gout_ref, gdec_ref,
    dx_ref, ds_ref, accx_ref, accb_ref, acch_ref,
    xs, u, dsil, ue, ge, dus, ya, qx, qb, gram, dgram, da, acc_x, acc_w, acc_g,
):
    step = pl.program_id(0)
    q, width = xm_ref.shape
    tokens = dx_ref.shape[0] - HALO
    c = tokens // q - 1 - step
    block = 2 * LANES

    @pl.when(step == 0)
    def _():
        accx_ref[...] = jnp.zeros_like(accx_ref)
        accb_ref[...] = jnp.zeros_like(accb_ref)
        acch_ref[...] = jnp.zeros_like(acch_ref)
        qx[q:, :] = jnp.zeros((8, width), F32)
        qb[q:, :] = jnp.zeros((8, 2 * STATE), F32)
        da[...] = jnp.zeros_like(da)
        ds_ref[...] = jnp.zeros_like(ds_ref)

    bpre = conv_rows(
        bm_ref[:, : 2 * STATE], bt_ref[:, : 2 * STATE], bcpar_ref[0:CONV, :], bcpar_ref[CONV : CONV + 1, :]
    )
    bsig = sigmoid(bpre)
    bc = bpre * bsig
    qb[0:q, :] = bsig * (1.0 + bpre * (1.0 - bsig))
    bmat, cmat = bc[:, :STATE].astype(BF16), bc[:, STATE:].astype(BF16)

    def conv_body(i, carry):
        sl = pl.ds(pl.multiple_of(i * block, block), block)
        pre = conv_rows(
            xm_ref[:, sl], xt_ref[:, sl], par_ref[0:CONV, sl], par_ref[CONV : CONV + 1, sl]
        )
        sig = sigmoid(pre)
        x = pre * sig
        xs[:, sl] = x
        dsil[:, sl] = sig * (1.0 + pre * (1.0 - sig))
        uu = x * dte_ref[:, sl]
        u[:, sl] = uu.astype(BF16)
        cume = cume_ref[:, sl]
        ue[:, sl] = (uu * jnp.exp(cume[q - 1 : q, :] - cume)).astype(BF16)
        ge[:, sl] = (gy_ref[:, sl] * jnp.exp(cume)).astype(BF16)
        return carry

    lax.fori_loop(0, width // block, conv_body, 0)

    end = cume_ref[q - 1 : q, :]
    adj = gloc_ref[0] + gdec_ref[0, 0:1, :] * gout_ref[...].astype(F32)
    entering = sloc_ref[0] + sdec_ref[0, 0:1, :] * sin_ref[...].astype(F32)
    kept = jnp.exp(end) * jnp.sum(adj * entering, axis=0, keepdims=True)
    adj_low, ent_low = adj.astype(BF16), entering.astype(BF16)
    dus[...] = dot_nn(bmat, adj_low)
    ya[...] = dot_nn(cmat, ent_low)
    db = dot_nt(ue[...], adj_low)
    dc = dot_nt(ge[...], ent_low)
    upper = iota((q, q), 1) >= iota((q, q), 0)
    gram[...] = jnp.where(upper, dot_nt(bmat, cmat), 0.0)
    dgram[...] = jnp.zeros_like(dgram)
    acc_x[...] = jnp.zeros_like(acc_x)
    acc_w[...] = jnp.zeros_like(acc_w)
    acc_g[...] = jnp.zeros_like(acc_g)
    later = (iota((q, q), 0) >= iota((q, q), 1)).astype(BF16)
    first = iota((q, LANES), 1) < HEADDIM

    def pair_body(p, carry):
        sl = pl.ds(pl.multiple_of(p * LANES, LANES), LANES)
        cume = cume_ref[:, sl]
        ul = u[:, sl]
        gy = gy_ref[:, sl]
        gl = gy.astype(BF16)
        du = jnp.zeros((q, LANES), F32)
        for s in range(2):
            mine = first == (s == 0)
            row = pl.ds(2 * p + s, 1)
            gap = cumt_ref[row, :] - cume[:, HEADDIM * s : HEADDIM * s + 1]
            decay = jnp.exp(jnp.minimum(gap, 0.0))
            pairs = gram[...] * decay
            dpairs = dot_nt(jnp.where(mine, ul, jnp.zeros_like(ul)), gl)
            dgram[...] += dpairs * decay
            through = dot_nn((dpairs * pairs).astype(BF16), later)
            da[row, :] = jnp.sum(
                jnp.where(iota((q, q), 0) < iota((q, q), 1), through, 0.0), axis=0, keepdims=True
            )
            du = du + dot_nn(pairs.astype(BF16), jnp.where(mine, gl, jnp.zeros_like(gl)))
        x = xs[:, sl]
        wide = dus[:, sl] * jnp.exp(cume[q - 1 : q, :] - cume)
        du = du + wide
        to_head = (iota((LANES, LANES), 1) == 2 * p + iota((LANES, LANES), 0) // HEADDIM).astype(BF16)
        dte = dte_ref[:, sl]
        acc_x[...] += dot_nn((x * du).astype(BF16), to_head)
        acc_w[...] += dot_nn((x * dte * wide).astype(BF16), to_head)
        acc_g[...] += dot_nn((gy * jnp.exp(cume) * ya[:, sl]).astype(BF16), to_head)
        qx[0:q, sl] = (dte * du + par_ref[CONV + 2 : CONV + 3, sl] * gy) * dsil[:, sl]
        return carry

    lax.fori_loop(0, width // LANES, pair_body, 0)

    def unconv_body(i, carry):
        sl = pl.ds(pl.multiple_of(i * block, block), block)
        weight = par_ref[0:CONV, sl]
        ext = qx[:, sl]
        cur = ext[0:q]
        dpre = weight[CONV - 1 : CONV] * cur
        for k in range(CONV - 1):
            dpre = dpre + weight[k : k + 1] * ext[CONV - 1 - k : CONV - 1 - k + q]
        dx_ref[pl.ds(pl.multiple_of(c * q, q), q), sl] = dpre.astype(BF16)
        past = jnp.concatenate([xt_ref[:, sl], xm_ref[:, sl]], axis=0)
        for k in range(CONV):
            start = 8 - (CONV - 1) + k
            accx_ref[k : k + 1, sl] += jnp.sum(cur * past[start : start + q], axis=0, keepdims=True)
        accx_ref[CONV : CONV + 1, sl] += jnp.sum(cur, axis=0, keepdims=True)
        head_rows = jnp.concatenate([jnp.zeros((HALO, block), F32), cur[0:8]], axis=0)
        before = jnp.zeros((HALO, block), F32)
        for k in range(CONV - 1):
            before = before + weight[k : k + 1] * head_rows[CONV - 1 - k : CONV - 1 - k + HALO]
        dx_ref[pl.ds(tokens, HALO), sl] = before.astype(BF16)
        qx[q:, sl] = cur[0:8]
        return carry

    lax.fori_loop(0, width // block, unconv_body, 0)

    dg = jnp.where(upper, dgram[...], 0.0)
    db = db + dot_split(dg, bc[:, STATE:])
    dc = dc + dot_split(dg.T, bc[:, :STATE])
    qb[0:q, 0:STATE] = qb[0:q, 0:STATE] * db
    qb[0:q, STATE:] = qb[0:q, STATE:] * dc
    weight = bcpar_ref[0:CONV, :]
    ext = qb[...]
    cur = ext[0:q]
    dpre = weight[CONV - 1 : CONV] * cur
    for k in range(CONV - 1):
        dpre = dpre + weight[k : k + 1] * ext[CONV - 1 - k : CONV - 1 - k + q]
    ds_ref[pl.ds(pl.multiple_of(c * q, q), q), 0 : 2 * STATE] = dpre.astype(BF16)
    past = jnp.concatenate([bt_ref[:, 0 : 2 * STATE], bm_ref[:, 0 : 2 * STATE]], axis=0)
    for k in range(CONV):
        start = 8 - (CONV - 1) + k
        accb_ref[k : k + 1, :] += jnp.sum(cur * past[start : start + q], axis=0, keepdims=True)
    accb_ref[CONV : CONV + 1, :] += jnp.sum(cur, axis=0, keepdims=True)
    head_rows = jnp.concatenate([jnp.zeros((HALO, 2 * STATE), F32), cur[0:8]], axis=0)
    before = jnp.zeros((HALO, 2 * STATE), F32)
    for k in range(CONV - 1):
        before = before + weight[k : k + 1] * head_rows[CONV - 1 - k : CONV - 1 - k + HALO]
    ds_ref[pl.ds(tokens, HALO), 0 : 2 * STATE] = before.astype(BF16)
    qb[q:, :] = cur[0:8]

    raw = bm_ref[:, 2 * STATE :] + hp_ref[0:1, :]
    dt = softplus(raw)
    rate = hp_ref[1:2, :]
    from_here = (iota((q, q), 1) >= iota((q, q), 0)).astype(F32)
    up_to_here = (iota((q, q), 1) < iota((q, q), 0)).astype(F32)
    kept_heads = dot_nt(jnp.broadcast_to(kept, (8, width)), head_spread(width), HIGHEST)
    total = (
        da[...].T
        + dot_nn(from_here, acc_g[...], HIGHEST)
        + dot_nn(up_to_here, acc_w[...], HIGHEST)
        + kept_heads[0:1, :]
    )
    d_raw = (acc_x[...] + rate * total) * sigmoid(raw)
    ds_ref[pl.ds(pl.multiple_of(c * q, q), q), 2 * STATE :] = d_raw.astype(BF16)
    acch_ref[0:1, :] += jnp.sum(d_raw, axis=0, keepdims=True)
    acch_ref[1:2, :] += rate * jnp.sum(dt * total, axis=0, keepdims=True)


def shape(dims, dtype):
    return jax.ShapeDtypeStruct(dims, dtype)


def whole(dims):
    return pl.BlockSpec(dims, lambda c: (0,) * len(dims))


def run(kernel, name, grid, in_specs, out_specs, out_shape, scratch, args, flops):
    return pl.pallas_call(
        kernel,
        grid=(grid,),
        in_specs=in_specs,
        out_specs=out_specs,
        out_shape=out_shape,
        scratch_shapes=scratch,
        name=name,
        compiler_params=pltpu.CompilerParams(
            dimension_semantics=("arbitrary",), vmem_limit_bytes=60 * 1024 * 1024
        ),
        cost_estimate=pl.CostEstimate(
            flops=flops, bytes_accessed=sum(a.size * a.dtype.itemsize for a in args), transcendentals=0
        ),
    )(*args)


def mixer_forward_state(x_ext, s_ext, par, bcpar, hp, tokens):
    width = x_ext.shape[1]
    small = s_ext.shape[1]
    n = tokens // CHUNK
    q = CHUNK
    tail = q // 8
    last = (tokens + HALO) // 8 - 1
    tail_map = lambda c: (jnp.where(c == 0, last, c * tail - 1), 0)
    heads_pad = -(-(width // HEADDIM) // 8) * 8
    return run(
        state_kernel,
        "scan_states",
        n,
        [
            pl.BlockSpec((q, width), lambda c: (c, 0)),
            pl.BlockSpec((8, width), tail_map),
            pl.BlockSpec((q, small), lambda c: (c, 0)),
            pl.BlockSpec((8, small), tail_map),
            whole(par.shape),
            whole(bcpar.shape),
            whole(hp.shape),
        ],
        [
            pl.BlockSpec((q, width), lambda c: (c, 0)),
            pl.BlockSpec((q, width), lambda c: (c, 0)),
            pl.BlockSpec((q, width), lambda c: (c, 0)),
            pl.BlockSpec((q, width), lambda c: (c, 0)),
            pl.BlockSpec((q, 2 * STATE), lambda c: (c, 0)),
            pl.BlockSpec((heads_pad, q), lambda c: (0, c)),
            pl.BlockSpec((1, STATE, width), lambda c: (c, 0, 0)),
            whole((STATE, width)),
            pl.BlockSpec((1, 1, width), lambda c: (c, 0, 0)),
        ],
        [
            shape((tokens, width), F32),
            shape((tokens, width), BF16),
            shape((tokens, width), F32),
            shape((tokens, width), F32),
            shape((tokens, 2 * STATE), F32),
            shape((heads_pad, tokens), F32),
            shape((n, STATE, width), F32),
            shape((STATE, width), BF16),
            shape((n, 1, width), F32),
        ],
        [
            pltpu.VMEM((STATE, width), F32),
            pltpu.VMEM((1, width), F32),
            pltpu.VMEM((q, width), BF16),
        ],
        (x_ext, x_ext, s_ext, s_ext, par, bcpar, hp),
        int(3e9),
    )


def mixer_forward_main(xs, u, cume, cumt, bc, sloc, sin, dec, z, gyn, par):
    tokens, width = xs.shape
    q = CHUNK
    n = tokens // q
    rows = pl.BlockSpec((q, width), lambda c: (c, 0))
    return run(
        main_kernel,
        "scan_outputs",
        n,
        [
            rows,
            rows,
            rows,
            pl.BlockSpec((cumt.shape[0], q), lambda c: (0, c)),
            pl.BlockSpec((q, 2 * STATE), lambda c: (c, 0)),
            pl.BlockSpec((1, STATE, width), lambda c: (c, 0, 0)),
            whole(sin.shape),
            pl.BlockSpec((1, 1, width), lambda c: (c, 0, 0)),
            rows,
            rows,
            whole(par.shape),
        ],
        [rows, pl.BlockSpec((8, q), lambda c: (0, c))],
        [shape((tokens, width), F32), shape((8, tokens), F32)],
        [
            pltpu.VMEM((q, q), F32),
            pltpu.VMEM((q, width), F32),
            pltpu.VMEM((q, LANES), F32),
            pltpu.VMEM((q, LANES), F32),
        ],
        (xs, u, cume, cumt, bc, sloc, sin, dec, z, gyn, par),
        int(10e9),
    )


def mixer_backward_gate(y, z, gyn, xs, cume, bc, stat, par):
    tokens, width = y.shape
    q = CHUNK
    n = tokens // q
    rows = pl.BlockSpec((q, width), lambda c: (n - 1 - c, 0))
    return run(
        gate_kernel,
        "gate_back",
        n,
        [
            rows,
            rows,
            rows,
            rows,
            rows,
            pl.BlockSpec((q, 2 * STATE), lambda c: (n - 1 - c, 0)),
            pl.BlockSpec((q, 8), lambda c: (n - 1 - c, 0)),
            whole(par.shape),
        ],
        [
            rows,
            rows,
            rows,
            pl.BlockSpec((1, STATE, width), lambda c: (n - 1 - c, 0, 0)),
            whole((STATE, width)),
            pl.BlockSpec((1, 1, width), lambda c: (n - 1 - c, 0, 0)),
            whole((8, width)),
        ],
        [
            shape((tokens, width), BF16),
            shape((tokens, width), F32),
            shape((tokens, width), BF16),
            shape((n, STATE, width), F32),
            shape((STATE, width), BF16),
            shape((n, 1, width), F32),
            shape((8, width), F32),
        ],
        [
            pltpu.VMEM((STATE, width), F32),
            pltpu.VMEM((1, width), F32),
            pltpu.VMEM((q, width), BF16),
        ],
        (y, z, gyn, xs, cume, bc, stat, par),
        int(5e9),
    )


def mixer_backward_main(
    x_ext, s_ext, par, bcpar, hp, cume, dte, cumt, gy, sloc, sin, sdec, gloc, gout, gdec
):
    tokens, width = cume.shape
    small = s_ext.shape[1]
    q = CHUNK
    n = tokens // q
    tail = q // 8
    last = (tokens + HALO) // 8 - 1
    rows = pl.BlockSpec((q, width), lambda c: (n - 1 - c, 0))
    tail_map = lambda c: (jnp.where(c == n - 1, last, (n - 1 - c) * tail - 1), 0)
    states = pl.BlockSpec((1, STATE, width), lambda c: (n - 1 - c, 0, 0))
    decays = pl.BlockSpec((1, 1, width), lambda c: (n - 1 - c, 0, 0))
    return run(
        back_kernel,
        "scan_back",
        n,
        [
            rows,
            pl.BlockSpec((8, width), tail_map),
            pl.BlockSpec((q, small), lambda c: (n - 1 - c, 0)),
            pl.BlockSpec((8, small), tail_map),
            whole(par.shape),
            whole(bcpar.shape),
            whole(hp.shape),
            rows,
            rows,
            pl.BlockSpec((cumt.shape[0], q), lambda c: (0, n - 1 - c)),
            rows,
            states,
            whole(sin.shape),
            decays,
            states,
            whole(gout.shape),
            decays,
        ],
        [
            whole((tokens + HALO, width)),
            whole((tokens + HALO, small)),
            whole((8, width)),
            whole((8, 2 * STATE)),
            whole((8, LANES)),
        ],
        [
            shape((tokens + HALO, width), BF16),
            shape((tokens + HALO, small), BF16),
            shape((8, width), F32),
            shape((8, 2 * STATE), F32),
            shape((8, LANES), F32),
        ],
        [
            pltpu.VMEM((q, width), F32),
            pltpu.VMEM((q, width), BF16),
            pltpu.VMEM((q, width), F32),
            pltpu.VMEM((q, width), BF16),
            pltpu.VMEM((q, width), BF16),
            pltpu.VMEM((q, width), F32),
            pltpu.VMEM((q, width), F32),
            pltpu.VMEM((q + 8, width), F32),
            pltpu.VMEM((q + 8, 2 * STATE), F32),
            pltpu.VMEM((q, q), F32),
            pltpu.VMEM((q, q), F32),
            pltpu.VMEM((LANES, q), F32),
            pltpu.VMEM((q, LANES), F32),
            pltpu.VMEM((q, LANES), F32),
            pltpu.VMEM((q, LANES), F32),
        ],
        (x_ext, x_ext, s_ext, s_ext, par, bcpar, hp, cume, dte, cumt, gy, sloc, sin, sdec, gloc, gout, gdec),
        int(30e9),
    )


MESH = pl.DeviceIdType.MESH


def flip(index, bit):
    return index + (1 - 2 * ((index // (1 << bit)) % 2)) * (1 << bit)


def flip_all(index, offset):
    bit = 0
    while offset >> bit:
        if (offset >> bit) & 1:
            index = flip(index, bit)
        bit += 1
    return index


def gather_kernel(
    tok_bits, row_bits, half_bit,
    in_ref, gain_ref, par_ref, small_ref, wx_ref, wz_ref, wo_ref,
    x_out, s_out, z_out, normed_out, rows_out, ws_out, wx_out, wz_out, wo_out, gains_out, pars_out,
    ws, wx, wz, wo, joined, rows, halo, normed, gains, pars, stage,
    send_sem, recv_sem, local_sem, stage_sem,
):
    tok, head = lax.axis_index("tok"), lax.axis_index("head")
    sets = 1 << len(row_bits)
    heads = 2 * sets
    half, mine = head // sets, head % sets
    own_rows, model = in_ref.shape
    share, own_width = wx_ref.shape
    tokens = own_rows * sets
    partners = [{"tok": flip(tok, b)} for b in tok_bits]
    partners += [{"head": flip_all(head, p)} for p in range(1, heads)]

    barrier = pltpu.get_barrier_semaphore()
    for partner in partners:
        pl.semaphore_signal(barrier, inc=1, device_id=partner, device_id_type=MESH)
    pl.semaphore_wait(barrier, len(partners))

    sent, stored, open_local = [], [], []

    def send(src, dst, device):
        k = len(sent)
        copy = pltpu.make_async_remote_copy(
            src_ref=src, dst_ref=dst, send_sem=send_sem.at[k], recv_sem=recv_sem.at[k],
            device_id=device, device_id_type=MESH,
        )
        copy.start()
        sent.append(copy)
        return copy

    def local(src, dst):
        copy = pltpu.make_async_copy(src, dst, local_sem.at[len(stored)])
        copy.start()
        stored.append(copy)
        open_local.append(copy)
        return copy

    def settle(copy):
        if any(copy is other for other in open_local):
            open_local[:] = [other for other in open_local if other is not copy]
            copy.wait()

    def arrive(copies):
        for copy in copies:
            copy.wait_recv()

    other_half = {"head": flip(head, half_bit)}
    lanes = pl.ds(pl.multiple_of(half * own_width, LANES), own_width)

    class Piece:
        def __init__(self, src, dst, part, order):
            size = share // 2
            self.rows = pl.ds(part * size, size)
            self.dst, self.order, self.held = dst, list(order), [0]
            slot = dst.at[tok, self.rows, lanes]
            self.flight = [send(src.at[self.rows], slot, other_half)]
            self.kept = local(src.at[self.rows], slot)

        def advance(self):
            arrive(self.flight)
            settle(self.kept)
            self.flight = []
            if self.order:
                bit = self.order.pop(0)
                for offset in self.held:
                    slot = self.dst.at[flip_all(tok, offset), self.rows]
                    self.flight.append(send(slot, slot, {"tok": flip(tok, bit)}))
                self.held = self.held + [offset ^ (1 << bit) for offset in self.held]

        def finish(self):
            while self.flight:
                self.advance()

    class Small(Piece):
        def __init__(self, src, dst, order):
            self.rows = pl.ds(0, share)
            self.dst, self.order, self.held = dst, list(order), [0]
            wide = pl.ds(pl.multiple_of(2 * STATE + half * LANES, LANES), LANES)
            slot = dst.at[tok, :, wide]
            part = src.at[:, pl.ds(2 * STATE, LANES)]
            self.flight = [send(part, slot, other_half)]
            settle(local(part, slot))
            self.kept = local(src.at[:, pl.ds(0, 2 * STATE)], dst.at[tok, :, pl.ds(0, 2 * STATE)])

    class Rows:
        def __init__(self, src, dst):
            self.dst, self.order, self.held = dst, list(row_bits), [0]
            self.src = src
            self.kept = local(src, dst.at[mine])
            self.flight = []
            if self.order:
                bit = self.order.pop(0)
                self.flight.append(send(src, dst.at[mine], {"head": flip(head, bit)}))
                self.held = [0, 1 << bit]

        def advance(self):
            arrive(self.flight)
            settle(self.kept)
            self.flight = []
            if self.order:
                bit = self.order.pop(0)
                for offset in self.held:
                    slot = self.dst.at[flip_all(mine, offset)]
                    self.flight.append(send(slot, slot, {"head": flip(head, bit)}))
                self.held = self.held + [offset ^ (1 << bit) for offset in self.held]

        def finish(self):
            settle(self.kept)
            while self.flight:
                self.advance()

    up = list(tok_bits)[1:] + [0]
    down = list(tok_bits)[1:][::-1] + [0]
    gain_copies = [
        send(gain_ref, gains.at[p], {"head": flip_all(head, p)}) for p in range(1, heads)
    ]
    gain_kept = local(gain_ref, gains.at[0])
    par_slot = pars.at[:, lanes]
    par_copy = send(par_ref, par_slot, other_half)
    par_kept = local(par_ref, par_slot)
    p_small = Small(small_ref, ws, up)
    p_xa = Piece(wx_ref, wx, 0, up)
    p_xb = Piece(wx_ref, wx, 1, down)
    p_za = Piece(wz_ref, wz, 0, up)
    p_zb = Piece(wz_ref, wz, 1, down)
    r_in = Rows(in_ref, rows)
    p_oa = Piece(wo_ref, wo, 0, up)
    p_ob = Piece(wo_ref, wo, 1, down)
    first, second, third = (p_small, p_xa, p_xb), (p_za, p_zb), (p_oa, p_ob)

    def advance(pieces):
        for piece in pieces:
            piece.advance()

    def normalise(src, start, count, scale):
        def body(i, carry):
            at = pl.ds(pl.multiple_of(start + i * 16, 16), 16)
            wide = src[pl.ds(pl.multiple_of(i * 16, 16), 16), :].astype(F32)
            inv = lax.rsqrt(jnp.sum(wide * wide, axis=1, keepdims=True) / model + EPS)
            normed[at, :] = (wide * inv * scale).astype(BF16)
            return carry

        lax.fori_loop(0, count // 16, body, 0, unroll=4 if count >= 64 else 1)

    def project(lhs, count, weight, out, width):
        tile = 256 if width % 256 == 0 else 3 * LANES
        steps = width // tile

        def out_copy(i):
            at = pl.ds(pl.multiple_of(i * tile, tile), tile)
            return pltpu.make_async_copy(
                stage.at[i % 2, pl.ds(0, count), pl.ds(0, tile)], out.at[:, at], stage_sem.at[i % 2]
            )

        def body(i, carry):
            @pl.when(i >= 2)
            def _():
                out_copy(i - 2).wait()

            at = pl.ds(pl.multiple_of(i * tile, tile), tile)
            block = weight[:, :, at].reshape(model, tile)
            stage[i % 2, 0:count, 0:tile] = dot_nn(lhs[...].reshape(count, model), block)
            out_copy(i).start()
            return carry

        lax.fori_loop(0, steps, body, 0)
        for i in range(max(steps - 2, 0), steps):
            out_copy(i).wait()

    def finish(pieces):
        for piece in pieces:
            piece.finish()

    def join_heads():
        def body(i, carry):
            low = ws[i, :, 2 * STATE : 2 * STATE + LANES].astype(F32)
            high = ws[i, :, 2 * STATE + LANES :].astype(F32)
            joined[i, :, : 2 * STATE] = ws[i, :, : 2 * STATE]
            joined[i, :, 2 * STATE :] = (low + pltpu.roll(high, own_width // HEADDIM, 1)).astype(BF16)
            return carry

        lax.fori_loop(0, ws.shape[0], body, 0)

    advance(first)
    advance(second)
    arrive(gain_copies)
    settle(gain_kept)
    scale = gains[0, 0:1, :]
    for p in range(1, heads):
        scale = scale + gains[p, 0:1, :]
    gains[0, 0:1, :] = scale
    advance(first)
    settle(r_in.kept)
    normalise(rows.at[mine], mine * own_rows, own_rows, scale)
    advance(second)
    advance(first)
    advance(third)
    advance(second)
    finish(first)
    join_heads()
    local(joined, ws_out)
    local(wx, wx_out)
    r_in.finish()
    tail = rows.at[sets - 1, pl.ds(own_rows - HALO, HALO), :]
    tail_copy = send(tail, halo, other_half)
    advance(third)
    for i in range(1, sets):
        other = flip_all(mine, i)
        normalise(rows.at[other], other * own_rows, own_rows, scale)
    tail_copy.wait_recv()
    normalise(halo, tokens, HALO, scale * half.astype(F32))
    local(rows, rows_out)
    local(normed, normed_out)
    project(normed, tokens + HALO, joined, s_out, s_out.shape[1])
    advance(third)
    project(normed, tokens + HALO, wx, x_out, wx.shape[2])
    finish(second)
    local(wz, wz_out)
    finish(third)
    local(wo, wo_out)
    project(normed.at[pl.ds(0, tokens)], tokens, wz, z_out, wz.shape[2])
    arrive([par_copy])
    settle(par_kept)
    local(pars, pars_out)
    local(gains.at[0], gains_out)
    for copy in list(open_local):
        settle(copy)
    for copy in sent:
        copy.wait_send()


def gather_and_project(block_in, gain, par, small, wx, wz, wo):
    tok_size, head_size = lax.axis_size("tok"), lax.axis_size("head")
    sets = head_size // HALVES
    tok_bits = range(tok_size.bit_length() - 1)
    row_bits = range(sets.bit_length() - 1)
    own_rows, model = block_in.shape
    share, own_width = wx.shape
    width = HALVES * own_width
    tokens = own_rows * sets
    lanes = 2 * STATE + HALVES * LANES
    anywhere = pl.BlockSpec(memory_space=pl.ANY)
    slots = (tok_size, share)
    copies = 128
    outs = [
        shape((tokens + HALO, width), F32),
        shape((tokens + HALO, 2 * STATE + LANES), F32),
        shape((tokens, width), F32),
        shape((tokens + HALO, model), BF16),
        shape((sets, own_rows, model), BF16),
        shape(slots + (2 * STATE + LANES,), BF16),
        shape(slots + (width,), BF16),
        shape(slots + (width,), BF16),
        shape(slots + (width,), BF16),
        shape((8, model), F32),
        shape((8, width), F32),
    ]
    return pl.pallas_call(
        functools.partial(gather_kernel, tok_bits, row_bits, sets.bit_length() - 1),
        in_specs=[anywhere] * 7,
        out_specs=[anywhere] * len(outs),
        out_shape=outs,
        scratch_shapes=[
            pltpu.VMEM(slots + (lanes,), BF16),
            pltpu.VMEM(slots + (width,), BF16),
            pltpu.VMEM(slots + (width,), BF16),
            pltpu.VMEM(slots + (width,), BF16),
            pltpu.VMEM(slots + (2 * STATE + LANES,), BF16),
            pltpu.VMEM((sets, own_rows, model), BF16),
            pltpu.VMEM((HALO, model), BF16),
            pltpu.VMEM((tokens + HALO, model), BF16),
            pltpu.VMEM((head_size, 8, model), F32),
            pltpu.VMEM((8, width), F32),
            pltpu.VMEM((2, tokens + HALO, 3 * LANES), F32),
            pltpu.SemaphoreType.DMA((copies,)),
            pltpu.SemaphoreType.DMA((copies,)),
            pltpu.SemaphoreType.DMA((32,)),
            pltpu.SemaphoreType.DMA((2,)),
        ],
        name="gather",
        compiler_params=pltpu.CompilerParams(
            collective_id=0, has_side_effects=True, vmem_limit_bytes=60 * 1024 * 1024
        ),
        cost_estimate=pl.CostEstimate(flops=int(12e9), bytes_accessed=int(60e6), transcendentals=0),
    )(block_in, gain, par, small, wx, wz, wo)


class Links:
    def __init__(self, send_sem, recv_sem, local_sem, tok_bits, row_bits):
        self.send_sem, self.recv_sem, self.local_sem = send_sem, recv_sem, local_sem
        self.tok_bits, self.row_bits = list(tok_bits), list(row_bits)
        self.tok, self.head = lax.axis_index("tok"), lax.axis_index("head")
        self.sets = 1 << len(self.row_bits)
        self.half, self.mine = self.head // self.sets, self.head % self.sets
        self.half_bit = len(self.row_bits)
        self.sent, self.drained, self.n_local, self.open_local = [], [], 0, []

    def enter(self):
        partners = [self.tok_peer(b) for b in self.tok_bits]
        partners += [self.head_peer(b) for b in self.row_bits + [self.half_bit]]
        barrier = pltpu.get_barrier_semaphore()
        for partner in partners:
            pl.semaphore_signal(barrier, inc=1, device_id=partner, device_id_type=MESH)
        pl.semaphore_wait(barrier, len(partners))

    def tok_peer(self, bit):
        return {"tok": flip(self.tok, bit)}

    def head_peer(self, bit):
        return {"head": flip(self.head, bit)}

    def send(self, src, dst, device):
        k = len(self.sent)
        copy = pltpu.make_async_remote_copy(
            src_ref=src,
            dst_ref=dst,
            send_sem=self.send_sem.at[k],
            recv_sem=self.recv_sem.at[k],
            device_id=device,
            device_id_type=MESH,
        )
        copy.start()
        self.sent.append(copy)
        return copy

    def local(self, src, dst):
        copy = pltpu.make_async_copy(src, dst, self.local_sem.at[self.n_local])
        copy.start()
        self.n_local += 1
        self.open_local.append(copy)
        return copy

    def settle(self, copies):
        for copy in copies:
            if any(copy is other for other in self.open_local):
                self.open_local = [other for other in self.open_local if other is not copy]
                copy.wait()

    def drain(self, copy):
        copy.wait_recv()
        copy.wait_send()
        self.drained.append(copy)

    def leave(self):
        self.settle(list(self.open_local))
        for copy in self.sent:
            if not any(copy is other for other in self.drained):
                copy.wait_send()


def add_rows(dst, src, count):
    def body(i, carry):
        at = pl.ds(pl.multiple_of(i * 16, 16), 16)
        dst[at, :] = (dst[at, :].astype(F32) + src[at, :].astype(F32)).astype(BF16)
        return carry

    lax.fori_loop(0, count // 16, body, 0)


class Sum:
    def __init__(self, links, src, keep, recv, final, out, part, parts, order):
        self.links, self.keep, self.recv, self.final, self.out = links, keep, recv, final, out
        self.size = keep.shape[1] // parts
        self.start = part * self.size
        self.rows = pl.ds(self.start, self.size)
        self.order = list(order)
        bit = self.order.pop(0)
        slots = range(1 << len(links.tok_bits))
        self.held = [o for o in slots if not (o >> bit) & 1]
        self.place = {o: i for i, o in enumerate(self.held)}
        self.base = len(self.held)
        self.into = [(i, i) for i in range(self.base)]
        self.flight = [
            links.send(
                src.at[flip_all(links.tok, o ^ (1 << bit)), self.rows],
                recv.at[self.place[o], self.rows],
                links.tok_peer(bit),
            )
            for o in self.held
        ]
        self.kept = [
            links.local(src.at[flip_all(links.tok, o), self.rows], keep.at[self.place[o], self.rows])
            for o in self.held
        ]
        self.tail = None

    def half_lanes(self, which):
        width = self.out.shape[1]
        return pl.ds(pl.multiple_of(which * width, LANES), width)

    def advance(self):
        if self.tail is not None:
            return
        for copy in self.flight:
            copy.wait_recv()
        self.links.settle(self.kept)
        for place, i in self.into:
            add_rows(self.keep.at[place, self.rows], self.recv.at[i, self.rows], self.size)
        self.flight, self.into, self.kept = [], [], []
        if not self.order:
            self.last()
            return
        bit = self.order.pop(0)
        stay = [o for o in self.held if not (o >> bit) & 1]
        for n, o in enumerate(stay):
            self.flight.append(
                self.links.send(
                    self.keep.at[self.place[o ^ (1 << bit)], self.rows],
                    self.recv.at[self.base + n, self.rows],
                    self.links.tok_peer(bit),
                )
            )
            self.into.append((self.place[o], self.base + n))
        self.base += len(stay)
        self.held = stay

    def last(self):
        width = self.out.shape[1]
        self.tail = self.links.send(
            self.keep.at[0, self.rows, self.half_lanes(1 - self.links.half)],
            self.recv.at[self.base, self.rows, pl.ds(0, width)],
            self.links.head_peer(self.links.half_bit),
        )

    def finish(self):
        while self.tail is None:
            self.advance()
        self.tail.wait_recv()
        width = self.out.shape[1]
        lanes = self.half_lanes(self.links.half)

        def body(i, carry):
            at = pl.ds(pl.multiple_of(self.start + i * 16, 16), 16)
            self.final[at, :] = self.keep[0, at, lanes].astype(F32) + self.recv[self.base, at, 0:width].astype(F32)
            return carry

        lax.fori_loop(0, self.size // 16, body, 0)
        self.links.local(self.final.at[self.rows], self.out.at[self.rows])


class SmallSum(Sum):
    def __init__(self, links, src, src_low, keep, low, recv, order):
        self.links, self.keep, self.low, self.recv = links, keep, low, recv
        self.order = list(order)
        bit = self.order.pop(0)
        slots = range(1 << len(links.tok_bits))
        self.held = [o for o in slots if not (o >> bit) & 1]
        self.place = {o: i for i, o in enumerate(self.held)}
        self.base = len(self.held)
        self.n_low = 0
        self.into = [(i, i) for i in range(self.base)]
        self.flight = [
            links.send(src_low.at[flip_all(links.tok, o ^ (1 << bit))], recv.at[self.place[o]], links.tok_peer(bit))
            for o in self.held
        ]
        self.kept = [links.local(src.at[flip_all(links.tok, o)], keep.at[self.place[o]]) for o in self.held]
        self.done = False

    def post(self, place, lanes, device):
        n = self.n_low
        self.low[n, :, 0:lanes] = self.keep[place, :, 0:lanes].astype(BF16)
        self.n_low += 1
        src, dst = self.low.at[n, :, pl.ds(0, lanes)], self.recv.at[self.base, :, pl.ds(0, lanes)]
        self.flight.append(self.links.send(src, dst, device))
        self.base += 1
        return self.base - 1

    def take(self):
        for copy in self.flight:
            copy.wait_recv()
        self.links.settle(self.kept)
        for place, i in self.into:
            self.keep[place, :, 0 : self.lanes_in] = self.keep[place, :, 0 : self.lanes_in] + self.recv[
                i, :, 0 : self.lanes_in
            ].astype(F32)
        self.flight, self.into, self.kept = [], [], []

    lanes_in = 2 * STATE + LANES

    def advance(self):
        if self.done:
            return
        self.take()
        if not self.order:
            self.into = [(0, self.post(0, self.lanes_in, self.links.head_peer(self.links.half_bit)))]
            self.done = True
            return
        bit = self.order.pop(0)
        stay = [o for o in self.held if not (o >> bit) & 1]
        self.into = [
            (self.place[o], self.post(self.place[o ^ (1 << bit)], self.lanes_in, self.links.tok_peer(bit)))
            for o in stay
        ]
        self.held = stay

    def finish(self):
        while not self.done:
            self.advance()
        self.take()
        self.lanes_in = 2 * STATE
        for bit in self.links.row_bits:
            self.into = [(0, self.post(0, self.lanes_in, self.links.head_peer(bit)))]
            self.take()


def reduce_kernel(
    tok_bits, row_bits,
    gx_ref, gz_ref, go_ref, gs_ref, gl_ref, dx_ref, ds_ref, dn_ref, rows_ref, wx_ref, ws_ref, cot_ref, gain_ref, per_ref, bc_ref,
    ox_ref, oz_ref, oo_ref, os_ref, dblock_ref, all_out, per_out,
    kx, kz, ko, ks, rx, rz, ro, rs, fx, fz, fo, ls,
    dx, ds, wx, ws, rows, cots, dnorm, base, low, got, halo_out, halo_in, sums, sums_got,
    send_sem, recv_sem, local_sem, chunk_sem,
):
    links = Links(send_sem, recv_sem, local_sem, tok_bits, row_bits)
    half, mine, sets = links.half, links.mine, links.sets
    own_rows, model = cot_ref.shape
    own_width = ox_ref.shape[1]
    tokens = own_rows * sets
    chunk = base.shape[0]
    links.enter()

    up = [0] + links.tok_bits[1:]
    down = [0] + links.tok_bits[1:][::-1]
    loads = [links.local(dx_ref, dx), links.local(ds_ref, ds), links.local(wx_ref, wx), links.local(ws_ref, ws)]
    s_small = SmallSum(links, gs_ref, gl_ref, ks, ls, rs, up)
    s_x = [Sum(links, gx_ref, kx, rx, fx, ox_ref, p, 2, (down, up)[p]) for p in range(2)]
    s_z = [Sum(links, gz_ref, kz, rz, fz, oz_ref, p, 2, (down, up)[p]) for p in range(2)]
    s_o = [Sum(links, go_ref, ko, ro, fo, oo_ref, p, 2, (down, up)[p]) for p in range(2)]
    row_load = links.local(rows_ref, rows)
    cot_load = links.local(cot_ref, cots)

    def advance(group):
        for each in group:
            each.advance()

    def project_back(at, count):
        lhs_x, lhs_s = dx[at, :], ds[at, :]
        return dot_nt(lhs_x, wx[...].reshape(model, wx.shape[2])) + dot_nt(lhs_s, ws[...].reshape(model, ws.shape[2]))

    def fetch(slot, i):
        at = pl.ds(pl.multiple_of(slot * own_rows + i * chunk, chunk), chunk)
        return pltpu.make_async_copy(dn_ref.at[at], base, chunk_sem.at[0])

    def slot_rows(slot):
        def body(i, carry):
            fetch(slot, i).start()
            total = project_back(pl.ds(pl.multiple_of(slot * own_rows + i * chunk, chunk), chunk), chunk)
            fetch(slot, i).wait()
            dnorm[slot, pl.ds(pl.multiple_of(i * chunk, chunk), chunk), :] = total + base[...]
            return carry

        lax.fori_loop(0, own_rows // chunk, body, 0)

    def fold(slot):
        keep = jnp.where(half == 0, 1.0, 0.0) * jnp.where(slot == sets - 1, 1.0, 0.0)
        tail = pl.ds(own_rows - HALO, HALO)
        dnorm[slot, tail, :] = dnorm[slot, tail, :] + keep * halo_in[...]

    def unit_rows(slot, at):
        wide = rows[slot, at, :].astype(F32)
        return wide, lax.rsqrt(jnp.sum(wide * wide, axis=1, keepdims=True) / model + EPS)

    def gain_part(slot):
        def body(i, total):
            at = pl.ds(pl.multiple_of(i * 16, 16), 16)
            wide, inv = unit_rows(slot, at)
            part = dnorm[slot, at, :] * wide * inv
            return total + part[0:8] + part[8:16]

        return lax.fori_loop(0, own_rows // 16, body, jnp.zeros((8, model), F32))

    links.settle(loads)
    halo_out[...] = project_back(pl.ds(tokens, HALO), HALO)
    away = list(range(1, sets))[::-1]
    slots = [flip_all(mine, o) for o in away]
    if slots:
        slot_rows(slots[0])
    halo_copy = links.send(halo_out, halo_in, links.head_peer(links.half_bit))
    advance([s_small])
    advance(s_x)
    for slot in slots[1:]:
        slot_rows(slot)
    links.settle([row_load])
    halo_copy.wait_recv()
    gain_sum = jnp.zeros((8, model), F32)
    for slot in slots:
        fold(slot)
        gain_sum = gain_sum + gain_part(slot)
    sums[0, :, pl.ds(0, model)] = gain_sum

    row_order = list(row_bits)[::-1]
    held = list(range(sets))
    places = 0

    def send_rows():
        nonlocal held, places
        bit = row_order.pop(0)
        stay = [o for o in held if not (o >> bit) & 1]
        flight = []
        for o in stay:
            slot = flip_all(mine, o ^ (1 << bit))

            def body(i, carry, slot=slot, place=places):
                at = pl.ds(pl.multiple_of(i * 16, 16), 16)
                low[place, at, :] = dnorm[slot, at, :].astype(BF16)
                return carry

            lax.fori_loop(0, own_rows // 16, body, 0)
            flight.append((o, places))
            places += 1
        held = stay
        return bit, flight

    def start_rows(bit, flight):
        return [(o, p, links.send(low.at[p], got.at[p], links.head_peer(bit))) for o, p in flight]

    def take_rows(copies):
        for o, place, copy in copies:
            copy.wait_recv()
            slot = flip_all(mine, o)

            def body(i, carry, slot=slot, place=place):
                at = pl.ds(pl.multiple_of(i * 16, 16), 16)
                dnorm[slot, at, :] = dnorm[slot, at, :] + got[place, at, :].astype(F32)
                return carry

            lax.fori_loop(0, own_rows // 16, body, 0)

    prepared = send_rows() if row_order else None
    advance(s_z)
    row_copies = start_rows(*prepared) if prepared else []
    slot_rows(mine)
    fold(mine)
    gain_sum = sums[0, :, pl.ds(0, model)] + gain_part(mine)
    gain_row = jnp.sum(gain_sum, axis=0, keepdims=True)
    advance(s_o)
    advance(s_x)
    advance([s_small])

    bc_width = bc_ref.shape[1]
    sums[0, :, pl.ds(0, model)] = jnp.concatenate(
        [gain_row, jnp.concatenate([bc_ref[0:7, :], jnp.zeros((7, model - bc_width), F32)], axis=1)], axis=0
    )
    sums[0, :, pl.ds(model, own_width)] = per_ref[:, pl.ds(pl.multiple_of((1 - half) * own_width, LANES), own_width)]
    advance(s_z)
    advance(s_x)
    stage = 0
    wide = sums.shape[2]
    copy = links.send(sums.at[0], sums_got.at[0], links.head_peer(links.half_bit))
    advance([s_small])
    advance(s_o)
    copy.wait_recv()
    sums[1, :, pl.ds(0, model)] = sums[0, :, pl.ds(0, model)] + sums_got[0, :, pl.ds(0, model)]
    sums[1, :, pl.ds(model, own_width)] = (
        per_ref[:, pl.ds(pl.multiple_of(half * own_width, LANES), own_width)] + sums_got[0, :, pl.ds(model, own_width)]
    )
    stage = 1
    peers = [links.head_peer(b) for b in row_bits] + [links.tok_peer(b) for b in tok_bits]
    todo = [s_z, s_o]
    for n, peer in enumerate(peers):
        copy = links.send(sums.at[stage], sums_got.at[stage], peer)
        if n < len(todo):
            advance(todo[n])
        copy.wait_recv()
        if n < len(row_bits):
            sums[stage + 1, :, pl.ds(0, model)] = (
                sums[stage, :, pl.ds(0, model)] + sums_got[stage, :, pl.ds(0, model)]
            )
            sums[stage + 1, :, pl.ds(model, own_width)] = sums[stage, :, pl.ds(model, own_width)]
        else:
            sums[stage + 1] = sums[stage] + sums_got[stage]
        stage += 1
    links.local(sums.at[stage, :, pl.ds(0, model)], all_out)
    links.local(sums.at[stage, :, pl.ds(model, own_width)], per_out)

    s_small.finish()
    links.local(ks.at[0], os_ref)
    for each in s_x:
        each.finish()

    while row_copies:
        take_rows(row_copies)
        row_copies = start_rows(*send_rows()) if row_order else []
    links.settle([cot_load])
    gain = gain_ref[0:1, :]

    def block_rows(i, carry):
        at = pl.ds(pl.multiple_of(i * 16, 16), 16)
        wide, inv = unit_rows(mine, at)
        scaled = dnorm[mine, at, :] * gain
        inner = jnp.sum(scaled * wide, axis=1, keepdims=True) / model
        dnorm[mine, at, :] = cots[at, :].astype(F32) + inv * scaled - wide * (inv * inv * inv * inner)
        return carry

    lax.fori_loop(0, own_rows // 16, block_rows, 0)
    links.local(dnorm.at[mine], dblock_ref)
    for each in s_z + s_o:
        each.finish()
    links.leave()


def reduce_sums(gx, gz, go, gs, gl, dx, ds, dn, rows, wx, ws, cot, gain, per, bc):
    tok_size, head_size = lax.axis_size("tok"), lax.axis_size("head")
    sets = head_size // HALVES
    tok_bits = range(tok_size.bit_length() - 1)
    row_bits = range(sets.bit_length() - 1)
    own_rows, model = cot.shape
    share, width = gx.shape[1:]
    lanes = gs.shape[2]
    own_width = width // HALVES
    anywhere = pl.BlockSpec(memory_space=pl.ANY)
    inside = pl.BlockSpec(memory_space=pltpu.VMEM)
    keep, slots = tok_size // 2, tok_size + len(row_bits)
    stages = len(tok_bits) + len(row_bits) + 1
    away = max(sets - 1, 1)
    copies = 32 * len(tok_bits)
    outs = [
        shape((share, own_width), F32),
        shape((share, own_width), F32),
        shape((share, own_width), F32),
        shape((share, lanes), F32),
        shape((own_rows, model), F32),
        shape((8, model), F32),
        shape((8, own_width), F32),
    ]
    return pl.pallas_call(
        functools.partial(reduce_kernel, tok_bits, row_bits),
        in_specs=[anywhere] * 12 + [inside] * 3,
        out_specs=[anywhere] * len(outs),
        out_shape=outs,
        scratch_shapes=[pltpu.VMEM((keep, share, width), BF16)] * 3
        + [pltpu.VMEM((keep, share, lanes), F32)]
        + [pltpu.VMEM((slots, share, width), BF16)] * 3
        + [pltpu.VMEM((slots, share, lanes), BF16)]
        + [pltpu.VMEM((share, own_width), F32)] * 3
        + [pltpu.VMEM((slots, share, lanes), BF16)]
        + [
            pltpu.VMEM(dx.shape, BF16),
            pltpu.VMEM(ds.shape, BF16),
            pltpu.VMEM(wx.shape, BF16),
            pltpu.VMEM(ws.shape, BF16),
            pltpu.VMEM(rows.shape, BF16),
            pltpu.VMEM(cot.shape, BF16),
            pltpu.VMEM((sets, own_rows, model), F32),
            pltpu.VMEM((min(CHUNK, own_rows), model), F32),
            pltpu.VMEM((away, own_rows, model), BF16),
            pltpu.VMEM((away, own_rows, model), BF16),
            pltpu.VMEM((HALO, model), F32),
            pltpu.VMEM((HALO, model), F32),
            pltpu.VMEM((stages + 1, 8, model + own_width), F32),
            pltpu.VMEM((stages, 8, model + own_width), F32),
            pltpu.SemaphoreType.DMA((copies,)),
            pltpu.SemaphoreType.DMA((copies,)),
            pltpu.SemaphoreType.DMA((copies,)),
            pltpu.SemaphoreType.DMA((1,)),
        ],
        name="reduce",
        compiler_params=pltpu.CompilerParams(
            collective_id=1, has_side_effects=True, vmem_limit_bytes=62 * 1024 * 1024
        ),
        cost_estimate=pl.CostEstimate(flops=int(12e9), bytes_accessed=int(60e6), transcendentals=0),
    )(gx, gz, go, gs, gl, dx, ds, dn, rows, wx, ws, cot, gain, per, bc)


def per_device(
    block_in,
    norm_gain,
    w_zx,
    w_bc,
    w_dt,
    conv_x_w,
    conv_x_b,
    conv_bc_w,
    conv_bc_b,
    dt_bias,
    a_log,
    d_skip,
    gate_gain,
    w_out,
    cotangent,
):
    head_size = lax.axis_size("head")
    tok_size = lax.axis_size("tok")
    sets = head_size // HALVES
    row_bits = range(sets.bit_length() - 1)
    half_bit = sets.bit_length() - 1
    half = bit_of("head", half_bit)
    own_rows, model = block_in.shape
    share, _, own_width = w_zx.shape
    own_heads = w_dt.shape[1]
    tokens = own_rows * sets

    def all_rows(value):
        for bit in row_bits:
            value = grow(value, "head", bit, 0)
        return value

    def lane_pad(v):
        return jnp.pad(v, (0, LANES - v.shape[0]))

    heads_row = jnp.concatenate([lane_pad(dt_bias), lane_pad(a_log), lane_pad(d_skip)])
    own_par = jnp.concatenate(
        [
            conv_x_w,
            conv_x_b[None],
            gate_gain[None],
            jnp.repeat(d_skip, HEADDIM)[None],
            jnp.pad(heads_row, (0, own_width - heads_row.shape[0]))[None],
        ]
    )
    gain_share = norm_gain.shape[0]
    own_gain = lax.dynamic_update_slice(
        jnp.zeros((8, model), F32),
        jnp.broadcast_to(norm_gain.astype(F32)[None], (8, gain_share)),
        (0, lax.axis_index("head") * gain_share),
    )
    small = jnp.concatenate([w_bc, jnp.pad(w_dt, ((0, 0), (0, LANES - own_heads)))], axis=1)
    x_ext, s_ext, z, normed_ext, rows, w_small, w_x, w_z, w_o, gain, par = gather_and_project(
        block_in, own_gain, own_par, small, w_zx[:, 1], w_zx[:, 0], w_out.T
    )
    later_cot, x_ext = lax.optimization_barrier((cotangent, x_ext))
    cot = all_rows(later_cot)
    gain = gain[0:1]
    normed = normed_ext[:tokens]
    slots_small, slots_x, gain_rows = w_small, w_x, gain
    w_z, w_o = w_z.reshape(model, w_z.shape[2]), w_o.reshape(model, w_o.shape[2])

    def of_heads(start):
        pieces = [
            par[CONV + 3, i * own_width + start : i * own_width + start + own_heads] for i in range(HALVES)
        ]
        return jnp.concatenate(pieces)

    rate = -jnp.exp(of_heads(LANES))
    hp = jnp.stack([lane_pad(of_heads(0)), lane_pad(rate)] + [jnp.zeros((LANES,), F32)] * 6)
    bcpar = jnp.concatenate([conv_bc_w, conv_bc_b[None], jnp.zeros((3, 2 * STATE), F32)])

    xs, u, cume, dte, bc, cumt, sloc, fin, sdec = mixer_forward_state(x_ext, s_ext, par, bcpar, hp, tokens)
    to_next = [(i, i + sets) for i in range(sets)]
    to_prev = [(i + sets, i) for i in range(sets)]
    sin = lax.ppermute(fin, "head", to_next)
    gyn = dot_nn(cot, w_o)
    y, stat = mixer_forward_main(xs, u, cume, cumt, bc, sloc, sin, sdec, z, gyn, par)
    stat = add_pairs(stat, "head", row_bits).T
    inv_gate = lax.rsqrt(stat[:, 0:1] / INNER + EPS)
    stat = jnp.concatenate(
        [inv_gate, inv_gate * inv_gate * inv_gate * stat[:, 1:2] / INNER, stat[:, 2:]], axis=1
    )
    yn, gy, dz, gloc, gin, gdec, acc_gate = mixer_backward_gate(y, z, gyn, xs, cume, bc, stat, par)
    gout = lax.ppermute(gin, "head", to_prev)

    def own_row_sum(value):
        for bit in list(row_bits)[::-1]:
            value = halve(value, "head", bit, 0)
        return value

    def slots_of(grad):
        return grad.astype(BF16).reshape(tok_size, share, grad.shape[1])

    branch = dot_nt(yn, w_o)
    block_out = block_in.astype(F32) + own_row_sum(branch)
    grad_o = slots_of(dot_tn(cot, yn))
    grad_z = slots_of(dot_tn(normed, dz))
    d_normed_z = dot_nt(dz, w_z)

    dx, ds, acc_x, acc_b, acc_h = mixer_backward_main(
        x_ext, s_ext, par, bcpar, hp, cume, dte, cumt, gy, sloc, sin, sdec, gloc, gout, gdec
    )
    grad_x = slots_of(dot_tn(normed_ext, dx))
    grad_small = dot_tn(normed_ext, ds).reshape(tok_size, share, ds.shape[1])

    per_channel = jnp.concatenate(
        [
            acc_x[: CONV + 1],
            acc_gate[0:1],
            jnp.concatenate(
                [
                    jnp.pad(
                        jnp.concatenate(
                            [
                                lane_pad(acc_h[0, i * own_heads : (i + 1) * own_heads]),
                                lane_pad(acc_h[1, i * own_heads : (i + 1) * own_heads]),
                                lane_pad(
                                    jnp.sum(
                                        acc_gate[1, i * own_width : (i + 1) * own_width].reshape(own_heads, HEADDIM),
                                        axis=1,
                                    )
                                ),
                            ]
                        ),
                        (0, own_width - 3 * LANES),
                    )
                    for i in range(HALVES)
                ]
            )[None],
            jnp.zeros((1, HALVES * own_width), F32),
        ]
    )

    d_w_x, d_w_z, d_w_o, d_small, d_block_in, all_sums, own_sums = reduce_sums(
        grad_x, grad_z, grad_o, grad_small, grad_small.astype(BF16), dx, ds, d_normed_z, rows, slots_x, slots_small, cotangent,
        gain_rows, per_channel, acc_b,
    )
    all_gain, bc_sums = all_sums[0], all_sums[1:, : 2 * STATE]
    d_w_bc = d_small[:, : 2 * STATE]
    d_w_dt = jnp.where(
        half == 0,
        d_small[:, 2 * STATE : 2 * STATE + own_heads],
        d_small[:, 2 * STATE + own_heads : 2 * STATE + 2 * own_heads],
    )
    d_norm_gain = lax.dynamic_slice_in_dim(all_gain, lax.axis_index("head") * gain_share, gain_share, 0)
    return (
        block_out,
        d_block_in,
        d_norm_gain,
        jnp.stack([d_w_z, d_w_x], axis=1),
        d_w_bc,
        d_w_dt,
        own_sums[:CONV],
        own_sums[CONV],
        bc_sums[:CONV],
        bc_sums[CONV],
        own_sums[CONV + 2, :own_heads],
        own_sums[CONV + 2, LANES : LANES + own_heads],
        own_sums[CONV + 2, 2 * LANES : 2 * LANES + own_heads],
        own_sums[CONV + 1],
        d_w_o.T,
    )


def solution(mesh):
    placed = (
        P(("tok", "head"), None),
        P("head"),
        P("tok", None, "head"),
        P("tok", None),
        P("tok", "head"),
        P(None, "head"),
        P("head"),
        P(),
        P(),
        P("head"),
        P("head"),
        P("head"),
        P("head"),
        P("head", "tok"),
        P(("tok", "head"), None),
    )
    return jax.shard_map(
        per_device,
        mesh=mesh,
        in_specs=placed,
        out_specs=(
            P(("tok", "head"), None),
            P(("tok", "head"), None),
            P("head"),
            P("tok", None, "head"),
            P("tok", None),
            P("tok", "head"),
            P(None, "head"),
            P("head"),
            P(),
            P(),
            P("head"),
            P("head"),
            P("head"),
            P("head"),
            P("head", "tok"),
        ),
        check_vma=False,
    )
```

```python
import functools

import jax
import jax.numpy as jnp
from jax import lax
from jax.experimental import pallas as pl
from jax.experimental.pallas import tpu as pltpu
from jax.sharding import PartitionSpec as P

HEADDIM = 64
STATE = 128
CONV = 4
INNER = 3072
CHUNK = 256
HALVES = 2
LANES = 128
HALO = 16

EPS = 1e-05
HIGHEST = lax.Precision.HIGHEST
F32 = jnp.float32
BF16 = jnp.bfloat16


def dot_nn(a, b, precision=None):
    return lax.dot_general(
        a, b, (((1,), (0,)), ((), ())), preferred_element_type=F32, precision=precision
    )


def dot_nt(a, b, precision=None):
    return lax.dot_general(
        a, b, (((1,), (1,)), ((), ())), preferred_element_type=F32, precision=precision
    )


def dot_tn(a, b):
    return lax.dot_general(a, b, (((0,), (0,)), ((), ())), preferred_element_type=F32)


def dot_split(a, b):
    a_top, b_top = a.astype(BF16), b.astype(BF16)
    a_rest = (a - a_top.astype(F32)).astype(BF16)
    b_rest = (b - b_top.astype(F32)).astype(BF16)
    return dot_nn(a_top, b_top) + (dot_nn(a_rest, b_top) + dot_nn(a_top, b_rest))


def iota(shape, dim):
    return lax.broadcasted_iota(jnp.int32, shape, dim)


def sigmoid(v):
    return 1.0 / (1.0 + jnp.exp(-v))


def softplus(v):
    return jnp.maximum(v, 0.0) + jnp.log1p(jnp.exp(-jnp.abs(v)))


def head_spread(width):
    return (iota((LANES, width), 1) // HEADDIM == iota((LANES, width), 0)).astype(F32)


def bit_of(axis, bit):
    return (lax.axis_index(axis) // (1 << bit)) % 2


def swap(value, axis, bit):
    size = lax.axis_size(axis)
    return lax.ppermute(value, axis, [(i, i ^ (1 << bit)) for i in range(size)])


def grow(value, axis, bit, dim):
    other = swap(value, axis, bit)
    low = bit_of(axis, bit) == 0
    return jnp.where(
        low,
        jnp.concatenate([value, other], dim),
        jnp.concatenate([other, value], dim),
    )


def halve(value, axis, bit, dim):
    mine = bit_of(axis, bit)
    if dim < value.ndim - 1:
        half = value.shape[dim] // 2
        keep = lax.dynamic_slice_in_dim(value, mine * half, half, dim)
        send = lax.dynamic_slice_in_dim(value, (1 - mine) * half, half, dim)
    else:
        low, high = jnp.split(value, 2, axis=dim)
        keep = jnp.where(mine == 0, low, high)
        send = jnp.where(mine == 0, high, low)
    return keep.astype(F32) + swap(send.astype(BF16), axis, bit).astype(F32)


def add_pairs(value, axis, bits):
    for bit in bits:
        value = value + swap(value, axis, bit)
    return value


MESH = pl.DeviceIdType.MESH


def flip(index, bit):
    return index + (1 - 2 * ((index // (1 << bit)) % 2)) * (1 << bit)


def flip_all(index, offset):
    bit = 0
    while offset >> bit:
        if (offset >> bit) & 1:
            index = flip(index, bit)
        bit += 1
    return index


def now(value):
    return value() if callable(value) else value


class Remote:
    def __init__(self, links, k, src, dst, device):
        self.links, self.k, self.src, self.dst, self.device = links, k, src, dst, device

    def make(self):
        return pltpu.make_async_remote_copy(
            src_ref=now(self.src),
            dst_ref=now(self.dst),
            send_sem=self.links.send_sem.at[self.k],
            recv_sem=self.links.recv_sem.at[self.k],
            device_id=now(self.device),
            device_id_type=MESH,
        )

    def start(self):
        self.make().start()

    def wait_recv(self):
        self.make().wait_recv()

    def wait_send(self):
        self.make().wait_send()


class Local:
    def __init__(self, links, k, src, dst):
        self.links, self.k, self.src, self.dst = links, k, src, dst

    def make(self):
        return pltpu.make_async_copy(now(self.src), now(self.dst), self.links.local_sem.at[self.k])

    def start(self):
        self.make().start()

    def wait(self):
        self.make().wait()


class Links:
    def __init__(self, send_sem, recv_sem, local_sem, tok_bits, row_bits):
        self.send_sem, self.recv_sem, self.local_sem = send_sem, recv_sem, local_sem
        self.tok_bits, self.row_bits = list(tok_bits), list(row_bits)
        self.tok, self.head = lax.axis_index("tok"), lax.axis_index("head")
        self.sets = 1 << len(self.row_bits)
        self.half, self.mine = self.head // self.sets, self.head % self.sets
        self.half_bit = len(self.row_bits)
        self.sent, self.drained, self.n_local, self.open_local = [], [], 0, []

    def enter(self):
        partners = [self.tok_peer(b) for b in self.tok_bits]
        partners += [self.head_peer(b) for b in self.row_bits + [self.half_bit]]
        barrier = pltpu.get_barrier_semaphore()
        for partner in partners:
            pl.semaphore_signal(barrier, inc=1, device_id=partner(), device_id_type=MESH)
        pl.semaphore_wait(barrier, len(partners))

    def tok_peer(self, bit):
        return lambda: {"tok": flip(self.tok, bit)}

    def head_peer(self, bit):
        return lambda: {"head": flip(self.head, bit)}

    def plan_send(self, src, dst, device):
        copy = Remote(self, len(self.sent), src, dst, device)
        self.sent.append(copy)
        return copy

    def send(self, src, dst, device):
        copy = self.plan_send(src, dst, device)
        copy.start()
        return copy

    def plan_local(self, src, dst):
        self.n_local += 1
        return Local(self, self.n_local - 1, src, dst)

    def local(self, src, dst):
        copy = self.plan_local(src, dst)
        copy.start()
        self.open_local.append(copy)
        return copy

    def settle(self, copies):
        for copy in copies:
            if any(copy is other for other in self.open_local):
                self.open_local = [other for other in self.open_local if other is not copy]
                copy.wait()

    def drain(self, copy):
        copy.wait_recv()
        copy.wait_send()
        self.drained.append(copy)

    def leave(self):
        self.settle(list(self.open_local))
        for copy in self.sent:
            if not any(copy is other for other in self.drained):
                copy.wait_send()


def add_rows(dst, src, count):
    def body(i, carry):
        at = pl.ds(pl.multiple_of(i * 16, 16), 16)
        dst[at, :] = (dst[at, :].astype(F32) + src[at, :].astype(F32)).astype(BF16)
        return carry

    lax.fori_loop(0, count // 16, body, 0)


class Sum:
    def __init__(self, links, src, keep, recv, final, out, part, parts, order):
        self.links, self.src, self.keep, self.recv, self.final = links, src, keep, recv, final
        self.size = keep.shape[1] // parts
        self.start = part * self.size
        self.width = out.shape[1]
        held = list(range(1 << len(links.tok_bits)))
        self.sends, self.adds, base = [], [], 0
        for number, bit in enumerate(order):
            stay = [o for o in held if not (o >> bit) & 1]
            if number == 0:
                place = {o: i for i, o in enumerate(stay)}
                self.loads = [links.plan_local(self.source(o), self.slot(place[o])) for o in stay]
            sends, adds = [], []
            for n, o in enumerate(stay):
                away = o ^ (1 << bit)
                src_ref = self.source(away) if number == 0 else self.slot(place[away])
                sends.append(links.plan_send(src_ref, self.landing(base + n), links.tok_peer(bit)))
                adds.append((place[o], base + n))
            base += len(stay)
            held = stay
            self.sends.append(sends)
            self.adds.append(adds)
        self.base = base
        self.tail = links.plan_send(
            lambda: self.keep.at[0, self.rows(), self.half_lanes(1 - self.links.half)],
            lambda: self.recv.at[base, self.rows(), pl.ds(0, self.width)],
            links.head_peer(links.half_bit),
        )
        self.store = links.plan_local(lambda: final.at[self.rows()], lambda: out.at[self.rows()])
        self.next = 0
        self.last = len(self.sends) + 1

    def rows(self):
        return pl.ds(self.start, self.size)

    def source(self, offset):
        return lambda: self.src.at[flip_all(self.links.tok, offset), self.rows()]

    def landing(self, i):
        return lambda: self.recv.at[i, self.rows()]

    def slot(self, i):
        return lambda: self.keep.at[i, self.rows()]

    def half_lanes(self, which):
        return pl.ds(pl.multiple_of(which * self.width, LANES), self.width)

    def step(self, k):
        if k == 0:
            for copy in self.sends[0] + self.loads:
                copy.start()
            return
        if k == self.last:
            self.tail.wait_recv()
            lanes = self.half_lanes(self.links.half)

            def body(i, carry):
                at = pl.ds(pl.multiple_of(self.start + i * 16, 16), 16)
                self.final[at, :] = self.keep[0, at, lanes].astype(F32) + self.recv[
                    self.base, at, 0 : self.width
                ].astype(F32)
                return carry

            lax.fori_loop(0, self.size // 16, body, 0)
            self.store.start()
            return
        for copy in self.sends[k - 1]:
            copy.wait_recv()
        if k == 1:
            for copy in self.loads:
                copy.wait()
        for place, i in self.adds[k - 1]:
            add_rows(now(self.slot(place)), now(self.landing(i)), self.size)
        for copy in self.sends[k] if k < len(self.sends) else [self.tail]:
            copy.start()

    def advance(self):
        if self.next < self.last:
            self.step(self.next)
            self.next += 1

    def finish(self):
        while self.next <= self.last:
            self.step(self.next)
            self.next += 1

    def close(self):
        self.store.wait()


class SmallSum(Sum):
    def __init__(self, links, src, src_low, keep, low, recv, order):
        self.links, self.keep, self.low, self.recv = links, keep, low, recv
        self.order = list(order)
        bit = self.order.pop(0)
        slots = range(1 << len(links.tok_bits))
        self.held = [o for o in slots if not (o >> bit) & 1]
        self.place = {o: i for i, o in enumerate(self.held)}
        self.base = len(self.held)
        self.n_low = 0
        self.into = [(i, i) for i in range(self.base)]
        self.flight = [
            links.send(src_low.at[flip_all(links.tok, o ^ (1 << bit))], recv.at[self.place[o]], links.tok_peer(bit))
            for o in self.held
        ]
        self.kept = [links.local(src.at[flip_all(links.tok, o)], keep.at[self.place[o]]) for o in self.held]
        self.done = False

    def post(self, place, lanes, device):
        n = self.n_low
        self.low[n, :, 0:lanes] = self.keep[place, :, 0:lanes].astype(BF16)
        self.n_low += 1
        src, dst = self.low.at[n, :, pl.ds(0, lanes)], self.recv.at[self.base, :, pl.ds(0, lanes)]
        self.flight.append(self.links.send(src, dst, device))
        self.base += 1
        return self.base - 1

    def take(self):
        for copy in self.flight:
            copy.wait_recv()
        self.links.settle(self.kept)
        for place, i in self.into:
            self.keep[place, :, 0 : self.lanes_in] = self.keep[place, :, 0 : self.lanes_in] + self.recv[
                i, :, 0 : self.lanes_in
            ].astype(F32)
        self.flight, self.into, self.kept = [], [], []

    lanes_in = 2 * STATE + LANES

    def advance(self):
        if self.done:
            return
        self.take()
        if not self.order:
            self.into = [(0, self.post(0, self.lanes_in, self.links.head_peer(self.links.half_bit)))]
            self.done = True
            return
        bit = self.order.pop(0)
        stay = [o for o in self.held if not (o >> bit) & 1]
        self.into = [
            (self.place[o], self.post(self.place[o ^ (1 << bit)], self.lanes_in, self.links.tok_peer(bit)))
            for o in stay
        ]
        self.held = stay

    def finish(self):
        while not self.done:
            self.advance()
        self.take()
        self.lanes_in = 2 * STATE
        for bit in self.links.row_bits:
            self.into = [(0, self.post(0, self.lanes_in, self.links.head_peer(bit)))]
            self.take()


def conv_rows(cur, tail, weight, bias):
    rows = cur.shape[0]
    ext = jnp.concatenate([tail, cur], axis=0)
    out = bias + weight[CONV - 1 : CONV] * cur
    for k in range(CONV - 1):
        start = 8 - (CONV - 1) + k
        out = out + weight[k : k + 1] * ext[start : start + rows]
    return out


def state_kernel(
    xm_ref, xt_ref, bm_ref, bt_ref, par_ref, bcpar_ref, hp_ref,
    xs_ref, u_ref, cume_ref, dte_ref, bc_ref, cumt_ref, sloc_ref, fin_ref, dec_ref,
    state, dsum, ue,
):
    c = pl.program_id(0)
    q, width = xm_ref.shape

    @pl.when(c == 0)
    def _():
        state[...] = jnp.zeros_like(state)
        dsum[...] = jnp.zeros_like(dsum)

    dt = softplus(bm_ref[:, 2 * STATE :] + hp_ref[0:1, :])
    tri = (iota((q, q), 0) >= iota((q, q), 1)).astype(F32)
    cum = dot_nn(tri, dt * hp_ref[1:2, :], HIGHEST)
    cumt_ref[...] = cum.T[: cumt_ref.shape[0], :]
    spread = head_spread(width)
    cume_ref[...] = dot_nn(cum, spread, HIGHEST)
    dte_ref[...] = dot_nn(dt, spread, HIGHEST)
    end = cume_ref[q - 1 : q, :]

    bpre = conv_rows(
        bm_ref[:, : 2 * STATE], bt_ref[:, : 2 * STATE], bcpar_ref[0:CONV, :], bcpar_ref[CONV : CONV + 1, :]
    )
    bc_ref[...] = bpre * sigmoid(bpre)

    block = 2 * LANES

    def body(i, carry):
        sl = pl.ds(pl.multiple_of(i * block, block), block)
        pre = conv_rows(
            xm_ref[:, sl], xt_ref[:, sl], par_ref[0:CONV, sl], par_ref[CONV : CONV + 1, sl]
        )
        xs = pre * sigmoid(pre)
        u = xs * dte_ref[:, sl]
        xs_ref[:, sl] = xs
        u_ref[:, sl] = u.astype(BF16)
        cume = cume_ref[:, sl]
        ue[:, sl] = (u * jnp.exp(cume[q - 1 : q, :] - cume)).astype(BF16)
        return carry

    lax.fori_loop(0, width // block, body, 0)
    sloc_ref[0] = state[...]
    dec_ref[0] = jnp.exp(dsum[...])
    state[...] = jnp.exp(end) * state[...] + dot_nn(bc_ref[:, :STATE].T.astype(BF16), ue[...])
    dsum[...] = dsum[...] + end
    fin_ref[...] = state[...].astype(BF16)


def main_kernel(
    xs_ref, u_ref, cume_ref, cumt_ref, bc_ref, sloc_ref, sin_ref, dec_ref, z_ref, gyn_ref, par_ref,
    y_ref, stat_ref,
    gram, ya, acc_sq, acc_in,
):
    q, width = xs_ref.shape
    bmat = bc_ref[:, :STATE].astype(BF16)
    cmat = bc_ref[:, STATE:].astype(BF16)
    lower = iota((q, q), 0) >= iota((q, q), 1)
    gram[...] = jnp.where(lower, dot_nt(cmat, bmat), 0.0)
    entering = sloc_ref[0] + dec_ref[0, 0:1, :] * sin_ref[...].astype(F32)
    ya[...] = dot_nn(cmat, entering.astype(BF16))
    acc_sq[...] = jnp.zeros_like(acc_sq)
    acc_in[...] = jnp.zeros_like(acc_in)
    first = iota((q, LANES), 1) < HEADDIM

    def body(p, carry):
        sl = pl.ds(pl.multiple_of(p * LANES, LANES), LANES)
        cume = cume_ref[:, sl]
        u = u_ref[:, sl]
        y = jnp.exp(cume) * ya[:, sl] + par_ref[CONV + 2 : CONV + 3, sl] * xs_ref[:, sl]
        for s in range(2):
            gap = cume[:, HEADDIM * s : HEADDIM * s + 1] - cumt_ref[pl.ds(2 * p + s, 1), :]
            pairs = (gram[...] * jnp.exp(jnp.minimum(gap, 0.0))).astype(BF16)
            y = y + dot_nn(pairs, jnp.where(first == (s == 0), u, jnp.zeros_like(u)))
        y_ref[:, sl] = y
        z = z_ref[:, sl]
        gated = y * z * sigmoid(z)
        acc_sq[...] += gated * gated
        acc_in[...] += gated * gyn_ref[:, sl] * par_ref[CONV + 1 : CONV + 2, sl]
        return carry

    lax.fori_loop(0, width // LANES, body, 0)
    ones = jnp.ones((8, LANES), F32)
    sums_sq = dot_nt(ones, acc_sq[...], HIGHEST)
    sums_in = dot_nt(ones, acc_in[...], HIGHEST)
    stat_ref[...] = jnp.where(iota(sums_sq.shape, 0) == 0, sums_sq, sums_in)


def gate_kernel(
    y_ref, z_ref, gyn_ref, xs_ref, cume_ref, bc_ref, stat_ref, par_ref,
    yn_ref, gy_ref, dz_ref, gloc_ref, gin_ref, dec_ref, acc_ref,
    adj, dsum, ge,
):
    q, width = y_ref.shape

    @pl.when(pl.program_id(0) == 0)
    def _():
        adj[...] = jnp.zeros_like(adj)
        dsum[...] = jnp.zeros_like(dsum)
        acc_ref[...] = jnp.zeros_like(acc_ref)

    end = cume_ref[q - 1 : q, :]
    inv = jnp.broadcast_to(stat_ref[:, 0:1], (q, LANES))
    back = jnp.broadcast_to(stat_ref[:, 1:2], (q, LANES))

    def body(p, carry):
        sl = pl.ds(pl.multiple_of(p * LANES, LANES), LANES)
        y, z, gyn = y_ref[:, sl], z_ref[:, sl], gyn_ref[:, sl]
        sig = sigmoid(z)
        sil = z * sig
        gated = y * sil
        gain = par_ref[CONV + 1 : CONV + 2, sl]
        unit = gated * inv
        yn_ref[:, sl] = (unit * gain).astype(BF16)
        d_gated = inv * gyn * gain - gated * back
        gy = d_gated * sil
        gy_ref[:, sl] = gy
        dz_ref[:, sl] = (d_gated * y * (sig * (1.0 + z * (1.0 - sig)))).astype(BF16)
        ge[:, sl] = (gy * jnp.exp(cume_ref[:, sl])).astype(BF16)
        acc_ref[0:1, sl] += jnp.sum(gyn * unit, axis=0, keepdims=True)
        acc_ref[1:2, sl] += jnp.sum(gy * xs_ref[:, sl], axis=0, keepdims=True)
        return carry

    lax.fori_loop(0, width // LANES, body, 0)
    gloc_ref[0] = adj[...]
    dec_ref[0] = jnp.exp(dsum[...])
    adj[...] = jnp.exp(end) * adj[...] + dot_nn(bc_ref[:, STATE:].T.astype(BF16), ge[...])
    dsum[...] = dsum[...] + end
    gin_ref[...] = adj[...].astype(BF16)


def back_kernel(
    tok_bits, row_bits,
    xm_ref, xt_ref, bm_ref, bt_ref, par_ref, bcpar_ref, hp_ref,
    cume_ref, dte_ref, cumt_ref, gy_ref, sloc_ref, sin_ref, sdec_ref, gloc_ref, gout_ref, gdec_ref,
    gz_ref, go_ref,
    dx_ref, ds_ref, accx_ref, accb_ref, acch_ref, oz_ref, oo_ref,
    xs, u, dsil, ue, ge, dus, ya, qx, qb, gram, dgram, da, acc_x, acc_w, acc_g,
    kz, ko, rz, ro, fz, fo, send_sem, recv_sem, local_sem,
):
    step = pl.program_id(0)
    q, width = xm_ref.shape
    tokens = dx_ref.shape[0] - HALO
    steps = tokens // q
    links = Links(send_sem, recv_sem, local_sem, tok_bits, row_bits)
    up = [0] + links.tok_bits[1:]
    down = [0] + links.tok_bits[1:][::-1]
    groups = [
        [Sum(links, gz_ref, kz, rz, fz, oz_ref, p, 2, (down, up)[p]) for p in range(2)],
        [Sum(links, go_ref, ko, ro, fo, oo_ref, p, 2, (down, up)[p]) for p in range(2)],
    ]
    plans = [[(0, 0), (0, 2), (1, 2), (2, 3)], [(0, 0), (0, 3), (2, 2), (3, 1)]]

    def go_on(point):
        for when in range(steps):

            @pl.when(step == when)
            def _():
                if (when, point) == (0, 0):
                    links.enter()
                for group, plan in zip(groups, plans):
                    for k, (number, place) in enumerate(plan):
                        if (min(number, steps - 1), place) == (when, point):
                            for each in group:
                                each.step(k)
                if (when, point) == (steps - 1, 3):
                    for group, plan in zip(groups, plans):
                        for k in range(len(plan), group[0].last + 1):
                            for each in group:
                                each.step(k)
                    for group in groups:
                        for each in group:
                            each.close()
                    links.leave()

    go_on(0)
    c = tokens // q - 1 - step
    block = 2 * LANES

    @pl.when(step == 0)
    def _():
        accx_ref[...] = jnp.zeros_like(accx_ref)
        accb_ref[...] = jnp.zeros_like(accb_ref)
        acch_ref[...] = jnp.zeros_like(acch_ref)
        qx[q:, :] = jnp.zeros((8, width), F32)
        qb[q:, :] = jnp.zeros((8, 2 * STATE), F32)
        da[...] = jnp.zeros_like(da)
        ds_ref[...] = jnp.zeros_like(ds_ref)

    bpre = conv_rows(
        bm_ref[:, : 2 * STATE], bt_ref[:, : 2 * STATE], bcpar_ref[0:CONV, :], bcpar_ref[CONV : CONV + 1, :]
    )
    bsig = sigmoid(bpre)
    bc = bpre * bsig
    qb[0:q, :] = bsig * (1.0 + bpre * (1.0 - bsig))
    bmat, cmat = bc[:, :STATE].astype(BF16), bc[:, STATE:].astype(BF16)

    def conv_body(i, carry):
        sl = pl.ds(pl.multiple_of(i * block, block), block)
        pre = conv_rows(
            xm_ref[:, sl], xt_ref[:, sl], par_ref[0:CONV, sl], par_ref[CONV : CONV + 1, sl]
        )
        sig = sigmoid(pre)
        x = pre * sig
        xs[:, sl] = x
        dsil[:, sl] = sig * (1.0 + pre * (1.0 - sig))
        uu = x * dte_ref[:, sl]
        u[:, sl] = uu.astype(BF16)
        cume = cume_ref[:, sl]
        ue[:, sl] = (uu * jnp.exp(cume[q - 1 : q, :] - cume)).astype(BF16)
        ge[:, sl] = (gy_ref[:, sl] * jnp.exp(cume)).astype(BF16)
        return carry

    lax.fori_loop(0, width // block, conv_body, 0)
    go_on(1)

    last = cume_ref[q - 1 : q, :]
    adj = gloc_ref[0] + gdec_ref[0, 0:1, :] * gout_ref[...].astype(F32)
    entering = sloc_ref[0] + sdec_ref[0, 0:1, :] * sin_ref[...].astype(F32)
    kept = jnp.exp(last) * jnp.sum(adj * entering, axis=0, keepdims=True)
    adj_low, ent_low = adj.astype(BF16), entering.astype(BF16)
    dus[...] = dot_nn(bmat, adj_low)
    ya[...] = dot_nn(cmat, ent_low)
    db = dot_nt(ue[...], adj_low)
    dc = dot_nt(ge[...], ent_low)
    upper = iota((q, q), 1) >= iota((q, q), 0)
    gram[...] = jnp.where(upper, dot_nt(bmat, cmat), 0.0)
    dgram[...] = jnp.zeros_like(dgram)
    acc_x[...] = jnp.zeros_like(acc_x)
    acc_w[...] = jnp.zeros_like(acc_w)
    acc_g[...] = jnp.zeros_like(acc_g)
    later = (iota((q, q), 0) >= iota((q, q), 1)).astype(BF16)
    first = iota((q, LANES), 1) < HEADDIM

    def pair_body(p, carry):
        sl = pl.ds(pl.multiple_of(p * LANES, LANES), LANES)
        cume = cume_ref[:, sl]
        ul = u[:, sl]
        gy = gy_ref[:, sl]
        gl = gy.astype(BF16)
        du = jnp.zeros((q, LANES), F32)
        for s in range(2):
            mine = first == (s == 0)
            row = pl.ds(2 * p + s, 1)
            gap = cumt_ref[row, :] - cume[:, HEADDIM * s : HEADDIM * s + 1]
            decay = jnp.exp(jnp.minimum(gap, 0.0))
            pairs = gram[...] * decay
            dpairs = dot_nt(jnp.where(mine, ul, jnp.zeros_like(ul)), gl)
            dgram[...] += dpairs * decay
            through = dot_nn((dpairs * pairs).astype(BF16), later)
            da[row, :] = jnp.sum(
                jnp.where(iota((q, q), 0) < iota((q, q), 1), through, 0.0), axis=0, keepdims=True
            )
            du = du + dot_nn(pairs.astype(BF16), jnp.where(mine, gl, jnp.zeros_like(gl)))
        x = xs[:, sl]
        wide = dus[:, sl] * jnp.exp(cume[q - 1 : q, :] - cume)
        du = du + wide
        to_head = (iota((LANES, LANES), 1) == 2 * p + iota((LANES, LANES), 0) // HEADDIM).astype(BF16)
        dte = dte_ref[:, sl]
        acc_x[...] += dot_nn((x * du).astype(BF16), to_head)
        acc_w[...] += dot_nn((x * dte * wide).astype(BF16), to_head)
        acc_g[...] += dot_nn((gy * jnp.exp(cume) * ya[:, sl]).astype(BF16), to_head)
        qx[0:q, sl] = (dte * du + par_ref[CONV + 2 : CONV + 3, sl] * gy) * dsil[:, sl]
        return carry

    lax.fori_loop(0, width // LANES, pair_body, 0)
    go_on(2)

    def unconv_body(i, carry):
        sl = pl.ds(pl.multiple_of(i * block, block), block)
        weight = par_ref[0:CONV, sl]
        ext = qx[:, sl]
        cur = ext[0:q]
        dpre = weight[CONV - 1 : CONV] * cur
        for k in range(CONV - 1):
            dpre = dpre + weight[k : k + 1] * ext[CONV - 1 - k : CONV - 1 - k + q]
        dx_ref[pl.ds(pl.multiple_of(c * q, q), q), sl] = dpre.astype(BF16)
        past = jnp.concatenate([xt_ref[:, sl], xm_ref[:, sl]], axis=0)
        for k in range(CONV):
            start = 8 - (CONV - 1) + k
            accx_ref[k : k + 1, sl] += jnp.sum(cur * past[start : start + q], axis=0, keepdims=True)
        accx_ref[CONV : CONV + 1, sl] += jnp.sum(cur, axis=0, keepdims=True)
        head_rows = jnp.concatenate([jnp.zeros((HALO, block), F32), cur[0:8]], axis=0)
        before = jnp.zeros((HALO, block), F32)
        for k in range(CONV - 1):
            before = before + weight[k : k + 1] * head_rows[CONV - 1 - k : CONV - 1 - k + HALO]
        dx_ref[pl.ds(tokens, HALO), sl] = before.astype(BF16)
        qx[q:, sl] = cur[0:8]
        return carry

    lax.fori_loop(0, width // block, unconv_body, 0)

    dg = jnp.where(upper, dgram[...], 0.0)
    db = db + dot_split(dg, bc[:, STATE:])
    dc = dc + dot_split(dg.T, bc[:, :STATE])
    qb[0:q, 0:STATE] = qb[0:q, 0:STATE] * db
    qb[0:q, STATE:] = qb[0:q, STATE:] * dc
    weight = bcpar_ref[0:CONV, :]
    ext = qb[...]
    cur = ext[0:q]
    dpre = weight[CONV - 1 : CONV] * cur
    for k in range(CONV - 1):
        dpre = dpre + weight[k : k + 1] * ext[CONV - 1 - k : CONV - 1 - k + q]
    ds_ref[pl.ds(pl.multiple_of(c * q, q), q), 0 : 2 * STATE] = dpre.astype(BF16)
    past = jnp.concatenate([bt_ref[:, 0 : 2 * STATE], bm_ref[:, 0 : 2 * STATE]], axis=0)
    for k in range(CONV):
        start = 8 - (CONV - 1) + k
        accb_ref[k : k + 1, :] += jnp.sum(cur * past[start : start + q], axis=0, keepdims=True)
    accb_ref[CONV : CONV + 1, :] += jnp.sum(cur, axis=0, keepdims=True)
    head_rows = jnp.concatenate([jnp.zeros((HALO, 2 * STATE), F32), cur[0:8]], axis=0)
    before = jnp.zeros((HALO, 2 * STATE), F32)
    for k in range(CONV - 1):
        before = before + weight[k : k + 1] * head_rows[CONV - 1 - k : CONV - 1 - k + HALO]
    ds_ref[pl.ds(tokens, HALO), 0 : 2 * STATE] = before.astype(BF16)
    qb[q:, :] = cur[0:8]

    raw = bm_ref[:, 2 * STATE :] + hp_ref[0:1, :]
    dt = softplus(raw)
    rate = hp_ref[1:2, :]
    from_here = (iota((q, q), 1) >= iota((q, q), 0)).astype(F32)
    up_to_here = (iota((q, q), 1) < iota((q, q), 0)).astype(F32)
    kept_heads = dot_nt(jnp.broadcast_to(kept, (8, width)), head_spread(width), HIGHEST)
    total = (
        da[...].T
        + dot_nn(from_here, acc_g[...], HIGHEST)
        + dot_nn(up_to_here, acc_w[...], HIGHEST)
        + kept_heads[0:1, :]
    )
    d_raw = (acc_x[...] + rate * total) * sigmoid(raw)
    ds_ref[pl.ds(pl.multiple_of(c * q, q), q), 2 * STATE :] = d_raw.astype(BF16)
    acch_ref[0:1, :] += jnp.sum(d_raw, axis=0, keepdims=True)
    acch_ref[1:2, :] += rate * jnp.sum(dt * total, axis=0, keepdims=True)
    go_on(3)


def shape(dims, dtype):
    return jax.ShapeDtypeStruct(dims, dtype)


def whole(dims):
    return pl.BlockSpec(dims, lambda c: (0,) * len(dims))


def run(kernel, name, grid, in_specs, out_specs, out_shape, scratch, args, flops, collective_id=None):
    return pl.pallas_call(
        kernel,
        grid=(grid,),
        in_specs=in_specs,
        out_specs=out_specs,
        out_shape=out_shape,
        scratch_shapes=scratch,
        name=name,
        compiler_params=pltpu.CompilerParams(
            dimension_semantics=("arbitrary",),
            vmem_limit_bytes=62 * 1024 * 1024,
            collective_id=collective_id,
            has_side_effects=collective_id is not None,
        ),
        cost_estimate=pl.CostEstimate(
            flops=flops, bytes_accessed=sum(a.size * a.dtype.itemsize for a in args), transcendentals=0
        ),
    )(*args)


def mixer_forward_state(x_ext, s_ext, par, bcpar, hp, tokens):
    width = x_ext.shape[1]
    small = s_ext.shape[1]
    n = tokens // CHUNK
    q = CHUNK
    tail = q // 8
    last = (tokens + HALO) // 8 - 1
    tail_map = lambda c: (jnp.where(c == 0, last, c * tail - 1), 0)
    heads_pad = -(-(width // HEADDIM) // 8) * 8
    return run(
        state_kernel,
        "scan_states",
        n,
        [
            pl.BlockSpec((q, width), lambda c: (c, 0)),
            pl.BlockSpec((8, width), tail_map),
            pl.BlockSpec((q, small), lambda c: (c, 0)),
            pl.BlockSpec((8, small), tail_map),
            whole(par.shape),
            whole(bcpar.shape),
            whole(hp.shape),
        ],
        [
            pl.BlockSpec((q, width), lambda c: (c, 0)),
            pl.BlockSpec((q, width), lambda c: (c, 0)),
            pl.BlockSpec((q, width), lambda c: (c, 0)),
            pl.BlockSpec((q, width), lambda c: (c, 0)),
            pl.BlockSpec((q, 2 * STATE), lambda c: (c, 0)),
            pl.BlockSpec((heads_pad, q), lambda c: (0, c)),
            pl.BlockSpec((1, STATE, width), lambda c: (c, 0, 0)),
            whole((STATE, width)),
            pl.BlockSpec((1, 1, width), lambda c: (c, 0, 0)),
        ],
        [
            shape((tokens, width), F32),
            shape((tokens, width), BF16),
            shape((tokens, width), F32),
            shape((tokens, width), F32),
            shape((tokens, 2 * STATE), F32),
            shape((heads_pad, tokens), F32),
            shape((n, STATE, width), F32),
            shape((STATE, width), BF16),
            shape((n, 1, width), F32),
        ],
        [
            pltpu.VMEM((STATE, width), F32),
            pltpu.VMEM((1, width), F32),
            pltpu.VMEM((q, width), BF16),
        ],
        (x_ext, x_ext, s_ext, s_ext, par, bcpar, hp),
        int(3e9),
    )


def mixer_forward_main(xs, u, cume, cumt, bc, sloc, sin, dec, z, gyn, par):
    tokens, width = xs.shape
    q = CHUNK
    n = tokens // q
    rows = pl.BlockSpec((q, width), lambda c: (c, 0))
    return run(
        main_kernel,
        "scan_outputs",
        n,
        [
            rows,
            rows,
            rows,
            pl.BlockSpec((cumt.shape[0], q), lambda c: (0, c)),
            pl.BlockSpec((q, 2 * STATE), lambda c: (c, 0)),
            pl.BlockSpec((1, STATE, width), lambda c: (c, 0, 0)),
            whole(sin.shape),
            pl.BlockSpec((1, 1, width), lambda c: (c, 0, 0)),
            rows,
            rows,
            whole(par.shape),
        ],
        [rows, pl.BlockSpec((8, q), lambda c: (0, c))],
        [shape((tokens, width), F32), shape((8, tokens), F32)],
        [
            pltpu.VMEM((q, q), F32),
            pltpu.VMEM((q, width), F32),
            pltpu.VMEM((q, LANES), F32),
            pltpu.VMEM((q, LANES), F32),
        ],
        (xs, u, cume, cumt, bc, sloc, sin, dec, z, gyn, par),
        int(10e9),
    )


def mixer_backward_gate(y, z, gyn, xs, cume, bc, stat, par):
    tokens, width = y.shape
    q = CHUNK
    n = tokens // q
    rows = pl.BlockSpec((q, width), lambda c: (n - 1 - c, 0))
    return run(
        gate_kernel,
        "gate_back",
        n,
        [
            rows,
            rows,
            rows,
            rows,
            rows,
            pl.BlockSpec((q, 2 * STATE), lambda c: (n - 1 - c, 0)),
            pl.BlockSpec((q, 8), lambda c: (n - 1 - c, 0)),
            whole(par.shape),
        ],
        [
            rows,
            rows,
            rows,
            pl.BlockSpec((1, STATE, width), lambda c: (n - 1 - c, 0, 0)),
            whole((STATE, width)),
            pl.BlockSpec((1, 1, width), lambda c: (n - 1 - c, 0, 0)),
            whole((8, width)),
        ],
        [
            shape((tokens, width), BF16),
            shape((tokens, width), F32),
            shape((tokens, width), BF16),
            shape((n, STATE, width), F32),
            shape((STATE, width), BF16),
            shape((n, 1, width), F32),
            shape((8, width), F32),
        ],
        [
            pltpu.VMEM((STATE, width), F32),
            pltpu.VMEM((1, width), F32),
            pltpu.VMEM((q, width), BF16),
        ],
        (y, z, gyn, xs, cume, bc, stat, par),
        int(5e9),
    )


def mixer_backward_main(
    x_ext, s_ext, par, bcpar, hp, cume, dte, cumt, gy, sloc, sin, sdec, gloc, gout, gdec, gz, go
):
    tok_size, head_size = lax.axis_size("tok"), lax.axis_size("head")
    tok_bits = range(tok_size.bit_length() - 1)
    row_bits = range((head_size // HALVES).bit_length() - 1)
    share = gz.shape[1]
    copies = 16 * len(tok_bits)
    tokens, width = cume.shape
    small = s_ext.shape[1]
    q = CHUNK
    n = tokens // q
    tail = q // 8
    last = (tokens + HALO) // 8 - 1
    rows = pl.BlockSpec((q, width), lambda c: (n - 1 - c, 0))
    tail_map = lambda c: (jnp.where(c == n - 1, last, (n - 1 - c) * tail - 1), 0)
    states = pl.BlockSpec((1, STATE, width), lambda c: (n - 1 - c, 0, 0))
    decays = pl.BlockSpec((1, 1, width), lambda c: (n - 1 - c, 0, 0))
    anywhere = pl.BlockSpec(memory_space=pl.ANY)
    return run(
        functools.partial(back_kernel, tok_bits, row_bits),
        "scan_back",
        n,
        [
            rows,
            pl.BlockSpec((8, width), tail_map),
            pl.BlockSpec((q, small), lambda c: (n - 1 - c, 0)),
            pl.BlockSpec((8, small), tail_map),
            whole(par.shape),
            whole(bcpar.shape),
            whole(hp.shape),
            rows,
            rows,
            pl.BlockSpec((cumt.shape[0], q), lambda c: (0, n - 1 - c)),
            rows,
            states,
            whole(sin.shape),
            decays,
            states,
            whole(gout.shape),
            decays,
            anywhere,
            anywhere,
        ],
        [
            whole((tokens + HALO, width)),
            whole((tokens + HALO, small)),
            whole((8, width)),
            whole((8, 2 * STATE)),
            whole((8, LANES)),
            anywhere,
            anywhere,
        ],
        [
            shape((tokens + HALO, width), BF16),
            shape((tokens + HALO, small), BF16),
            shape((8, width), F32),
            shape((8, 2 * STATE), F32),
            shape((8, LANES), F32),
            shape((share, width // HALVES), F32),
            shape((share, width // HALVES), F32),
        ],
        [
            pltpu.VMEM((q, width), F32),
            pltpu.VMEM((q, width), BF16),
            pltpu.VMEM((q, width), F32),
            pltpu.VMEM((q, width), BF16),
            pltpu.VMEM((q, width), BF16),
            pltpu.VMEM((q, width), F32),
            pltpu.VMEM((q, width), F32),
            pltpu.VMEM((q + 8, width), F32),
            pltpu.VMEM((q + 8, 2 * STATE), F32),
            pltpu.VMEM((q, q), F32),
            pltpu.VMEM((q, q), F32),
            pltpu.VMEM((LANES, q), F32),
            pltpu.VMEM((q, LANES), F32),
            pltpu.VMEM((q, LANES), F32),
            pltpu.VMEM((q, LANES), F32),
        ]
        + [pltpu.VMEM((tok_size // 2, share, width), BF16)] * 2
        + [pltpu.VMEM((tok_size, share, width), BF16)] * 2
        + [pltpu.VMEM((share, width // HALVES), F32)] * 2
        + [pltpu.SemaphoreType.DMA((copies,))] * 3,
        (x_ext, x_ext, s_ext, s_ext, par, bcpar, hp, cume, dte, cumt, gy, sloc, sin, sdec, gloc, gout, gdec, gz, go),
        int(30e9),
        collective_id=2,
    )


def gather_kernel(
    tok_bits, row_bits, half_bit,
    in_ref, gain_ref, par_ref, small_ref, wx_ref, wz_ref, wo_ref,
    x_out, s_out, z_out, normed_out, rows_out, ws_out, wx_out, wz_out, wo_out, gains_out, pars_out,
    ws, wx, wz, wo, joined, rows, halo, normed, gains, pars, stage,
    send_sem, recv_sem, local_sem, stage_sem,
):
    tok, head = lax.axis_index("tok"), lax.axis_index("head")
    sets = 1 << len(row_bits)
    heads = 2 * sets
    half, mine = head // sets, head % sets
    own_rows, model = in_ref.shape
    share, own_width = wx_ref.shape
    tokens = own_rows * sets
    partners = [{"tok": flip(tok, b)} for b in tok_bits]
    partners += [{"head": flip_all(head, p)} for p in range(1, heads)]

    barrier = pltpu.get_barrier_semaphore()
    for partner in partners:
        pl.semaphore_signal(barrier, inc=1, device_id=partner, device_id_type=MESH)
    pl.semaphore_wait(barrier, len(partners))

    sent, stored, open_local = [], [], []

    def send(src, dst, device):
        k = len(sent)
        copy = pltpu.make_async_remote_copy(
            src_ref=src, dst_ref=dst, send_sem=send_sem.at[k], recv_sem=recv_sem.at[k],
            device_id=device, device_id_type=MESH,
        )
        copy.start()
        sent.append(copy)
        return copy

    def local(src, dst):
        copy = pltpu.make_async_copy(src, dst, local_sem.at[len(stored)])
        copy.start()
        stored.append(copy)
        open_local.append(copy)
        return copy

    def settle(copy):
        if any(copy is other for other in open_local):
            open_local[:] = [other for other in open_local if other is not copy]
            copy.wait()

    def arrive(copies):
        for copy in copies:
            copy.wait_recv()

    other_half = {"head": flip(head, half_bit)}
    lanes = pl.ds(pl.multiple_of(half * own_width, LANES), own_width)

    class Piece:
        def __init__(self, src, dst, part, order):
            size = share // 2
            self.rows = pl.ds(part * size, size)
            self.dst, self.order, self.held = dst, list(order), [0]
            slot = dst.at[tok, self.rows, lanes]
            self.flight = [send(src.at[self.rows], slot, other_half)]
            self.kept = local(src.at[self.rows], slot)

        def advance(self):
            arrive(self.flight)
            settle(self.kept)
            self.flight = []
            if self.order:
                bit = self.order.pop(0)
                for offset in self.held:
                    slot = self.dst.at[flip_all(tok, offset), self.rows]
                    self.flight.append(send(slot, slot, {"tok": flip(tok, bit)}))
                self.held = self.held + [offset ^ (1 << bit) for offset in self.held]

        def finish(self):
            while self.flight:
                self.advance()

    class Small(Piece):
        def __init__(self, src, dst, order):
            self.rows = pl.ds(0, share)
            self.dst, self.order, self.held = dst, list(order), [0]
            wide = pl.ds(pl.multiple_of(2 * STATE + half * LANES, LANES), LANES)
            slot = dst.at[tok, :, wide]
            part = src.at[:, pl.ds(2 * STATE, LANES)]
            self.flight = [send(part, slot, other_half)]
            settle(local(part, slot))
            self.kept = local(src.at[:, pl.ds(0, 2 * STATE)], dst.at[tok, :, pl.ds(0, 2 * STATE)])

    class Rows:
        def __init__(self, src, dst):
            self.dst, self.order, self.held = dst, list(row_bits), [0]
            self.src = src
            self.kept = local(src, dst.at[mine])
            self.flight = []
            if self.order:
                bit = self.order.pop(0)
                self.flight.append(send(src, dst.at[mine], {"head": flip(head, bit)}))
                self.held = [0, 1 << bit]

        def advance(self):
            arrive(self.flight)
            settle(self.kept)
            self.flight = []
            if self.order:
                bit = self.order.pop(0)
                for offset in self.held:
                    slot = self.dst.at[flip_all(mine, offset)]
                    self.flight.append(send(slot, slot, {"head": flip(head, bit)}))
                self.held = self.held + [offset ^ (1 << bit) for offset in self.held]

        def finish(self):
            settle(self.kept)
            while self.flight:
                self.advance()

    up = list(tok_bits)[1:] + [0]
    down = list(tok_bits)[1:][::-1] + [0]
    gain_copies = [
        send(gain_ref, gains.at[p], {"head": flip_all(head, p)}) for p in range(1, heads)
    ]
    gain_kept = local(gain_ref, gains.at[0])
    par_slot = pars.at[:, lanes]
    par_copy = send(par_ref, par_slot, other_half)
    par_kept = local(par_ref, par_slot)
    p_small = Small(small_ref, ws, up)
    p_xa = Piece(wx_ref, wx, 0, up)
    p_xb = Piece(wx_ref, wx, 1, down)
    p_za = Piece(wz_ref, wz, 0, up)
    p_zb = Piece(wz_ref, wz, 1, down)
    r_in = Rows(in_ref, rows)
    p_oa = Piece(wo_ref, wo, 0, up)
    p_ob = Piece(wo_ref, wo, 1, down)
    first, second, third = (p_small, p_xa, p_xb), (p_za, p_zb), (p_oa, p_ob)

    def advance(pieces):
        for piece in pieces:
            piece.advance()

    def normalise(src, start, count, scale):
        def body(i, carry):
            at = pl.ds(pl.multiple_of(start + i * 16, 16), 16)
            wide = src[pl.ds(pl.multiple_of(i * 16, 16), 16), :].astype(F32)
            inv = lax.rsqrt(jnp.sum(wide * wide, axis=1, keepdims=True) / model + EPS)
            normed[at, :] = (wide * inv * scale).astype(BF16)
            return carry

        lax.fori_loop(0, count // 16, body, 0, unroll=4 if count >= 64 else 1)

    def project(lhs, count, weight, out, width):
        tile = 256 if width % 256 == 0 else 3 * LANES
        steps = width // tile

        def out_copy(i):
            at = pl.ds(pl.multiple_of(i * tile, tile), tile)
            return pltpu.make_async_copy(
                stage.at[i % 2, pl.ds(0, count), pl.ds(0, tile)], out.at[:, at], stage_sem.at[i % 2]
            )

        def body(i, carry):
            @pl.when(i >= 2)
            def _():
                out_copy(i - 2).wait()

            at = pl.ds(pl.multiple_of(i * tile, tile), tile)
            block = weight[:, :, at].reshape(model, tile)
            stage[i % 2, 0:count, 0:tile] = dot_nn(lhs[...].reshape(count, model), block)
            out_copy(i).start()
            return carry

        lax.fori_loop(0, steps, body, 0)
        for i in range(max(steps - 2, 0), steps):
            out_copy(i).wait()

    def finish(pieces):
        for piece in pieces:
            piece.finish()

    def join_heads():
        def body(i, carry):
            low = ws[i, :, 2 * STATE : 2 * STATE + LANES].astype(F32)
            high = ws[i, :, 2 * STATE + LANES :].astype(F32)
            joined[i, :, : 2 * STATE] = ws[i, :, : 2 * STATE]
            joined[i, :, 2 * STATE :] = (low + pltpu.roll(high, own_width // HEADDIM, 1)).astype(BF16)
            return carry

        lax.fori_loop(0, ws.shape[0], body, 0)

    advance(first)
    advance(second)
    arrive(gain_copies)
    settle(gain_kept)
    scale = gains[0, 0:1, :]
    for p in range(1, heads):
        scale = scale + gains[p, 0:1, :]
    gains[0, 0:1, :] = scale
    advance(first)
    settle(r_in.kept)
    normalise(rows.at[mine], mine * own_rows, own_rows, scale)
    advance(second)
    advance(first)
    advance(third)
    advance(second)
    finish(first)
    join_heads()
    local(joined, ws_out)
    local(wx, wx_out)
    r_in.finish()
    tail = rows.at[sets - 1, pl.ds(own_rows - HALO, HALO), :]
    tail_copy = send(tail, halo, other_half)
    advance(third)
    for i in range(1, sets):
        other = flip_all(mine, i)
        normalise(rows.at[other], other * own_rows, own_rows, scale)
    tail_copy.wait_recv()
    normalise(halo, tokens, HALO, scale * half.astype(F32))
    local(rows, rows_out)
    local(normed, normed_out)
    project(normed, tokens + HALO, joined, s_out, s_out.shape[1])
    advance(third)
    project(normed, tokens + HALO, wx, x_out, wx.shape[2])
    finish(second)
    local(wz, wz_out)
    finish(third)
    local(wo, wo_out)
    project(normed.at[pl.ds(0, tokens)], tokens, wz, z_out, wz.shape[2])
    arrive([par_copy])
    settle(par_kept)
    local(pars, pars_out)
    local(gains.at[0], gains_out)
    for copy in list(open_local):
        settle(copy)
    for copy in sent:
        copy.wait_send()


def gather_and_project(block_in, gain, par, small, wx, wz, wo):
    tok_size, head_size = lax.axis_size("tok"), lax.axis_size("head")
    sets = head_size // HALVES
    tok_bits = range(tok_size.bit_length() - 1)
    row_bits = range(sets.bit_length() - 1)
    own_rows, model = block_in.shape
    share, own_width = wx.shape
    width = HALVES * own_width
    tokens = own_rows * sets
    lanes = 2 * STATE + HALVES * LANES
    anywhere = pl.BlockSpec(memory_space=pl.ANY)
    slots = (tok_size, share)
    copies = 128
    outs = [
        shape((tokens + HALO, width), F32),
        shape((tokens + HALO, 2 * STATE + LANES), F32),
        shape((tokens, width), F32),
        shape((tokens + HALO, model), BF16),
        shape((sets, own_rows, model), BF16),
        shape(slots + (2 * STATE + LANES,), BF16),
        shape(slots + (width,), BF16),
        shape(slots + (width,), BF16),
        shape(slots + (width,), BF16),
        shape((8, model), F32),
        shape((8, width), F32),
    ]
    return pl.pallas_call(
        functools.partial(gather_kernel, tok_bits, row_bits, sets.bit_length() - 1),
        in_specs=[anywhere] * 7,
        out_specs=[anywhere] * len(outs),
        out_shape=outs,
        scratch_shapes=[
            pltpu.VMEM(slots + (lanes,), BF16),
            pltpu.VMEM(slots + (width,), BF16),
            pltpu.VMEM(slots + (width,), BF16),
            pltpu.VMEM(slots + (width,), BF16),
            pltpu.VMEM(slots + (2 * STATE + LANES,), BF16),
            pltpu.VMEM((sets, own_rows, model), BF16),
            pltpu.VMEM((HALO, model), BF16),
            pltpu.VMEM((tokens + HALO, model), BF16),
            pltpu.VMEM((head_size, 8, model), F32),
            pltpu.VMEM((8, width), F32),
            pltpu.VMEM((2, tokens + HALO, 3 * LANES), F32),
            pltpu.SemaphoreType.DMA((copies,)),
            pltpu.SemaphoreType.DMA((copies,)),
            pltpu.SemaphoreType.DMA((32,)),
            pltpu.SemaphoreType.DMA((2,)),
        ],
        name="gather",
        compiler_params=pltpu.CompilerParams(
            collective_id=0, has_side_effects=True, vmem_limit_bytes=60 * 1024 * 1024
        ),
        cost_estimate=pl.CostEstimate(flops=int(12e9), bytes_accessed=int(60e6), transcendentals=0),
    )(block_in, gain, par, small, wx, wz, wo)


def reduce_kernel(
    tok_bits, row_bits,
    gx_ref, gs_ref, gl_ref, dx_ref, ds_ref, dn_ref, rows_ref, wx_ref, ws_ref, cot_ref, gain_ref, per_ref, bc_ref,
    ox_ref, os_ref, dblock_ref, all_out, per_out,
    kx, ks, rx, rs, fx, ls,
    dx, ds, wx, ws, rows, cots, dnorm, base, low, got, halo_out, halo_in, sums, sums_got,
    send_sem, recv_sem, local_sem, chunk_sem,
):
    links = Links(send_sem, recv_sem, local_sem, tok_bits, row_bits)
    half, mine, sets = links.half, links.mine, links.sets
    own_rows, model = cot_ref.shape
    own_width = ox_ref.shape[1]
    tokens = own_rows * sets
    chunk = base.shape[0]
    links.enter()

    up = [0] + links.tok_bits[1:]
    down = [0] + links.tok_bits[1:][::-1]
    loads = [links.local(dx_ref, dx), links.local(ds_ref, ds), links.local(wx_ref, wx), links.local(ws_ref, ws)]
    s_small = SmallSum(links, gs_ref, gl_ref, ks, ls, rs, up)
    s_x = [Sum(links, gx_ref, kx, rx, fx, ox_ref, p, 2, (down, up)[p]) for p in range(2)]
    for each in s_x:
        each.advance()
    row_load = links.local(rows_ref, rows)
    cot_load = links.local(cot_ref, cots)

    def advance(group):
        for each in group:
            each.advance()

    def project_back(at, count):
        lhs_x, lhs_s = dx[at, :], ds[at, :]
        return dot_nt(lhs_x, wx[...].reshape(model, wx.shape[2])) + dot_nt(lhs_s, ws[...].reshape(model, ws.shape[2]))

    def fetch(slot, i):
        at = pl.ds(pl.multiple_of(slot * own_rows + i * chunk, chunk), chunk)
        return pltpu.make_async_copy(dn_ref.at[at], base, chunk_sem.at[0])

    def slot_rows(slot):
        def body(i, carry):
            fetch(slot, i).start()
            total = project_back(pl.ds(pl.multiple_of(slot * own_rows + i * chunk, chunk), chunk), chunk)
            fetch(slot, i).wait()
            dnorm[slot, pl.ds(pl.multiple_of(i * chunk, chunk), chunk), :] = total + base[...]
            return carry

        lax.fori_loop(0, own_rows // chunk, body, 0)

    def fold(slot):
        keep = jnp.where(half == 0, 1.0, 0.0) * jnp.where(slot == sets - 1, 1.0, 0.0)
        tail = pl.ds(own_rows - HALO, HALO)
        dnorm[slot, tail, :] = dnorm[slot, tail, :] + keep * halo_in[...]

    def unit_rows(slot, at):
        wide = rows[slot, at, :].astype(F32)
        return wide, lax.rsqrt(jnp.sum(wide * wide, axis=1, keepdims=True) / model + EPS)

    def gain_part(slot):
        def body(i, total):
            at = pl.ds(pl.multiple_of(i * 16, 16), 16)
            wide, inv = unit_rows(slot, at)
            part = dnorm[slot, at, :] * wide * inv
            return total + part[0:8] + part[8:16]

        return lax.fori_loop(0, own_rows // 16, body, jnp.zeros((8, model), F32))

    links.settle(loads)
    halo_out[...] = project_back(pl.ds(tokens, HALO), HALO)
    away = list(range(1, sets))[::-1]
    slots = [flip_all(mine, o) for o in away]
    if slots:
        slot_rows(slots[0])
    halo_copy = links.send(halo_out, halo_in, links.head_peer(links.half_bit))
    advance([s_small])
    advance(s_x)
    for slot in slots[1:]:
        slot_rows(slot)
    links.settle([row_load])
    halo_copy.wait_recv()
    gain_sum = jnp.zeros((8, model), F32)
    for slot in slots:
        fold(slot)
        gain_sum = gain_sum + gain_part(slot)
    sums[0, :, pl.ds(0, model)] = gain_sum

    row_order = list(row_bits)[::-1]
    held = list(range(sets))
    places = 0

    def send_rows():
        nonlocal held, places
        bit = row_order.pop(0)
        stay = [o for o in held if not (o >> bit) & 1]
        flight = []
        for o in stay:
            slot = flip_all(mine, o ^ (1 << bit))

            def body(i, carry, slot=slot, place=places):
                at = pl.ds(pl.multiple_of(i * 16, 16), 16)
                low[place, at, :] = dnorm[slot, at, :].astype(BF16)
                return carry

            lax.fori_loop(0, own_rows // 16, body, 0)
            flight.append((o, places))
            places += 1
        held = stay
        return bit, flight

    def start_rows(bit, flight):
        return [(o, p, links.send(low.at[p], got.at[p], links.head_peer(bit))) for o, p in flight]

    def take_rows(copies):
        for o, place, copy in copies:
            copy.wait_recv()
            slot = flip_all(mine, o)

            def body(i, carry, slot=slot, place=place):
                at = pl.ds(pl.multiple_of(i * 16, 16), 16)
                dnorm[slot, at, :] = dnorm[slot, at, :] + got[place, at, :].astype(F32)
                return carry

            lax.fori_loop(0, own_rows // 16, body, 0)

    prepared = send_rows() if row_order else None
    row_copies = start_rows(*prepared) if prepared else []
    slot_rows(mine)
    fold(mine)
    gain_sum = sums[0, :, pl.ds(0, model)] + gain_part(mine)
    gain_row = jnp.sum(gain_sum, axis=0, keepdims=True)
    advance(s_x)
    advance([s_small])

    bc_width = bc_ref.shape[1]
    sums[0, :, pl.ds(0, model)] = jnp.concatenate(
        [gain_row, jnp.concatenate([bc_ref[0:7, :], jnp.zeros((7, model - bc_width), F32)], axis=1)], axis=0
    )
    sums[0, :, pl.ds(model, own_width)] = per_ref[:, pl.ds(pl.multiple_of((1 - half) * own_width, LANES), own_width)]
    advance(s_x)
    copy = links.send(sums.at[0], sums_got.at[0], links.head_peer(links.half_bit))
    advance([s_small])
    copy.wait_recv()
    sums[1, :, pl.ds(0, model)] = sums[0, :, pl.ds(0, model)] + sums_got[0, :, pl.ds(0, model)]
    sums[1, :, pl.ds(model, own_width)] = (
        per_ref[:, pl.ds(pl.multiple_of(half * own_width, LANES), own_width)] + sums_got[0, :, pl.ds(model, own_width)]
    )
    stage = 1
    peers = [links.head_peer(b) for b in row_bits] + [links.tok_peer(b) for b in tok_bits]
    for n, peer in enumerate(peers):
        copy = links.send(sums.at[stage], sums_got.at[stage], peer)
        copy.wait_recv()
        if n < len(row_bits):
            sums[stage + 1, :, pl.ds(0, model)] = (
                sums[stage, :, pl.ds(0, model)] + sums_got[stage, :, pl.ds(0, model)]
            )
            sums[stage + 1, :, pl.ds(model, own_width)] = sums[stage, :, pl.ds(model, own_width)]
        else:
            sums[stage + 1] = sums[stage] + sums_got[stage]
        stage += 1
    links.local(sums.at[stage, :, pl.ds(0, model)], all_out)
    links.local(sums.at[stage, :, pl.ds(model, own_width)], per_out)

    s_small.finish()
    links.local(ks.at[0], os_ref)
    for each in s_x:
        each.finish()

    while row_copies:
        take_rows(row_copies)
        row_copies = start_rows(*send_rows()) if row_order else []
    links.settle([cot_load])
    gain = gain_ref[0:1, :]

    def block_rows(i, carry):
        at = pl.ds(pl.multiple_of(i * 16, 16), 16)
        wide, inv = unit_rows(mine, at)
        scaled = dnorm[mine, at, :] * gain
        inner = jnp.sum(scaled * wide, axis=1, keepdims=True) / model
        dnorm[mine, at, :] = cots[at, :].astype(F32) + inv * scaled - wide * (inv * inv * inv * inner)
        return carry

    lax.fori_loop(0, own_rows // 16, block_rows, 0)
    links.local(dnorm.at[mine], dblock_ref)
    for each in s_x:
        each.close()
    links.leave()


def reduce_sums(gx, gs, gl, dx, ds, dn, rows, wx, ws, cot, gain, per, bc):
    tok_size, head_size = lax.axis_size("tok"), lax.axis_size("head")
    sets = head_size // HALVES
    tok_bits = range(tok_size.bit_length() - 1)
    row_bits = range(sets.bit_length() - 1)
    own_rows, model = cot.shape
    share, width = gx.shape[1:]
    lanes = gs.shape[2]
    own_width = width // HALVES
    anywhere = pl.BlockSpec(memory_space=pl.ANY)
    inside = pl.BlockSpec(memory_space=pltpu.VMEM)
    keep, slots = tok_size // 2, tok_size + len(row_bits)
    stages = len(tok_bits) + len(row_bits) + 1
    away = max(sets - 1, 1)
    copies = 32 * len(tok_bits)
    outs = [
        shape((share, own_width), F32),
        shape((share, lanes), F32),
        shape((own_rows, model), F32),
        shape((8, model), F32),
        shape((8, own_width), F32),
    ]
    return pl.pallas_call(
        functools.partial(reduce_kernel, tok_bits, row_bits),
        in_specs=[anywhere] * 10 + [inside] * 3,
        out_specs=[anywhere] * len(outs),
        out_shape=outs,
        scratch_shapes=[pltpu.VMEM((keep, share, width), BF16)]
        + [pltpu.VMEM((keep, share, lanes), F32)]
        + [pltpu.VMEM((slots, share, width), BF16)]
        + [pltpu.VMEM((slots, share, lanes), BF16)]
        + [pltpu.VMEM((share, own_width), F32)]
        + [pltpu.VMEM((slots, share, lanes), BF16)]
        + [
            pltpu.VMEM(dx.shape, BF16),
            pltpu.VMEM(ds.shape, BF16),
            pltpu.VMEM(wx.shape, BF16),
            pltpu.VMEM(ws.shape, BF16),
            pltpu.VMEM(rows.shape, BF16),
            pltpu.VMEM(cot.shape, BF16),
            pltpu.VMEM((sets, own_rows, model), F32),
            pltpu.VMEM((min(CHUNK, own_rows), model), F32),
            pltpu.VMEM((away, own_rows, model), BF16),
            pltpu.VMEM((away, own_rows, model), BF16),
            pltpu.VMEM((HALO, model), F32),
            pltpu.VMEM((HALO, model), F32),
            pltpu.VMEM((stages + 1, 8, model + own_width), F32),
            pltpu.VMEM((stages, 8, model + own_width), F32),
            pltpu.SemaphoreType.DMA((copies,)),
            pltpu.SemaphoreType.DMA((copies,)),
            pltpu.SemaphoreType.DMA((copies,)),
            pltpu.SemaphoreType.DMA((1,)),
        ],
        name="reduce",
        compiler_params=pltpu.CompilerParams(
            collective_id=1, has_side_effects=True, vmem_limit_bytes=62 * 1024 * 1024
        ),
        cost_estimate=pl.CostEstimate(flops=int(12e9), bytes_accessed=int(60e6), transcendentals=0),
    )(gx, gs, gl, dx, ds, dn, rows, wx, ws, cot, gain, per, bc)


def per_device(
    block_in,
    norm_gain,
    w_zx,
    w_bc,
    w_dt,
    conv_x_w,
    conv_x_b,
    conv_bc_w,
    conv_bc_b,
    dt_bias,
    a_log,
    d_skip,
    gate_gain,
    w_out,
    cotangent,
):
    head_size = lax.axis_size("head")
    tok_size = lax.axis_size("tok")
    sets = head_size // HALVES
    row_bits = range(sets.bit_length() - 1)
    half_bit = sets.bit_length() - 1
    half = bit_of("head", half_bit)
    own_rows, model = block_in.shape
    share, _, own_width = w_zx.shape
    own_heads = w_dt.shape[1]
    tokens = own_rows * sets

    def all_rows(value):
        for bit in row_bits:
            value = grow(value, "head", bit, 0)
        return value

    def lane_pad(v):
        return jnp.pad(v, (0, LANES - v.shape[0]))

    heads_row = jnp.concatenate([lane_pad(dt_bias), lane_pad(a_log), lane_pad(d_skip)])
    own_par = jnp.concatenate(
        [
            conv_x_w,
            conv_x_b[None],
            gate_gain[None],
            jnp.repeat(d_skip, HEADDIM)[None],
            jnp.pad(heads_row, (0, own_width - heads_row.shape[0]))[None],
        ]
    )
    gain_share = norm_gain.shape[0]
    own_gain = lax.dynamic_update_slice(
        jnp.zeros((8, model), F32),
        jnp.broadcast_to(norm_gain.astype(F32)[None], (8, gain_share)),
        (0, lax.axis_index("head") * gain_share),
    )
    small = jnp.concatenate([w_bc, jnp.pad(w_dt, ((0, 0), (0, LANES - own_heads)))], axis=1)
    x_ext, s_ext, z, normed_ext, rows, w_small, w_x, w_z, w_o, gain, par = gather_and_project(
        block_in, own_gain, own_par, small, w_zx[:, 1], w_zx[:, 0], w_out.T
    )
    later_cot, x_ext = lax.optimization_barrier((cotangent, x_ext))
    cot = all_rows(later_cot)
    gain = gain[0:1]
    normed = normed_ext[:tokens]
    slots_small, slots_x, gain_rows = w_small, w_x, gain
    w_z, w_o = w_z.reshape(model, w_z.shape[2]), w_o.reshape(model, w_o.shape[2])

    def of_heads(start):
        pieces = [
            par[CONV + 3, i * own_width + start : i * own_width + start + own_heads] for i in range(HALVES)
        ]
        return jnp.concatenate(pieces)

    rate = -jnp.exp(of_heads(LANES))
    hp = jnp.stack([lane_pad(of_heads(0)), lane_pad(rate)] + [jnp.zeros((LANES,), F32)] * 6)
    bcpar = jnp.concatenate([conv_bc_w, conv_bc_b[None], jnp.zeros((3, 2 * STATE), F32)])

    xs, u, cume, dte, bc, cumt, sloc, fin, sdec = mixer_forward_state(x_ext, s_ext, par, bcpar, hp, tokens)
    to_next = [(i, i + sets) for i in range(sets)]
    to_prev = [(i + sets, i) for i in range(sets)]
    sin = lax.ppermute(fin, "head", to_next)
    gyn = dot_nn(cot, w_o)
    y, stat = mixer_forward_main(xs, u, cume, cumt, bc, sloc, sin, sdec, z, gyn, par)
    stat = add_pairs(stat, "head", row_bits).T
    inv_gate = lax.rsqrt(stat[:, 0:1] / INNER + EPS)
    stat = jnp.concatenate(
        [inv_gate, inv_gate * inv_gate * inv_gate * stat[:, 1:2] / INNER, stat[:, 2:]], axis=1
    )
    yn, gy, dz, gloc, gin, gdec, acc_gate = mixer_backward_gate(y, z, gyn, xs, cume, bc, stat, par)
    gout = lax.ppermute(gin, "head", to_prev)

    def own_row_sum(value):
        for bit in list(row_bits)[::-1]:
            value = halve(value, "head", bit, 0)
        return value

    def slots_of(grad):
        return grad.astype(BF16).reshape(tok_size, share, grad.shape[1])

    branch = dot_nt(yn, w_o)
    block_out = block_in.astype(F32) + own_row_sum(branch)
    grad_o = slots_of(dot_tn(cot, yn))
    grad_z = slots_of(dot_tn(normed, dz))
    d_normed_z = dot_nt(dz, w_z)

    dx, ds, acc_x, acc_b, acc_h, d_w_z, d_w_o = mixer_backward_main(
        x_ext, s_ext, par, bcpar, hp, cume, dte, cumt, gy, sloc, sin, sdec, gloc, gout, gdec, grad_z, grad_o
    )
    grad_x = slots_of(dot_tn(normed_ext, dx))
    grad_small = dot_tn(normed_ext, ds).reshape(tok_size, share, ds.shape[1])

    per_channel = jnp.concatenate(
        [
            acc_x[: CONV + 1],
            acc_gate[0:1],
            jnp.concatenate(
                [
                    jnp.pad(
                        jnp.concatenate(
                            [
                                lane_pad(acc_h[0, i * own_heads : (i + 1) * own_heads]),
                                lane_pad(acc_h[1, i * own_heads : (i + 1) * own_heads]),
                                lane_pad(
                                    jnp.sum(
                                        acc_gate[1, i * own_width : (i + 1) * own_width].reshape(own_heads, HEADDIM),
                                        axis=1,
                                    )
                                ),
                            ]
                        ),
                        (0, own_width - 3 * LANES),
                    )
                    for i in range(HALVES)
                ]
            )[None],
            jnp.zeros((1, HALVES * own_width), F32),
        ]
    )

    d_w_x, d_small, d_block_in, all_sums, own_sums = reduce_sums(
        grad_x, grad_small, grad_small.astype(BF16), dx, ds, d_normed_z, rows, slots_x, slots_small, cotangent,
        gain_rows, per_channel, acc_b,
    )
    all_gain, bc_sums = all_sums[0], all_sums[1:, : 2 * STATE]
    d_w_bc = d_small[:, : 2 * STATE]
    d_w_dt = jnp.where(
        half == 0,
        d_small[:, 2 * STATE : 2 * STATE + own_heads],
        d_small[:, 2 * STATE + own_heads : 2 * STATE + 2 * own_heads],
    )
    d_norm_gain = lax.dynamic_slice_in_dim(all_gain, lax.axis_index("head") * gain_share, gain_share, 0)
    return (
        block_out,
        d_block_in,
        d_norm_gain,
        jnp.stack([d_w_z, d_w_x], axis=1),
        d_w_bc,
        d_w_dt,
        own_sums[:CONV],
        own_sums[CONV],
        bc_sums[:CONV],
        bc_sums[CONV],
        own_sums[CONV + 2, :own_heads],
        own_sums[CONV + 2, LANES : LANES + own_heads],
        own_sums[CONV + 2, 2 * LANES : 2 * LANES + own_heads],
        own_sums[CONV + 1],
        d_w_o.T,
    )


def solution(mesh):
    placed = (
        P(("tok", "head"), None),
        P("head"),
        P("tok", None, "head"),
        P("tok", None),
        P("tok", "head"),
        P(None, "head"),
        P("head"),
        P(),
        P(),
        P("head"),
        P("head"),
        P("head"),
        P("head"),
        P("head", "tok"),
        P(("tok", "head"), None),
    )
    return jax.shard_map(
        per_device,
        mesh=mesh,
        in_specs=placed,
        out_specs=(
            P(("tok", "head"), None),
            P(("tok", "head"), None),
            P("head"),
            P("tok", None, "head"),
            P("tok", None),
            P("tok", "head"),
            P(None, "head"),
            P("head"),
            P(),
            P(),
            P("head"),
            P("head"),
            P("head"),
            P("head"),
            P("head", "tok"),
        ),
        check_vma=False,
    )
```

```python
import functools

import jax
import jax.numpy as jnp
from jax import lax
from jax.experimental import pallas as pl
from jax.experimental.pallas import tpu as pltpu
from jax.sharding import PartitionSpec as P

HEADDIM = 64
STATE = 128
CONV = 4
INNER = 3072
CHUNK = 256
HALVES = 2
LANES = 128
HALO = 16

EPS = 1e-05
HIGHEST = lax.Precision.HIGHEST
F32 = jnp.float32
BF16 = jnp.bfloat16


def dot_nn(a, b, precision=None):
    return lax.dot_general(
        a, b, (((1,), (0,)), ((), ())), preferred_element_type=F32, precision=precision
    )


def dot_nt(a, b, precision=None):
    return lax.dot_general(
        a, b, (((1,), (1,)), ((), ())), preferred_element_type=F32, precision=precision
    )


def dot_tn(a, b):
    return lax.dot_general(a, b, (((0,), (0,)), ((), ())), preferred_element_type=F32)


def dot_split(a, b):
    a_top, b_top = a.astype(BF16), b.astype(BF16)
    a_rest = (a - a_top.astype(F32)).astype(BF16)
    b_rest = (b - b_top.astype(F32)).astype(BF16)
    return dot_nn(a_top, b_top) + (dot_nn(a_rest, b_top) + dot_nn(a_top, b_rest))


def iota(shape, dim):
    return lax.broadcasted_iota(jnp.int32, shape, dim)


def sigmoid(v):
    return 1.0 / (1.0 + jnp.exp(-v))


def softplus(v):
    return jnp.maximum(v, 0.0) + jnp.log1p(jnp.exp(-jnp.abs(v)))


def head_spread(width):
    return (iota((LANES, width), 1) // HEADDIM == iota((LANES, width), 0)).astype(F32)


def bit_of(axis, bit):
    return (lax.axis_index(axis) // (1 << bit)) % 2


def swap(value, axis, bit):
    size = lax.axis_size(axis)
    return lax.ppermute(value, axis, [(i, i ^ (1 << bit)) for i in range(size)])


def grow(value, axis, bit, dim):
    other = swap(value, axis, bit)
    low = bit_of(axis, bit) == 0
    return jnp.where(
        low,
        jnp.concatenate([value, other], dim),
        jnp.concatenate([other, value], dim),
    )


def halve(value, axis, bit, dim):
    mine = bit_of(axis, bit)
    if dim < value.ndim - 1:
        half = value.shape[dim] // 2
        keep = lax.dynamic_slice_in_dim(value, mine * half, half, dim)
        send = lax.dynamic_slice_in_dim(value, (1 - mine) * half, half, dim)
    else:
        low, high = jnp.split(value, 2, axis=dim)
        keep = jnp.where(mine == 0, low, high)
        send = jnp.where(mine == 0, high, low)
    return keep.astype(F32) + swap(send.astype(BF16), axis, bit).astype(F32)


def add_pairs(value, axis, bits):
    for bit in bits:
        value = value + swap(value, axis, bit)
    return value


MESH = pl.DeviceIdType.MESH


def flip(index, bit):
    return index + (1 - 2 * ((index // (1 << bit)) % 2)) * (1 << bit)


def flip_all(index, offset):
    bit = 0
    while offset >> bit:
        if (offset >> bit) & 1:
            index = flip(index, bit)
        bit += 1
    return index


def now(value):
    return value() if callable(value) else value


class Remote:
    def __init__(self, links, k, src, dst, device):
        self.links, self.k, self.src, self.dst, self.device = links, k, src, dst, device

    def make(self):
        return pltpu.make_async_remote_copy(
            src_ref=now(self.src),
            dst_ref=now(self.dst),
            send_sem=self.links.send_sem.at[self.k],
            recv_sem=self.links.recv_sem.at[self.k],
            device_id=now(self.device),
            device_id_type=MESH,
        )

    def start(self):
        self.make().start()

    def wait_recv(self):
        self.make().wait_recv()

    def wait_send(self):
        self.make().wait_send()


class Local:
    def __init__(self, links, k, src, dst):
        self.links, self.k, self.src, self.dst = links, k, src, dst

    def make(self):
        return pltpu.make_async_copy(now(self.src), now(self.dst), self.links.local_sem.at[self.k])

    def start(self):
        self.make().start()

    def wait(self):
        self.make().wait()


class Links:
    def __init__(self, send_sem, recv_sem, local_sem, tok_bits, row_bits):
        self.send_sem, self.recv_sem, self.local_sem = send_sem, recv_sem, local_sem
        self.tok_bits, self.row_bits = list(tok_bits), list(row_bits)
        self.tok, self.head = lax.axis_index("tok"), lax.axis_index("head")
        self.sets = 1 << len(self.row_bits)
        self.half, self.mine = self.head // self.sets, self.head % self.sets
        self.half_bit = len(self.row_bits)
        self.sent, self.drained, self.n_local, self.open_local = [], [], 0, []

    def enter(self):
        partners = [self.tok_peer(b) for b in self.tok_bits]
        partners += [self.head_peer(b) for b in self.row_bits + [self.half_bit]]
        barrier = pltpu.get_barrier_semaphore()
        for partner in partners:
            pl.semaphore_signal(barrier, inc=1, device_id=partner(), device_id_type=MESH)
        pl.semaphore_wait(barrier, len(partners))

    def tok_peer(self, bit):
        return lambda: {"tok": flip(self.tok, bit)}

    def head_peer(self, bit):
        return lambda: {"head": flip(self.head, bit)}

    def plan_send(self, src, dst, device):
        copy = Remote(self, len(self.sent), src, dst, device)
        self.sent.append(copy)
        return copy

    def send(self, src, dst, device):
        copy = self.plan_send(src, dst, device)
        copy.start()
        return copy

    def plan_local(self, src, dst):
        self.n_local += 1
        return Local(self, self.n_local - 1, src, dst)

    def local(self, src, dst):
        copy = self.plan_local(src, dst)
        copy.start()
        self.open_local.append(copy)
        return copy

    def settle(self, copies):
        for copy in copies:
            if any(copy is other for other in self.open_local):
                self.open_local = [other for other in self.open_local if other is not copy]
                copy.wait()

    def drain(self, copy):
        copy.wait_recv()
        copy.wait_send()
        self.drained.append(copy)

    def leave(self):
        self.settle(list(self.open_local))
        for copy in self.sent:
            if not any(copy is other for other in self.drained):
                copy.wait_send()


def add_rows(dst, src, count):
    def body(i, carry):
        at = pl.ds(pl.multiple_of(i * 16, 16), 16)
        dst[at, :] = (dst[at, :].astype(F32) + src[at, :].astype(F32)).astype(BF16)
        return carry

    lax.fori_loop(0, count // 16, body, 0)


class Sum:
    def __init__(self, links, src, keep, recv, final, out, part, parts, order):
        self.links, self.src, self.keep, self.recv, self.final = links, src, keep, recv, final
        self.size = keep.shape[1] // parts
        self.start = part * self.size
        self.width = out.shape[1]
        held = list(range(1 << len(links.tok_bits)))
        self.sends, self.adds, base = [], [], 0
        for number, bit in enumerate(order):
            stay = [o for o in held if not (o >> bit) & 1]
            if number == 0:
                place = {o: i for i, o in enumerate(stay)}
                self.loads = [links.plan_local(self.source(o), self.slot(place[o])) for o in stay]
            sends, adds = [], []
            for n, o in enumerate(stay):
                away = o ^ (1 << bit)
                src_ref = self.source(away) if number == 0 else self.slot(place[away])
                sends.append(links.plan_send(src_ref, self.landing(base + n), links.tok_peer(bit)))
                adds.append((place[o], base + n))
            base += len(stay)
            held = stay
            self.sends.append(sends)
            self.adds.append(adds)
        self.base = base
        self.tail = links.plan_send(
            lambda: self.keep.at[0, self.rows(), self.half_lanes(1 - self.links.half)],
            lambda: self.recv.at[base, self.rows(), pl.ds(0, self.width)],
            links.head_peer(links.half_bit),
        )
        self.store = links.plan_local(lambda: final.at[self.rows()], lambda: out.at[self.rows()])
        self.next = 0
        self.last = len(self.sends) + 1

    def rows(self):
        return pl.ds(self.start, self.size)

    def source(self, offset):
        return lambda: self.src.at[flip_all(self.links.tok, offset), self.rows()]

    def landing(self, i):
        return lambda: self.recv.at[i, self.rows()]

    def slot(self, i):
        return lambda: self.keep.at[i, self.rows()]

    def half_lanes(self, which):
        return pl.ds(pl.multiple_of(which * self.width, LANES), self.width)

    def step(self, k):
        if k == 0:
            for copy in self.sends[0] + self.loads:
                copy.start()
            return
        if k == self.last:
            self.tail.wait_recv()
            lanes = self.half_lanes(self.links.half)

            def body(i, carry):
                at = pl.ds(pl.multiple_of(self.start + i * 16, 16), 16)
                self.final[at, :] = self.keep[0, at, lanes].astype(F32) + self.recv[
                    self.base, at, 0 : self.width
                ].astype(F32)
                return carry

            lax.fori_loop(0, self.size // 16, body, 0)
            self.store.start()
            return
        for copy in self.sends[k - 1]:
            copy.wait_recv()
        if k == 1:
            for copy in self.loads:
                copy.wait()
        for place, i in self.adds[k - 1]:
            add_rows(now(self.slot(place)), now(self.landing(i)), self.size)
        for copy in self.sends[k] if k < len(self.sends) else [self.tail]:
            copy.start()

    def advance(self):
        if self.next < self.last:
            self.step(self.next)
            self.next += 1

    def finish(self):
        while self.next <= self.last:
            self.step(self.next)
            self.next += 1

    def close(self):
        self.store.wait()


class SmallSum(Sum):
    def __init__(self, links, src, src_low, keep, low, recv, order):
        self.links, self.keep, self.low, self.recv = links, keep, low, recv
        self.order = list(order)
        bit = self.order.pop(0)
        slots = range(1 << len(links.tok_bits))
        self.held = [o for o in slots if not (o >> bit) & 1]
        self.place = {o: i for i, o in enumerate(self.held)}
        self.base = len(self.held)
        self.n_low = 0
        self.into = [(i, i) for i in range(self.base)]
        self.flight = [
            links.send(src_low.at[flip_all(links.tok, o ^ (1 << bit))], recv.at[self.place[o]], links.tok_peer(bit))
            for o in self.held
        ]
        self.kept = [links.local(src.at[flip_all(links.tok, o)], keep.at[self.place[o]]) for o in self.held]
        self.done = False

    def post(self, place, lanes, device):
        n = self.n_low
        self.low[n, :, 0:lanes] = self.keep[place, :, 0:lanes].astype(BF16)
        self.n_low += 1
        src, dst = self.low.at[n, :, pl.ds(0, lanes)], self.recv.at[self.base, :, pl.ds(0, lanes)]
        self.flight.append(self.links.send(src, dst, device))
        self.base += 1
        return self.base - 1

    def take(self):
        for copy in self.flight:
            copy.wait_recv()
        self.links.settle(self.kept)
        for place, i in self.into:
            self.keep[place, :, 0 : self.lanes_in] = self.keep[place, :, 0 : self.lanes_in] + self.recv[
                i, :, 0 : self.lanes_in
            ].astype(F32)
        self.flight, self.into, self.kept = [], [], []

    lanes_in = 2 * STATE + LANES

    def advance(self):
        if self.done:
            return
        self.take()
        if not self.order:
            self.into = [(0, self.post(0, self.lanes_in, self.links.head_peer(self.links.half_bit)))]
            self.done = True
            return
        bit = self.order.pop(0)
        stay = [o for o in self.held if not (o >> bit) & 1]
        self.into = [
            (self.place[o], self.post(self.place[o ^ (1 << bit)], self.lanes_in, self.links.tok_peer(bit)))
            for o in stay
        ]
        self.held = stay

    def finish(self):
        while not self.done:
            self.advance()
        self.take()
        self.lanes_in = 2 * STATE
        for bit in self.links.row_bits:
            self.into = [(0, self.post(0, self.lanes_in, self.links.head_peer(bit)))]
            self.take()


def conv_rows(cur, tail, weight, bias):
    rows = cur.shape[0]
    ext = jnp.concatenate([tail, cur], axis=0)
    out = bias + weight[CONV - 1 : CONV] * cur
    for k in range(CONV - 1):
        start = 8 - (CONV - 1) + k
        out = out + weight[k : k + 1] * ext[start : start + rows]
    return out


def state_kernel(
    xm_ref, xt_ref, bm_ref, bt_ref, par_ref, bcpar_ref, hp_ref,
    xs_ref, u_ref, cume_ref, dte_ref, bc_ref, cumt_ref, sloc_ref, fin_ref, dec_ref,
    state, dsum, ue,
):
    c = pl.program_id(0)
    q, width = xm_ref.shape

    @pl.when(c == 0)
    def _():
        state[...] = jnp.zeros_like(state)
        dsum[...] = jnp.zeros_like(dsum)

    dt = softplus(bm_ref[:, 2 * STATE :] + hp_ref[0:1, :])
    tri = (iota((q, q), 0) >= iota((q, q), 1)).astype(F32)
    cum = dot_nn(tri, dt * hp_ref[1:2, :], HIGHEST)
    cumt_ref[...] = cum.T[: cumt_ref.shape[0], :]
    spread = head_spread(width)
    cume_ref[...] = dot_nn(cum, spread, HIGHEST)
    dte_ref[...] = dot_nn(dt, spread, HIGHEST)
    end = cume_ref[q - 1 : q, :]

    bpre = conv_rows(
        bm_ref[:, : 2 * STATE], bt_ref[:, : 2 * STATE], bcpar_ref[0:CONV, :], bcpar_ref[CONV : CONV + 1, :]
    )
    bc_ref[...] = bpre * sigmoid(bpre)

    block = 2 * LANES

    def body(i, carry):
        sl = pl.ds(pl.multiple_of(i * block, block), block)
        pre = conv_rows(
            xm_ref[:, sl], xt_ref[:, sl], par_ref[0:CONV, sl], par_ref[CONV : CONV + 1, sl]
        )
        xs = pre * sigmoid(pre)
        u = xs * dte_ref[:, sl]
        xs_ref[:, sl] = xs
        u_ref[:, sl] = u.astype(BF16)
        cume = cume_ref[:, sl]
        ue[:, sl] = (u * jnp.exp(cume[q - 1 : q, :] - cume)).astype(BF16)
        return carry

    lax.fori_loop(0, width // block, body, 0)
    sloc_ref[0] = state[...]
    dec_ref[0] = jnp.exp(dsum[...])
    state[...] = jnp.exp(end) * state[...] + dot_nn(bc_ref[:, :STATE].T.astype(BF16), ue[...])
    dsum[...] = dsum[...] + end
    fin_ref[...] = state[...].astype(BF16)


def main_kernel(
    xs_ref, u_ref, cume_ref, cumt_ref, bc_ref, sloc_ref, sin_ref, dec_ref, z_ref, gyn_ref, par_ref,
    y_ref, stat_ref,
    gram, ya, acc_sq, acc_in,
):
    q, width = xs_ref.shape
    bmat = bc_ref[:, :STATE].astype(BF16)
    cmat = bc_ref[:, STATE:].astype(BF16)
    lower = iota((q, q), 0) >= iota((q, q), 1)
    gram[...] = jnp.where(lower, dot_nt(cmat, bmat), 0.0)
    entering = sloc_ref[0] + dec_ref[0, 0:1, :] * sin_ref[...].astype(F32)
    ya[...] = dot_nn(cmat, entering.astype(BF16))
    acc_sq[...] = jnp.zeros_like(acc_sq)
    acc_in[...] = jnp.zeros_like(acc_in)
    first = iota((q, LANES), 1) < HEADDIM

    def body(p, carry):
        sl = pl.ds(pl.multiple_of(p * LANES, LANES), LANES)
        cume = cume_ref[:, sl]
        u = u_ref[:, sl]
        y = jnp.exp(cume) * ya[:, sl] + par_ref[CONV + 2 : CONV + 3, sl] * xs_ref[:, sl]
        for s in range(2):
            gap = cume[:, HEADDIM * s : HEADDIM * s + 1] - cumt_ref[pl.ds(2 * p + s, 1), :]
            pairs = (gram[...] * jnp.exp(jnp.minimum(gap, 0.0))).astype(BF16)
            y = y + dot_nn(pairs, jnp.where(first == (s == 0), u, jnp.zeros_like(u)))
        y_ref[:, sl] = y
        z = z_ref[:, sl]
        gated = y * z * sigmoid(z)
        acc_sq[...] += gated * gated
        acc_in[...] += gated * gyn_ref[:, sl] * par_ref[CONV + 1 : CONV + 2, sl]
        return carry

    lax.fori_loop(0, width // LANES, body, 0)
    ones = jnp.ones((8, LANES), F32)
    sums_sq = dot_nt(ones, acc_sq[...], HIGHEST)
    sums_in = dot_nt(ones, acc_in[...], HIGHEST)
    stat_ref[...] = jnp.where(iota(sums_sq.shape, 0) == 0, sums_sq, sums_in)


def gate_kernel(
    y_ref, z_ref, gyn_ref, xs_ref, cume_ref, bc_ref, stat_ref, par_ref,
    yn_ref, gy_ref, dz_ref, gloc_ref, gin_ref, dec_ref, acc_ref,
    adj, dsum, ge,
):
    q, width = y_ref.shape

    @pl.when(pl.program_id(0) == 0)
    def _():
        adj[...] = jnp.zeros_like(adj)
        dsum[...] = jnp.zeros_like(dsum)
        acc_ref[...] = jnp.zeros_like(acc_ref)

    end = cume_ref[q - 1 : q, :]
    inv = jnp.broadcast_to(stat_ref[:, 0:1], (q, LANES))
    back = jnp.broadcast_to(stat_ref[:, 1:2], (q, LANES))

    def body(p, carry):
        sl = pl.ds(pl.multiple_of(p * LANES, LANES), LANES)
        y, z, gyn = y_ref[:, sl], z_ref[:, sl], gyn_ref[:, sl]
        sig = sigmoid(z)
        sil = z * sig
        gated = y * sil
        gain = par_ref[CONV + 1 : CONV + 2, sl]
        unit = gated * inv
        yn_ref[:, sl] = (unit * gain).astype(BF16)
        d_gated = inv * gyn * gain - gated * back
        gy = d_gated * sil
        gy_ref[:, sl] = gy
        dz_ref[:, sl] = (d_gated * y * (sig * (1.0 + z * (1.0 - sig)))).astype(BF16)
        ge[:, sl] = (gy * jnp.exp(cume_ref[:, sl])).astype(BF16)
        acc_ref[0:1, sl] += jnp.sum(gyn * unit, axis=0, keepdims=True)
        acc_ref[1:2, sl] += jnp.sum(gy * xs_ref[:, sl], axis=0, keepdims=True)
        return carry

    lax.fori_loop(0, width // LANES, body, 0)
    gloc_ref[0] = adj[...]
    dec_ref[0] = jnp.exp(dsum[...])
    adj[...] = jnp.exp(end) * adj[...] + dot_nn(bc_ref[:, STATE:].T.astype(BF16), ge[...])
    dsum[...] = dsum[...] + end
    gin_ref[...] = adj[...].astype(BF16)


def back_kernel(
    tok_bits, row_bits,
    xm_ref, xt_ref, bm_ref, bt_ref, par_ref, bcpar_ref, hp_ref,
    cume_ref, dte_ref, cumt_ref, gy_ref, sloc_ref, sin_ref, sdec_ref, gloc_ref, gout_ref, gdec_ref,
    gz_ref, go_ref,
    dx_ref, ds_ref, accx_ref, accb_ref, acch_ref, oz_ref, oo_ref,
    xs, u, dsil, ue, ge, dus, ya, qx, qb, gram, dgram, da, acc_x, acc_w, acc_g,
    kz, ko, rz, ro, fz, fo, send_sem, recv_sem, local_sem,
):
    step = pl.program_id(0)
    q, width = xm_ref.shape
    tokens = dx_ref.shape[0] - HALO
    steps = tokens // q
    links = Links(send_sem, recv_sem, local_sem, tok_bits, row_bits)
    up = [0] + links.tok_bits[1:]
    down = [0] + links.tok_bits[1:][::-1]
    groups = [
        [Sum(links, gz_ref, kz, rz, fz, oz_ref, p, 2, (down, up)[p]) for p in range(2)],
        [Sum(links, go_ref, ko, ro, fo, oo_ref, p, 2, (down, up)[p]) for p in range(2)],
    ]
    plans = [[(0, 0), (0, 2), (1, 2), (2, 3)], [(0, 0), (0, 3), (2, 2), (3, 1)]]

    def go_on(point):
        for when in range(steps):

            @pl.when(step == when)
            def _():
                if (when, point) == (0, 0):
                    links.enter()
                for group, plan in zip(groups, plans):
                    for k, (number, place) in enumerate(plan):
                        if (min(number, steps - 1), place) == (when, point):
                            for each in group:
                                each.step(k)
                if (when, point) == (steps - 1, 3):
                    for group, plan in zip(groups, plans):
                        for k in range(len(plan), group[0].last + 1):
                            for each in group:
                                each.step(k)
                    for group in groups:
                        for each in group:
                            each.close()
                    links.leave()

    go_on(0)
    c = tokens // q - 1 - step
    block = 2 * LANES

    @pl.when(step == 0)
    def _():
        accx_ref[...] = jnp.zeros_like(accx_ref)
        accb_ref[...] = jnp.zeros_like(accb_ref)
        acch_ref[...] = jnp.zeros_like(acch_ref)
        qx[q:, :] = jnp.zeros((8, width), F32)
        qb[q:, :] = jnp.zeros((8, 2 * STATE), F32)
        da[...] = jnp.zeros_like(da)
        ds_ref[...] = jnp.zeros_like(ds_ref)

    bpre = conv_rows(
        bm_ref[:, : 2 * STATE], bt_ref[:, : 2 * STATE], bcpar_ref[0:CONV, :], bcpar_ref[CONV : CONV + 1, :]
    )
    bsig = sigmoid(bpre)
    bc = bpre * bsig
    qb[0:q, :] = bsig * (1.0 + bpre * (1.0 - bsig))
    bmat, cmat = bc[:, :STATE].astype(BF16), bc[:, STATE:].astype(BF16)

    def conv_body(i, carry):
        sl = pl.ds(pl.multiple_of(i * block, block), block)
        pre = conv_rows(
            xm_ref[:, sl], xt_ref[:, sl], par_ref[0:CONV, sl], par_ref[CONV : CONV + 1, sl]
        )
        sig = sigmoid(pre)
        x = pre * sig
        xs[:, sl] = x
        dsil[:, sl] = sig * (1.0 + pre * (1.0 - sig))
        uu = x * dte_ref[:, sl]
        u[:, sl] = uu.astype(BF16)
        cume = cume_ref[:, sl]
        ue[:, sl] = (uu * jnp.exp(cume[q - 1 : q, :] - cume)).astype(BF16)
        ge[:, sl] = (gy_ref[:, sl] * jnp.exp(cume)).astype(BF16)
        return carry

    lax.fori_loop(0, width // block, conv_body, 0)
    go_on(1)

    last = cume_ref[q - 1 : q, :]
    adj = gloc_ref[0] + gdec_ref[0, 0:1, :] * gout_ref[...].astype(F32)
    entering = sloc_ref[0] + sdec_ref[0, 0:1, :] * sin_ref[...].astype(F32)
    kept = jnp.exp(last) * jnp.sum(adj * entering, axis=0, keepdims=True)
    adj_low, ent_low = adj.astype(BF16), entering.astype(BF16)
    dus[...] = dot_nn(bmat, adj_low)
    ya[...] = dot_nn(cmat, ent_low)
    db = dot_nt(ue[...], adj_low)
    dc = dot_nt(ge[...], ent_low)
    upper = iota((q, q), 1) >= iota((q, q), 0)
    gram[...] = jnp.where(upper, dot_nt(bmat, cmat), 0.0)
    dgram[...] = jnp.zeros_like(dgram)
    acc_x[...] = jnp.zeros_like(acc_x)
    acc_w[...] = jnp.zeros_like(acc_w)
    acc_g[...] = jnp.zeros_like(acc_g)
    later = (iota((q, q), 0) >= iota((q, q), 1)).astype(BF16)
    first = iota((q, LANES), 1) < HEADDIM

    def pair_body(p, carry):
        sl = pl.ds(pl.multiple_of(p * LANES, LANES), LANES)
        cume = cume_ref[:, sl]
        ul = u[:, sl]
        gy = gy_ref[:, sl]
        gl = gy.astype(BF16)
        du = jnp.zeros((q, LANES), F32)
        for s in range(2):
            mine = first == (s == 0)
            row = pl.ds(2 * p + s, 1)
            gap = cumt_ref[row, :] - cume[:, HEADDIM * s : HEADDIM * s + 1]
            decay = jnp.exp(jnp.minimum(gap, 0.0))
            pairs = gram[...] * decay
            dpairs = dot_nt(jnp.where(mine, ul, jnp.zeros_like(ul)), gl)
            dgram[...] += dpairs * decay
            through = dot_nn((dpairs * pairs).astype(BF16), later)
            da[row, :] = jnp.sum(
                jnp.where(iota((q, q), 0) < iota((q, q), 1), through, 0.0), axis=0, keepdims=True
            )
            du = du + dot_nn(pairs.astype(BF16), jnp.where(mine, gl, jnp.zeros_like(gl)))
        x = xs[:, sl]
        wide = dus[:, sl] * jnp.exp(cume[q - 1 : q, :] - cume)
        du = du + wide
        to_head = (iota((LANES, LANES), 1) == 2 * p + iota((LANES, LANES), 0) // HEADDIM).astype(BF16)
        dte = dte_ref[:, sl]
        acc_x[...] += dot_nn((x * du).astype(BF16), to_head)
        acc_w[...] += dot_nn((x * dte * wide).astype(BF16), to_head)
        acc_g[...] += dot_nn((gy * jnp.exp(cume) * ya[:, sl]).astype(BF16), to_head)
        qx[0:q, sl] = (dte * du + par_ref[CONV + 2 : CONV + 3, sl] * gy) * dsil[:, sl]
        return carry

    lax.fori_loop(0, width // LANES, pair_body, 0)
    go_on(2)

    def unconv_body(i, carry):
        sl = pl.ds(pl.multiple_of(i * block, block), block)
        weight = par_ref[0:CONV, sl]
        ext = qx[:, sl]
        cur = ext[0:q]
        dpre = weight[CONV - 1 : CONV] * cur
        for k in range(CONV - 1):
            dpre = dpre + weight[k : k + 1] * ext[CONV - 1 - k : CONV - 1 - k + q]
        dx_ref[pl.ds(pl.multiple_of(c * q, q), q), sl] = dpre.astype(BF16)
        past = jnp.concatenate([xt_ref[:, sl], xm_ref[:, sl]], axis=0)
        for k in range(CONV):
            start = 8 - (CONV - 1) + k
            accx_ref[k : k + 1, sl] += jnp.sum(cur * past[start : start + q], axis=0, keepdims=True)
        accx_ref[CONV : CONV + 1, sl] += jnp.sum(cur, axis=0, keepdims=True)
        head_rows = jnp.concatenate([jnp.zeros((HALO, block), F32), cur[0:8]], axis=0)
        before = jnp.zeros((HALO, block), F32)
        for k in range(CONV - 1):
            before = before + weight[k : k + 1] * head_rows[CONV - 1 - k : CONV - 1 - k + HALO]
        dx_ref[pl.ds(tokens, HALO), sl] = before.astype(BF16)
        qx[q:, sl] = cur[0:8]
        return carry

    lax.fori_loop(0, width // block, unconv_body, 0)

    dg = jnp.where(upper, dgram[...], 0.0)
    db = db + dot_split(dg, bc[:, STATE:])
    dc = dc + dot_split(dg.T, bc[:, :STATE])
    qb[0:q, 0:STATE] = qb[0:q, 0:STATE] * db
    qb[0:q, STATE:] = qb[0:q, STATE:] * dc
    weight = bcpar_ref[0:CONV, :]
    ext = qb[...]
    cur = ext[0:q]
    dpre = weight[CONV - 1 : CONV] * cur
    for k in range(CONV - 1):
        dpre = dpre + weight[k : k + 1] * ext[CONV - 1 - k : CONV - 1 - k + q]
    ds_ref[pl.ds(pl.multiple_of(c * q, q), q), 0 : 2 * STATE] = dpre.astype(BF16)
    past = jnp.concatenate([bt_ref[:, 0 : 2 * STATE], bm_ref[:, 0 : 2 * STATE]], axis=0)
    for k in range(CONV):
        start = 8 - (CONV - 1) + k
        accb_ref[k : k + 1, :] += jnp.sum(cur * past[start : start + q], axis=0, keepdims=True)
    accb_ref[CONV : CONV + 1, :] += jnp.sum(cur, axis=0, keepdims=True)
    head_rows = jnp.concatenate([jnp.zeros((HALO, 2 * STATE), F32), cur[0:8]], axis=0)
    before = jnp.zeros((HALO, 2 * STATE), F32)
    for k in range(CONV - 1):
        before = before + weight[k : k + 1] * head_rows[CONV - 1 - k : CONV - 1 - k + HALO]
    ds_ref[pl.ds(tokens, HALO), 0 : 2 * STATE] = before.astype(BF16)
    qb[q:, :] = cur[0:8]

    raw = bm_ref[:, 2 * STATE :] + hp_ref[0:1, :]
    dt = softplus(raw)
    rate = hp_ref[1:2, :]
    from_here = (iota((q, q), 1) >= iota((q, q), 0)).astype(F32)
    up_to_here = (iota((q, q), 1) < iota((q, q), 0)).astype(F32)
    kept_heads = dot_nt(jnp.broadcast_to(kept, (8, width)), head_spread(width), HIGHEST)
    total = (
        da[...].T
        + dot_nn(from_here, acc_g[...], HIGHEST)
        + dot_nn(up_to_here, acc_w[...], HIGHEST)
        + kept_heads[0:1, :]
    )
    d_raw = (acc_x[...] + rate * total) * sigmoid(raw)
    ds_ref[pl.ds(pl.multiple_of(c * q, q), q), 2 * STATE :] = d_raw.astype(BF16)
    acch_ref[0:1, :] += jnp.sum(d_raw, axis=0, keepdims=True)
    acch_ref[1:2, :] += rate * jnp.sum(dt * total, axis=0, keepdims=True)
    go_on(3)


def shape(dims, dtype):
    return jax.ShapeDtypeStruct(dims, dtype)


def whole(dims):
    return pl.BlockSpec(dims, lambda c: (0,) * len(dims))


def run(kernel, name, grid, in_specs, out_specs, out_shape, scratch, args, flops, collective_id=None):
    return pl.pallas_call(
        kernel,
        grid=(grid,),
        in_specs=in_specs,
        out_specs=out_specs,
        out_shape=out_shape,
        scratch_shapes=scratch,
        name=name,
        compiler_params=pltpu.CompilerParams(
            dimension_semantics=("arbitrary",),
            vmem_limit_bytes=62 * 1024 * 1024,
            collective_id=collective_id,
            has_side_effects=collective_id is not None,
        ),
        cost_estimate=pl.CostEstimate(
            flops=flops, bytes_accessed=sum(a.size * a.dtype.itemsize for a in args), transcendentals=0
        ),
    )(*args)


def mixer_forward_state(x_ext, s_ext, par, bcpar, hp, tokens):
    width = x_ext.shape[1]
    small = s_ext.shape[1]
    n = tokens // CHUNK
    q = CHUNK
    tail = q // 8
    last = (tokens + HALO) // 8 - 1
    tail_map = lambda c: (jnp.where(c == 0, last, c * tail - 1), 0)
    heads_pad = -(-(width // HEADDIM) // 8) * 8
    return run(
        state_kernel,
        "scan_states",
        n,
        [
            pl.BlockSpec((q, width), lambda c: (c, 0)),
            pl.BlockSpec((8, width), tail_map),
            pl.BlockSpec((q, small), lambda c: (c, 0)),
            pl.BlockSpec((8, small), tail_map),
            whole(par.shape),
            whole(bcpar.shape),
            whole(hp.shape),
        ],
        [
            pl.BlockSpec((q, width), lambda c: (c, 0)),
            pl.BlockSpec((q, width), lambda c: (c, 0)),
            pl.BlockSpec((q, width), lambda c: (c, 0)),
            pl.BlockSpec((q, width), lambda c: (c, 0)),
            pl.BlockSpec((q, 2 * STATE), lambda c: (c, 0)),
            pl.BlockSpec((heads_pad, q), lambda c: (0, c)),
            pl.BlockSpec((1, STATE, width), lambda c: (c, 0, 0)),
            whole((STATE, width)),
            pl.BlockSpec((1, 1, width), lambda c: (c, 0, 0)),
        ],
        [
            shape((tokens, width), F32),
            shape((tokens, width), BF16),
            shape((tokens, width), F32),
            shape((tokens, width), F32),
            shape((tokens, 2 * STATE), F32),
            shape((heads_pad, tokens), F32),
            shape((n, STATE, width), F32),
            shape((STATE, width), BF16),
            shape((n, 1, width), F32),
        ],
        [
            pltpu.VMEM((STATE, width), F32),
            pltpu.VMEM((1, width), F32),
            pltpu.VMEM((q, width), BF16),
        ],
        (x_ext, x_ext, s_ext, s_ext, par, bcpar, hp),
        int(3e9),
    )


def mixer_forward_main(xs, u, cume, cumt, bc, sloc, sin, dec, z, gyn, par):
    tokens, width = xs.shape
    q = CHUNK
    n = tokens // q
    rows = pl.BlockSpec((q, width), lambda c: (c, 0))
    return run(
        main_kernel,
        "scan_outputs",
        n,
        [
            rows,
            rows,
            rows,
            pl.BlockSpec((cumt.shape[0], q), lambda c: (0, c)),
            pl.BlockSpec((q, 2 * STATE), lambda c: (c, 0)),
            pl.BlockSpec((1, STATE, width), lambda c: (c, 0, 0)),
            whole(sin.shape),
            pl.BlockSpec((1, 1, width), lambda c: (c, 0, 0)),
            rows,
            rows,
            whole(par.shape),
        ],
        [rows, pl.BlockSpec((8, q), lambda c: (0, c))],
        [shape((tokens, width), F32), shape((8, tokens), F32)],
        [
            pltpu.VMEM((q, q), F32),
            pltpu.VMEM((q, width), F32),
            pltpu.VMEM((q, LANES), F32),
            pltpu.VMEM((q, LANES), F32),
        ],
        (xs, u, cume, cumt, bc, sloc, sin, dec, z, gyn, par),
        int(10e9),
    )


def mixer_backward_gate(y, z, gyn, xs, cume, bc, stat, par):
    tokens, width = y.shape
    q = CHUNK
    n = tokens // q
    rows = pl.BlockSpec((q, width), lambda c: (n - 1 - c, 0))
    return run(
        gate_kernel,
        "gate_back",
        n,
        [
            rows,
            rows,
            rows,
            rows,
            rows,
            pl.BlockSpec((q, 2 * STATE), lambda c: (n - 1 - c, 0)),
            pl.BlockSpec((q, 8), lambda c: (n - 1 - c, 0)),
            whole(par.shape),
        ],
        [
            rows,
            rows,
            rows,
            pl.BlockSpec((1, STATE, width), lambda c: (n - 1 - c, 0, 0)),
            whole((STATE, width)),
            pl.BlockSpec((1, 1, width), lambda c: (n - 1 - c, 0, 0)),
            whole((8, width)),
        ],
        [
            shape((tokens, width), BF16),
            shape((tokens, width), F32),
            shape((tokens, width), BF16),
            shape((n, STATE, width), F32),
            shape((STATE, width), BF16),
            shape((n, 1, width), F32),
            shape((8, width), F32),
        ],
        [
            pltpu.VMEM((STATE, width), F32),
            pltpu.VMEM((1, width), F32),
            pltpu.VMEM((q, width), BF16),
        ],
        (y, z, gyn, xs, cume, bc, stat, par),
        int(5e9),
    )


def mixer_backward_main(
    x_ext, s_ext, par, bcpar, hp, cume, dte, cumt, gy, sloc, sin, sdec, gloc, gout, gdec, gz, go
):
    tok_size, head_size = lax.axis_size("tok"), lax.axis_size("head")
    tok_bits = range(tok_size.bit_length() - 1)
    row_bits = range((head_size // HALVES).bit_length() - 1)
    share = gz.shape[1]
    copies = 16 * len(tok_bits)
    tokens, width = cume.shape
    small = s_ext.shape[1]
    q = CHUNK
    n = tokens // q
    tail = q // 8
    last = (tokens + HALO) // 8 - 1
    rows = pl.BlockSpec((q, width), lambda c: (n - 1 - c, 0))
    tail_map = lambda c: (jnp.where(c == n - 1, last, (n - 1 - c) * tail - 1), 0)
    states = pl.BlockSpec((1, STATE, width), lambda c: (n - 1 - c, 0, 0))
    decays = pl.BlockSpec((1, 1, width), lambda c: (n - 1 - c, 0, 0))
    anywhere = pl.BlockSpec(memory_space=pl.ANY)
    return run(
        functools.partial(back_kernel, tok_bits, row_bits),
        "scan_back",
        n,
        [
            rows,
            pl.BlockSpec((8, width), tail_map),
            pl.BlockSpec((q, small), lambda c: (n - 1 - c, 0)),
            pl.BlockSpec((8, small), tail_map),
            whole(par.shape),
            whole(bcpar.shape),
            whole(hp.shape),
            rows,
            rows,
            pl.BlockSpec((cumt.shape[0], q), lambda c: (0, n - 1 - c)),
            rows,
            states,
            whole(sin.shape),
            decays,
            states,
            whole(gout.shape),
            decays,
            anywhere,
            anywhere,
        ],
        [
            whole((tokens + HALO, width)),
            whole((tokens + HALO, small)),
            whole((8, width)),
            whole((8, 2 * STATE)),
            whole((8, LANES)),
            anywhere,
            anywhere,
        ],
        [
            shape((tokens + HALO, width), BF16),
            shape((tokens + HALO, small), BF16),
            shape((8, width), F32),
            shape((8, 2 * STATE), F32),
            shape((8, LANES), F32),
            shape((share, width // HALVES), F32),
            shape((share, width // HALVES), F32),
        ],
        [
            pltpu.VMEM((q, width), F32),
            pltpu.VMEM((q, width), BF16),
            pltpu.VMEM((q, width), F32),
            pltpu.VMEM((q, width), BF16),
            pltpu.VMEM((q, width), BF16),
            pltpu.VMEM((q, width), F32),
            pltpu.VMEM((q, width), F32),
            pltpu.VMEM((q + 8, width), F32),
            pltpu.VMEM((q + 8, 2 * STATE), F32),
            pltpu.VMEM((q, q), F32),
            pltpu.VMEM((q, q), F32),
            pltpu.VMEM((LANES, q), F32),
            pltpu.VMEM((q, LANES), F32),
            pltpu.VMEM((q, LANES), F32),
            pltpu.VMEM((q, LANES), F32),
        ]
        + [pltpu.VMEM((tok_size // 2, share, width), BF16)] * 2
        + [pltpu.VMEM((tok_size, share, width), BF16)] * 2
        + [pltpu.VMEM((share, width // HALVES), F32)] * 2
        + [pltpu.SemaphoreType.DMA((copies,))] * 3,
        (x_ext, x_ext, s_ext, s_ext, par, bcpar, hp, cume, dte, cumt, gy, sloc, sin, sdec, gloc, gout, gdec, gz, go),
        int(30e9),
        collective_id=2,
    )


def gather_kernel(
    tok_bits, row_bits, half_bit,
    in_ref, gain_ref, par_ref, small_ref, wx_ref, wz_ref, wo_ref,
    x_out, s_out, z_out, normed_out, ws_out, wx_out, wz_out, wo_out, gains_out, pars_out,
    ws, wx, wz, wo, joined, rows, halo, normed, gains, gain_all, pars, stage,
    send_sem, recv_sem, local_sem, stage_sem,
):
    tok, head = lax.axis_index("tok"), lax.axis_index("head")
    sets = 1 << len(row_bits)
    heads = 2 * sets
    half, mine = head // sets, head % sets
    own_rows, model = in_ref.shape
    share, own_width = wx_ref.shape
    tokens = own_rows * sets
    partners = [{"tok": flip(tok, b)} for b in tok_bits]
    partners += [{"head": flip_all(head, p)} for p in range(1, heads)]

    barrier = pltpu.get_barrier_semaphore()
    for partner in partners:
        pl.semaphore_signal(barrier, inc=1, device_id=partner, device_id_type=MESH)
    pl.semaphore_wait(barrier, len(partners))

    sent, stored, open_local = [], [], []

    def send(src, dst, device):
        k = len(sent)
        copy = pltpu.make_async_remote_copy(
            src_ref=src, dst_ref=dst, send_sem=send_sem.at[k], recv_sem=recv_sem.at[k],
            device_id=device, device_id_type=MESH,
        )
        copy.start()
        sent.append(copy)
        return copy

    def local(src, dst):
        copy = pltpu.make_async_copy(src, dst, local_sem.at[len(stored)])
        copy.start()
        stored.append(copy)
        open_local.append(copy)
        return copy

    def settle(copy):
        if any(copy is other for other in open_local):
            open_local[:] = [other for other in open_local if other is not copy]
            copy.wait()

    def arrive(copies):
        for copy in copies:
            copy.wait_recv()

    other_half = {"head": flip(head, half_bit)}
    lanes = pl.ds(pl.multiple_of(half * own_width, LANES), own_width)

    class Own:
        def __init__(self, src, dst, rows_at, src_lanes, dst_lanes, order):
            self.rows, self.lanes = rows_at, dst_lanes
            self.dst, self.order = dst, list(order)
            slot = dst.at[tok, self.rows, self.lanes]
            bit = self.order.pop(0)
            self.flight = [send(src.at[self.rows, src_lanes], slot, {"tok": flip(tok, bit)})]
            self.kept = local(src.at[self.rows, src_lanes], slot)
            self.held = [0, 1 << bit]

        def advance(self):
            arrive(self.flight)
            settle(self.kept)
            self.flight = []
            if self.order:
                bit = self.order.pop(0)
                for offset in self.held:
                    slot = self.dst.at[flip_all(tok, offset), self.rows, self.lanes]
                    self.flight.append(send(slot, slot, {"tok": flip(tok, bit)}))
                self.held = self.held + [offset ^ (1 << bit) for offset in self.held]

        def finish(self):
            while self.flight:
                self.advance()

    class Other(Own):
        def __init__(self, src, dst, rows_at, src_lanes, sent_lanes, dst_lanes, order):
            self.rows, self.lanes = rows_at, dst_lanes
            self.dst, self.order, self.held, self.kept = dst, list(order), [0], None
            self.flight = [send(src.at[self.rows, src_lanes], dst.at[tok, self.rows, sent_lanes], other_half)]

    class Rows:
        def __init__(self, src, dst):
            self.dst, self.order, self.held = dst, list(row_bits), [0]
            self.src = src
            self.kept = local(src, dst.at[mine])
            self.flight = []
            if self.order:
                bit = self.order.pop(0)
                self.flight.append(send(src, dst.at[mine], {"head": flip(head, bit)}))
                self.held = [0, 1 << bit]

        def advance(self):
            arrive(self.flight)
            settle(self.kept)
            self.flight = []
            if self.order:
                bit = self.order.pop(0)
                for offset in self.held:
                    slot = self.dst.at[flip_all(mine, offset)]
                    self.flight.append(send(slot, slot, {"head": flip(head, bit)}))
                self.held = self.held + [offset ^ (1 << bit) for offset in self.held]

        def finish(self):
            settle(self.kept)
            while self.flight:
                self.advance()

    up = list(tok_bits)[1:] + [0]
    down = list(tok_bits)[1:][::-1] + [0]
    gain_copies = [
        send(gain_ref, gains.at[head], {"head": flip_all(head, p)}) for p in range(1, heads)
    ]
    gain_kept = local(gain_ref, gains.at[head])
    par_slot = pars.at[:, lanes]
    par_copy = send(par_ref, par_slot, other_half)
    par_kept = local(par_ref, par_slot)
    own_all = pl.ds(0, own_width)
    there = pl.ds(pl.multiple_of((1 - half) * own_width, LANES), own_width)
    parts = [pl.ds(n * (share // 2), share // 2) for n in range(2)]

    def own_pieces(src, dst):
        return [Own(src, dst, parts[n], own_all, lanes, (up, down)[n]) for n in range(2)]

    def other_pieces(src, dst):
        return [Other(src, dst, parts[n], own_all, lanes, there, (up, down)[n]) for n in range(2)]

    def step_lanes(which):
        return pl.ds(pl.multiple_of(2 * STATE + which * LANES, LANES), LANES)

    every, bc_lanes, own_steps = pl.ds(0, share), pl.ds(0, 2 * STATE), pl.ds(2 * STATE, LANES)
    x_other = other_pieces(wx_ref, wx)
    x_other.append(Other(small_ref, ws, every, own_steps, step_lanes(half), step_lanes(1 - half), down))
    x_own = own_pieces(wx_ref, wx)
    x_own.append(Own(small_ref, ws, every, bc_lanes, bc_lanes, up))
    x_own.append(Own(small_ref, ws, every, own_steps, step_lanes(half), down))
    z_own = own_pieces(wz_ref, wz)
    z_other = other_pieces(wz_ref, wz)
    r_in = Rows(in_ref, rows)
    o_own = own_pieces(wo_ref, wo)
    o_other = other_pieces(wo_ref, wo)

    def advance(pieces):
        for piece in pieces:
            piece.advance()

    def normalise(src, start, count, scale):
        def body(i, carry):
            at = pl.ds(pl.multiple_of(start + i * 16, 16), 16)
            wide = src[pl.ds(pl.multiple_of(i * 16, 16), 16), :].astype(F32)
            inv = lax.rsqrt(jnp.sum(wide * wide, axis=1, keepdims=True) / model + EPS)
            normed[at, :] = (wide * inv * scale).astype(BF16)
            return carry

        lax.fori_loop(0, count // 16, body, 0, unroll=4 if count >= 64 else 1)

    def project(lhs, count, weight, out, width):
        tile = 256 if width % 256 == 0 else 3 * LANES
        steps = width // tile

        def out_copy(i):
            at = pl.ds(pl.multiple_of(i * tile, tile), tile)
            return pltpu.make_async_copy(
                stage.at[i % 2, pl.ds(0, count), pl.ds(0, tile)], out.at[:, at], stage_sem.at[i % 2]
            )

        def body(i, carry):
            @pl.when(i >= 2)
            def _():
                out_copy(i - 2).wait()

            at = pl.ds(pl.multiple_of(i * tile, tile), tile)
            block = weight[:, :, at].reshape(model, tile)
            stage[i % 2, 0:count, 0:tile] = dot_nn(lhs[...].reshape(count, model), block)
            out_copy(i).start()
            return carry

        lax.fori_loop(0, steps, body, 0)
        for i in range(max(steps - 2, 0), steps):
            out_copy(i).wait()

    def finish(pieces):
        for piece in pieces:
            piece.finish()

    def join_heads():
        def body(i, carry):
            low = ws[i, :, 2 * STATE : 2 * STATE + LANES].astype(F32)
            high = ws[i, :, 2 * STATE + LANES :].astype(F32)
            joined[i, :, : 2 * STATE] = ws[i, :, : 2 * STATE]
            joined[i, :, 2 * STATE :] = (low + pltpu.roll(high, own_width // HEADDIM, 1)).astype(BF16)
            return carry

        lax.fori_loop(0, ws.shape[0], body, 0)

    advance(x_own)
    arrive(gain_copies)
    settle(gain_kept)
    gain_share = model // heads
    scale = jnp.concatenate([gains[g, 0:1, 0:gain_share] for g in range(heads)], axis=1)
    gain_all[...] = jnp.broadcast_to(scale, (8, model))
    advance(x_other)
    advance(x_own)
    settle(r_in.kept)
    normalise(rows.at[mine], mine * own_rows, own_rows, scale)
    advance(x_other)
    advance(z_own)
    advance(z_other)
    advance(x_other)
    advance(z_own)
    advance(o_own)
    advance(z_other)
    finish(x_own)
    finish(x_other)
    join_heads()
    local(joined, ws_out)
    local(wx, wx_out)
    r_in.finish()
    tail = rows.at[sets - 1, pl.ds(own_rows - HALO, HALO), :]
    tail_copy = send(tail, halo, other_half)
    for i in range(1, sets):
        other = flip_all(mine, i)
        normalise(rows.at[other], other * own_rows, own_rows, scale)
    advance(o_other)
    advance(o_own)
    advance(z_other)
    tail_copy.wait_recv()
    normalise(halo, tokens, HALO, scale * half.astype(F32))
    local(normed, normed_out)
    project(normed, tokens + HALO, joined, s_out, s_out.shape[1])
    advance(o_other)
    project(normed, tokens + HALO, wx, x_out, wx.shape[2])
    finish(z_own)
    finish(z_other)
    local(wz, wz_out)
    advance(o_other)
    project(normed.at[pl.ds(0, tokens)], tokens, wz, z_out, wz.shape[2])
    finish(o_own)
    finish(o_other)
    local(wo, wo_out)
    arrive([par_copy])
    settle(par_kept)
    local(pars, pars_out)
    local(gain_all, gains_out)
    for copy in list(open_local):
        settle(copy)
    for copy in sent:
        copy.wait_send()


def gather_and_project(block_in, gain, par, small, wx, wz, wo):
    tok_size, head_size = lax.axis_size("tok"), lax.axis_size("head")
    sets = head_size // HALVES
    tok_bits = range(tok_size.bit_length() - 1)
    row_bits = range(sets.bit_length() - 1)
    own_rows, model = block_in.shape
    share, own_width = wx.shape
    width = HALVES * own_width
    tokens = own_rows * sets
    lanes = 2 * STATE + HALVES * LANES
    anywhere = pl.BlockSpec(memory_space=pl.ANY)
    slots = (tok_size, share)
    copies = 16 * tok_size
    outs = [
        shape((tokens + HALO, width), F32),
        shape((tokens + HALO, 2 * STATE + LANES), F32),
        shape((tokens, width), F32),
        shape((tokens + HALO, model), BF16),
        shape(slots + (2 * STATE + LANES,), BF16),
        shape(slots + (width,), BF16),
        shape(slots + (width,), BF16),
        shape(slots + (width,), BF16),
        shape((8, model), F32),
        shape((8, width), F32),
    ]
    return pl.pallas_call(
        functools.partial(gather_kernel, tok_bits, row_bits, sets.bit_length() - 1),
        in_specs=[anywhere] * 7,
        out_specs=[anywhere] * len(outs),
        out_shape=outs,
        scratch_shapes=[
            pltpu.VMEM(slots + (lanes,), BF16),
            pltpu.VMEM(slots + (width,), BF16),
            pltpu.VMEM(slots + (width,), BF16),
            pltpu.VMEM(slots + (width,), BF16),
            pltpu.VMEM(slots + (2 * STATE + LANES,), BF16),
            pltpu.VMEM((sets, own_rows, model), BF16),
            pltpu.VMEM((HALO, model), BF16),
            pltpu.VMEM((tokens + HALO, model), BF16),
            pltpu.VMEM((head_size,) + gain.shape, F32),
            pltpu.VMEM((8, model), F32),
            pltpu.VMEM((8, width), F32),
            pltpu.VMEM((2, tokens + HALO, 3 * LANES), F32),
            pltpu.SemaphoreType.DMA((copies,)),
            pltpu.SemaphoreType.DMA((copies,)),
            pltpu.SemaphoreType.DMA((32,)),
            pltpu.SemaphoreType.DMA((2,)),
        ],
        name="gather",
        compiler_params=pltpu.CompilerParams(
            collective_id=0, has_side_effects=True, vmem_limit_bytes=60 * 1024 * 1024
        ),
        cost_estimate=pl.CostEstimate(flops=int(12e9), bytes_accessed=int(60e6), transcendentals=0),
    )(block_in, gain, par, small, wx, wz, wo)


def reduce_kernel(
    tok_bits, row_bits,
    gx_ref, gs_ref, gl_ref, dx_ref, ds_ref, dn_ref, norm_ref, in_ref, wx_ref, ws_ref, cot_ref, gain_ref, per_ref, bc_ref,
    ox_ref, os_ref, dblock_ref, gain_out, rest_out,
    kx, ks, rx, rs, fx, ls,
    dx, ds, wx, ws, norms, own_in, cots, dnorm, low, got, halo_out, halo_in, sums, sums_got, per_got, bc_got, bc_own,
    send_sem, recv_sem, local_sem,
):
    links = Links(send_sem, recv_sem, local_sem, tok_bits, row_bits)
    half, mine, sets = links.half, links.mine, links.sets
    own_rows, model = cot_ref.shape
    own_width = ox_ref.shape[1]
    tokens = own_rows * sets
    chunk = min(CHUNK, own_rows)
    loads = [
        links.local(src, dst)
        for src, dst in ((dx_ref, dx), (ds_ref, ds), (wx_ref, wx), (ws_ref, ws), (dn_ref, dnorm))
    ]
    links.enter()

    up = [0] + links.tok_bits[1:]
    down = [0] + links.tok_bits[1:][::-1]
    s_small = SmallSum(links, gs_ref, gl_ref, ks, ls, rs, up)
    s_x = [Sum(links, gx_ref, kx, rx, fx, ox_ref, p, 2, (down, up)[p]) for p in range(2)]

    def advance(group):
        for each in group:
            each.advance()

    advance(s_x)
    late_loads = [
        links.local(norm_ref.at[pl.ds(0, tokens)], norms), links.local(in_ref, own_in), links.local(cot_ref, cots)
    ]

    def project_back(at):
        lhs_x, lhs_s = dx[at, :], ds[at, :]
        return dot_nt(lhs_x, wx[...].reshape(model, wx.shape[2])) + dot_nt(lhs_s, ws[...].reshape(model, ws.shape[2]))

    def slot_rows(slot):
        def body(i, carry):
            here = pl.ds(pl.multiple_of(i * chunk, chunk), chunk)
            total = project_back(pl.ds(pl.multiple_of(slot * own_rows + i * chunk, chunk), chunk))
            dnorm[slot, here, :] = dnorm[slot, here, :] + total
            return carry

        lax.fori_loop(0, own_rows // chunk, body, 0)

    def fold(slot):
        keep = jnp.where(half == 0, 1.0, 0.0) * jnp.where(slot == sets - 1, 1.0, 0.0)
        tail = pl.ds(own_rows - HALO, HALO)
        dnorm[slot, tail, :] = dnorm[slot, tail, :] + keep * halo_in[...]

    def rows_at(i, count):
        return pl.ds(pl.multiple_of(i * count, count), count)

    def gain_part(slot, start):
        def body(i, total):
            normed = norms[pl.ds(pl.multiple_of(slot * own_rows + i * 16, 16), 16), :].astype(F32)
            part = dnorm[slot, rows_at(i, 16), :] * normed
            return total + part[0:8] + part[8:16]

        return lax.fori_loop(0, own_rows // 16, body, start, unroll=2)

    everywhere, rest, owned = pl.ds(0, model), pl.ds(model, own_width + bc_ref.shape[1]), pl.ds(model, own_width)
    bc_lanes = pl.ds(model + own_width, bc_ref.shape[1])

    def channel_lanes(which):
        return pl.ds(pl.multiple_of(which * own_width, LANES), own_width)

    early = [
        links.send(per_ref.at[:, channel_lanes(1 - half)], per_got, links.head_peer(links.half_bit)),
        links.send(bc_ref, bc_got.at[0], links.head_peer(links.half_bit)),
    ]

    links.settle(loads)
    halo_out[...] = project_back(pl.ds(tokens, HALO))
    away = list(range(1, sets))[::-1]
    slots = [flip_all(mine, o) for o in away]
    if slots:
        slot_rows(slots[0])
    halo_copy = links.send(halo_out, halo_in, links.head_peer(links.half_bit))
    for copy in early:
        copy.wait_recv()
    sums[0, :, owned] = per_ref[:, channel_lanes(half)] + per_got[...]
    bc_total = bc_ref[...] + bc_got[0]
    for n, bit in enumerate(links.row_bits):
        bc_own[n] = bc_total
        copy = links.send(bc_own.at[n], bc_got.at[n + 1], links.head_peer(bit))
        copy.wait_recv()
        bc_total = bc_total + bc_got[n + 1]
    sums[0, :, bc_lanes] = bc_total
    for slot in slots[1:]:
        slot_rows(slot)
    halo_copy.wait_recv()
    for slot in slots:
        fold(slot)

    row_order = list(row_bits)[::-1]
    held = list(range(sets))
    places = 0

    def send_rows():
        nonlocal held, places
        bit = row_order.pop(0)
        stay = [o for o in held if not (o >> bit) & 1]
        copies = []
        for o in stay:
            slot = flip_all(mine, o ^ (1 << bit))

            def body(i, carry, slot=slot, place=places):
                low[place, rows_at(i, 32), :] = dnorm[slot, rows_at(i, 32), :].astype(BF16)
                return carry

            lax.fori_loop(0, own_rows // 32, body, 0)
            copies.append((o, places, bit))
            places += 1
        held = stay
        return copies

    def start_rows(copies):
        return [(o, p, links.send(low.at[p], got.at[p], links.head_peer(bit))) for o, p, bit in copies]

    def take_rows(copies):
        for o, place, copy in copies:
            copy.wait_recv()
            slot = flip_all(mine, o)

            def body(i, carry, slot=slot, place=place):
                at = rows_at(i, 32)
                dnorm[slot, at, :] = dnorm[slot, at, :] + got[place, at, :].astype(F32)
                return carry

            lax.fori_loop(0, own_rows // 32, body, 0)

    prepared = send_rows() if row_order else []
    advance([s_small])
    row_copies = start_rows(prepared)
    advance(s_x)
    slot_rows(mine)
    fold(mine)
    links.settle(late_loads)
    gain_sum = jnp.zeros((8, model), F32)
    for slot in slots + [mine]:
        gain_sum = gain_part(slot, gain_sum)
    gain = gain_ref[0:1, :]
    gain_row = jnp.sum(gain_sum, axis=0, keepdims=True) / gain

    sums[0, :, everywhere] = jnp.concatenate([gain_row, jnp.zeros((7, model), F32)], axis=0)
    advance([s_small])
    between = {0: s_x, 1: [s_small], 2: s_x}
    for n, bit in enumerate(tok_bits):
        copy = links.send(sums.at[n], sums_got.at[n], links.tok_peer(bit))
        advance(between.get(n, []))
        copy.wait_recv()
        sums[n + 1] = sums[n] + sums_got[n]
    n = len(tok_bits)
    links.local(sums.at[n, :, rest], rest_out)
    advance([s_small])
    for bit in links.row_bits + [links.half_bit]:
        copy = links.send(sums.at[n, :, everywhere], sums_got.at[n, :, everywhere], links.head_peer(bit))
        copy.wait_recv()
        sums[n + 1, :, everywhere] = sums[n, :, everywhere] + sums_got[n, :, everywhere]
        n += 1
    links.local(sums.at[n, :, everywhere], gain_out)

    s_small.finish()
    links.local(ks.at[0], os_ref)

    while row_copies:
        if not row_order:
            break
        take_rows(row_copies)
        row_copies = start_rows(send_rows())
    for _, _, copy in row_copies:
        copy.wait_recv()

    def block_rows(i, carry):
        at = rows_at(i, 32)
        wide = own_in[at, :].astype(F32)
        inv = lax.rsqrt(jnp.sum(wide * wide, axis=1, keepdims=True) / model + EPS)
        total = dnorm[mine, at, :]
        for _, place, _ in row_copies:
            total = total + got[place, at, :].astype(F32)
        scaled = total * gain
        inner = jnp.sum(scaled * wide, axis=1, keepdims=True) / model
        dnorm[mine, at, :] = cots[at, :].astype(F32) + inv * scaled - wide * (inv * inv * inv * inner)
        return carry

    lax.fori_loop(0, own_rows // 32, block_rows, 0)
    links.local(dnorm.at[mine], dblock_ref)
    for each in s_x:
        each.finish()
    for each in s_x:
        each.close()
    links.leave()


def reduce_sums(gx, gs, gl, dx, ds, dn, normed, block_in, wx, ws, cot, gain, per, bc):
    tok_size, head_size = lax.axis_size("tok"), lax.axis_size("head")
    sets = head_size // HALVES
    tok_bits = range(tok_size.bit_length() - 1)
    row_bits = range(sets.bit_length() - 1)
    own_rows, model = cot.shape
    share, width = gx.shape[1:]
    lanes = gs.shape[2]
    own_width = width // HALVES
    anywhere = pl.BlockSpec(memory_space=pl.ANY)
    inside = pl.BlockSpec(memory_space=pltpu.VMEM)
    keep, slots = tok_size // 2, tok_size + len(row_bits)
    stages = len(tok_bits) + len(row_bits) + 1
    away = max(sets - 1, 1)
    copies = 32 * len(tok_bits)
    outs = [
        shape((share, own_width), F32),
        shape((share, lanes), F32),
        shape((own_rows, model), F32),
        shape((8, model), F32),
        shape((8, own_width + bc.shape[1]), F32),
    ]
    return pl.pallas_call(
        functools.partial(reduce_kernel, tok_bits, row_bits),
        in_specs=[anywhere] * 11 + [inside] * 3,
        out_specs=[anywhere] * len(outs),
        out_shape=outs,
        scratch_shapes=[pltpu.VMEM((keep, share, width), BF16)]
        + [pltpu.VMEM((keep, share, lanes), F32)]
        + [pltpu.VMEM((slots, share, width), BF16)]
        + [pltpu.VMEM((slots, share, lanes), BF16)]
        + [pltpu.VMEM((share, own_width), F32)]
        + [pltpu.VMEM((slots, share, lanes), BF16)]
        + [
            pltpu.VMEM(dx.shape, BF16),
            pltpu.VMEM(ds.shape, BF16),
            pltpu.VMEM(wx.shape, BF16),
            pltpu.VMEM(ws.shape, BF16),
            pltpu.VMEM((own_rows * sets, model), BF16),
            pltpu.VMEM(cot.shape, BF16),
            pltpu.VMEM(cot.shape, BF16),
            pltpu.VMEM((sets, own_rows, model), F32),
            pltpu.VMEM((away, own_rows, model), BF16),
            pltpu.VMEM((away, own_rows, model), BF16),
            pltpu.VMEM((HALO, model), F32),
            pltpu.VMEM((HALO, model), F32),
            pltpu.VMEM((stages + 1, 8, model + own_width + bc.shape[1]), F32),
            pltpu.VMEM((stages, 8, model + own_width + bc.shape[1]), F32),
            pltpu.VMEM((8, own_width), F32),
            pltpu.VMEM((len(row_bits) + 1,) + bc.shape, F32),
            pltpu.VMEM((max(len(row_bits), 1),) + bc.shape, F32),
            pltpu.SemaphoreType.DMA((copies,)),
            pltpu.SemaphoreType.DMA((copies,)),
            pltpu.SemaphoreType.DMA((copies,)),
        ],
        name="reduce",
        compiler_params=pltpu.CompilerParams(
            collective_id=1, has_side_effects=True, vmem_limit_bytes=62 * 1024 * 1024
        ),
        cost_estimate=pl.CostEstimate(flops=int(12e9), bytes_accessed=int(60e6), transcendentals=0),
    )(gx, gs, gl, dx, ds, dn.reshape(sets, own_rows, model), normed, block_in, wx, ws, cot, gain, per, bc)


def per_device(
    block_in,
    norm_gain,
    w_zx,
    w_bc,
    w_dt,
    conv_x_w,
    conv_x_b,
    conv_bc_w,
    conv_bc_b,
    dt_bias,
    a_log,
    d_skip,
    gate_gain,
    w_out,
    cotangent,
):
    head_size = lax.axis_size("head")
    tok_size = lax.axis_size("tok")
    sets = head_size // HALVES
    row_bits = range(sets.bit_length() - 1)
    half_bit = sets.bit_length() - 1
    half = bit_of("head", half_bit)
    own_rows, model = block_in.shape
    share, _, own_width = w_zx.shape
    own_heads = w_dt.shape[1]
    tokens = own_rows * sets

    def all_rows(value):
        for bit in row_bits:
            value = grow(value, "head", bit, 0)
        return value

    def lane_pad(v):
        return jnp.pad(v, (0, LANES - v.shape[0]))

    heads_row = jnp.concatenate([lane_pad(dt_bias), lane_pad(a_log), lane_pad(d_skip)])
    own_par = jnp.concatenate(
        [
            conv_x_w,
            conv_x_b[None],
            gate_gain[None],
            jnp.repeat(d_skip, HEADDIM)[None],
            jnp.pad(heads_row, (0, own_width - heads_row.shape[0]))[None],
        ]
    )
    gain_share = norm_gain.shape[0]
    own_gain = jnp.broadcast_to(
        jnp.pad(norm_gain.astype(F32), (0, -gain_share % LANES))[None], (8, gain_share + -gain_share % LANES)
    )
    small = jnp.concatenate([w_bc, jnp.pad(w_dt, ((0, 0), (0, LANES - own_heads)))], axis=1)
    x_ext, s_ext, z, normed_ext, w_small, w_x, w_z, w_o, gain, par = gather_and_project(
        block_in, own_gain, own_par, small, w_zx[:, 1], w_zx[:, 0], w_out.T
    )
    later_cot, x_ext = lax.optimization_barrier((cotangent, x_ext))
    cot = all_rows(later_cot)
    gain = gain[0:1]
    normed = normed_ext[:tokens]
    slots_small, slots_x, gain_rows = w_small, w_x, gain
    w_z, w_o = w_z.reshape(model, w_z.shape[2]), w_o.reshape(model, w_o.shape[2])

    def of_heads(start):
        pieces = [
            par[CONV + 3, i * own_width + start : i * own_width + start + own_heads] for i in range(HALVES)
        ]
        return jnp.concatenate(pieces)

    rate = -jnp.exp(of_heads(LANES))
    hp = jnp.stack([lane_pad(of_heads(0)), lane_pad(rate)] + [jnp.zeros((LANES,), F32)] * 6)
    bcpar = jnp.concatenate([conv_bc_w, conv_bc_b[None], jnp.zeros((3, 2 * STATE), F32)])

    xs, u, cume, dte, bc, cumt, sloc, fin, sdec = mixer_forward_state(x_ext, s_ext, par, bcpar, hp, tokens)
    to_next = [(i, i + sets) for i in range(sets)]
    to_prev = [(i + sets, i) for i in range(sets)]
    sin = lax.ppermute(fin, "head", to_next)
    gyn = dot_nn(cot, w_o)
    y, stat = mixer_forward_main(xs, u, cume, cumt, bc, sloc, sin, sdec, z, gyn, par)
    stat = add_pairs(stat, "head", row_bits).T
    inv_gate = lax.rsqrt(stat[:, 0:1] / INNER + EPS)
    stat = jnp.concatenate(
        [inv_gate, inv_gate * inv_gate * inv_gate * stat[:, 1:2] / INNER, stat[:, 2:]], axis=1
    )
    yn, gy, dz, gloc, gin, gdec, acc_gate = mixer_backward_gate(y, z, gyn, xs, cume, bc, stat, par)
    gout = lax.ppermute(gin, "head", to_prev)

    def own_row_sum(value):
        for bit in list(row_bits)[::-1]:
            value = halve(value, "head", bit, 0)
        return value

    def slots_of(grad):
        return grad.astype(BF16).reshape(tok_size, share, grad.shape[1])

    branch = dot_nt(yn, w_o)
    block_out = block_in.astype(F32) + own_row_sum(branch)
    grad_o = slots_of(dot_tn(cot, yn))
    grad_z = slots_of(dot_tn(normed, dz))
    d_normed_z = dot_nt(dz, w_z)

    dx, ds, acc_x, acc_b, acc_h, d_w_z, d_w_o = mixer_backward_main(
        x_ext, s_ext, par, bcpar, hp, cume, dte, cumt, gy, sloc, sin, sdec, gloc, gout, gdec, grad_z, grad_o
    )
    grad_x = slots_of(dot_tn(normed_ext, dx))
    grad_small = dot_tn(normed_ext, ds).reshape(tok_size, share, ds.shape[1])

    per_channel = jnp.concatenate(
        [
            acc_x[: CONV + 1],
            acc_gate[0:1],
            jnp.concatenate(
                [
                    jnp.pad(
                        jnp.concatenate(
                            [
                                lane_pad(acc_h[0, i * own_heads : (i + 1) * own_heads]),
                                lane_pad(acc_h[1, i * own_heads : (i + 1) * own_heads]),
                                lane_pad(
                                    jnp.sum(
                                        acc_gate[1, i * own_width : (i + 1) * own_width].reshape(own_heads, HEADDIM),
                                        axis=1,
                                    )
                                ),
                            ]
                        ),
                        (0, own_width - 3 * LANES),
                    )
                    for i in range(HALVES)
                ]
            )[None],
            jnp.zeros((1, HALVES * own_width), F32),
        ]
    )

    d_w_x, d_small, d_block_in, gain_sums, own_sums = reduce_sums(
        grad_x, grad_small, grad_small.astype(BF16), dx, ds, d_normed_z, normed_ext, block_in, slots_x, slots_small, cotangent,
        gain_rows, per_channel, acc_b,
    )
    all_gain, bc_sums = gain_sums[0], own_sums[:, own_width:]
    own_sums = own_sums[:, :own_width]
    d_w_bc = d_small[:, : 2 * STATE]
    d_w_dt = jnp.where(
        half == 0,
        d_small[:, 2 * STATE : 2 * STATE + own_heads],
        d_small[:, 2 * STATE + own_heads : 2 * STATE + 2 * own_heads],
    )
    d_norm_gain = lax.dynamic_slice_in_dim(all_gain, lax.axis_index("head") * gain_share, gain_share, 0)
    return (
        block_out,
        d_block_in,
        d_norm_gain,
        jnp.stack([d_w_z, d_w_x], axis=1),
        d_w_bc,
        d_w_dt,
        own_sums[:CONV],
        own_sums[CONV],
        bc_sums[:CONV],
        bc_sums[CONV],
        own_sums[CONV + 2, :own_heads],
        own_sums[CONV + 2, LANES : LANES + own_heads],
        own_sums[CONV + 2, 2 * LANES : 2 * LANES + own_heads],
        own_sums[CONV + 1],
        d_w_o.T,
    )


def solution(mesh):
    placed = (
        P(("tok", "head"), None),
        P("head"),
        P("tok", None, "head"),
        P("tok", None),
        P("tok", "head"),
        P(None, "head"),
        P("head"),
        P(),
        P(),
        P("head"),
        P("head"),
        P("head"),
        P("head"),
        P("head", "tok"),
        P(("tok", "head"), None),
    )
    return jax.shard_map(
        per_device,
        mesh=mesh,
        in_specs=placed,
        out_specs=(
            P(("tok", "head"), None),
            P(("tok", "head"), None),
            P("head"),
            P("tok", None, "head"),
            P("tok", None),
            P("tok", "head"),
            P(None, "head"),
            P("head"),
            P(),
            P(),
            P("head"),
            P("head"),
            P("head"),
            P("head"),
            P("head", "tok"),
        ),
        check_vma=False,
    )
```

```python
import functools

import jax
import jax.numpy as jnp
from jax import lax
from jax.experimental import pallas as pl
from jax.experimental.pallas import tpu as pltpu
from jax.sharding import PartitionSpec as P

HEADDIM = 64
STATE = 128
CONV = 4
INNER = 3072
CHUNK = 256
HALVES = 2
LANES = 128
HALO = 16

EPS = 1e-05
LOG2E = 1.4426950408889634
HIGHEST = lax.Precision.HIGHEST
F32 = jnp.float32
BF16 = jnp.bfloat16


def dot_nn(a, b, precision=None):
    return lax.dot_general(
        a, b, (((1,), (0,)), ((), ())), preferred_element_type=F32, precision=precision
    )


def dot_nt(a, b, precision=None):
    return lax.dot_general(
        a, b, (((1,), (1,)), ((), ())), preferred_element_type=F32, precision=precision
    )


def dot_tn(a, b):
    return lax.dot_general(a, b, (((0,), (0,)), ((), ())), preferred_element_type=F32)


def dot_split(a, b):
    a_top, b_top = a.astype(BF16), b.astype(BF16)
    a_rest = (a - a_top.astype(F32)).astype(BF16)
    b_rest = (b - b_top.astype(F32)).astype(BF16)
    return dot_nn(a_top, b_top) + (dot_nn(a_rest, b_top) + dot_nn(a_top, b_rest))


def iota(shape, dim):
    return lax.broadcasted_iota(jnp.int32, shape, dim)


def sigmoid(v):
    return 0.5 + 0.5 * jnp.tanh(0.5 * v)


def softplus(v):
    return jnp.maximum(v, 0.0) + jnp.log1p(jnp.exp(-jnp.abs(v)))


def thirds(a):
    top = a.astype(BF16)
    rest = a - top.astype(F32)
    middle = rest.astype(BF16)
    return top, middle, (rest - middle.astype(F32)).astype(BF16)


def sums_of(zero_one, a):
    width = a.shape[1]
    wide = dot_nn(zero_one, jnp.concatenate(thirds(a), axis=1))
    return wide[:, 0:width] + wide[:, width : 2 * width] + wide[:, 2 * width :]


def bit_of(axis, bit):
    return (lax.axis_index(axis) // (1 << bit)) % 2


def swap(value, axis, bit):
    size = lax.axis_size(axis)
    return lax.ppermute(value, axis, [(i, i ^ (1 << bit)) for i in range(size)])


def grow(value, axis, bit, dim):
    other = swap(value, axis, bit)
    low = bit_of(axis, bit) == 0
    return jnp.where(
        low,
        jnp.concatenate([value, other], dim),
        jnp.concatenate([other, value], dim),
    )


def halve(value, axis, bit, dim):
    mine = bit_of(axis, bit)
    if dim < value.ndim - 1:
        half = value.shape[dim] // 2
        keep = lax.dynamic_slice_in_dim(value, mine * half, half, dim)
        send = lax.dynamic_slice_in_dim(value, (1 - mine) * half, half, dim)
    else:
        low, high = jnp.split(value, 2, axis=dim)
        keep = jnp.where(mine == 0, low, high)
        send = jnp.where(mine == 0, high, low)
    return keep.astype(F32) + swap(send.astype(BF16), axis, bit).astype(F32)


def add_pairs(value, axis, bits):
    for bit in bits:
        value = value + swap(value, axis, bit)
    return value


MESH = pl.DeviceIdType.MESH


def flip(index, bit):
    return index + (1 - 2 * ((index // (1 << bit)) % 2)) * (1 << bit)


def flip_all(index, offset):
    bit = 0
    while offset >> bit:
        if (offset >> bit) & 1:
            index = flip(index, bit)
        bit += 1
    return index


def now(value):
    return value() if callable(value) else value


class Remote:
    def __init__(self, links, k, src, dst, device):
        self.links, self.k, self.src, self.dst, self.device = links, k, src, dst, device

    def make(self):
        return pltpu.make_async_remote_copy(
            src_ref=now(self.src),
            dst_ref=now(self.dst),
            send_sem=self.links.send_sem.at[self.k],
            recv_sem=self.links.recv_sem.at[self.k],
            device_id=now(self.device),
            device_id_type=MESH,
        )

    def start(self):
        self.make().start()

    def wait_recv(self):
        self.make().wait_recv()

    def wait_send(self):
        self.make().wait_send()


class Local:
    def __init__(self, links, k, src, dst):
        self.links, self.k, self.src, self.dst = links, k, src, dst

    def make(self):
        return pltpu.make_async_copy(now(self.src), now(self.dst), self.links.local_sem.at[self.k])

    def start(self):
        self.make().start()

    def wait(self):
        self.make().wait()


class Links:
    def __init__(self, send_sem, recv_sem, local_sem, tok_bits, row_bits):
        self.send_sem, self.recv_sem, self.local_sem = send_sem, recv_sem, local_sem
        self.tok_bits, self.row_bits = list(tok_bits), list(row_bits)
        self.tok, self.head = lax.axis_index("tok"), lax.axis_index("head")
        self.sets = 1 << len(self.row_bits)
        self.half, self.mine = self.head // self.sets, self.head % self.sets
        self.half_bit = len(self.row_bits)
        self.sent, self.drained, self.n_local, self.open_local = [], [], 0, []

    def enter(self):
        partners = [self.tok_peer(b) for b in self.tok_bits]
        partners += [self.head_peer(b) for b in self.row_bits + [self.half_bit]]
        barrier = pltpu.get_barrier_semaphore()
        for partner in partners:
            pl.semaphore_signal(barrier, inc=1, device_id=partner(), device_id_type=MESH)
        pl.semaphore_wait(barrier, len(partners))

    def tok_peer(self, bit):
        return lambda: {"tok": flip(self.tok, bit)}

    def head_peer(self, bit):
        return lambda: {"head": flip(self.head, bit)}

    def plan_send(self, src, dst, device):
        copy = Remote(self, len(self.sent), src, dst, device)
        self.sent.append(copy)
        return copy

    def send(self, src, dst, device):
        copy = self.plan_send(src, dst, device)
        copy.start()
        return copy

    def plan_local(self, src, dst):
        self.n_local += 1
        return Local(self, self.n_local - 1, src, dst)

    def local(self, src, dst):
        copy = self.plan_local(src, dst)
        copy.start()
        self.open_local.append(copy)
        return copy

    def settle(self, copies):
        for copy in copies:
            if any(copy is other for other in self.open_local):
                self.open_local = [other for other in self.open_local if other is not copy]
                copy.wait()

    def drain(self, copy):
        copy.wait_recv()
        copy.wait_send()
        self.drained.append(copy)

    def leave(self):
        self.settle(list(self.open_local))
        for copy in self.sent:
            if not any(copy is other for other in self.drained):
                copy.wait_send()


def add_rows(dst, src, count):
    def body(i, carry):
        at = pl.ds(pl.multiple_of(i * 16, 16), 16)
        dst[at, :] = (dst[at, :].astype(F32) + src[at, :].astype(F32)).astype(BF16)
        return carry

    lax.fori_loop(0, count // 16, body, 0)


class Sum:
    def __init__(self, links, src, keep, recv, final, out, part, parts, order):
        self.links, self.src, self.keep, self.recv, self.final = links, src, keep, recv, final
        self.size = keep.shape[1] // parts
        self.start = part * self.size
        self.width = out.shape[1]
        self.whole = final is not None
        held = list(range(1 << len(links.tok_bits)))
        self.sends, self.adds, base = [], [], 0
        for number, bit in enumerate(order):
            stay = [o for o in held if not (o >> bit) & 1]
            if number == 0:
                place = {o: i for i, o in enumerate(stay)}
                self.loads = [links.plan_local(self.source(o), self.slot(place[o])) for o in stay]
            sends, adds = [], []
            for n, o in enumerate(stay):
                away = o ^ (1 << bit)
                src_ref = self.source(away) if number == 0 else self.slot(place[away])
                sends.append(links.plan_send(src_ref, self.landing(base + n), links.tok_peer(bit)))
                adds.append((place[o], base + n))
            base += len(stay)
            held = stay
            self.sends.append(sends)
            self.adds.append(adds)
        self.base = base
        if self.whole:
            self.tail = links.plan_send(
                lambda: self.keep.at[0, self.rows(), self.half_lanes(1 - self.links.half)],
                lambda: self.recv.at[base, self.rows(), pl.ds(0, self.width)],
                links.head_peer(links.half_bit),
            )
            self.store = links.plan_local(lambda: final.at[self.rows()], lambda: out.at[self.rows()])
        else:
            self.store = links.plan_local(self.slot(0), lambda: out.at[self.rows()])
        self.next = 0
        self.last = len(self.sends) + self.whole

    def rows(self):
        return pl.ds(self.start, self.size)

    def source(self, offset):
        return lambda: self.src.at[flip_all(self.links.tok, offset), self.rows()]

    def landing(self, i):
        return lambda: self.recv.at[i, self.rows()]

    def slot(self, i):
        return lambda: self.keep.at[i, self.rows()]

    def half_lanes(self, which):
        return pl.ds(pl.multiple_of(which * self.width, LANES), self.width)

    def step(self, k):
        if k == 0:
            for copy in self.sends[0] + self.loads:
                copy.start()
            return
        if k == self.last and self.whole:
            self.tail.wait_recv()
            lanes = self.half_lanes(self.links.half)

            def body(i, carry):
                at = pl.ds(pl.multiple_of(self.start + i * 16, 16), 16)
                self.final[at, :] = self.keep[0, at, lanes].astype(F32) + self.recv[
                    self.base, at, 0 : self.width
                ].astype(F32)
                return carry

            lax.fori_loop(0, self.size // 16, body, 0)
            self.store.start()
            return
        for copy in self.sends[k - 1]:
            copy.wait_recv()
        if k == 1:
            for copy in self.loads:
                copy.wait()
        for place, i in self.adds[k - 1]:
            add_rows(now(self.slot(place)), now(self.landing(i)), self.size)
        if k < len(self.sends):
            for copy in self.sends[k]:
                copy.start()
        elif self.whole:
            self.tail.start()
        else:
            self.store.start()

    def advance(self):
        if self.next < self.last:
            self.step(self.next)
            self.next += 1

    def finish(self):
        while self.next <= self.last:
            self.step(self.next)
            self.next += 1

    def close(self):
        self.store.wait()


class SmallSum(Sum):
    def __init__(self, links, src, src_low, keep, low, recv, order):
        self.links, self.keep, self.low, self.recv = links, keep, low, recv
        self.order = list(order)
        bit = self.order.pop(0)
        slots = range(1 << len(links.tok_bits))
        self.held = [o for o in slots if not (o >> bit) & 1]
        self.place = {o: i for i, o in enumerate(self.held)}
        self.base = len(self.held)
        self.n_low = 0
        self.into = [(i, i) for i in range(self.base)]
        self.flight = [
            links.send(src_low.at[flip_all(links.tok, o ^ (1 << bit))], recv.at[self.place[o]], links.tok_peer(bit))
            for o in self.held
        ]
        self.kept = [links.local(src.at[flip_all(links.tok, o)], keep.at[self.place[o]]) for o in self.held]
        self.done = False

    def post(self, place, lanes, device):
        n = self.n_low
        self.low[n, :, 0:lanes] = self.keep[place, :, 0:lanes].astype(BF16)
        self.n_low += 1
        src, dst = self.low.at[n, :, pl.ds(0, lanes)], self.recv.at[self.base, :, pl.ds(0, lanes)]
        self.flight.append(self.links.send(src, dst, device))
        self.base += 1
        return self.base - 1

    def take(self):
        for copy in self.flight:
            copy.wait_recv()
        self.links.settle(self.kept)
        for place, i in self.into:
            self.keep[place, :, 0 : self.lanes_in] = self.keep[place, :, 0 : self.lanes_in] + self.recv[
                i, :, 0 : self.lanes_in
            ].astype(F32)
        self.flight, self.into, self.kept = [], [], []

    lanes_in = 2 * STATE + LANES

    def advance(self):
        if self.done:
            return
        self.take()
        if not self.order:
            self.into = [(0, self.post(0, self.lanes_in, self.links.head_peer(self.links.half_bit)))]
            self.done = True
            return
        bit = self.order.pop(0)
        stay = [o for o in self.held if not (o >> bit) & 1]
        self.into = [
            (self.place[o], self.post(self.place[o ^ (1 << bit)], self.lanes_in, self.links.tok_peer(bit)))
            for o in stay
        ]
        self.held = stay

    def finish(self):
        while not self.done:
            self.advance()
        self.take()
        self.lanes_in = 2 * STATE
        for bit in self.links.row_bits:
            self.into = [(0, self.post(0, self.lanes_in, self.links.head_peer(bit)))]
            self.take()


def conv_rows(cur, tail, weight, bias):
    rows = cur.shape[0]
    ext = jnp.concatenate([tail, cur], axis=0)
    out = bias + weight[CONV - 1 : CONV] * cur
    for k in range(CONV - 1):
        start = 8 - (CONV - 1) + k
        out = out + weight[k : k + 1] * ext[start : start + rows]
    return out


def state_kernel(
    xm_ref, xt_ref, bm_ref, bt_ref, par_ref, bcpar_ref, hp_ref,
    xs_ref, u_ref, cume_ref, dte_ref, bc_ref, cumt_ref, sloc_ref, fin_ref, dec_ref,
    state, dsum, ue, spread,
):
    c = pl.program_id(0)
    q, width = xm_ref.shape

    @pl.when(c == 0)
    def _():
        state[...] = jnp.zeros_like(state)
        dsum[...] = jnp.zeros_like(dsum)
        row = iota((3 * LANES, width), 0) % LANES
        spread[...] = jnp.where(iota((3 * LANES, width), 1) // HEADDIM == row, 1.0, 0.0).astype(BF16)

    dt = softplus(bm_ref[:, 2 * STATE :] + hp_ref[0:1, :])
    tri = jnp.where(iota((q, q), 0) >= iota((q, q), 1), 1.0, 0.0).astype(BF16)
    cum = sums_of(tri, dt * (hp_ref[1:2, :] * LOG2E))
    cumt_ref[...] = cum.T[: cumt_ref.shape[0], :]
    cume_ref[...] = dot_nn(jnp.concatenate(thirds(cum), axis=1), spread[...])
    dte_ref[...] = dot_nn(jnp.concatenate(thirds(dt), axis=1), spread[...])
    end = cume_ref[q - 1 : q, :]

    bpre = conv_rows(
        bm_ref[:, : 2 * STATE], bt_ref[:, : 2 * STATE], bcpar_ref[0:CONV, :], bcpar_ref[CONV : CONV + 1, :]
    )
    bc_ref[...] = bpre * sigmoid(bpre)

    block = 2 * LANES

    def body(i, carry):
        sl = pl.ds(pl.multiple_of(i * block, block), block)
        pre = conv_rows(
            xm_ref[:, sl], xt_ref[:, sl], par_ref[0:CONV, sl], par_ref[CONV : CONV + 1, sl]
        )
        xs = pre * sigmoid(pre)
        u = xs * dte_ref[:, sl]
        xs_ref[:, sl] = xs
        u_ref[:, sl] = u.astype(BF16)
        cume = cume_ref[:, sl]
        ue[:, sl] = (u * jnp.exp2(cume[q - 1 : q, :] - cume)).astype(BF16)
        return carry

    lax.fori_loop(0, width // block, body, 0)
    sloc_ref[0] = state[...]
    dec_ref[0] = jnp.exp2(dsum[...])
    state[...] = jnp.exp2(end) * state[...] + dot_nn(bc_ref[:, :STATE].T.astype(BF16), ue[...])
    dsum[...] = dsum[...] + end
    fin_ref[...] = state[...].astype(BF16)


def main_kernel(
    xs_ref, u_ref, cume_ref, cumt_ref, bc_ref, sloc_ref, sin_ref, dec_ref, z_ref, gyn_ref, par_ref,
    y_ref, stat_ref,
    gram, ya, acc_sq, acc_in,
):
    q, width = xs_ref.shape
    bmat = bc_ref[:, :STATE].astype(BF16)
    cmat = bc_ref[:, STATE:].astype(BF16)
    lower = iota((q, q), 0) >= iota((q, q), 1)
    gram[...] = jnp.where(lower, dot_nt(cmat, bmat), 0.0)
    entering = sloc_ref[0] + dec_ref[0, 0:1, :] * sin_ref[...].astype(F32)
    ya[...] = dot_nn(cmat, entering.astype(BF16))
    acc_sq[...] = jnp.zeros_like(acc_sq)
    acc_in[...] = jnp.zeros_like(acc_in)
    first = iota((q, LANES), 1) < HEADDIM
    hq = q // 2

    def body(p, carry):
        sl = pl.ds(pl.multiple_of(p * LANES, LANES), LANES)
        cume = cume_ref[:, sl]
        u = u_ref[:, sl]
        y = jnp.exp2(cume) * ya[:, sl] + par_ref[CONV + 2 : CONV + 3, sl] * xs_ref[:, sl]
        low_y, high_y = y[:hq], y[hq:]
        for s in range(2):
            column = cume[:, HEADDIM * s : HEADDIM * s + 1]
            row = cumt_ref[pl.ds(2 * p + s, 1), :]
            mine = jnp.where(first == (s == 0), u, jnp.zeros_like(u))
            gap = column[:hq] - row[:, :hq]
            pairs = (gram[:hq, :hq] * jnp.exp2(jnp.minimum(gap, 0.0))).astype(BF16)
            low_y = low_y + dot_nn(pairs, mine[:hq])
            gap = column[hq:] - row
            pairs = (gram[hq:, :] * jnp.exp2(jnp.minimum(gap, 0.0))).astype(BF16)
            high_y = high_y + dot_nn(pairs, mine)
        y = jnp.concatenate([low_y, high_y], axis=0)
        y_ref[:, sl] = y
        z = z_ref[:, sl]
        gated = y * z * sigmoid(z)
        acc_sq[...] += gated * gated
        acc_in[...] += gated * gyn_ref[:, sl] * par_ref[CONV + 1 : CONV + 2, sl]
        return carry

    lax.fori_loop(0, width // LANES, body, 0)
    ones = jnp.ones((8, LANES), F32)
    sums_sq = dot_nt(ones, acc_sq[...], HIGHEST)
    sums_in = dot_nt(ones, acc_in[...], HIGHEST)
    stat_ref[...] = jnp.where(iota(sums_sq.shape, 0) == 0, sums_sq, sums_in)


def gate_kernel(
    y_ref, z_ref, gyn_ref, cume_ref, bc_ref, stat_ref, par_ref,
    yn_ref, gy_ref, dz_ref, gloc_ref, gin_ref, dec_ref, acc_ref,
    adj, dsum, ge,
):
    q, width = y_ref.shape

    @pl.when(pl.program_id(0) == 0)
    def _():
        adj[...] = jnp.zeros_like(adj)
        dsum[...] = jnp.zeros_like(dsum)
        acc_ref[...] = jnp.zeros_like(acc_ref)

    end = cume_ref[q - 1 : q, :]
    inv = jnp.broadcast_to(stat_ref[:, 0:1], (q, LANES))
    back = jnp.broadcast_to(stat_ref[:, 1:2], (q, LANES))

    def body(p, carry):
        sl = pl.ds(pl.multiple_of(p * LANES, LANES), LANES)
        y, z, gyn = y_ref[:, sl], z_ref[:, sl], gyn_ref[:, sl]
        sig = sigmoid(z)
        sil = z * sig
        gated = y * sil
        gain = par_ref[CONV + 1 : CONV + 2, sl]
        unit = gated * inv
        yn_ref[:, sl] = (unit * gain).astype(BF16)
        d_gated = inv * gyn * gain - gated * back
        gy = d_gated * sil
        gy_ref[:, sl] = gy.astype(BF16)
        dz_ref[:, sl] = (d_gated * y * (sig * (1.0 + z * (1.0 - sig)))).astype(BF16)
        ge[:, sl] = (gy * jnp.exp2(cume_ref[:, sl])).astype(BF16)
        acc_ref[0:1, sl] += jnp.sum(gyn * unit, axis=0, keepdims=True)
        return carry

    lax.fori_loop(0, width // LANES, body, 0)
    gloc_ref[0] = adj[...]
    dec_ref[0] = jnp.exp2(dsum[...])
    adj[...] = jnp.exp2(end) * adj[...] + dot_nn(bc_ref[:, STATE:].T.astype(BF16), ge[...])
    dsum[...] = dsum[...] + end
    gin_ref[...] = adj[...].astype(BF16)


def back_kernel(
    tok_bits, row_bits,
    xm_ref, xt_ref, bm_ref, bt_ref, par_ref, bcpar_ref, hp_ref,
    cume_ref, dte_ref, cumt_ref, gy_ref, sloc_ref, sin_ref, sdec_ref, gloc_ref, gout_ref, gdec_ref,
    gz_ref, go_ref,
    dx_ref, ds_ref, accx_ref, accb_ref, acch_ref, oz_ref, oo_ref,
    xs, u, dsil, ue, ge, dus, ya, qx, qb, gram, dgram, da, acc_x, acc_w, acc_g, acc_k, kept,
    kz, ko, rz, ro, fz, send_sem, recv_sem, local_sem,
):
    step = pl.program_id(0)
    q, width = xm_ref.shape
    tokens = dx_ref.shape[0] - HALO
    steps = tokens // q
    links = Links(send_sem, recv_sem, local_sem, tok_bits, row_bits)
    up = [0] + links.tok_bits[1:]
    down = [0] + links.tok_bits[1:][::-1]
    groups = [
        [Sum(links, gz_ref, kz, rz, fz, oz_ref, p, 2, (down, up)[p]) for p in range(2)],
        [Sum(links, go_ref, ko, ro, None, oo_ref, p, 2, (down, up)[p]) for p in range(2)],
    ]
    plans = [[(0, 0), (0, 2), (1, 2), (2, 3)], [(0, 0), (0, 3), (2, 2)]]

    def go_on(point):
        for when in range(steps):

            @pl.when(step == when)
            def _():
                if (when, point) == (0, 0):
                    links.enter()
                for group, plan in zip(groups, plans):
                    for k, (number, place) in enumerate(plan):
                        if (min(number, steps - 1), place) == (when, point):
                            for each in group:
                                each.step(k)
                if (when, point) == (steps - 1, 3):
                    for group, plan in list(zip(groups, plans))[::-1]:
                        for k in range(len(plan), group[0].last + 1):
                            for each in group:
                                each.step(k)
                    for group in groups:
                        for each in group:
                            each.close()
                    links.leave()

    go_on(0)
    c = tokens // q - 1 - step
    block = 2 * LANES

    @pl.when(step == 0)
    def _():
        accx_ref[...] = jnp.zeros_like(accx_ref)
        accb_ref[...] = jnp.zeros_like(accb_ref)
        acch_ref[...] = jnp.zeros_like(acch_ref)
        qx[q:, :] = jnp.zeros((8, width), F32)
        qb[q:, :] = jnp.zeros((8, 2 * STATE), F32)
        da[...] = jnp.zeros_like(da)
        ds_ref[...] = jnp.zeros_like(ds_ref)

    bpre = conv_rows(
        bm_ref[:, : 2 * STATE], bt_ref[:, : 2 * STATE], bcpar_ref[0:CONV, :], bcpar_ref[CONV : CONV + 1, :]
    )
    bsig = sigmoid(bpre)
    bc = bpre * bsig
    qb[0:q, :] = bsig * (1.0 + bpre * (1.0 - bsig))
    bmat, cmat = bc[:, :STATE].astype(BF16), bc[:, STATE:].astype(BF16)

    def conv_body(i, carry):
        sl = pl.ds(pl.multiple_of(i * block, block), block)
        pre = conv_rows(
            xm_ref[:, sl], xt_ref[:, sl], par_ref[0:CONV, sl], par_ref[CONV : CONV + 1, sl]
        )
        sig = sigmoid(pre)
        x = pre * sig
        xs[:, sl] = x
        dsil[:, sl] = sig * (1.0 + pre * (1.0 - sig))
        uu = x * dte_ref[:, sl]
        u[:, sl] = uu.astype(BF16)
        cume = cume_ref[:, sl]
        ue[:, sl] = (uu * jnp.exp2(cume[q - 1 : q, :] - cume)).astype(BF16)
        gy = gy_ref[:, sl].astype(F32)
        ge[:, sl] = (gy * jnp.exp2(cume)).astype(BF16)
        accx_ref[CONV + 1 : CONV + 2, sl] += jnp.sum(gy * x, axis=0, keepdims=True)
        return carry

    lax.fori_loop(0, width // block, conv_body, 0)
    go_on(1)

    last = cume_ref[q - 1 : q, :]
    adj = gloc_ref[0] + gdec_ref[0, 0:1, :] * gout_ref[...].astype(F32)
    entering = sloc_ref[0] + sdec_ref[0, 0:1, :] * sin_ref[...].astype(F32)
    kept_parts = thirds(jnp.exp2(last) * jnp.sum(adj * entering, axis=0, keepdims=True))
    kept[...] = jnp.concatenate(list(kept_parts) + [jnp.zeros((13, width), BF16)], axis=0)
    adj_low, ent_low = adj.astype(BF16), entering.astype(BF16)
    dus[...] = dot_nn(bmat, adj_low)
    ya[...] = dot_nn(cmat, ent_low)
    db = dot_nt(ue[...], adj_low)
    dc = dot_nt(ge[...], ent_low)
    upper = iota((q, q), 1) >= iota((q, q), 0)
    gram[...] = jnp.where(upper, dot_nt(bmat, cmat), 0.0)
    dgram[...] = jnp.zeros_like(dgram)
    acc_x[...] = jnp.zeros_like(acc_x)
    acc_k[...] = jnp.zeros_like(acc_k)
    acc_w[...] = jnp.zeros_like(acc_w)
    acc_g[...] = jnp.zeros_like(acc_g)
    later = jnp.where(iota((q, q), 0) >= iota((q, q), 1), 1.0, 0.0).astype(BF16)
    first = iota((q, LANES), 1) < HEADDIM
    hq = q // 2
    before_top = iota((hq, q), 0) < iota((hq, q), 1)
    before_low = iota((hq, hq), 0) < iota((hq, hq), 1)

    def pair_body(p, carry):
        sl = pl.ds(pl.multiple_of(p * LANES, LANES), LANES)
        cume = cume_ref[:, sl]
        ul = u[:, sl]
        gl = gy_ref[:, sl]
        gy = gl.astype(F32)
        low_du = jnp.zeros((hq, LANES), F32)
        high_du = jnp.zeros((hq, LANES), F32)
        for s in range(2):
            mine = first == (s == 0)
            row = pl.ds(2 * p + s, 1)
            column = cume[:, HEADDIM * s : HEADDIM * s + 1]
            later_row = cumt_ref[row, :]
            um = jnp.where(mine, ul, jnp.zeros_like(ul))
            gm = jnp.where(mine, gl, jnp.zeros_like(gl))
            decay = jnp.exp2(jnp.minimum(later_row - column[:hq], 0.0))
            pairs = gram[:hq, :] * decay
            dpairs = dot_nt(um[:hq], gl)
            dgram[:hq, :] += dpairs * decay
            through = dot_nn((dpairs * pairs).astype(BF16), later)
            total = jnp.sum(jnp.where(before_top, through, 0.0), axis=0, keepdims=True)
            low_du = low_du + dot_nn(pairs.astype(BF16), gm)
            decay = jnp.exp2(jnp.minimum(later_row[:, hq:] - column[hq:], 0.0))
            pairs = gram[hq:, hq:] * decay
            dpairs = dot_nt(um[hq:], gl[hq:])
            dgram[hq:, hq:] += dpairs * decay
            through = dot_nn((dpairs * pairs).astype(BF16), later[hq:, hq:])
            more = jnp.sum(jnp.where(before_low, through, 0.0), axis=0, keepdims=True)
            da[row, :] = total + jnp.concatenate([jnp.zeros((1, hq), F32), more], axis=1)
            high_du = high_du + dot_nn(pairs.astype(BF16), gm[hq:])
        du = jnp.concatenate([low_du, high_du], axis=0)
        x = xs[:, sl]
        wide = dus[:, sl] * jnp.exp2(cume[q - 1 : q, :] - cume)
        du = du + wide
        to_head = (iota((LANES, LANES), 1) == 2 * p + iota((LANES, LANES), 0) // HEADDIM).astype(BF16)
        dte = dte_ref[:, sl]
        acc_x[...] += dot_nn((x * du).astype(BF16), to_head)
        acc_w[...] += dot_nn((x * dte * wide).astype(BF16), to_head)
        acc_g[...] += dot_nn((gy * jnp.exp2(cume) * ya[:, sl]).astype(BF16), to_head)
        acc_k[...] += dot_nn(kept[:, sl], to_head)
        qx[0:q, sl] = (dte * du + par_ref[CONV + 2 : CONV + 3, sl] * gy) * dsil[:, sl]
        return carry

    lax.fori_loop(0, width // LANES, pair_body, 0)
    go_on(2)

    def unconv_body(i, carry):
        sl = pl.ds(pl.multiple_of(i * block, block), block)
        weight = par_ref[0:CONV, sl]
        ext = qx[:, sl]
        cur = ext[0:q]
        dpre = weight[CONV - 1 : CONV] * cur
        for k in range(CONV - 1):
            dpre = dpre + weight[k : k + 1] * ext[CONV - 1 - k : CONV - 1 - k + q]
        dx_ref[pl.ds(pl.multiple_of(c * q, q), q), sl] = dpre.astype(BF16)
        past = jnp.concatenate([xt_ref[:, sl], xm_ref[:, sl]], axis=0)
        for k in range(CONV):
            start = 8 - (CONV - 1) + k
            accx_ref[k : k + 1, sl] += jnp.sum(cur * past[start : start + q], axis=0, keepdims=True)
        accx_ref[CONV : CONV + 1, sl] += jnp.sum(cur, axis=0, keepdims=True)
        head_rows = jnp.concatenate([jnp.zeros((HALO, block), F32), cur[0:8]], axis=0)
        before = jnp.zeros((HALO, block), F32)
        for k in range(CONV - 1):
            before = before + weight[k : k + 1] * head_rows[CONV - 1 - k : CONV - 1 - k + HALO]
        dx_ref[pl.ds(tokens, HALO), sl] = before.astype(BF16)
        qx[q:, sl] = cur[0:8]
        return carry

    lax.fori_loop(0, width // block, unconv_body, 0)

    dg = jnp.where(upper, dgram[...], 0.0)
    db = db + dot_split(dg, bc[:, STATE:])
    dc = dc + dot_split(dg.T, bc[:, :STATE])
    qb[0:q, 0:STATE] = qb[0:q, 0:STATE] * db
    qb[0:q, STATE:] = qb[0:q, STATE:] * dc
    weight = bcpar_ref[0:CONV, :]
    ext = qb[...]
    cur = ext[0:q]
    dpre = weight[CONV - 1 : CONV] * cur
    for k in range(CONV - 1):
        dpre = dpre + weight[k : k + 1] * ext[CONV - 1 - k : CONV - 1 - k + q]
    ds_ref[pl.ds(pl.multiple_of(c * q, q), q), 0 : 2 * STATE] = dpre.astype(BF16)
    past = jnp.concatenate([bt_ref[:, 0 : 2 * STATE], bm_ref[:, 0 : 2 * STATE]], axis=0)
    for k in range(CONV):
        start = 8 - (CONV - 1) + k
        accb_ref[k : k + 1, :] += jnp.sum(cur * past[start : start + q], axis=0, keepdims=True)
    accb_ref[CONV : CONV + 1, :] += jnp.sum(cur, axis=0, keepdims=True)
    head_rows = jnp.concatenate([jnp.zeros((HALO, 2 * STATE), F32), cur[0:8]], axis=0)
    before = jnp.zeros((HALO, 2 * STATE), F32)
    for k in range(CONV - 1):
        before = before + weight[k : k + 1] * head_rows[CONV - 1 - k : CONV - 1 - k + HALO]
    ds_ref[pl.ds(tokens, HALO), 0 : 2 * STATE] = before.astype(BF16)
    qb[q:, :] = cur[0:8]

    raw = bm_ref[:, 2 * STATE :] + hp_ref[0:1, :]
    dt = softplus(raw)
    rate = hp_ref[1:2, :]
    from_here = jnp.where(iota((q, q), 1) >= iota((q, q), 0), 1.0, 0.0).astype(BF16)
    up_to_here = jnp.where(iota((q, q), 1) < iota((q, q), 0), 1.0, 0.0).astype(BF16)
    total = (
        da[...].T
        + sums_of(from_here, acc_g[...])
        + sums_of(up_to_here, acc_w[...])
        + jnp.sum(acc_k[0:3, :], axis=0, keepdims=True)
    )
    d_raw = (acc_x[...] + rate * total) * sigmoid(raw)
    ds_ref[pl.ds(pl.multiple_of(c * q, q), q), 2 * STATE :] = d_raw.astype(BF16)
    acch_ref[0:1, :] += jnp.sum(d_raw, axis=0, keepdims=True)
    acch_ref[1:2, :] += rate * jnp.sum(dt * total, axis=0, keepdims=True)
    go_on(3)


def shape(dims, dtype):
    return jax.ShapeDtypeStruct(dims, dtype)


def whole(dims):
    return pl.BlockSpec(dims, lambda c: (0,) * len(dims))


def run(kernel, name, grid, in_specs, out_specs, out_shape, scratch, args, flops, collective_id=None):
    return pl.pallas_call(
        kernel,
        grid=(grid,),
        in_specs=in_specs,
        out_specs=out_specs,
        out_shape=out_shape,
        scratch_shapes=scratch,
        name=name,
        compiler_params=pltpu.CompilerParams(
            dimension_semantics=("arbitrary",),
            vmem_limit_bytes=62 * 1024 * 1024,
            collective_id=collective_id,
            has_side_effects=collective_id is not None,
        ),
        cost_estimate=pl.CostEstimate(
            flops=flops, bytes_accessed=sum(a.size * a.dtype.itemsize for a in args), transcendentals=0
        ),
    )(*args)


def mixer_forward_state(x_ext, s_ext, par, bcpar, hp, tokens):
    width = x_ext.shape[1]
    small = s_ext.shape[1]
    n = tokens // CHUNK
    q = CHUNK
    tail = q // 8
    last = (tokens + HALO) // 8 - 1
    tail_map = lambda c: (jnp.where(c == 0, last, c * tail - 1), 0)
    heads_pad = -(-(width // HEADDIM) // 8) * 8
    return run(
        state_kernel,
        "scan_states",
        n,
        [
            pl.BlockSpec((q, width), lambda c: (c, 0)),
            pl.BlockSpec((8, width), tail_map),
            pl.BlockSpec((q, small), lambda c: (c, 0)),
            pl.BlockSpec((8, small), tail_map),
            whole(par.shape),
            whole(bcpar.shape),
            whole(hp.shape),
        ],
        [
            pl.BlockSpec((q, width), lambda c: (c, 0)),
            pl.BlockSpec((q, width), lambda c: (c, 0)),
            pl.BlockSpec((q, width), lambda c: (c, 0)),
            pl.BlockSpec((q, width), lambda c: (c, 0)),
            pl.BlockSpec((q, 2 * STATE), lambda c: (c, 0)),
            pl.BlockSpec((heads_pad, q), lambda c: (0, c)),
            pl.BlockSpec((1, STATE, width), lambda c: (c, 0, 0)),
            whole((STATE, width)),
            pl.BlockSpec((1, 1, width), lambda c: (c, 0, 0)),
        ],
        [
            shape((tokens, width), F32),
            shape((tokens, width), BF16),
            shape((tokens, width), F32),
            shape((tokens, width), F32),
            shape((tokens, 2 * STATE), F32),
            shape((heads_pad, tokens), F32),
            shape((n, STATE, width), F32),
            shape((STATE, width), BF16),
            shape((n, 1, width), F32),
        ],
        [
            pltpu.VMEM((STATE, width), F32),
            pltpu.VMEM((1, width), F32),
            pltpu.VMEM((q, width), BF16),
            pltpu.VMEM((3 * LANES, width), BF16),
        ],
        (x_ext, x_ext, s_ext, s_ext, par, bcpar, hp),
        int(3e9),
    )


def mixer_forward_main(xs, u, cume, cumt, bc, sloc, sin, dec, z, gyn, par):
    tokens, width = xs.shape
    q = CHUNK
    n = tokens // q
    rows = pl.BlockSpec((q, width), lambda c: (c, 0))
    return run(
        main_kernel,
        "scan_outputs",
        n,
        [
            rows,
            rows,
            rows,
            pl.BlockSpec((cumt.shape[0], q), lambda c: (0, c)),
            pl.BlockSpec((q, 2 * STATE), lambda c: (c, 0)),
            pl.BlockSpec((1, STATE, width), lambda c: (c, 0, 0)),
            whole(sin.shape),
            pl.BlockSpec((1, 1, width), lambda c: (c, 0, 0)),
            rows,
            rows,
            whole(par.shape),
        ],
        [rows, pl.BlockSpec((8, q), lambda c: (0, c))],
        [shape((tokens, width), F32), shape((8, tokens), F32)],
        [
            pltpu.VMEM((q, q), F32),
            pltpu.VMEM((q, width), F32),
            pltpu.VMEM((q, LANES), F32),
            pltpu.VMEM((q, LANES), F32),
        ],
        (xs, u, cume, cumt, bc, sloc, sin, dec, z, gyn, par),
        int(10e9),
    )


def mixer_backward_gate(y, z, gyn, cume, bc, stat, par):
    tokens, width = y.shape
    q = CHUNK
    n = tokens // q
    rows = pl.BlockSpec((q, width), lambda c: (n - 1 - c, 0))
    return run(
        gate_kernel,
        "gate_back",
        n,
        [
            rows,
            rows,
            rows,
            rows,
            pl.BlockSpec((q, 2 * STATE), lambda c: (n - 1 - c, 0)),
            pl.BlockSpec((q, 8), lambda c: (n - 1 - c, 0)),
            whole(par.shape),
        ],
        [
            rows,
            rows,
            rows,
            pl.BlockSpec((1, STATE, width), lambda c: (n - 1 - c, 0, 0)),
            whole((STATE, width)),
            pl.BlockSpec((1, 1, width), lambda c: (n - 1 - c, 0, 0)),
            whole((8, width)),
        ],
        [
            shape((tokens, width), BF16),
            shape((tokens, width), BF16),
            shape((tokens, width), BF16),
            shape((n, STATE, width), F32),
            shape((STATE, width), BF16),
            shape((n, 1, width), F32),
            shape((8, width), F32),
        ],
        [
            pltpu.VMEM((STATE, width), F32),
            pltpu.VMEM((1, width), F32),
            pltpu.VMEM((q, width), BF16),
        ],
        (y, z, gyn, cume, bc, stat, par),
        int(5e9),
    )


def mixer_backward_main(
    x_ext, s_ext, par, bcpar, hp, cume, dte, cumt, gy, sloc, sin, sdec, gloc, gout, gdec, gz, go
):
    tok_size, head_size = lax.axis_size("tok"), lax.axis_size("head")
    tok_bits = range(tok_size.bit_length() - 1)
    row_bits = range((head_size // HALVES).bit_length() - 1)
    share = gz.shape[1]
    copies = 16 * len(tok_bits)
    tokens, width = cume.shape
    small = s_ext.shape[1]
    q = CHUNK
    n = tokens // q
    tail = q // 8
    last = (tokens + HALO) // 8 - 1
    rows = pl.BlockSpec((q, width), lambda c: (n - 1 - c, 0))
    tail_map = lambda c: (jnp.where(c == n - 1, last, (n - 1 - c) * tail - 1), 0)
    states = pl.BlockSpec((1, STATE, width), lambda c: (n - 1 - c, 0, 0))
    decays = pl.BlockSpec((1, 1, width), lambda c: (n - 1 - c, 0, 0))
    anywhere = pl.BlockSpec(memory_space=pl.ANY)
    return run(
        functools.partial(back_kernel, tok_bits, row_bits),
        "scan_back",
        n,
        [
            rows,
            pl.BlockSpec((8, width), tail_map),
            pl.BlockSpec((q, small), lambda c: (n - 1 - c, 0)),
            pl.BlockSpec((8, small), tail_map),
            whole(par.shape),
            whole(bcpar.shape),
            whole(hp.shape),
            rows,
            rows,
            pl.BlockSpec((cumt.shape[0], q), lambda c: (0, n - 1 - c)),
            rows,
            states,
            whole(sin.shape),
            decays,
            states,
            whole(gout.shape),
            decays,
            anywhere,
            anywhere,
        ],
        [
            whole((tokens + HALO, width)),
            whole((tokens + HALO, small)),
            whole((8, width)),
            whole((8, 2 * STATE)),
            whole((8, LANES)),
            anywhere,
            anywhere,
        ],
        [
            shape((tokens + HALO, width), BF16),
            shape((tokens + HALO, small), BF16),
            shape((8, width), F32),
            shape((8, 2 * STATE), F32),
            shape((8, LANES), F32),
            shape((share, width // HALVES), F32),
            shape((share, width), BF16),
        ],
        [
            pltpu.VMEM((q, width), F32),
            pltpu.VMEM((q, width), BF16),
            pltpu.VMEM((q, width), F32),
            pltpu.VMEM((q, width), BF16),
            pltpu.VMEM((q, width), BF16),
            pltpu.VMEM((q, width), F32),
            pltpu.VMEM((q, width), F32),
            pltpu.VMEM((q + 8, width), F32),
            pltpu.VMEM((q + 8, 2 * STATE), F32),
            pltpu.VMEM((q, q), F32),
            pltpu.VMEM((q, q), F32),
            pltpu.VMEM((LANES, q), F32),
            pltpu.VMEM((q, LANES), F32),
            pltpu.VMEM((q, LANES), F32),
            pltpu.VMEM((q, LANES), F32),
            pltpu.VMEM((16, LANES), F32),
            pltpu.VMEM((16, width), BF16),
        ]
        + [pltpu.VMEM((tok_size // 2, share, width), BF16)] * 2
        + [pltpu.VMEM((tok_size, share, width), BF16)] * 2
        + [pltpu.VMEM((share, width // HALVES), F32)]
        + [pltpu.SemaphoreType.DMA((copies,))] * 3,
        (x_ext, x_ext, s_ext, s_ext, par, bcpar, hp, cume, dte, cumt, gy, sloc, sin, sdec, gloc, gout, gdec, gz, go),
        int(30e9),
        collective_id=2,
    )


def gather_kernel(
    tok_bits, row_bits, half_bit,
    in_ref, gain_ref, par_ref, small_ref, wx_ref, wz_ref, wo_ref,
    x_out, s_out, normed_out, ws_out, wx_out, wz_out, wo_out, gains_out, pars_out,
    ws, wx, wz, wo, joined, rows, halo, normed, gains, gain_all, pars, stage,
    send_sem, recv_sem, local_sem, stage_sem,
):
    tok, head = lax.axis_index("tok"), lax.axis_index("head")
    sets = 1 << len(row_bits)
    heads = 2 * sets
    half, mine = head // sets, head % sets
    own_rows, model = in_ref.shape
    share, own_width = wx_ref.shape
    tokens = own_rows * sets
    partners = [{"tok": flip(tok, b)} for b in tok_bits]
    partners += [{"head": flip_all(head, p)} for p in range(1, heads)]

    barrier = pltpu.get_barrier_semaphore()
    for partner in partners:
        pl.semaphore_signal(barrier, inc=1, device_id=partner, device_id_type=MESH)
    pl.semaphore_wait(barrier, len(partners))

    sent, stored, open_local = [], [], []

    def send(src, dst, device):
        k = len(sent)
        copy = pltpu.make_async_remote_copy(
            src_ref=src, dst_ref=dst, send_sem=send_sem.at[k], recv_sem=recv_sem.at[k],
            device_id=device, device_id_type=MESH,
        )
        copy.start()
        sent.append(copy)
        return copy

    def local(src, dst):
        copy = pltpu.make_async_copy(src, dst, local_sem.at[len(stored)])
        copy.start()
        stored.append(copy)
        open_local.append(copy)
        return copy

    def settle(copy):
        if any(copy is other for other in open_local):
            open_local[:] = [other for other in open_local if other is not copy]
            copy.wait()

    def arrive(copies):
        for copy in copies:
            copy.wait_recv()

    other_half = {"head": flip(head, half_bit)}
    lanes = pl.ds(pl.multiple_of(half * own_width, LANES), own_width)

    class Own:
        def __init__(self, src, dst, rows_at, src_lanes, dst_lanes, order):
            self.rows, self.lanes = rows_at, dst_lanes
            self.dst, self.order = dst, list(order)
            slot = dst.at[tok, self.rows, self.lanes]
            bit = self.order.pop(0)
            self.flight = [send(src.at[self.rows, src_lanes], slot, {"tok": flip(tok, bit)})]
            self.kept = local(src.at[self.rows, src_lanes], slot)
            self.held = [0, 1 << bit]

        def advance(self):
            arrive(self.flight)
            settle(self.kept)
            self.flight = []
            if self.order:
                bit = self.order.pop(0)
                for offset in self.held:
                    slot = self.dst.at[flip_all(tok, offset), self.rows, self.lanes]
                    self.flight.append(send(slot, slot, {"tok": flip(tok, bit)}))
                self.held = self.held + [offset ^ (1 << bit) for offset in self.held]

        def finish(self):
            while self.flight:
                self.advance()

    class Other(Own):
        def __init__(self, src, dst, rows_at, src_lanes, sent_lanes, dst_lanes, order):
            self.rows, self.lanes = rows_at, dst_lanes
            self.dst, self.order, self.held, self.kept = dst, list(order), [0], None
            self.flight = [send(src.at[self.rows, src_lanes], dst.at[tok, self.rows, sent_lanes], other_half)]

    class Rows:
        def __init__(self, src, dst):
            self.dst, self.order, self.held = dst, list(row_bits), [0]
            self.src = src
            self.kept = local(src, dst.at[mine])
            self.flight = []
            if self.order:
                bit = self.order.pop(0)
                self.flight.append(send(src, dst.at[mine], {"head": flip(head, bit)}))
                self.held = [0, 1 << bit]

        def advance(self):
            arrive(self.flight)
            settle(self.kept)
            self.flight = []
            if self.order:
                bit = self.order.pop(0)
                for offset in self.held:
                    slot = self.dst.at[flip_all(mine, offset)]
                    self.flight.append(send(slot, slot, {"head": flip(head, bit)}))
                self.held = self.held + [offset ^ (1 << bit) for offset in self.held]

        def finish(self):
            settle(self.kept)
            while self.flight:
                self.advance()

    up = list(tok_bits)[1:] + [0]
    down = list(tok_bits)[1:][::-1] + [0]
    gain_copies = [
        send(gain_ref, gains.at[head], {"head": flip_all(head, p)}) for p in range(1, heads)
    ]
    gain_kept = local(gain_ref, gains.at[head])
    par_slot = pars.at[:, lanes]
    par_copy = send(par_ref, par_slot, other_half)
    par_kept = local(par_ref, par_slot)
    own_all = pl.ds(0, own_width)
    there = pl.ds(pl.multiple_of((1 - half) * own_width, LANES), own_width)
    parts = [pl.ds(n * (share // 2), share // 2) for n in range(2)]

    def own_pieces(src, dst):
        return [Own(src, dst, parts[n], own_all, lanes, (up, down)[n]) for n in range(2)]

    def other_pieces(src, dst):
        return [Other(src, dst, parts[n], own_all, lanes, there, (up, down)[n]) for n in range(2)]

    def step_lanes(which):
        return pl.ds(pl.multiple_of(2 * STATE + which * LANES, LANES), LANES)

    every, bc_lanes, own_steps = pl.ds(0, share), pl.ds(0, 2 * STATE), pl.ds(2 * STATE, LANES)
    x_other = other_pieces(wx_ref, wx)
    x_other.append(Other(small_ref, ws, every, own_steps, step_lanes(half), step_lanes(1 - half), down))
    x_own = own_pieces(wx_ref, wx)
    x_own.append(Own(small_ref, ws, every, bc_lanes, bc_lanes, up))
    x_own.append(Own(small_ref, ws, every, own_steps, step_lanes(half), down))
    z_own = own_pieces(wz_ref, wz)
    z_other = other_pieces(wz_ref, wz)
    r_in = Rows(in_ref, rows)
    o_own = own_pieces(wo_ref, wo)
    o_other = other_pieces(wo_ref, wo)

    def advance(pieces):
        for piece in pieces:
            piece.advance()

    def normalise(src, start, count, scale):
        def body(i, carry):
            at = pl.ds(pl.multiple_of(start + i * 16, 16), 16)
            wide = src[pl.ds(pl.multiple_of(i * 16, 16), 16), :].astype(F32)
            inv = lax.rsqrt(jnp.sum(wide * wide, axis=1, keepdims=True) / model + EPS)
            normed[at, :] = (wide * inv * scale).astype(BF16)
            return carry

        lax.fori_loop(0, count // 16, body, 0, unroll=4 if count >= 64 else 1)

    def project(lhs, count, weight, out, width):
        tile = 256 if width % 256 == 0 else 3 * LANES
        steps = width // tile

        def out_copy(i):
            at = pl.ds(pl.multiple_of(i * tile, tile), tile)
            return pltpu.make_async_copy(
                stage.at[i % 2, pl.ds(0, count), pl.ds(0, tile)], out.at[:, at], stage_sem.at[i % 2]
            )

        def body(i, carry):
            @pl.when(i >= 2)
            def _():
                out_copy(i - 2).wait()

            at = pl.ds(pl.multiple_of(i * tile, tile), tile)
            block = weight[:, :, at].reshape(model, tile)
            stage[i % 2, 0:count, 0:tile] = dot_nn(lhs[...].reshape(count, model), block)
            out_copy(i).start()
            return carry

        lax.fori_loop(0, steps, body, 0)
        for i in range(max(steps - 2, 0), steps):
            out_copy(i).wait()

    def finish(pieces):
        for piece in pieces:
            piece.finish()

    def join_heads():
        def body(i, carry):
            low = ws[i, :, 2 * STATE : 2 * STATE + LANES].astype(F32)
            high = ws[i, :, 2 * STATE + LANES :].astype(F32)
            joined[i, :, : 2 * STATE] = ws[i, :, : 2 * STATE]
            joined[i, :, 2 * STATE :] = (low + pltpu.roll(high, own_width // HEADDIM, 1)).astype(BF16)
            return carry

        lax.fori_loop(0, ws.shape[0], body, 0)

    advance(x_own)
    arrive(gain_copies)
    settle(gain_kept)
    gain_share = model // heads
    scale = jnp.concatenate([gains[g, 0:1, 0:gain_share] for g in range(heads)], axis=1)
    gain_all[...] = jnp.broadcast_to(scale, (8, model))
    advance(x_other)
    advance(x_own)
    settle(r_in.kept)
    normalise(rows.at[mine], mine * own_rows, own_rows, scale)
    advance(x_other)
    advance(z_own)
    advance(z_other)
    advance(x_other)
    advance(z_own)
    advance(o_own)
    advance(z_other)
    finish(x_own)
    finish(x_other)
    join_heads()
    local(joined, ws_out)
    local(wx, wx_out)
    r_in.finish()
    tail = rows.at[sets - 1, pl.ds(own_rows - HALO, HALO), :]
    tail_copy = send(tail, halo, other_half)
    for i in range(1, sets):
        other = flip_all(mine, i)
        normalise(rows.at[other], other * own_rows, own_rows, scale)
    advance(o_other)
    advance(o_own)
    advance(z_other)
    tail_copy.wait_recv()
    normalise(halo, tokens, HALO, scale * half.astype(F32))
    local(normed, normed_out)
    project(normed, tokens + HALO, joined, s_out, s_out.shape[1])
    advance(o_other)
    project(normed, tokens + HALO, wx, x_out, wx.shape[2])
    finish(z_own)
    finish(z_other)
    local(wz, wz_out)
    advance(o_other)
    finish(o_own)
    finish(o_other)
    local(wo, wo_out)
    arrive([par_copy])
    settle(par_kept)
    local(pars, pars_out)
    local(gain_all, gains_out)
    for copy in list(open_local):
        settle(copy)
    for copy in sent:
        copy.wait_send()


def gather_and_project(block_in, gain, par, small, wx, wz, wo):
    tok_size, head_size = lax.axis_size("tok"), lax.axis_size("head")
    sets = head_size // HALVES
    tok_bits = range(tok_size.bit_length() - 1)
    row_bits = range(sets.bit_length() - 1)
    own_rows, model = block_in.shape
    share, own_width = wx.shape
    width = HALVES * own_width
    tokens = own_rows * sets
    lanes = 2 * STATE + HALVES * LANES
    anywhere = pl.BlockSpec(memory_space=pl.ANY)
    slots = (tok_size, share)
    copies = 16 * tok_size
    outs = [
        shape((tokens + HALO, width), F32),
        shape((tokens + HALO, 2 * STATE + LANES), F32),
        shape((tokens + HALO, model), BF16),
        shape(slots + (2 * STATE + LANES,), BF16),
        shape(slots + (width,), BF16),
        shape(slots + (width,), BF16),
        shape(slots + (width,), BF16),
        shape((8, model), F32),
        shape((8, width), F32),
    ]
    return pl.pallas_call(
        functools.partial(gather_kernel, tok_bits, row_bits, sets.bit_length() - 1),
        in_specs=[anywhere] * 7,
        out_specs=[anywhere] * len(outs),
        out_shape=outs,
        scratch_shapes=[
            pltpu.VMEM(slots + (lanes,), BF16),
            pltpu.VMEM(slots + (width,), BF16),
            pltpu.VMEM(slots + (width,), BF16),
            pltpu.VMEM(slots + (width,), BF16),
            pltpu.VMEM(slots + (2 * STATE + LANES,), BF16),
            pltpu.VMEM((sets, own_rows, model), BF16),
            pltpu.VMEM((HALO, model), BF16),
            pltpu.VMEM((tokens + HALO, model), BF16),
            pltpu.VMEM((head_size,) + gain.shape, F32),
            pltpu.VMEM((8, model), F32),
            pltpu.VMEM((8, width), F32),
            pltpu.VMEM((2, tokens + HALO, 3 * LANES), F32),
            pltpu.SemaphoreType.DMA((copies,)),
            pltpu.SemaphoreType.DMA((copies,)),
            pltpu.SemaphoreType.DMA((32,)),
            pltpu.SemaphoreType.DMA((2,)),
        ],
        name="gather",
        compiler_params=pltpu.CompilerParams(
            collective_id=0, has_side_effects=True, vmem_limit_bytes=60 * 1024 * 1024
        ),
        cost_estimate=pl.CostEstimate(flops=int(12e9), bytes_accessed=int(60e6), transcendentals=0),
    )(block_in, gain, par, small, wx, wz, wo)


def reduce_kernel(
    tok_bits, row_bits,
    gx_ref, to_ref, gs_ref, gl_ref, dx_ref, ds_ref, dn_ref, norm_ref, in_ref, wx_ref, ws_ref, cot_ref, gain_ref, per_ref, bc_ref,
    ox_ref, oo_ref, os_ref, dblock_ref, gain_out, rest_out,
    kx, ks, rx, rs, fx, ls, own_o, got_o, fo,
    dx, ds, wx, ws, norms, own_in, cots, dnorm, low, got, halo_out, halo_in, sums, sums_got, per_got, bc_got, bc_own,
    send_sem, recv_sem, local_sem,
):
    links = Links(send_sem, recv_sem, local_sem, tok_bits, row_bits)
    half, mine, sets = links.half, links.mine, links.sets
    own_rows, model = cot_ref.shape
    own_width = ox_ref.shape[1]
    tokens = own_rows * sets
    chunk = min(CHUNK, own_rows)
    loads = [
        links.local(src, dst)
        for src, dst in ((dx_ref, dx), (ds_ref, ds), (wx_ref, wx), (ws_ref, ws), (dn_ref, dnorm))
    ]
    links.enter()

    up = [0] + links.tok_bits[1:]
    down = [0] + links.tok_bits[1:][::-1]
    s_small = SmallSum(links, gs_ref, gl_ref, ks, ls, rs, up)
    s_x = [Sum(links, gx_ref, kx, rx, fx, ox_ref, p, 2, (down, up)[p]) for p in range(2)]

    def advance(group):
        for each in group:
            each.advance()

    advance(s_x)
    late_loads = [
        links.local(norm_ref.at[pl.ds(0, tokens)], norms), links.local(in_ref, own_in), links.local(cot_ref, cots)
    ]

    def project_back(at):
        lhs_x, lhs_s = dx[at, :], ds[at, :]
        return dot_nt(lhs_x, wx[...].reshape(model, wx.shape[2])) + dot_nt(lhs_s, ws[...].reshape(model, ws.shape[2]))

    def slot_rows(slot, first=0, count=None):
        def body(i, carry):
            here = pl.ds(pl.multiple_of(i * chunk, chunk), chunk)
            total = project_back(pl.ds(pl.multiple_of(slot * own_rows + i * chunk, chunk), chunk))
            dnorm[slot, here, :] = dnorm[slot, here, :] + total
            return carry

        lax.fori_loop(first, own_rows // chunk if count is None else first + count, body, 0)

    def fold(slot):
        keep = jnp.where(half == 0, 1.0, 0.0) * jnp.where(slot == sets - 1, 1.0, 0.0)
        tail = pl.ds(own_rows - HALO, HALO)
        dnorm[slot, tail, :] = dnorm[slot, tail, :] + keep * halo_in[...]

    def rows_at(i, count):
        return pl.ds(pl.multiple_of(i * count, count), count)

    def gain_part(slot, start):
        def body(i, total):
            normed = norms[pl.ds(pl.multiple_of(slot * own_rows + i * 16, 16), 16), :].astype(F32)
            part = dnorm[slot, rows_at(i, 16), :] * normed
            return total + part[0:8] + part[8:16]

        return lax.fori_loop(0, own_rows // 16, body, start, unroll=2)

    everywhere, rest, owned = pl.ds(0, model), pl.ds(model, own_width + bc_ref.shape[1]), pl.ds(model, own_width)
    bc_lanes = pl.ds(model + own_width, bc_ref.shape[1])

    def channel_lanes(which):
        return pl.ds(pl.multiple_of(which * own_width, LANES), own_width)

    o_load = links.local(to_ref.at[:, channel_lanes(half)], own_o)
    early = [
        links.send(per_ref.at[:, channel_lanes(1 - half)], per_got, links.head_peer(links.half_bit)),
        links.send(bc_ref, bc_got.at[0], links.head_peer(links.half_bit)),
    ]

    links.settle(loads)
    halo_out[...] = project_back(pl.ds(tokens, HALO))
    away = list(range(1, sets))[::-1]
    slots = [flip_all(mine, o) for o in away]
    early_rows = sets == 2 and own_rows > chunk
    pieces = own_rows // chunk
    row_pieces = []

    def lower(piece, slot):
        def body(i, carry):
            at = pl.ds(pl.multiple_of(piece * chunk + i * 32, 32), 32)
            low[0, at, :] = dnorm[slot, at, :].astype(BF16)
            return carry

        lax.fori_loop(0, chunk // 32, body, 0)

    def send_piece(piece):
        at = pl.ds(piece * chunk, chunk)
        row_pieces.append(links.send(low.at[0, at], got.at[0, at], links.head_peer(0)))

    if early_rows:
        slot_rows(slots[0], 0, 1)
        lower(0, slots[0])
    elif slots:
        slot_rows(slots[0])
    halo_copy = links.send(halo_out, halo_in, links.head_peer(links.half_bit))
    for copy in early:
        copy.wait_recv()
    sums[0, :, owned] = per_ref[:, channel_lanes(half)] + per_got[...]
    bc_total = bc_ref[...] + bc_got[0]
    for n, bit in enumerate(links.row_bits):
        bc_own[n] = bc_total
        copy = links.send(bc_own.at[n], bc_got.at[n + 1], links.head_peer(bit))
        copy.wait_recv()
        bc_total = bc_total + bc_got[n + 1]
    sums[0, :, bc_lanes] = bc_total
    if early_rows:
        send_piece(0)
        slot_rows(slots[0], 1, pieces - 1)
    for slot in slots[1:]:
        slot_rows(slot)
    halo_copy.wait_recv()
    for slot in slots:
        fold(slot)

    row_order = list(row_bits)[::-1]
    held = list(range(sets))
    places = 0

    def send_rows():
        nonlocal held, places
        bit = row_order.pop(0)
        stay = [o for o in held if not (o >> bit) & 1]
        copies = []
        for o in stay:
            slot = flip_all(mine, o ^ (1 << bit))

            def body(i, carry, slot=slot, place=places):
                low[place, rows_at(i, 32), :] = dnorm[slot, rows_at(i, 32), :].astype(BF16)
                return carry

            lax.fori_loop(0, own_rows // 32, body, 0)
            copies.append((o, places, bit))
            places += 1
        held = stay
        return copies

    def start_rows(copies):
        return [(o, p, links.send(low.at[p], got.at[p], links.head_peer(bit))) for o, p, bit in copies]

    def take_rows(copies):
        for o, place, copy in copies:
            copy.wait_recv()
            slot = flip_all(mine, o)

            def body(i, carry, slot=slot, place=place):
                at = rows_at(i, 32)
                dnorm[slot, at, :] = dnorm[slot, at, :] + got[place, at, :].astype(F32)
                return carry

            lax.fori_loop(0, own_rows // 32, body, 0)

    if early_rows:
        for piece in range(1, pieces):
            lower(piece, slots[0])
        row_order, row_copies = [], [(0, 0, None)]
        advance([s_small])
        for piece in range(1, pieces):
            send_piece(piece)
    else:
        prepared = send_rows() if row_order else []
        advance([s_small])
        row_copies = start_rows(prepared)
    o_tail = links.send(to_ref.at[:, channel_lanes(1 - half)], got_o, links.head_peer(links.half_bit))
    advance(s_x)
    slot_rows(mine)
    fold(mine)
    links.settle(late_loads)
    gain_sum = jnp.zeros((8, model), F32)
    for slot in slots + [mine]:
        gain_sum = gain_part(slot, gain_sum)
    gain = gain_ref[0:1, :]
    gain_row = jnp.sum(gain_sum, axis=0, keepdims=True) / gain

    sums[0, :, everywhere] = jnp.concatenate([gain_row, jnp.zeros((7, model), F32)], axis=0)
    advance([s_small])
    between = {0: s_x, 1: [s_small], 2: s_x}
    for n, bit in enumerate(tok_bits):
        copy = links.send(sums.at[n], sums_got.at[n], links.tok_peer(bit))
        advance(between.get(n, []))
        copy.wait_recv()
        sums[n + 1] = sums[n] + sums_got[n]
    n = len(tok_bits)
    links.local(sums.at[n, :, rest], rest_out)
    advance([s_small])
    for bit in links.row_bits + [links.half_bit]:
        copy = links.send(sums.at[n, :, everywhere], sums_got.at[n, :, everywhere], links.head_peer(bit))
        copy.wait_recv()
        sums[n + 1, :, everywhere] = sums[n, :, everywhere] + sums_got[n, :, everywhere]
        n += 1
    links.local(sums.at[n, :, everywhere], gain_out)

    s_small.finish()
    links.local(ks.at[0], os_ref)

    while row_copies:
        if not row_order:
            break
        take_rows(row_copies)
        row_copies = start_rows(send_rows())
    for copy in row_pieces if early_rows else [copy for _, _, copy in row_copies]:
        copy.wait_recv()

    def block_rows(i, carry):
        at = rows_at(i, 32)
        wide = own_in[at, :].astype(F32)
        inv = lax.rsqrt(jnp.sum(wide * wide, axis=1, keepdims=True) / model + EPS)
        total = dnorm[mine, at, :]
        for _, place, _ in row_copies:
            total = total + got[place, at, :].astype(F32)
        scaled = total * gain
        inner = jnp.sum(scaled * wide, axis=1, keepdims=True) / model
        dnorm[mine, at, :] = cots[at, :].astype(F32) + inv * scaled - wide * (inv * inv * inv * inner)
        return carry

    lax.fori_loop(0, own_rows // 32, block_rows, 0)
    links.local(dnorm.at[mine], dblock_ref)
    o_tail.wait_recv()
    links.settle([o_load])

    def o_rows(i, carry):
        at = rows_at(i, 32)
        fo[at, :] = own_o[at, :].astype(F32) + got_o[at, :].astype(F32)
        return carry

    lax.fori_loop(0, fo.shape[0] // 32, o_rows, 0)
    links.local(fo, oo_ref)
    for each in s_x:
        each.finish()
    for each in s_x:
        each.close()
    links.leave()


def reduce_sums(gx, to, gs, gl, dx, ds, dn, normed, block_in, wx, ws, cot, gain, per, bc):
    tok_size, head_size = lax.axis_size("tok"), lax.axis_size("head")
    sets = head_size // HALVES
    tok_bits = range(tok_size.bit_length() - 1)
    row_bits = range(sets.bit_length() - 1)
    own_rows, model = cot.shape
    share, width = gx.shape[1:]
    lanes = gs.shape[2]
    own_width = width // HALVES
    anywhere = pl.BlockSpec(memory_space=pl.ANY)
    inside = pl.BlockSpec(memory_space=pltpu.VMEM)
    keep, slots = tok_size // 2, tok_size + len(row_bits)
    stages = len(tok_bits) + len(row_bits) + 1
    away = max(sets - 1, 1)
    copies = 32 * len(tok_bits)
    outs = [
        shape((share, own_width), F32),
        shape((share, own_width), F32),
        shape((share, lanes), F32),
        shape((own_rows, model), F32),
        shape((8, model), F32),
        shape((8, own_width + bc.shape[1]), F32),
    ]
    return pl.pallas_call(
        functools.partial(reduce_kernel, tok_bits, row_bits),
        in_specs=[anywhere] * 12 + [inside] * 3,
        out_specs=[anywhere] * len(outs),
        out_shape=outs,
        scratch_shapes=[pltpu.VMEM((keep, share, width), BF16)]
        + [pltpu.VMEM((keep, share, lanes), F32)]
        + [pltpu.VMEM((slots, share, width), BF16)]
        + [pltpu.VMEM((slots, share, lanes), BF16)]
        + [pltpu.VMEM((share, own_width), F32)]
        + [pltpu.VMEM((slots, share, lanes), BF16)]
        + [pltpu.VMEM((share, own_width), BF16)] * 2
        + [pltpu.VMEM((share, own_width), F32)]
        + [
            pltpu.VMEM(dx.shape, BF16),
            pltpu.VMEM(ds.shape, BF16),
            pltpu.VMEM(wx.shape, BF16),
            pltpu.VMEM(ws.shape, BF16),
            pltpu.VMEM((own_rows * sets, model), BF16),
            pltpu.VMEM(cot.shape, BF16),
            pltpu.VMEM(cot.shape, BF16),
            pltpu.VMEM((sets, own_rows, model), F32),
            pltpu.VMEM((away, own_rows, model), BF16),
            pltpu.VMEM((away, own_rows, model), BF16),
            pltpu.VMEM((HALO, model), F32),
            pltpu.VMEM((HALO, model), F32),
            pltpu.VMEM((stages + 1, 8, model + own_width + bc.shape[1]), F32),
            pltpu.VMEM((stages, 8, model + own_width + bc.shape[1]), F32),
            pltpu.VMEM((8, own_width), F32),
            pltpu.VMEM((len(row_bits) + 1,) + bc.shape, F32),
            pltpu.VMEM((max(len(row_bits), 1),) + bc.shape, F32),
            pltpu.SemaphoreType.DMA((copies,)),
            pltpu.SemaphoreType.DMA((copies,)),
            pltpu.SemaphoreType.DMA((copies,)),
        ],
        name="reduce",
        compiler_params=pltpu.CompilerParams(
            collective_id=1, has_side_effects=True, vmem_limit_bytes=62 * 1024 * 1024
        ),
        cost_estimate=pl.CostEstimate(flops=int(12e9), bytes_accessed=int(60e6), transcendentals=0),
    )(gx, to, gs, gl, dx, ds, dn.reshape(sets, own_rows, model), normed, block_in, wx, ws, cot, gain, per, bc)


def per_device(
    block_in,
    norm_gain,
    w_zx,
    w_bc,
    w_dt,
    conv_x_w,
    conv_x_b,
    conv_bc_w,
    conv_bc_b,
    dt_bias,
    a_log,
    d_skip,
    gate_gain,
    w_out,
    cotangent,
):
    head_size = lax.axis_size("head")
    tok_size = lax.axis_size("tok")
    sets = head_size // HALVES
    row_bits = range(sets.bit_length() - 1)
    half_bit = sets.bit_length() - 1
    half = bit_of("head", half_bit)
    own_rows, model = block_in.shape
    share, _, own_width = w_zx.shape
    own_heads = w_dt.shape[1]
    tokens = own_rows * sets

    def all_rows(value):
        for bit in row_bits:
            value = grow(value, "head", bit, 0)
        return value

    def lane_pad(v):
        return jnp.pad(v, (0, LANES - v.shape[0]))

    heads_row = jnp.concatenate([lane_pad(dt_bias), lane_pad(a_log), lane_pad(d_skip)])
    own_par = jnp.concatenate(
        [
            conv_x_w,
            conv_x_b[None],
            gate_gain[None],
            jnp.repeat(d_skip, HEADDIM)[None],
            jnp.pad(heads_row, (0, own_width - heads_row.shape[0]))[None],
        ]
    )
    gain_share = norm_gain.shape[0]
    own_gain = jnp.broadcast_to(
        jnp.pad(norm_gain.astype(F32), (0, -gain_share % LANES))[None], (8, gain_share + -gain_share % LANES)
    )
    small = jnp.concatenate([w_bc, jnp.pad(w_dt, ((0, 0), (0, LANES - own_heads)))], axis=1)
    x_ext, s_ext, normed_ext, w_small, w_x, w_z, w_o, gain, par = gather_and_project(
        block_in, own_gain, own_par, small, w_zx[:, 1], w_zx[:, 0], w_out.T
    )
    later_cot, x_ext = lax.optimization_barrier((cotangent, x_ext))
    cot = all_rows(later_cot)
    gain = gain[0:1]
    normed = normed_ext[:tokens]
    slots_small, slots_x, gain_rows = w_small, w_x, gain
    w_z, w_o = w_z.reshape(model, w_z.shape[2]), w_o.reshape(model, w_o.shape[2])

    def of_heads(start):
        pieces = [
            par[CONV + 3, i * own_width + start : i * own_width + start + own_heads] for i in range(HALVES)
        ]
        return jnp.concatenate(pieces)

    rate = -jnp.exp(of_heads(LANES))
    hp = jnp.stack([lane_pad(of_heads(0)), lane_pad(rate)] + [jnp.zeros((LANES,), F32)] * 6)
    bcpar = jnp.concatenate([conv_bc_w, conv_bc_b[None], jnp.zeros((3, 2 * STATE), F32)])

    xs, u, cume, dte, bc, cumt, sloc, fin, sdec = mixer_forward_state(x_ext, s_ext, par, bcpar, hp, tokens)
    to_next = [(i, i + sets) for i in range(sets)]
    to_prev = [(i + sets, i) for i in range(sets)]
    sin = lax.ppermute(fin, "head", to_next)
    z = dot_nn(normed, w_z)
    gyn = dot_nn(cot, w_o)
    y, stat = mixer_forward_main(xs, u, cume, cumt, bc, sloc, sin, sdec, z, gyn, par)
    stat = add_pairs(stat, "head", row_bits).T
    inv_gate = lax.rsqrt(stat[:, 0:1] / INNER + EPS)
    stat = jnp.concatenate(
        [inv_gate, inv_gate * inv_gate * inv_gate * stat[:, 1:2] / INNER, stat[:, 2:]], axis=1
    )
    yn, gy, dz, gloc, gin, gdec, acc_gate = mixer_backward_gate(y, z, gyn, cume, bc, stat, par)
    gout = lax.ppermute(gin, "head", to_prev)

    def own_row_sum(value):
        for bit in list(row_bits)[::-1]:
            value = halve(value, "head", bit, 0)
        return value

    def slots_of(grad):
        return grad.astype(BF16).reshape(tok_size, share, grad.shape[1])

    branch = dot_nt(yn, w_o)
    block_out = block_in.astype(F32) + own_row_sum(branch)
    grad_o = slots_of(dot_tn(cot, yn))
    grad_z = slots_of(dot_tn(normed, dz))
    d_normed_z = dot_nt(dz, w_z)

    dx, ds, acc_x, acc_b, acc_h, d_w_z, tail_o = mixer_backward_main(
        x_ext, s_ext, par, bcpar, hp, cume, dte, cumt, gy, sloc, sin, sdec, gloc, gout, gdec, grad_z, grad_o
    )
    grad_x = slots_of(dot_tn(normed_ext, dx))
    grad_small = dot_tn(normed_ext, ds).reshape(tok_size, share, ds.shape[1])

    per_channel = jnp.concatenate(
        [
            acc_x[: CONV + 1],
            acc_gate[0:1],
            jnp.concatenate(
                [
                    jnp.pad(
                        jnp.concatenate(
                            [
                                lane_pad(acc_h[0, i * own_heads : (i + 1) * own_heads]),
                                lane_pad(acc_h[1, i * own_heads : (i + 1) * own_heads]),
                                lane_pad(
                                    jnp.sum(
                                        acc_x[CONV + 1, i * own_width : (i + 1) * own_width].reshape(own_heads, HEADDIM),
                                        axis=1,
                                    )
                                ),
                            ]
                        ),
                        (0, own_width - 3 * LANES),
                    )
                    for i in range(HALVES)
                ]
            )[None],
            jnp.zeros((1, HALVES * own_width), F32),
        ]
    )

    d_w_x, d_w_o, d_small, d_block_in, gain_sums, own_sums = reduce_sums(
        grad_x, tail_o, grad_small, grad_small.astype(BF16), dx, ds, d_normed_z, normed_ext, block_in, slots_x, slots_small, cotangent,
        gain_rows, per_channel, acc_b,
    )
    all_gain, bc_sums = gain_sums[0], own_sums[:, own_width:]
    own_sums = own_sums[:, :own_width]
    d_w_bc = d_small[:, : 2 * STATE]
    d_w_dt = jnp.where(
        half == 0,
        d_small[:, 2 * STATE : 2 * STATE + own_heads],
        d_small[:, 2 * STATE + own_heads : 2 * STATE + 2 * own_heads],
    )
    d_norm_gain = lax.dynamic_slice_in_dim(all_gain, lax.axis_index("head") * gain_share, gain_share, 0)
    return (
        block_out,
        d_block_in,
        d_norm_gain,
        jnp.stack([d_w_z, d_w_x], axis=1),
        d_w_bc,
        d_w_dt,
        own_sums[:CONV],
        own_sums[CONV],
        bc_sums[:CONV],
        bc_sums[CONV],
        own_sums[CONV + 2, :own_heads],
        own_sums[CONV + 2, LANES : LANES + own_heads],
        own_sums[CONV + 2, 2 * LANES : 2 * LANES + own_heads],
        own_sums[CONV + 1],
        d_w_o.T,
    )


def solution(mesh):
    placed = (
        P(("tok", "head"), None),
        P("head"),
        P("tok", None, "head"),
        P("tok", None),
        P("tok", "head"),
        P(None, "head"),
        P("head"),
        P(),
        P(),
        P("head"),
        P("head"),
        P("head"),
        P("head"),
        P("head", "tok"),
        P(("tok", "head"), None),
    )
    return jax.shard_map(
        per_device,
        mesh=mesh,
        in_specs=placed,
        out_specs=(
            P(("tok", "head"), None),
            P(("tok", "head"), None),
            P("head"),
            P("tok", None, "head"),
            P("tok", None),
            P("tok", "head"),
            P(None, "head"),
            P("head"),
            P(),
            P(),
            P("head"),
            P("head"),
            P("head"),
            P("head"),
            P("head", "tok"),
        ),
        check_vma=False,
    )
```

```python
import functools

import jax
import jax.numpy as jnp
from jax import lax
from jax.experimental import pallas as pl
from jax.experimental.pallas import tpu as pltpu
from jax.sharding import PartitionSpec as P

HEADDIM = 64
STATE = 128
CONV = 4
INNER = 3072
CHUNK = 256
HALVES = 2
LANES = 128
HALO = 16

EPS = 1e-05
LOG2E = 1.4426950408889634
HIGHEST = lax.Precision.HIGHEST
F32 = jnp.float32
BF16 = jnp.bfloat16


def dot_nn(a, b, precision=None):
    return lax.dot_general(
        a, b, (((1,), (0,)), ((), ())), preferred_element_type=F32, precision=precision
    )


def dot_nt(a, b, precision=None):
    return lax.dot_general(
        a, b, (((1,), (1,)), ((), ())), preferred_element_type=F32, precision=precision
    )


def dot_tn(a, b):
    return lax.dot_general(a, b, (((0,), (0,)), ((), ())), preferred_element_type=F32)


def dot_split(a, b):
    a_top, b_top = a.astype(BF16), b.astype(BF16)
    a_rest = (a - a_top.astype(F32)).astype(BF16)
    b_rest = (b - b_top.astype(F32)).astype(BF16)
    return dot_nn(a_top, b_top) + (dot_nn(a_rest, b_top) + dot_nn(a_top, b_rest))


def iota(shape, dim):
    return lax.broadcasted_iota(jnp.int32, shape, dim)


def sigmoid(v):
    return 0.5 + 0.5 * jnp.tanh(0.5 * v)


def softplus(v):
    return jnp.maximum(v, 0.0) + jnp.log1p(jnp.exp(-jnp.abs(v)))


def thirds(a):
    top = a.astype(BF16)
    rest = a - top.astype(F32)
    middle = rest.astype(BF16)
    return top, middle, (rest - middle.astype(F32)).astype(BF16)


def sums_of(zero_one, a):
    width = a.shape[1]
    wide = dot_nn(zero_one, jnp.concatenate(thirds(a), axis=1))
    return wide[:, 0:width] + wide[:, width : 2 * width] + wide[:, 2 * width :]


def bit_of(axis, bit):
    return (lax.axis_index(axis) // (1 << bit)) % 2


def swap(value, axis, bit):
    size = lax.axis_size(axis)
    return lax.ppermute(value, axis, [(i, i ^ (1 << bit)) for i in range(size)])


def grow(value, axis, bit, dim):
    other = swap(value, axis, bit)
    low = bit_of(axis, bit) == 0
    return jnp.where(
        low,
        jnp.concatenate([value, other], dim),
        jnp.concatenate([other, value], dim),
    )


def halve(value, axis, bit, dim):
    mine = bit_of(axis, bit)
    if dim < value.ndim - 1:
        half = value.shape[dim] // 2
        keep = lax.dynamic_slice_in_dim(value, mine * half, half, dim)
        send = lax.dynamic_slice_in_dim(value, (1 - mine) * half, half, dim)
    else:
        low, high = jnp.split(value, 2, axis=dim)
        keep = jnp.where(mine == 0, low, high)
        send = jnp.where(mine == 0, high, low)
    return keep.astype(F32) + swap(send.astype(BF16), axis, bit).astype(F32)


def add_pairs(value, axis, bits):
    for bit in bits:
        value = value + swap(value, axis, bit)
    return value


MESH = pl.DeviceIdType.MESH


def flip(index, bit):
    return index + (1 - 2 * ((index // (1 << bit)) % 2)) * (1 << bit)


def flip_all(index, offset):
    bit = 0
    while offset >> bit:
        if (offset >> bit) & 1:
            index = flip(index, bit)
        bit += 1
    return index


def now(value):
    return value() if callable(value) else value


class Remote:
    def __init__(self, links, k, src, dst, device):
        self.links, self.k, self.src, self.dst, self.device = links, k, src, dst, device

    def make(self):
        return pltpu.make_async_remote_copy(
            src_ref=now(self.src),
            dst_ref=now(self.dst),
            send_sem=self.links.send_sem.at[self.k],
            recv_sem=self.links.recv_sem.at[self.k],
            device_id=now(self.device),
            device_id_type=MESH,
        )

    def start(self):
        self.make().start()

    def wait_recv(self):
        self.make().wait_recv()

    def wait_send(self):
        self.make().wait_send()


class Local:
    def __init__(self, links, k, src, dst):
        self.links, self.k, self.src, self.dst = links, k, src, dst

    def make(self):
        return pltpu.make_async_copy(now(self.src), now(self.dst), self.links.local_sem.at[self.k])

    def start(self):
        self.make().start()

    def wait(self):
        self.make().wait()


class Links:
    def __init__(self, send_sem, recv_sem, local_sem, tok_bits, row_bits):
        self.send_sem, self.recv_sem, self.local_sem = send_sem, recv_sem, local_sem
        self.tok_bits, self.row_bits = list(tok_bits), list(row_bits)
        self.tok, self.head = lax.axis_index("tok"), lax.axis_index("head")
        self.sets = 1 << len(self.row_bits)
        self.half, self.mine = self.head // self.sets, self.head % self.sets
        self.half_bit = len(self.row_bits)
        self.sent, self.drained, self.n_local, self.open_local = [], [], 0, []

    def enter(self):
        partners = [self.tok_peer(b) for b in self.tok_bits]
        partners += [self.head_peer(b) for b in self.row_bits + [self.half_bit]]
        barrier = pltpu.get_barrier_semaphore()
        for partner in partners:
            pl.semaphore_signal(barrier, inc=1, device_id=partner(), device_id_type=MESH)
        pl.semaphore_wait(barrier, len(partners))

    def tok_peer(self, bit):
        return lambda: {"tok": flip(self.tok, bit)}

    def head_peer(self, bit):
        return lambda: {"head": flip(self.head, bit)}

    def plan_send(self, src, dst, device):
        copy = Remote(self, len(self.sent), src, dst, device)
        self.sent.append(copy)
        return copy

    def send(self, src, dst, device):
        copy = self.plan_send(src, dst, device)
        copy.start()
        return copy

    def plan_local(self, src, dst):
        self.n_local += 1
        return Local(self, self.n_local - 1, src, dst)

    def local(self, src, dst):
        copy = self.plan_local(src, dst)
        copy.start()
        self.open_local.append(copy)
        return copy

    def settle(self, copies):
        for copy in copies:
            if any(copy is other for other in self.open_local):
                self.open_local = [other for other in self.open_local if other is not copy]
                copy.wait()

    def drain(self, copy):
        copy.wait_recv()
        copy.wait_send()
        self.drained.append(copy)

    def leave(self):
        self.settle(list(self.open_local))
        for copy in self.sent:
            if not any(copy is other for other in self.drained):
                copy.wait_send()


def add_rows(dst, src, count):
    def body(i, carry):
        at = pl.ds(pl.multiple_of(i * 16, 16), 16)
        dst[at, :] = (dst[at, :].astype(F32) + src[at, :].astype(F32)).astype(BF16)
        return carry

    lax.fori_loop(0, count // 16, body, 0)


class Sum:
    def __init__(self, links, src, keep, recv, final, out, part, parts, order):
        self.links, self.src, self.keep, self.recv, self.final = links, src, keep, recv, final
        self.size = keep.shape[1] // parts
        self.start = part * self.size
        self.width = out.shape[1]
        self.whole = final is not None
        held = list(range(1 << len(links.tok_bits)))
        self.sends, self.adds, base = [], [], 0
        for number, bit in enumerate(order):
            stay = [o for o in held if not (o >> bit) & 1]
            if number == 0:
                place = {o: i for i, o in enumerate(stay)}
                self.loads = [links.plan_local(self.source(o), self.slot(place[o])) for o in stay]
            sends, adds = [], []
            for n, o in enumerate(stay):
                away = o ^ (1 << bit)
                src_ref = self.source(away) if number == 0 else self.slot(place[away])
                sends.append(links.plan_send(src_ref, self.landing(base + n), links.tok_peer(bit)))
                adds.append((place[o], base + n))
            base += len(stay)
            held = stay
            self.sends.append(sends)
            self.adds.append(adds)
        self.base = base
        if self.whole:
            self.tail = links.plan_send(
                lambda: self.keep.at[0, self.rows(), self.half_lanes(1 - self.links.half)],
                lambda: self.recv.at[base, self.rows(), pl.ds(0, self.width)],
                links.head_peer(links.half_bit),
            )
            self.store = links.plan_local(lambda: final.at[self.rows()], lambda: out.at[self.rows()])
        else:
            self.store = links.plan_local(self.slot(0), lambda: out.at[self.rows()])
        self.next = 0
        self.last = len(self.sends) + self.whole

    def rows(self):
        return pl.ds(self.start, self.size)

    def source(self, offset):
        return lambda: self.src.at[flip_all(self.links.tok, offset), self.rows()]

    def landing(self, i):
        return lambda: self.recv.at[i, self.rows()]

    def slot(self, i):
        return lambda: self.keep.at[i, self.rows()]

    def half_lanes(self, which):
        return pl.ds(pl.multiple_of(which * self.width, LANES), self.width)

    def step(self, k):
        if k == 0:
            for copy in self.sends[0] + self.loads:
                copy.start()
            return
        if k == self.last and self.whole:
            self.tail.wait_recv()
            lanes = self.half_lanes(self.links.half)

            def body(i, carry):
                at = pl.ds(pl.multiple_of(self.start + i * 16, 16), 16)
                self.final[at, :] = self.keep[0, at, lanes].astype(F32) + self.recv[
                    self.base, at, 0 : self.width
                ].astype(F32)
                return carry

            lax.fori_loop(0, self.size // 16, body, 0)
            self.store.start()
            return
        for copy in self.sends[k - 1]:
            copy.wait_recv()
        if k == 1:
            for copy in self.loads:
                copy.wait()
        for place, i in self.adds[k - 1]:
            add_rows(now(self.slot(place)), now(self.landing(i)), self.size)
        if k < len(self.sends):
            for copy in self.sends[k]:
                copy.start()
        elif self.whole:
            self.tail.start()
        else:
            self.store.start()

    def advance(self):
        if self.next < self.last:
            self.step(self.next)
            self.next += 1

    def finish(self):
        while self.next <= self.last:
            self.step(self.next)
            self.next += 1

    def close(self):
        self.store.wait()


class SmallSum(Sum):
    def __init__(self, links, src, src_low, keep, low, recv, order):
        self.links, self.keep, self.low, self.recv = links, keep, low, recv
        self.order = list(order)
        bit = self.order.pop(0)
        slots = range(1 << len(links.tok_bits))
        self.held = [o for o in slots if not (o >> bit) & 1]
        self.place = {o: i for i, o in enumerate(self.held)}
        self.base = len(self.held)
        self.n_low = 0
        self.into = [(i, i) for i in range(self.base)]
        self.flight = [
            links.send(src_low.at[flip_all(links.tok, o ^ (1 << bit))], recv.at[self.place[o]], links.tok_peer(bit))
            for o in self.held
        ]
        self.kept = [links.local(src.at[flip_all(links.tok, o)], keep.at[self.place[o]]) for o in self.held]
        self.done = False

    def post(self, place, lanes, device):
        n = self.n_low
        self.low[n, :, 0:lanes] = self.keep[place, :, 0:lanes].astype(BF16)
        self.n_low += 1
        src, dst = self.low.at[n, :, pl.ds(0, lanes)], self.recv.at[self.base, :, pl.ds(0, lanes)]
        self.flight.append(self.links.send(src, dst, device))
        self.base += 1
        return self.base - 1

    def take(self):
        for copy in self.flight:
            copy.wait_recv()
        self.links.settle(self.kept)
        for place, i in self.into:
            self.keep[place, :, 0 : self.lanes_in] = self.keep[place, :, 0 : self.lanes_in] + self.recv[
                i, :, 0 : self.lanes_in
            ].astype(F32)
        self.flight, self.into, self.kept = [], [], []

    lanes_in = 2 * STATE + LANES

    def advance(self):
        if self.done:
            return
        self.take()
        if not self.order:
            self.into = [(0, self.post(0, self.lanes_in, self.links.head_peer(self.links.half_bit)))]
            self.done = True
            return
        bit = self.order.pop(0)
        stay = [o for o in self.held if not (o >> bit) & 1]
        self.into = [
            (self.place[o], self.post(self.place[o ^ (1 << bit)], self.lanes_in, self.links.tok_peer(bit)))
            for o in stay
        ]
        self.held = stay

    def finish(self):
        while not self.done:
            self.advance()
        self.take()
        self.lanes_in = 2 * STATE
        for bit in self.links.row_bits:
            self.into = [(0, self.post(0, self.lanes_in, self.links.head_peer(bit)))]
            self.take()


def conv_rows(cur, tail, weight, bias):
    rows = cur.shape[0]
    ext = jnp.concatenate([tail, cur], axis=0)
    out = bias + weight[CONV - 1 : CONV] * cur
    for k in range(CONV - 1):
        start = 8 - (CONV - 1) + k
        out = out + weight[k : k + 1] * ext[start : start + rows]
    return out


def state_kernel(
    xm_ref, xt_ref, bm_ref, bt_ref, par_ref, bcpar_ref, hp_ref,
    xs_ref, u_ref, cume_ref, dte_ref, dsil_ref, bc_ref, cumt_ref, sloc_ref, fin_ref, dec_ref,
    state, dsum, ue, spread,
):
    c = pl.program_id(0)
    q, width = xm_ref.shape

    @pl.when(c == 0)
    def _():
        state[...] = jnp.zeros_like(state)
        dsum[...] = jnp.zeros_like(dsum)
        row = iota((3 * LANES, width), 0) % LANES
        spread[...] = jnp.where(iota((3 * LANES, width), 1) // HEADDIM == row, 1.0, 0.0).astype(BF16)

    dt = softplus(bm_ref[:, 2 * STATE :] + hp_ref[0:1, :])
    tri = jnp.where(iota((q, q), 0) >= iota((q, q), 1), 1.0, 0.0).astype(BF16)
    cum = sums_of(tri, dt * (hp_ref[1:2, :] * LOG2E))
    cumt_ref[...] = cum.T[: cumt_ref.shape[0], :]
    cume_ref[...] = dot_nn(jnp.concatenate(thirds(cum), axis=1), spread[...])
    dte_ref[...] = dot_nn(jnp.concatenate(thirds(dt), axis=1), spread[...])
    end = cume_ref[q - 1 : q, :]

    bpre = conv_rows(
        bm_ref[:, : 2 * STATE], bt_ref[:, : 2 * STATE], bcpar_ref[0:CONV, :], bcpar_ref[CONV : CONV + 1, :]
    )
    bc_ref[...] = bpre * sigmoid(bpre)

    block = 2 * LANES

    def body(i, carry):
        sl = pl.ds(pl.multiple_of(i * block, block), block)
        pre = conv_rows(
            xm_ref[:, sl], xt_ref[:, sl], par_ref[0:CONV, sl], par_ref[CONV : CONV + 1, sl]
        )
        sig = sigmoid(pre)
        xs = pre * sig
        u = xs * dte_ref[:, sl]
        xs_ref[:, sl] = xs
        dsil_ref[:, sl] = sig * (1.0 + pre * (1.0 - sig))
        u_ref[:, sl] = u.astype(BF16)
        cume = cume_ref[:, sl]
        ue[:, sl] = (u * jnp.exp2(cume[q - 1 : q, :] - cume)).astype(BF16)
        return carry

    lax.fori_loop(0, width // block, body, 0)
    sloc_ref[0] = state[...]
    dec_ref[0] = jnp.exp2(dsum[...])
    state[...] = jnp.exp2(end) * state[...] + dot_nn(bc_ref[:, :STATE].T.astype(BF16), ue[...])
    dsum[...] = dsum[...] + end
    fin_ref[...] = state[...].astype(BF16)


def main_kernel(
    xs_ref, u_ref, cume_ref, cumt_ref, bc_ref, sloc_ref, sin_ref, dec_ref, z_ref, gyn_ref, par_ref,
    y_ref, stat_ref,
    gram, ya, acc_sq, acc_in,
):
    q, width = xs_ref.shape
    bmat = bc_ref[:, :STATE].astype(BF16)
    cmat = bc_ref[:, STATE:].astype(BF16)
    lower = iota((q, q), 0) >= iota((q, q), 1)
    gram[...] = jnp.where(lower, dot_nt(cmat, bmat), 0.0)
    entering = sloc_ref[0] + dec_ref[0, 0:1, :] * sin_ref[...].astype(F32)
    ya[...] = dot_nn(cmat, entering.astype(BF16))
    acc_sq[...] = jnp.zeros_like(acc_sq)
    acc_in[...] = jnp.zeros_like(acc_in)
    first = iota((q, LANES), 1) < HEADDIM
    hq = q // 2

    def body(p, carry):
        sl = pl.ds(pl.multiple_of(p * LANES, LANES), LANES)
        cume = cume_ref[:, sl]
        u = u_ref[:, sl]
        y = jnp.exp2(cume) * ya[:, sl] + par_ref[CONV + 2 : CONV + 3, sl] * xs_ref[:, sl]
        low_y, high_y = y[:hq], y[hq:]
        for s in range(2):
            column = cume[:, HEADDIM * s : HEADDIM * s + 1]
            row = cumt_ref[pl.ds(2 * p + s, 1), :]
            mine = jnp.where(first == (s == 0), u, jnp.zeros_like(u))
            gap = column[:hq] - row[:, :hq]
            pairs = (gram[:hq, :hq] * jnp.exp2(jnp.minimum(gap, 0.0))).astype(BF16)
            low_y = low_y + dot_nn(pairs, mine[:hq])
            gap = column[hq:] - row
            pairs = (gram[hq:, :] * jnp.exp2(jnp.minimum(gap, 0.0))).astype(BF16)
            high_y = high_y + dot_nn(pairs, mine)
        y = jnp.concatenate([low_y, high_y], axis=0)
        y_ref[:, sl] = y
        z = z_ref[:, sl]
        gated = y * z * sigmoid(z)
        acc_sq[...] += gated * gated
        acc_in[...] += gated * gyn_ref[:, sl] * par_ref[CONV + 1 : CONV + 2, sl]
        return carry

    lax.fori_loop(0, width // LANES, body, 0)
    ones = jnp.ones((8, LANES), F32)
    sums_sq = dot_nt(ones, acc_sq[...], HIGHEST)
    sums_in = dot_nt(ones, acc_in[...], HIGHEST)
    stat_ref[...] = jnp.where(iota(sums_sq.shape, 0) == 0, sums_sq, sums_in)


def gate_kernel(
    y_ref, z_ref, gyn_ref, cume_ref, bc_ref, stat_ref, par_ref,
    yn_ref, gy_ref, dz_ref, gloc_ref, gin_ref, dec_ref, acc_ref,
    adj, dsum, ge,
):
    q, width = y_ref.shape

    @pl.when(pl.program_id(0) == 0)
    def _():
        adj[...] = jnp.zeros_like(adj)
        dsum[...] = jnp.zeros_like(dsum)
        acc_ref[...] = jnp.zeros_like(acc_ref)

    end = cume_ref[q - 1 : q, :]
    inv = jnp.broadcast_to(stat_ref[:, 0:1], (q, LANES))
    back = jnp.broadcast_to(stat_ref[:, 1:2], (q, LANES))

    def body(p, carry):
        sl = pl.ds(pl.multiple_of(p * LANES, LANES), LANES)
        y, z, gyn = y_ref[:, sl], z_ref[:, sl], gyn_ref[:, sl]
        sig = sigmoid(z)
        sil = z * sig
        gated = y * sil
        gain = par_ref[CONV + 1 : CONV + 2, sl]
        unit = gated * inv
        yn_ref[:, sl] = (unit * gain).astype(BF16)
        d_gated = inv * gyn * gain - gated * back
        gy = d_gated * sil
        gy_ref[:, sl] = gy.astype(BF16)
        dz_ref[:, sl] = (d_gated * y * (sig * (1.0 + z * (1.0 - sig)))).astype(BF16)
        ge[:, sl] = (gy * jnp.exp2(cume_ref[:, sl])).astype(BF16)
        acc_ref[0:1, sl] += jnp.sum(gyn * unit, axis=0, keepdims=True)
        return carry

    lax.fori_loop(0, width // LANES, body, 0)
    gloc_ref[0] = adj[...]
    dec_ref[0] = jnp.exp2(dsum[...])
    adj[...] = jnp.exp2(end) * adj[...] + dot_nn(bc_ref[:, STATE:].T.astype(BF16), ge[...])
    dsum[...] = dsum[...] + end
    gin_ref[...] = adj[...].astype(BF16)


def back_kernel(
    tok_bits, row_bits,
    xm_ref, xt_ref, bm_ref, bt_ref, par_ref, bcpar_ref, hp_ref,
    cume_ref, dte_ref, xs, dsil, u, cumt_ref, gy_ref, sloc_ref, sin_ref, sdec_ref, gloc_ref, gout_ref, gdec_ref,
    gz_ref, go_ref,
    dx_ref, ds_ref, accx_ref, accb_ref, acch_ref, oz_ref, oo_ref,
    ue, ge, dus, ya, qx, qb, gram, dgram, da, acc_x, acc_w, acc_g, acc_k, kept,
    kz, ko, rz, ro, fz, send_sem, recv_sem, local_sem,
):
    step = pl.program_id(0)
    q, width = xm_ref.shape
    tokens = dx_ref.shape[0] - HALO
    steps = tokens // q
    links = Links(send_sem, recv_sem, local_sem, tok_bits, row_bits)
    up = [0] + links.tok_bits[1:]
    down = [0] + links.tok_bits[1:][::-1]
    groups = [
        [Sum(links, gz_ref, kz, rz, fz, oz_ref, p, 2, (down, up)[p]) for p in range(2)],
        [Sum(links, go_ref, ko, ro, None, oo_ref, p, 2, (down, up)[p]) for p in range(2)],
    ]
    plans = [[(0, 0), (0, 2), (1, 2), (2, 3)], [(0, 0), (0, 3), (2, 2)]]

    def go_on(point):
        for when in range(steps):

            @pl.when(step == when)
            def _():
                if (when, point) == (0, 0):
                    links.enter()
                for group, plan in zip(groups, plans):
                    for k, (number, place) in enumerate(plan):
                        if (min(number, steps - 1), place) == (when, point):
                            for each in group:
                                each.step(k)
                if (when, point) == (steps - 1, 3):
                    for group, plan in list(zip(groups, plans))[::-1]:
                        for k in range(len(plan), group[0].last + 1):
                            for each in group:
                                each.step(k)
                    for group in groups:
                        for each in group:
                            each.close()
                    links.leave()

    go_on(0)
    c = tokens // q - 1 - step
    block = 2 * LANES

    @pl.when(step == 0)
    def _():
        accx_ref[...] = jnp.zeros_like(accx_ref)
        accb_ref[...] = jnp.zeros_like(accb_ref)
        acch_ref[...] = jnp.zeros_like(acch_ref)
        qx[q:, :] = jnp.zeros((8, width), F32)
        qb[q:, :] = jnp.zeros((8, 2 * STATE), F32)
        da[...] = jnp.zeros_like(da)
        ds_ref[...] = jnp.zeros_like(ds_ref)

    bpre = conv_rows(
        bm_ref[:, : 2 * STATE], bt_ref[:, : 2 * STATE], bcpar_ref[0:CONV, :], bcpar_ref[CONV : CONV + 1, :]
    )
    bsig = sigmoid(bpre)
    bc = bpre * bsig
    qb[0:q, :] = bsig * (1.0 + bpre * (1.0 - bsig))
    bmat, cmat = bc[:, :STATE].astype(BF16), bc[:, STATE:].astype(BF16)

    def conv_body(i, carry):
        sl = pl.ds(pl.multiple_of(i * block, block), block)
        x = xs[:, sl]
        uu = x * dte_ref[:, sl]
        cume = cume_ref[:, sl]
        ue[:, sl] = (uu * jnp.exp2(cume[q - 1 : q, :] - cume)).astype(BF16)
        gy = gy_ref[:, sl].astype(F32)
        ge[:, sl] = (gy * jnp.exp2(cume)).astype(BF16)
        accx_ref[CONV + 1 : CONV + 2, sl] += jnp.sum(gy * x, axis=0, keepdims=True)
        return carry

    lax.fori_loop(0, width // block, conv_body, 0)
    go_on(1)

    last = cume_ref[q - 1 : q, :]
    adj = gloc_ref[0] + gdec_ref[0, 0:1, :] * gout_ref[...].astype(F32)
    entering = sloc_ref[0] + sdec_ref[0, 0:1, :] * sin_ref[...].astype(F32)
    kept_parts = thirds(jnp.exp2(last) * jnp.sum(adj * entering, axis=0, keepdims=True))
    kept[...] = jnp.concatenate(list(kept_parts) + [jnp.zeros((13, width), BF16)], axis=0)
    adj_low, ent_low = adj.astype(BF16), entering.astype(BF16)
    dus[...] = dot_nn(bmat, adj_low)
    ya[...] = dot_nn(cmat, ent_low)
    db = dot_nt(ue[...], adj_low)
    dc = dot_nt(ge[...], ent_low)
    upper = iota((q, q), 1) >= iota((q, q), 0)
    gram[...] = jnp.where(upper, dot_nt(bmat, cmat), 0.0)
    dgram[...] = jnp.zeros_like(dgram)
    acc_x[...] = jnp.zeros_like(acc_x)
    acc_k[...] = jnp.zeros_like(acc_k)
    acc_w[...] = jnp.zeros_like(acc_w)
    acc_g[...] = jnp.zeros_like(acc_g)
    later = jnp.where(iota((q, q), 0) >= iota((q, q), 1), 1.0, 0.0).astype(BF16)
    first = iota((q, LANES), 1) < HEADDIM
    hq = q // 2
    before_top = iota((hq, q), 0) < iota((hq, q), 1)
    before_low = iota((hq, hq), 0) < iota((hq, hq), 1)

    def pair_body(p, carry):
        sl = pl.ds(pl.multiple_of(p * LANES, LANES), LANES)
        cume = cume_ref[:, sl]
        ul = u[:, sl]
        gl = gy_ref[:, sl]
        gy = gl.astype(F32)
        low_du = jnp.zeros((hq, LANES), F32)
        high_du = jnp.zeros((hq, LANES), F32)
        for s in range(2):
            mine = first == (s == 0)
            row = pl.ds(2 * p + s, 1)
            column = cume[:, HEADDIM * s : HEADDIM * s + 1]
            later_row = cumt_ref[row, :]
            um = jnp.where(mine, ul, jnp.zeros_like(ul))
            gm = jnp.where(mine, gl, jnp.zeros_like(gl))
            decay = jnp.exp2(jnp.minimum(later_row - column[:hq], 0.0))
            pairs = gram[:hq, :] * decay
            dpairs = dot_nt(um[:hq], gl)
            dgram[:hq, :] += dpairs * decay
            through = dot_nn((dpairs * pairs).astype(BF16), later)
            total = jnp.sum(jnp.where(before_top, through, 0.0), axis=0, keepdims=True)
            low_du = low_du + dot_nn(pairs.astype(BF16), gm)
            decay = jnp.exp2(jnp.minimum(later_row[:, hq:] - column[hq:], 0.0))
            pairs = gram[hq:, hq:] * decay
            dpairs = dot_nt(um[hq:], gl[hq:])
            dgram[hq:, hq:] += dpairs * decay
            through = dot_nn((dpairs * pairs).astype(BF16), later[hq:, hq:])
            more = jnp.sum(jnp.where(before_low, through, 0.0), axis=0, keepdims=True)
            da[row, :] = total + jnp.concatenate([jnp.zeros((1, hq), F32), more], axis=1)
            high_du = high_du + dot_nn(pairs.astype(BF16), gm[hq:])
        du = jnp.concatenate([low_du, high_du], axis=0)
        x = xs[:, sl]
        wide = dus[:, sl] * jnp.exp2(cume[q - 1 : q, :] - cume)
        du = du + wide
        to_head = (iota((LANES, LANES), 1) == 2 * p + iota((LANES, LANES), 0) // HEADDIM).astype(BF16)
        dte = dte_ref[:, sl]
        acc_x[...] += dot_nn((x * du).astype(BF16), to_head)
        acc_w[...] += dot_nn((x * dte * wide).astype(BF16), to_head)
        acc_g[...] += dot_nn((gy * jnp.exp2(cume) * ya[:, sl]).astype(BF16), to_head)
        acc_k[...] += dot_nn(kept[:, sl], to_head)
        qx[0:q, sl] = (dte * du + par_ref[CONV + 2 : CONV + 3, sl] * gy) * dsil[:, sl]
        return carry

    lax.fori_loop(0, width // LANES, pair_body, 0)
    go_on(2)

    def unconv_body(i, carry):
        sl = pl.ds(pl.multiple_of(i * block, block), block)
        weight = par_ref[0:CONV, sl]
        ext = qx[:, sl]
        cur = ext[0:q]
        dpre = weight[CONV - 1 : CONV] * cur
        for k in range(CONV - 1):
            dpre = dpre + weight[k : k + 1] * ext[CONV - 1 - k : CONV - 1 - k + q]
        dx_ref[pl.ds(pl.multiple_of(c * q, q), q), sl] = dpre.astype(BF16)
        past = jnp.concatenate([xt_ref[:, sl], xm_ref[:, sl]], axis=0)
        for k in range(CONV):
            start = 8 - (CONV - 1) + k
            accx_ref[k : k + 1, sl] += jnp.sum(cur * past[start : start + q], axis=0, keepdims=True)
        accx_ref[CONV : CONV + 1, sl] += jnp.sum(cur, axis=0, keepdims=True)
        head_rows = jnp.concatenate([jnp.zeros((HALO, block), F32), cur[0:8]], axis=0)
        before = jnp.zeros((HALO, block), F32)
        for k in range(CONV - 1):
            before = before + weight[k : k + 1] * head_rows[CONV - 1 - k : CONV - 1 - k + HALO]
        dx_ref[pl.ds(tokens, HALO), sl] = before.astype(BF16)
        qx[q:, sl] = cur[0:8]
        return carry

    lax.fori_loop(0, width // block, unconv_body, 0)

    dg = jnp.where(upper, dgram[...], 0.0)
    db = db + dot_split(dg, bc[:, STATE:])
    dc = dc + dot_split(dg.T, bc[:, :STATE])
    qb[0:q, 0:STATE] = qb[0:q, 0:STATE] * db
    qb[0:q, STATE:] = qb[0:q, STATE:] * dc
    weight = bcpar_ref[0:CONV, :]
    ext = qb[...]
    cur = ext[0:q]
    dpre = weight[CONV - 1 : CONV] * cur
    for k in range(CONV - 1):
        dpre = dpre + weight[k : k + 1] * ext[CONV - 1 - k : CONV - 1 - k + q]
    ds_ref[pl.ds(pl.multiple_of(c * q, q), q), 0 : 2 * STATE] = dpre.astype(BF16)
    past = jnp.concatenate([bt_ref[:, 0 : 2 * STATE], bm_ref[:, 0 : 2 * STATE]], axis=0)
    for k in range(CONV):
        start = 8 - (CONV - 1) + k
        accb_ref[k : k + 1, :] += jnp.sum(cur * past[start : start + q], axis=0, keepdims=True)
    accb_ref[CONV : CONV + 1, :] += jnp.sum(cur, axis=0, keepdims=True)
    head_rows = jnp.concatenate([jnp.zeros((HALO, 2 * STATE), F32), cur[0:8]], axis=0)
    before = jnp.zeros((HALO, 2 * STATE), F32)
    for k in range(CONV - 1):
        before = before + weight[k : k + 1] * head_rows[CONV - 1 - k : CONV - 1 - k + HALO]
    ds_ref[pl.ds(tokens, HALO), 0 : 2 * STATE] = before.astype(BF16)
    qb[q:, :] = cur[0:8]

    raw = bm_ref[:, 2 * STATE :] + hp_ref[0:1, :]
    dt = softplus(raw)
    rate = hp_ref[1:2, :]
    from_here = jnp.where(iota((q, q), 1) >= iota((q, q), 0), 1.0, 0.0).astype(BF16)
    up_to_here = jnp.where(iota((q, q), 1) < iota((q, q), 0), 1.0, 0.0).astype(BF16)
    total = (
        da[...].T
        + sums_of(from_here, acc_g[...])
        + sums_of(up_to_here, acc_w[...])
        + jnp.sum(acc_k[0:3, :], axis=0, keepdims=True)
    )
    d_raw = (acc_x[...] + rate * total) * sigmoid(raw)
    ds_ref[pl.ds(pl.multiple_of(c * q, q), q), 2 * STATE :] = d_raw.astype(BF16)
    acch_ref[0:1, :] += jnp.sum(d_raw, axis=0, keepdims=True)
    acch_ref[1:2, :] += rate * jnp.sum(dt * total, axis=0, keepdims=True)
    go_on(3)


def shape(dims, dtype):
    return jax.ShapeDtypeStruct(dims, dtype)


def whole(dims):
    return pl.BlockSpec(dims, lambda c: (0,) * len(dims))


def run(kernel, name, grid, in_specs, out_specs, out_shape, scratch, args, flops, collective_id=None):
    return pl.pallas_call(
        kernel,
        grid=(grid,),
        in_specs=in_specs,
        out_specs=out_specs,
        out_shape=out_shape,
        scratch_shapes=scratch,
        name=name,
        compiler_params=pltpu.CompilerParams(
            dimension_semantics=("arbitrary",),
            vmem_limit_bytes=62 * 1024 * 1024,
            collective_id=collective_id,
            has_side_effects=collective_id is not None,
        ),
        cost_estimate=pl.CostEstimate(
            flops=flops, bytes_accessed=sum(a.size * a.dtype.itemsize for a in args), transcendentals=0
        ),
    )(*args)


def mixer_forward_state(x_ext, s_ext, par, bcpar, hp, tokens):
    width = x_ext.shape[1]
    small = s_ext.shape[1]
    n = tokens // CHUNK
    q = CHUNK
    tail = q // 8
    last = (tokens + HALO) // 8 - 1
    tail_map = lambda c: (jnp.where(c == 0, last, c * tail - 1), 0)
    heads_pad = -(-(width // HEADDIM) // 8) * 8
    return run(
        state_kernel,
        "scan_states",
        n,
        [
            pl.BlockSpec((q, width), lambda c: (c, 0)),
            pl.BlockSpec((8, width), tail_map),
            pl.BlockSpec((q, small), lambda c: (c, 0)),
            pl.BlockSpec((8, small), tail_map),
            whole(par.shape),
            whole(bcpar.shape),
            whole(hp.shape),
        ],
        [
            pl.BlockSpec((q, width), lambda c: (c, 0)),
            pl.BlockSpec((q, width), lambda c: (c, 0)),
            pl.BlockSpec((q, width), lambda c: (c, 0)),
            pl.BlockSpec((q, width), lambda c: (c, 0)),
            pl.BlockSpec((q, width), lambda c: (c, 0)),
            pl.BlockSpec((q, 2 * STATE), lambda c: (c, 0)),
            pl.BlockSpec((heads_pad, q), lambda c: (0, c)),
            pl.BlockSpec((1, STATE, width), lambda c: (c, 0, 0)),
            whole((STATE, width)),
            pl.BlockSpec((1, 1, width), lambda c: (c, 0, 0)),
        ],
        [
            shape((tokens, width), F32),
            shape((tokens, width), BF16),
            shape((tokens, width), F32),
            shape((tokens, width), F32),
            shape((tokens, width), F32),
            shape((tokens, 2 * STATE), F32),
            shape((heads_pad, tokens), F32),
            shape((n, STATE, width), F32),
            shape((STATE, width), BF16),
            shape((n, 1, width), F32),
        ],
        [
            pltpu.VMEM((STATE, width), F32),
            pltpu.VMEM((1, width), F32),
            pltpu.VMEM((q, width), BF16),
            pltpu.VMEM((3 * LANES, width), BF16),
        ],
        (x_ext, x_ext, s_ext, s_ext, par, bcpar, hp),
        int(3e9),
    )


def mixer_forward_main(xs, u, cume, cumt, bc, sloc, sin, dec, z, gyn, par):
    tokens, width = xs.shape
    q = CHUNK
    n = tokens // q
    rows = pl.BlockSpec((q, width), lambda c: (c, 0))
    return run(
        main_kernel,
        "scan_outputs",
        n,
        [
            rows,
            rows,
            rows,
            pl.BlockSpec((cumt.shape[0], q), lambda c: (0, c)),
            pl.BlockSpec((q, 2 * STATE), lambda c: (c, 0)),
            pl.BlockSpec((1, STATE, width), lambda c: (c, 0, 0)),
            whole(sin.shape),
            pl.BlockSpec((1, 1, width), lambda c: (c, 0, 0)),
            rows,
            rows,
            whole(par.shape),
        ],
        [rows, pl.BlockSpec((8, q), lambda c: (0, c))],
        [shape((tokens, width), F32), shape((8, tokens), F32)],
        [
            pltpu.VMEM((q, q), F32),
            pltpu.VMEM((q, width), F32),
            pltpu.VMEM((q, LANES), F32),
            pltpu.VMEM((q, LANES), F32),
        ],
        (xs, u, cume, cumt, bc, sloc, sin, dec, z, gyn, par),
        int(10e9),
    )


def mixer_backward_gate(y, z, gyn, cume, bc, stat, par):
    tokens, width = y.shape
    q = CHUNK
    n = tokens // q
    rows = pl.BlockSpec((q, width), lambda c: (n - 1 - c, 0))
    return run(
        gate_kernel,
        "gate_back",
        n,
        [
            rows,
            rows,
            rows,
            rows,
            pl.BlockSpec((q, 2 * STATE), lambda c: (n - 1 - c, 0)),
            pl.BlockSpec((q, 8), lambda c: (n - 1 - c, 0)),
            whole(par.shape),
        ],
        [
            rows,
            rows,
            rows,
            pl.BlockSpec((1, STATE, width), lambda c: (n - 1 - c, 0, 0)),
            whole((STATE, width)),
            pl.BlockSpec((1, 1, width), lambda c: (n - 1 - c, 0, 0)),
            whole((8, width)),
        ],
        [
            shape((tokens, width), BF16),
            shape((tokens, width), BF16),
            shape((tokens, width), BF16),
            shape((n, STATE, width), F32),
            shape((STATE, width), BF16),
            shape((n, 1, width), F32),
            shape((8, width), F32),
        ],
        [
            pltpu.VMEM((STATE, width), F32),
            pltpu.VMEM((1, width), F32),
            pltpu.VMEM((q, width), BF16),
        ],
        (y, z, gyn, cume, bc, stat, par),
        int(5e9),
    )


def mixer_backward_main(
    x_ext, s_ext, par, bcpar, hp, cume, dte, xs, dsil, u, cumt, gy, sloc, sin, sdec, gloc, gout, gdec, gz, go
):
    tok_size, head_size = lax.axis_size("tok"), lax.axis_size("head")
    tok_bits = range(tok_size.bit_length() - 1)
    row_bits = range((head_size // HALVES).bit_length() - 1)
    share = gz.shape[1]
    copies = 16 * len(tok_bits)
    tokens, width = cume.shape
    small = s_ext.shape[1]
    q = CHUNK
    n = tokens // q
    tail = q // 8
    last = (tokens + HALO) // 8 - 1
    rows = pl.BlockSpec((q, width), lambda c: (n - 1 - c, 0))
    tail_map = lambda c: (jnp.where(c == n - 1, last, (n - 1 - c) * tail - 1), 0)
    states = pl.BlockSpec((1, STATE, width), lambda c: (n - 1 - c, 0, 0))
    decays = pl.BlockSpec((1, 1, width), lambda c: (n - 1 - c, 0, 0))
    anywhere = pl.BlockSpec(memory_space=pl.ANY)
    return run(
        functools.partial(back_kernel, tok_bits, row_bits),
        "scan_back",
        n,
        [
            rows,
            pl.BlockSpec((8, width), tail_map),
            pl.BlockSpec((q, small), lambda c: (n - 1 - c, 0)),
            pl.BlockSpec((8, small), tail_map),
            whole(par.shape),
            whole(bcpar.shape),
            whole(hp.shape),
            rows,
            rows,
            rows,
            rows,
            rows,
            pl.BlockSpec((cumt.shape[0], q), lambda c: (0, n - 1 - c)),
            rows,
            states,
            whole(sin.shape),
            decays,
            states,
            whole(gout.shape),
            decays,
            anywhere,
            anywhere,
        ],
        [
            whole((tokens + HALO, width)),
            whole((tokens + HALO, small)),
            whole((8, width)),
            whole((8, 2 * STATE)),
            whole((8, LANES)),
            anywhere,
            anywhere,
        ],
        [
            shape((tokens + HALO, width), BF16),
            shape((tokens + HALO, small), BF16),
            shape((8, width), F32),
            shape((8, 2 * STATE), F32),
            shape((8, LANES), F32),
            shape((share, width // HALVES), F32),
            shape((share, width), BF16),
        ],
        [
            pltpu.VMEM((q, width), BF16),
            pltpu.VMEM((q, width), BF16),
            pltpu.VMEM((q, width), F32),
            pltpu.VMEM((q, width), F32),
            pltpu.VMEM((q + 8, width), F32),
            pltpu.VMEM((q + 8, 2 * STATE), F32),
            pltpu.VMEM((q, q), F32),
            pltpu.VMEM((q, q), F32),
            pltpu.VMEM((LANES, q), F32),
            pltpu.VMEM((q, LANES), F32),
            pltpu.VMEM((q, LANES), F32),
            pltpu.VMEM((q, LANES), F32),
            pltpu.VMEM((16, LANES), F32),
            pltpu.VMEM((16, width), BF16),
        ]
        + [pltpu.VMEM((tok_size // 2, share, width), BF16)] * 2
        + [pltpu.VMEM((tok_size, share, width), BF16)] * 2
        + [pltpu.VMEM((share, width // HALVES), F32)]
        + [pltpu.SemaphoreType.DMA((copies,))] * 3,
        (x_ext, x_ext, s_ext, s_ext, par, bcpar, hp, cume, dte, xs, dsil, u, cumt, gy, sloc, sin, sdec, gloc, gout, gdec, gz, go),
        int(30e9),
        collective_id=2,
    )


def gather_kernel(
    tok_bits, row_bits, half_bit,
    in_ref, gain_ref, par_ref, small_ref, wx_ref, wz_ref, wo_ref,
    x_out, s_out, normed_out, ws_out, wx_out, wz_out, wo_out, gains_out, pars_out,
    ws, wx, wz, wo, joined, rows, halo, normed, gains, gain_all, pars, stage,
    send_sem, recv_sem, local_sem, stage_sem,
):
    tok, head = lax.axis_index("tok"), lax.axis_index("head")
    sets = 1 << len(row_bits)
    heads = 2 * sets
    half, mine = head // sets, head % sets
    own_rows, model = in_ref.shape
    share, own_width = wx_ref.shape
    tokens = own_rows * sets
    partners = [{"tok": flip(tok, b)} for b in tok_bits]
    partners += [{"head": flip_all(head, p)} for p in range(1, heads)]

    barrier = pltpu.get_barrier_semaphore()
    for partner in partners:
        pl.semaphore_signal(barrier, inc=1, device_id=partner, device_id_type=MESH)
    pl.semaphore_wait(barrier, len(partners))

    sent, stored, open_local = [], [], []

    def send(src, dst, device):
        k = len(sent)
        copy = pltpu.make_async_remote_copy(
            src_ref=src, dst_ref=dst, send_sem=send_sem.at[k], recv_sem=recv_sem.at[k],
            device_id=device, device_id_type=MESH,
        )
        copy.start()
        sent.append(copy)
        return copy

    def local(src, dst):
        copy = pltpu.make_async_copy(src, dst, local_sem.at[len(stored)])
        copy.start()
        stored.append(copy)
        open_local.append(copy)
        return copy

    def settle(copy):
        if any(copy is other for other in open_local):
            open_local[:] = [other for other in open_local if other is not copy]
            copy.wait()

    def arrive(copies):
        for copy in copies:
            copy.wait_recv()

    other_half = {"head": flip(head, half_bit)}
    lanes = pl.ds(pl.multiple_of(half * own_width, LANES), own_width)

    class Own:
        def __init__(self, src, dst, rows_at, src_lanes, dst_lanes, order):
            self.rows, self.lanes = rows_at, dst_lanes
            self.dst, self.order = dst, list(order)
            slot = dst.at[tok, self.rows, self.lanes]
            bit = self.order.pop(0)
            self.flight = [send(src.at[self.rows, src_lanes], slot, {"tok": flip(tok, bit)})]
            self.kept = local(src.at[self.rows, src_lanes], slot)
            self.held = [0, 1 << bit]

        def advance(self):
            arrive(self.flight)
            settle(self.kept)
            self.flight = []
            if self.order:
                bit = self.order.pop(0)
                for offset in self.held:
                    slot = self.dst.at[flip_all(tok, offset), self.rows, self.lanes]
                    self.flight.append(send(slot, slot, {"tok": flip(tok, bit)}))
                self.held = self.held + [offset ^ (1 << bit) for offset in self.held]

        def finish(self):
            while self.flight:
                self.advance()

    class Other(Own):
        def __init__(self, src, dst, rows_at, src_lanes, sent_lanes, dst_lanes, order):
            self.rows, self.lanes = rows_at, dst_lanes
            self.dst, self.order, self.held, self.kept = dst, list(order), [0], None
            self.flight = [send(src.at[self.rows, src_lanes], dst.at[tok, self.rows, sent_lanes], other_half)]

    class Rows:
        def __init__(self, src, dst):
            self.dst, self.order, self.held = dst, list(row_bits), [0]
            self.src = src
            self.kept = local(src, dst.at[mine])
            self.flight = []
            if self.order:
                bit = self.order.pop(0)
                self.flight.append(send(src, dst.at[mine], {"head": flip(head, bit)}))
                self.held = [0, 1 << bit]

        def advance(self):
            arrive(self.flight)
            settle(self.kept)
            self.flight = []
            if self.order:
                bit = self.order.pop(0)
                for offset in self.held:
                    slot = self.dst.at[flip_all(mine, offset)]
                    self.flight.append(send(slot, slot, {"head": flip(head, bit)}))
                self.held = self.held + [offset ^ (1 << bit) for offset in self.held]

        def finish(self):
            settle(self.kept)
            while self.flight:
                self.advance()

    up = list(tok_bits)[1:] + [0]
    down = list(tok_bits)[1:][::-1] + [0]
    gain_copies = [
        send(gain_ref, gains.at[head], {"head": flip_all(head, p)}) for p in range(1, heads)
    ]
    gain_kept = local(gain_ref, gains.at[head])
    par_slot = pars.at[:, lanes]
    par_copy = send(par_ref, par_slot, other_half)
    par_kept = local(par_ref, par_slot)
    own_all = pl.ds(0, own_width)
    there = pl.ds(pl.multiple_of((1 - half) * own_width, LANES), own_width)
    parts = [pl.ds(n * (share // 2), share // 2) for n in range(2)]

    def own_pieces(src, dst):
        return [Own(src, dst, parts[n], own_all, lanes, (up, down)[n]) for n in range(2)]

    def other_pieces(src, dst):
        return [Other(src, dst, parts[n], own_all, lanes, there, (up, down)[n]) for n in range(2)]

    def step_lanes(which):
        return pl.ds(pl.multiple_of(2 * STATE + which * LANES, LANES), LANES)

    every, bc_lanes, own_steps = pl.ds(0, share), pl.ds(0, 2 * STATE), pl.ds(2 * STATE, LANES)
    x_other = other_pieces(wx_ref, wx)
    x_other.append(Other(small_ref, ws, every, own_steps, step_lanes(half), step_lanes(1 - half), down))
    x_own = own_pieces(wx_ref, wx)
    x_own.append(Own(small_ref, ws, every, bc_lanes, bc_lanes, up))
    x_own.append(Own(small_ref, ws, every, own_steps, step_lanes(half), down))
    z_own = own_pieces(wz_ref, wz)
    z_other = other_pieces(wz_ref, wz)
    r_in = Rows(in_ref, rows)
    o_own = own_pieces(wo_ref, wo)
    o_other = other_pieces(wo_ref, wo)

    def advance(pieces):
        for piece in pieces:
            piece.advance()

    def normalise(src, start, count, scale):
        def body(i, carry):
            at = pl.ds(pl.multiple_of(start + i * 16, 16), 16)
            wide = src[pl.ds(pl.multiple_of(i * 16, 16), 16), :].astype(F32)
            inv = lax.rsqrt(jnp.sum(wide * wide, axis=1, keepdims=True) / model + EPS)
            normed[at, :] = (wide * inv * scale).astype(BF16)
            return carry

        lax.fori_loop(0, count // 16, body, 0, unroll=4 if count >= 64 else 1)

    def project(lhs, count, weight, out, width):
        tile = 256 if width % 256 == 0 else 3 * LANES
        steps = width // tile

        def out_copy(i):
            at = pl.ds(pl.multiple_of(i * tile, tile), tile)
            return pltpu.make_async_copy(
                stage.at[i % 2, pl.ds(0, count), pl.ds(0, tile)], out.at[:, at], stage_sem.at[i % 2]
            )

        def body(i, carry):
            @pl.when(i >= 2)
            def _():
                out_copy(i - 2).wait()

            at = pl.ds(pl.multiple_of(i * tile, tile), tile)
            block = weight[:, :, at].reshape(model, tile)
            stage[i % 2, 0:count, 0:tile] = dot_nn(lhs[...].reshape(count, model), block)
            out_copy(i).start()
            return carry

        lax.fori_loop(0, steps, body, 0)
        for i in range(max(steps - 2, 0), steps):
            out_copy(i).wait()

    def finish(pieces):
        for piece in pieces:
            piece.finish()

    def join_heads():
        def body(i, carry):
            low = ws[i, :, 2 * STATE : 2 * STATE + LANES].astype(F32)
            high = ws[i, :, 2 * STATE + LANES :].astype(F32)
            joined[i, :, : 2 * STATE] = ws[i, :, : 2 * STATE]
            joined[i, :, 2 * STATE :] = (low + pltpu.roll(high, own_width // HEADDIM, 1)).astype(BF16)
            return carry

        lax.fori_loop(0, ws.shape[0], body, 0)

    advance(x_own)
    arrive(gain_copies)
    settle(gain_kept)
    gain_share = model // heads
    scale = jnp.concatenate([gains[g, 0:1, 0:gain_share] for g in range(heads)], axis=1)
    gain_all[...] = jnp.broadcast_to(scale, (8, model))
    advance(x_other)
    advance(x_own)
    settle(r_in.kept)
    normalise(rows.at[mine], mine * own_rows, own_rows, scale)
    advance(x_other)
    advance(z_own)
    advance(z_other)
    advance(x_other)
    advance(z_own)
    advance(o_own)
    advance(z_other)
    finish(x_own)
    finish(x_other)
    join_heads()
    local(joined, ws_out)
    local(wx, wx_out)
    r_in.finish()
    tail = rows.at[sets - 1, pl.ds(own_rows - HALO, HALO), :]
    tail_copy = send(tail, halo, other_half)
    for i in range(1, sets):
        other = flip_all(mine, i)
        normalise(rows.at[other], other * own_rows, own_rows, scale)
    advance(o_other)
    advance(o_own)
    advance(z_other)
    tail_copy.wait_recv()
    normalise(halo, tokens, HALO, scale * half.astype(F32))
    local(normed, normed_out)
    project(normed, tokens + HALO, joined, s_out, s_out.shape[1])
    advance(o_other)
    project(normed, tokens + HALO, wx, x_out, wx.shape[2])
    finish(z_own)
    finish(z_other)
    local(wz, wz_out)
    advance(o_other)
    finish(o_own)
    finish(o_other)
    local(wo, wo_out)
    arrive([par_copy])
    settle(par_kept)
    local(pars, pars_out)
    local(gain_all, gains_out)
    for copy in list(open_local):
        settle(copy)
    for copy in sent:
        copy.wait_send()


def gather_and_project(block_in, gain, par, small, wx, wz, wo):
    tok_size, head_size = lax.axis_size("tok"), lax.axis_size("head")
    sets = head_size // HALVES
    tok_bits = range(tok_size.bit_length() - 1)
    row_bits = range(sets.bit_length() - 1)
    own_rows, model = block_in.shape
    share, own_width = wx.shape
    width = HALVES * own_width
    tokens = own_rows * sets
    lanes = 2 * STATE + HALVES * LANES
    anywhere = pl.BlockSpec(memory_space=pl.ANY)
    slots = (tok_size, share)
    copies = 16 * tok_size
    outs = [
        shape((tokens + HALO, width), F32),
        shape((tokens + HALO, 2 * STATE + LANES), F32),
        shape((tokens + HALO, model), BF16),
        shape(slots + (2 * STATE + LANES,), BF16),
        shape(slots + (width,), BF16),
        shape(slots + (width,), BF16),
        shape(slots + (width,), BF16),
        shape((8, model), F32),
        shape((8, width), F32),
    ]
    return pl.pallas_call(
        functools.partial(gather_kernel, tok_bits, row_bits, sets.bit_length() - 1),
        in_specs=[anywhere] * 7,
        out_specs=[anywhere] * len(outs),
        out_shape=outs,
        scratch_shapes=[
            pltpu.VMEM(slots + (lanes,), BF16),
            pltpu.VMEM(slots + (width,), BF16),
            pltpu.VMEM(slots + (width,), BF16),
            pltpu.VMEM(slots + (width,), BF16),
            pltpu.VMEM(slots + (2 * STATE + LANES,), BF16),
            pltpu.VMEM((sets, own_rows, model), BF16),
            pltpu.VMEM((HALO, model), BF16),
            pltpu.VMEM((tokens + HALO, model), BF16),
            pltpu.VMEM((head_size,) + gain.shape, F32),
            pltpu.VMEM((8, model), F32),
            pltpu.VMEM((8, width), F32),
            pltpu.VMEM((2, tokens + HALO, 3 * LANES), F32),
            pltpu.SemaphoreType.DMA((copies,)),
            pltpu.SemaphoreType.DMA((copies,)),
            pltpu.SemaphoreType.DMA((32,)),
            pltpu.SemaphoreType.DMA((2,)),
        ],
        name="gather",
        compiler_params=pltpu.CompilerParams(
            collective_id=0, has_side_effects=True, vmem_limit_bytes=60 * 1024 * 1024
        ),
        cost_estimate=pl.CostEstimate(flops=int(12e9), bytes_accessed=int(60e6), transcendentals=0),
    )(block_in, gain, par, small, wx, wz, wo)


def reduce_kernel(
    tok_bits, row_bits,
    gx_ref, to_ref, gs_ref, gl_ref, dx_ref, ds_ref, dz_ref, norm_ref, in_ref, wx_ref, wz_ref, ws_ref, cot_ref, gain_ref, per_ref, bc_ref,
    ox_ref, oo_ref, os_ref, dblock_ref, gain_out, rest_out,
    kx, ks, rx, rs, fx, ls, own_o, got_o, fo,
    dx, ds, dz, wx, wz, ws, norms, own_in, cots, dnorm, low, got, halo_out, halo_in, sums, sums_got, per_got, bc_got, bc_own,
    send_sem, recv_sem, local_sem,
):
    links = Links(send_sem, recv_sem, local_sem, tok_bits, row_bits)
    half, mine, sets = links.half, links.mine, links.sets
    own_rows, model = cot_ref.shape
    own_width = ox_ref.shape[1]
    tokens = own_rows * sets
    chunk = min(CHUNK, own_rows)
    loads = [
        links.local(src, dst)
        for src, dst in ((dx_ref, dx), (ds_ref, ds), (dz_ref, dz), (wx_ref, wx), (wz_ref, wz), (ws_ref, ws))
    ]
    links.enter()

    up = [0] + links.tok_bits[1:]
    down = [0] + links.tok_bits[1:][::-1]
    s_small = SmallSum(links, gs_ref, gl_ref, ks, ls, rs, up)
    s_x = [Sum(links, gx_ref, kx, rx, fx, ox_ref, p, 2, (down, up)[p]) for p in range(2)]

    def advance(group):
        for each in group:
            each.advance()

    advance(s_x)
    late_loads = [
        links.local(norm_ref.at[pl.ds(0, tokens)], norms), links.local(in_ref, own_in), links.local(cot_ref, cots)
    ]

    def project_back(at):
        lhs_x, lhs_s = dx[at, :], ds[at, :]
        return dot_nt(lhs_x, wx[...].reshape(model, wx.shape[2])) + dot_nt(lhs_s, ws[...].reshape(model, ws.shape[2]))

    def slot_rows(slot, first=0, count=None):
        def body(i, carry):
            here = pl.ds(pl.multiple_of(i * chunk, chunk), chunk)
            at = pl.ds(pl.multiple_of(slot * own_rows + i * chunk, chunk), chunk)
            gates = dot_nt(dz[at, :], wz[...].reshape(model, wz.shape[2]))
            dnorm[slot, here, :] = project_back(at) + gates
            return carry

        lax.fori_loop(first, own_rows // chunk if count is None else first + count, body, 0)

    def fold(slot):
        keep = jnp.where(half == 0, 1.0, 0.0) * jnp.where(slot == sets - 1, 1.0, 0.0)
        tail = pl.ds(own_rows - HALO, HALO)
        dnorm[slot, tail, :] = dnorm[slot, tail, :] + keep * halo_in[...]

    def rows_at(i, count):
        return pl.ds(pl.multiple_of(i * count, count), count)

    def gain_part(slot, start):
        def body(i, total):
            normed = norms[pl.ds(pl.multiple_of(slot * own_rows + i * 16, 16), 16), :].astype(F32)
            part = dnorm[slot, rows_at(i, 16), :] * normed
            return total + part[0:8] + part[8:16]

        return lax.fori_loop(0, own_rows // 16, body, start, unroll=2)

    everywhere, rest, owned = pl.ds(0, model), pl.ds(model, own_width + bc_ref.shape[1]), pl.ds(model, own_width)
    bc_lanes = pl.ds(model + own_width, bc_ref.shape[1])

    def channel_lanes(which):
        return pl.ds(pl.multiple_of(which * own_width, LANES), own_width)

    o_load = links.local(to_ref.at[:, channel_lanes(half)], own_o)
    early = [
        links.send(per_ref.at[:, channel_lanes(1 - half)], per_got, links.head_peer(links.half_bit)),
        links.send(bc_ref, bc_got.at[0], links.head_peer(links.half_bit)),
    ]

    o_tail = links.send(to_ref.at[:, channel_lanes(1 - half)], got_o, links.head_peer(links.half_bit))

    links.settle(loads)
    away = list(range(1, sets))[::-1]
    slots = [flip_all(mine, o) for o in away]
    early_rows = sets == 2 and own_rows > chunk
    pieces = own_rows // chunk
    row_pieces = []

    def lower(piece, slot):
        def body(i, carry):
            at = pl.ds(pl.multiple_of(piece * chunk + i * 32, 32), 32)
            low[0, at, :] = dnorm[slot, at, :].astype(BF16)
            return carry

        lax.fori_loop(0, chunk // 32, body, 0)

    def send_piece(piece):
        at = pl.ds(piece * chunk, chunk)
        row_pieces.append(links.send(low.at[0, at], got.at[0, at], links.head_peer(0)))

    if early_rows:
        slot_rows(slots[0], 0, 1)
        lower(0, slots[0])
    elif slots:
        slot_rows(slots[0])
    for copy in early:
        copy.wait_recv()
    sums[0, :, owned] = per_ref[:, channel_lanes(half)] + per_got[...]
    bc_total = bc_ref[...] + bc_got[0]
    for n, bit in enumerate(links.row_bits):
        bc_own[n] = bc_total
        bc_copy = links.send(bc_own.at[n], bc_got.at[n + 1], links.head_peer(bit))
        if not early_rows:
            bc_copy.wait_recv()
            bc_total = bc_total + bc_got[n + 1]
    halo_out[...] = project_back(pl.ds(tokens, HALO))
    if early_rows:
        send_piece(0)
    halo_copy = links.send(halo_out, halo_in, links.head_peer(links.half_bit))
    if early_rows:
        advance(s_x)
        advance([s_small])
        slot_rows(slots[0], 1, pieces - 1)
        bc_copy.wait_recv()
        bc_total = bc_ref[...] + bc_got[0] + bc_got[1]
    sums[0, :, bc_lanes] = bc_total
    for slot in slots[1:]:
        slot_rows(slot)
    halo_copy.wait_recv()
    for slot in slots:
        fold(slot)

    row_order = list(row_bits)[::-1]
    held = list(range(sets))
    places = 0

    def send_rows():
        nonlocal held, places
        bit = row_order.pop(0)
        stay = [o for o in held if not (o >> bit) & 1]
        copies = []
        for o in stay:
            slot = flip_all(mine, o ^ (1 << bit))

            def body(i, carry, slot=slot, place=places):
                low[place, rows_at(i, 32), :] = dnorm[slot, rows_at(i, 32), :].astype(BF16)
                return carry

            lax.fori_loop(0, own_rows // 32, body, 0)
            copies.append((o, places, bit))
            places += 1
        held = stay
        return copies

    def start_rows(copies):
        return [(o, p, links.send(low.at[p], got.at[p], links.head_peer(bit))) for o, p, bit in copies]

    def take_rows(copies):
        for o, place, copy in copies:
            copy.wait_recv()
            slot = flip_all(mine, o)

            def body(i, carry, slot=slot, place=place):
                at = rows_at(i, 32)
                dnorm[slot, at, :] = dnorm[slot, at, :] + got[place, at, :].astype(F32)
                return carry

            lax.fori_loop(0, own_rows // 32, body, 0)

    if early_rows:
        for piece in range(1, pieces):
            lower(piece, slots[0])
        row_order, row_copies = [], [(0, 0, None)]
        for piece in range(1, pieces):
            send_piece(piece)
    else:
        prepared = send_rows() if row_order else []
        advance([s_small])
        row_copies = start_rows(prepared)
    if not early_rows:
        advance(s_x)
    slot_rows(mine)
    if early_rows:
        advance(s_x)
    fold(mine)
    links.settle(late_loads)
    gain_sum = jnp.zeros((8, model), F32)
    for slot in slots + [mine]:
        gain_sum = gain_part(slot, gain_sum)
    gain = gain_ref[0:1, :]
    gain_row = jnp.sum(gain_sum, axis=0, keepdims=True) / gain

    sums[0, :, everywhere] = jnp.concatenate([gain_row, jnp.zeros((7, model), F32)], axis=0)
    advance([s_small])
    between = {0: s_x, 2: [s_small]} if not early_rows else {2: [s_small]}
    for n, bit in enumerate(tok_bits):
        copy = links.send(sums.at[n], sums_got.at[n], links.tok_peer(bit))
        advance(between.get(n, []))
        copy.wait_recv()
        sums[n + 1] = sums[n] + sums_got[n]
    n = len(tok_bits)
    links.local(sums.at[n, :, rest], rest_out)
    while not s_small.done:
        s_small.advance()

    def exchange_gain(bit):
        return links.send(sums.at[n, :, everywhere], sums_got.at[n, :, everywhere], links.head_peer(bit))

    def take_gain(copy):
        copy.wait_recv()
        sums[n + 1, :, everywhere] = sums[n, :, everywhere] + sums_got[n, :, everywhere]

    gain_copy = exchange_gain(links.half_bit)
    for each in s_x:
        while each.next < each.last:
            each.advance()

    while row_copies:
        if not row_order:
            break
        take_rows(row_copies)
        row_copies = start_rows(send_rows())
    for copy in row_pieces if early_rows else [copy for _, _, copy in row_copies]:
        copy.wait_recv()

    def block_rows(i, carry):
        at = rows_at(i, 32)
        wide = own_in[at, :].astype(F32)
        inv = lax.rsqrt(jnp.sum(wide * wide, axis=1, keepdims=True) / model + EPS)
        total = dnorm[mine, at, :]
        for _, place, _ in row_copies:
            total = total + got[place, at, :].astype(F32)
        scaled = total * gain
        inner = jnp.sum(scaled * wide, axis=1, keepdims=True) / model
        dnorm[mine, at, :] = cots[at, :].astype(F32) + inv * scaled - wide * (inv * inv * inv * inner)
        return carry

    lax.fori_loop(0, own_rows // 32, block_rows, 0)
    links.local(dnorm.at[mine], dblock_ref)
    take_gain(gain_copy)
    n += 1
    for bit in links.row_bits:
        gain_copy = exchange_gain(bit)
        if bit == links.row_bits[0]:
            s_small.finish()
        take_gain(gain_copy)
        n += 1
    if not links.row_bits:
        s_small.finish()
    links.local(sums.at[n, :, everywhere], gain_out)
    links.local(ks.at[0], os_ref)
    o_tail.wait_recv()
    links.settle([o_load])

    def o_rows(i, carry):
        at = rows_at(i, 32)
        fo[at, :] = own_o[at, :].astype(F32) + got_o[at, :].astype(F32)
        return carry

    lax.fori_loop(0, fo.shape[0] // 32, o_rows, 0)
    links.local(fo, oo_ref)
    for each in s_x:
        each.finish()
    for each in s_x:
        each.close()
    links.leave()


def reduce_sums(gx, to, gs, gl, dx, ds, dz, normed, block_in, wx, wz, ws, cot, gain, per, bc):
    tok_size, head_size = lax.axis_size("tok"), lax.axis_size("head")
    sets = head_size // HALVES
    tok_bits = range(tok_size.bit_length() - 1)
    row_bits = range(sets.bit_length() - 1)
    own_rows, model = cot.shape
    share, width = gx.shape[1:]
    lanes = gs.shape[2]
    own_width = width // HALVES
    anywhere = pl.BlockSpec(memory_space=pl.ANY)
    inside = pl.BlockSpec(memory_space=pltpu.VMEM)
    keep, slots = tok_size // 2, tok_size + len(row_bits)
    stages = len(tok_bits) + len(row_bits) + 1
    away = max(sets - 1, 1)
    copies = 32 * len(tok_bits)
    outs = [
        shape((share, own_width), F32),
        shape((share, own_width), F32),
        shape((share, lanes), F32),
        shape((own_rows, model), F32),
        shape((8, model), F32),
        shape((8, own_width + bc.shape[1]), F32),
    ]
    return pl.pallas_call(
        functools.partial(reduce_kernel, tok_bits, row_bits),
        in_specs=[anywhere] * 13 + [inside] * 3,
        out_specs=[anywhere] * len(outs),
        out_shape=outs,
        scratch_shapes=[pltpu.VMEM((keep, share, width), BF16)]
        + [pltpu.VMEM((keep, share, lanes), F32)]
        + [pltpu.VMEM((slots, share, width), BF16)]
        + [pltpu.VMEM((slots, share, lanes), BF16)]
        + [pltpu.VMEM((share, own_width), F32)]
        + [pltpu.VMEM((slots, share, lanes), BF16)]
        + [pltpu.VMEM((share, own_width), BF16)] * 2
        + [pltpu.VMEM((share, own_width), F32)]
        + [
            pltpu.VMEM(dx.shape, BF16),
            pltpu.VMEM(ds.shape, BF16),
            pltpu.VMEM(dz.shape, BF16),
            pltpu.VMEM(wx.shape, BF16),
            pltpu.VMEM(wz.shape, BF16),
            pltpu.VMEM(ws.shape, BF16),
            pltpu.VMEM((own_rows * sets, model), BF16),
            pltpu.VMEM(cot.shape, BF16),
            pltpu.VMEM(cot.shape, BF16),
            pltpu.VMEM((sets, own_rows, model), F32),
            pltpu.VMEM((away, own_rows, model), BF16),
            pltpu.VMEM((away, own_rows, model), BF16),
            pltpu.VMEM((HALO, model), F32),
            pltpu.VMEM((HALO, model), F32),
            pltpu.VMEM((stages + 1, 8, model + own_width + bc.shape[1]), F32),
            pltpu.VMEM((stages, 8, model + own_width + bc.shape[1]), F32),
            pltpu.VMEM((8, own_width), F32),
            pltpu.VMEM((len(row_bits) + 1,) + bc.shape, F32),
            pltpu.VMEM((max(len(row_bits), 1),) + bc.shape, F32),
            pltpu.SemaphoreType.DMA((copies,)),
            pltpu.SemaphoreType.DMA((copies,)),
            pltpu.SemaphoreType.DMA((copies,)),
        ],
        name="reduce",
        compiler_params=pltpu.CompilerParams(
            collective_id=1, has_side_effects=True, vmem_limit_bytes=62 * 1024 * 1024
        ),
        cost_estimate=pl.CostEstimate(flops=int(12e9), bytes_accessed=int(60e6), transcendentals=0),
    )(gx, to, gs, gl, dx, ds, dz, normed, block_in, wx, wz, ws, cot, gain, per, bc)


def per_device(
    block_in,
    norm_gain,
    w_zx,
    w_bc,
    w_dt,
    conv_x_w,
    conv_x_b,
    conv_bc_w,
    conv_bc_b,
    dt_bias,
    a_log,
    d_skip,
    gate_gain,
    w_out,
    cotangent,
):
    head_size = lax.axis_size("head")
    tok_size = lax.axis_size("tok")
    sets = head_size // HALVES
    row_bits = range(sets.bit_length() - 1)
    half_bit = sets.bit_length() - 1
    half = bit_of("head", half_bit)
    own_rows, model = block_in.shape
    share, _, own_width = w_zx.shape
    own_heads = w_dt.shape[1]
    tokens = own_rows * sets

    def all_rows(value):
        for bit in row_bits:
            value = grow(value, "head", bit, 0)
        return value

    def lane_pad(v):
        return jnp.pad(v, (0, LANES - v.shape[0]))

    heads_row = jnp.concatenate([lane_pad(dt_bias), lane_pad(a_log), lane_pad(d_skip)])
    own_par = jnp.concatenate(
        [
            conv_x_w,
            conv_x_b[None],
            gate_gain[None],
            jnp.repeat(d_skip, HEADDIM)[None],
            jnp.pad(heads_row, (0, own_width - heads_row.shape[0]))[None],
        ]
    )
    gain_share = norm_gain.shape[0]
    own_gain = jnp.broadcast_to(
        jnp.pad(norm_gain.astype(F32), (0, -gain_share % LANES))[None], (8, gain_share + -gain_share % LANES)
    )
    small = jnp.concatenate([w_bc, jnp.pad(w_dt, ((0, 0), (0, LANES - own_heads)))], axis=1)
    x_ext, s_ext, normed_ext, w_small, w_x, w_z, w_o, gain, par = gather_and_project(
        block_in, own_gain, own_par, small, w_zx[:, 1], w_zx[:, 0], w_out.T
    )
    later_cot, x_ext = lax.optimization_barrier((cotangent, x_ext))
    cot = all_rows(later_cot)
    gain = gain[0:1]
    normed = normed_ext[:tokens]
    slots_small, slots_x, slots_z, gain_rows = w_small, w_x, w_z, gain
    w_z, w_o = w_z.reshape(model, w_z.shape[2]), w_o.reshape(model, w_o.shape[2])

    def of_heads(start):
        pieces = [
            par[CONV + 3, i * own_width + start : i * own_width + start + own_heads] for i in range(HALVES)
        ]
        return jnp.concatenate(pieces)

    rate = -jnp.exp(of_heads(LANES))
    hp = jnp.stack([lane_pad(of_heads(0)), lane_pad(rate)] + [jnp.zeros((LANES,), F32)] * 6)
    bcpar = jnp.concatenate([conv_bc_w, conv_bc_b[None], jnp.zeros((3, 2 * STATE), F32)])

    xs, u, cume, dte, dsil, bc, cumt, sloc, fin, sdec = mixer_forward_state(x_ext, s_ext, par, bcpar, hp, tokens)
    to_next = [(i, i + sets) for i in range(sets)]
    to_prev = [(i + sets, i) for i in range(sets)]
    sin = lax.ppermute(fin, "head", to_next)
    z = dot_nn(normed, w_z)
    gyn = dot_nn(cot, w_o)
    y, stat = mixer_forward_main(xs, u, cume, cumt, bc, sloc, sin, sdec, z, gyn, par)
    stat = add_pairs(stat, "head", row_bits).T
    inv_gate = lax.rsqrt(stat[:, 0:1] / INNER + EPS)
    stat = jnp.concatenate(
        [inv_gate, inv_gate * inv_gate * inv_gate * stat[:, 1:2] / INNER, stat[:, 2:]], axis=1
    )
    yn, gy, dz, gloc, gin, gdec, acc_gate = mixer_backward_gate(y, z, gyn, cume, bc, stat, par)
    gout = lax.ppermute(gin, "head", to_prev)

    def own_row_sum(value):
        for bit in list(row_bits)[::-1]:
            value = halve(value, "head", bit, 0)
        return value

    def slots_of(grad):
        return grad.astype(BF16).reshape(tok_size, share, grad.shape[1])

    branch = dot_nt(yn, w_o)
    block_out = block_in.astype(F32) + own_row_sum(branch)
    grad_o = slots_of(dot_tn(cot, yn))
    grad_z = slots_of(dot_tn(normed, dz))
    dx, ds, acc_x, acc_b, acc_h, d_w_z, tail_o = mixer_backward_main(
        x_ext, s_ext, par, bcpar, hp, cume, dte, xs, dsil, u, cumt, gy, sloc, sin, sdec, gloc, gout, gdec, grad_z, grad_o
    )
    grad_x = slots_of(dot_tn(normed_ext, dx))
    grad_small = dot_tn(normed_ext, ds).reshape(tok_size, share, ds.shape[1])

    per_channel = jnp.concatenate(
        [
            acc_x[: CONV + 1],
            acc_gate[0:1],
            jnp.concatenate(
                [
                    jnp.pad(
                        jnp.concatenate(
                            [
                                lane_pad(acc_h[0, i * own_heads : (i + 1) * own_heads]),
                                lane_pad(acc_h[1, i * own_heads : (i + 1) * own_heads]),
                                lane_pad(
                                    jnp.sum(
                                        acc_x[CONV + 1, i * own_width : (i + 1) * own_width].reshape(own_heads, HEADDIM),
                                        axis=1,
                                    )
                                ),
                            ]
                        ),
                        (0, own_width - 3 * LANES),
                    )
                    for i in range(HALVES)
                ]
            )[None],
            jnp.zeros((1, HALVES * own_width), F32),
        ]
    )

    d_w_x, d_w_o, d_small, d_block_in, gain_sums, own_sums = reduce_sums(
        grad_x, tail_o, grad_small, grad_small.astype(BF16), dx, ds, dz, normed_ext, block_in, slots_x, slots_z, slots_small, cotangent,
        gain_rows, per_channel, acc_b,
    )
    all_gain, bc_sums = gain_sums[0], own_sums[:, own_width:]
    own_sums = own_sums[:, :own_width]
    d_w_bc = d_small[:, : 2 * STATE]
    d_w_dt = jnp.where(
        half == 0,
        d_small[:, 2 * STATE : 2 * STATE + own_heads],
        d_small[:, 2 * STATE + own_heads : 2 * STATE + 2 * own_heads],
    )
    d_norm_gain = lax.dynamic_slice_in_dim(all_gain, lax.axis_index("head") * gain_share, gain_share, 0)
    return (
        block_out,
        d_block_in,
        d_norm_gain,
        jnp.stack([d_w_z, d_w_x], axis=1),
        d_w_bc,
        d_w_dt,
        own_sums[:CONV],
        own_sums[CONV],
        bc_sums[:CONV],
        bc_sums[CONV],
        own_sums[CONV + 2, :own_heads],
        own_sums[CONV + 2, LANES : LANES + own_heads],
        own_sums[CONV + 2, 2 * LANES : 2 * LANES + own_heads],
        own_sums[CONV + 1],
        d_w_o.T,
    )


def solution(mesh):
    placed = (
        P(("tok", "head"), None),
        P("head"),
        P("tok", None, "head"),
        P("tok", None),
        P("tok", "head"),
        P(None, "head"),
        P("head"),
        P(),
        P(),
        P("head"),
        P("head"),
        P("head"),
        P("head"),
        P("head", "tok"),
        P(("tok", "head"), None),
    )
    return jax.shard_map(
        per_device,
        mesh=mesh,
        in_specs=placed,
        out_specs=(
            P(("tok", "head"), None),
            P(("tok", "head"), None),
            P("head"),
            P("tok", None, "head"),
            P("tok", None),
            P("tok", "head"),
            P(None, "head"),
            P("head"),
            P(),
            P(),
            P("head"),
            P("head"),
            P("head"),
            P("head"),
            P("head", "tok"),
        ),
        check_vma=False,
    )
```

```python
import functools

import jax
import jax.numpy as jnp
from jax import lax
from jax.experimental import pallas as pl
from jax.experimental.pallas import tpu as pltpu
from jax.sharding import PartitionSpec as P

HEADDIM = 64
STATE = 128
CONV = 4
INNER = 3072
CHUNK = 256
HALVES = 2
LANES = 128
HALO = 16

EPS = 1e-05
LOG2E = 1.4426950408889634
HIGHEST = lax.Precision.HIGHEST
F32 = jnp.float32
BF16 = jnp.bfloat16


def dot_nn(a, b, precision=None):
    return lax.dot_general(
        a, b, (((1,), (0,)), ((), ())), preferred_element_type=F32, precision=precision
    )


def dot_nt(a, b, precision=None):
    return lax.dot_general(
        a, b, (((1,), (1,)), ((), ())), preferred_element_type=F32, precision=precision
    )


def dot_tn(a, b):
    return lax.dot_general(a, b, (((0,), (0,)), ((), ())), preferred_element_type=F32)


def dot_split(a, b):
    a_top, b_top = a.astype(BF16), b.astype(BF16)
    a_rest = (a - a_top.astype(F32)).astype(BF16)
    b_rest = (b - b_top.astype(F32)).astype(BF16)
    return dot_nn(a_top, b_top) + (dot_nn(a_rest, b_top) + dot_nn(a_top, b_rest))


def iota(shape, dim):
    return lax.broadcasted_iota(jnp.int32, shape, dim)


def sigmoid(v):
    return 0.5 + 0.5 * jnp.tanh(0.5 * v)


def softplus(v):
    return jnp.maximum(v, 0.0) + jnp.log1p(jnp.exp(-jnp.abs(v)))


def thirds(a):
    top = a.astype(BF16)
    rest = a - top.astype(F32)
    middle = rest.astype(BF16)
    return top, middle, (rest - middle.astype(F32)).astype(BF16)


def sums_of(zero_one, a):
    width = a.shape[1]
    wide = dot_nn(zero_one, jnp.concatenate(thirds(a), axis=1))
    return wide[:, 0:width] + wide[:, width : 2 * width] + wide[:, 2 * width :]


def bit_of(axis, bit):
    return (lax.axis_index(axis) // (1 << bit)) % 2


def swap(value, axis, bit):
    size = lax.axis_size(axis)
    return lax.ppermute(value, axis, [(i, i ^ (1 << bit)) for i in range(size)])


def grow(value, axis, bit, dim):
    other = swap(value, axis, bit)
    low = bit_of(axis, bit) == 0
    return jnp.where(
        low,
        jnp.concatenate([value, other], dim),
        jnp.concatenate([other, value], dim),
    )


def halve(value, axis, bit, dim):
    mine = bit_of(axis, bit)
    if dim < value.ndim - 1:
        half = value.shape[dim] // 2
        keep = lax.dynamic_slice_in_dim(value, mine * half, half, dim)
        send = lax.dynamic_slice_in_dim(value, (1 - mine) * half, half, dim)
    else:
        low, high = jnp.split(value, 2, axis=dim)
        keep = jnp.where(mine == 0, low, high)
        send = jnp.where(mine == 0, high, low)
    return keep.astype(F32) + swap(send.astype(BF16), axis, bit).astype(F32)


def add_pairs(value, axis, bits):
    for bit in bits:
        value = value + swap(value, axis, bit)
    return value


MESH = pl.DeviceIdType.MESH


def flip(index, bit):
    return index + (1 - 2 * ((index // (1 << bit)) % 2)) * (1 << bit)


def flip_all(index, offset):
    bit = 0
    while offset >> bit:
        if (offset >> bit) & 1:
            index = flip(index, bit)
        bit += 1
    return index


def now(value):
    return value() if callable(value) else value


class Remote:
    def __init__(self, links, k, src, dst, device):
        self.links, self.k, self.src, self.dst, self.device = links, k, src, dst, device

    def make(self):
        return pltpu.make_async_remote_copy(
            src_ref=now(self.src),
            dst_ref=now(self.dst),
            send_sem=self.links.send_sem.at[self.k],
            recv_sem=self.links.recv_sem.at[self.k],
            device_id=now(self.device),
            device_id_type=MESH,
        )

    def start(self):
        self.make().start()

    def wait_recv(self):
        self.make().wait_recv()

    def wait_send(self):
        self.make().wait_send()


class Local:
    def __init__(self, links, k, src, dst):
        self.links, self.k, self.src, self.dst = links, k, src, dst

    def make(self):
        return pltpu.make_async_copy(now(self.src), now(self.dst), self.links.local_sem.at[self.k])

    def start(self):
        self.make().start()

    def wait(self):
        self.make().wait()


class Links:
    def __init__(self, send_sem, recv_sem, local_sem, tok_bits, row_bits):
        self.send_sem, self.recv_sem, self.local_sem = send_sem, recv_sem, local_sem
        self.tok_bits, self.row_bits = list(tok_bits), list(row_bits)
        self.tok, self.head = lax.axis_index("tok"), lax.axis_index("head")
        self.sets = 1 << len(self.row_bits)
        self.half, self.mine = self.head // self.sets, self.head % self.sets
        self.half_bit = len(self.row_bits)
        self.sent, self.drained, self.n_local, self.open_local = [], [], 0, []

    def enter(self):
        partners = [self.tok_peer(b) for b in self.tok_bits]
        partners += [self.head_peer(b) for b in self.row_bits + [self.half_bit]]
        barrier = pltpu.get_barrier_semaphore()
        for partner in partners:
            pl.semaphore_signal(barrier, inc=1, device_id=partner(), device_id_type=MESH)
        pl.semaphore_wait(barrier, len(partners))

    def tok_peer(self, bit):
        return lambda: {"tok": flip(self.tok, bit)}

    def head_peer(self, bit):
        return lambda: {"head": flip(self.head, bit)}

    def plan_send(self, src, dst, device):
        copy = Remote(self, len(self.sent), src, dst, device)
        self.sent.append(copy)
        return copy

    def send(self, src, dst, device):
        copy = self.plan_send(src, dst, device)
        copy.start()
        return copy

    def plan_local(self, src, dst):
        self.n_local += 1
        return Local(self, self.n_local - 1, src, dst)

    def local(self, src, dst):
        copy = self.plan_local(src, dst)
        copy.start()
        self.open_local.append(copy)
        return copy

    def settle(self, copies):
        for copy in copies:
            if any(copy is other for other in self.open_local):
                self.open_local = [other for other in self.open_local if other is not copy]
                copy.wait()

    def drain(self, copy):
        copy.wait_recv()
        copy.wait_send()
        self.drained.append(copy)

    def leave(self):
        self.settle(list(self.open_local))
        for copy in self.sent:
            if not any(copy is other for other in self.drained):
                copy.wait_send()


def add_rows(dst, src, count):
    def body(i, carry):
        at = pl.ds(pl.multiple_of(i * 16, 16), 16)
        dst[at, :] = (dst[at, :].astype(F32) + src[at, :].astype(F32)).astype(BF16)
        return carry

    lax.fori_loop(0, count // 16, body, 0)


class Sum:
    def __init__(self, links, src, keep, recv, final, out, part, parts, order):
        self.links, self.src, self.keep, self.recv, self.final = links, src, keep, recv, final
        self.size = keep.shape[1] // parts
        self.start = part * self.size
        self.width = out.shape[1]
        self.whole = final is not None
        held = list(range(1 << len(links.tok_bits)))
        self.sends, self.adds, base = [], [], 0
        for number, bit in enumerate(order):
            stay = [o for o in held if not (o >> bit) & 1]
            if number == 0:
                place = {o: i for i, o in enumerate(stay)}
                self.loads = [links.plan_local(self.source(o), self.slot(place[o])) for o in stay]
            sends, adds = [], []
            for n, o in enumerate(stay):
                away = o ^ (1 << bit)
                src_ref = self.source(away) if number == 0 else self.slot(place[away])
                sends.append(links.plan_send(src_ref, self.landing(base + n), links.tok_peer(bit)))
                adds.append((place[o], base + n))
            base += len(stay)
            held = stay
            self.sends.append(sends)
            self.adds.append(adds)
        self.base = base
        if self.whole:
            self.tail = links.plan_send(
                lambda: self.keep.at[0, self.rows(), self.half_lanes(1 - self.links.half)],
                lambda: self.recv.at[base, self.rows(), pl.ds(0, self.width)],
                links.head_peer(links.half_bit),
            )
            self.store = links.plan_local(lambda: final.at[self.rows()], lambda: out.at[self.rows()])
        else:
            self.store = links.plan_local(self.slot(0), lambda: out.at[self.rows()])
        self.next = 0
        self.last = len(self.sends) + self.whole

    def rows(self):
        return pl.ds(self.start, self.size)

    def source(self, offset):
        return lambda: self.src.at[flip_all(self.links.tok, offset), self.rows()]

    def landing(self, i):
        return lambda: self.recv.at[i, self.rows()]

    def slot(self, i):
        return lambda: self.keep.at[i, self.rows()]

    def half_lanes(self, which):
        return pl.ds(pl.multiple_of(which * self.width, LANES), self.width)

    def step(self, k):
        if k == 0:
            for copy in self.sends[0] + self.loads:
                copy.start()
            return
        if k == self.last and self.whole:
            self.tail.wait_recv()
            lanes = self.half_lanes(self.links.half)

            def body(i, carry):
                at = pl.ds(pl.multiple_of(self.start + i * 16, 16), 16)
                self.final[at, :] = self.keep[0, at, lanes].astype(F32) + self.recv[
                    self.base, at, 0 : self.width
                ].astype(F32)
                return carry

            lax.fori_loop(0, self.size // 16, body, 0)
            self.store.start()
            return
        for copy in self.sends[k - 1]:
            copy.wait_recv()
        if k == 1:
            for copy in self.loads:
                copy.wait()
        for place, i in self.adds[k - 1]:
            add_rows(now(self.slot(place)), now(self.landing(i)), self.size)
        if k < len(self.sends):
            for copy in self.sends[k]:
                copy.start()
        elif self.whole:
            self.tail.start()
        else:
            self.store.start()

    def advance(self):
        if self.next < self.last:
            self.step(self.next)
            self.next += 1

    def finish(self):
        while self.next <= self.last:
            self.step(self.next)
            self.next += 1

    def close(self):
        self.store.wait()


class SmallSum(Sum):
    def __init__(self, links, src, src_low, keep, low, recv, order):
        self.links, self.keep, self.low, self.recv = links, keep, low, recv
        self.order = list(order)
        bit = self.order.pop(0)
        slots = range(1 << len(links.tok_bits))
        self.held = [o for o in slots if not (o >> bit) & 1]
        self.place = {o: i for i, o in enumerate(self.held)}
        self.base = len(self.held)
        self.n_low = 0
        self.into = [(i, i) for i in range(self.base)]
        self.flight = [
            links.send(src_low.at[flip_all(links.tok, o ^ (1 << bit))], recv.at[self.place[o]], links.tok_peer(bit))
            for o in self.held
        ]
        self.kept = [links.local(src.at[flip_all(links.tok, o)], keep.at[self.place[o]]) for o in self.held]
        self.done = False

    def post(self, place, lanes, device):
        n = self.n_low
        self.low[n, :, 0:lanes] = self.keep[place, :, 0:lanes].astype(BF16)
        self.n_low += 1
        src, dst = self.low.at[n, :, pl.ds(0, lanes)], self.recv.at[self.base, :, pl.ds(0, lanes)]
        self.flight.append(self.links.send(src, dst, device))
        self.base += 1
        return self.base - 1

    def take(self):
        for copy in self.flight:
            copy.wait_recv()
        self.links.settle(self.kept)
        for place, i in self.into:
            self.keep[place, :, 0 : self.lanes_in] = self.keep[place, :, 0 : self.lanes_in] + self.recv[
                i, :, 0 : self.lanes_in
            ].astype(F32)
        self.flight, self.into, self.kept = [], [], []

    lanes_in = 2 * STATE + LANES

    def advance(self):
        if self.done:
            return
        self.take()
        if not self.order:
            self.into = [(0, self.post(0, self.lanes_in, self.links.head_peer(self.links.half_bit)))]
            self.done = True
            return
        bit = self.order.pop(0)
        stay = [o for o in self.held if not (o >> bit) & 1]
        self.into = [
            (self.place[o], self.post(self.place[o ^ (1 << bit)], self.lanes_in, self.links.tok_peer(bit)))
            for o in stay
        ]
        self.held = stay

    def finish(self):
        while not self.done:
            self.advance()
        self.take()
        self.lanes_in = 2 * STATE
        for bit in self.links.row_bits:
            self.into = [(0, self.post(0, self.lanes_in, self.links.head_peer(bit)))]
            self.take()


def conv_rows(cur, tail, weight, bias):
    rows = cur.shape[0]
    ext = jnp.concatenate([tail, cur], axis=0)
    out = bias + weight[CONV - 1 : CONV] * cur
    for k in range(CONV - 1):
        start = 8 - (CONV - 1) + k
        out = out + weight[k : k + 1] * ext[start : start + rows]
    return out


def state_kernel(
    xm_ref, xt_ref, bm_ref, bt_ref, par_ref, bcpar_ref, hp_ref,
    xs_ref, u_ref, cume_ref, dte_ref, dsil_ref, bc_ref, cumt_ref, sloc_ref, fin_ref, dec_ref,
    state, dsum, ue, spread,
):
    c = pl.program_id(0)
    q, width = xm_ref.shape

    @pl.when(c == 0)
    def _():
        state[...] = jnp.zeros_like(state)
        dsum[...] = jnp.zeros_like(dsum)
        row = iota((3 * LANES, width), 0) % LANES
        spread[...] = jnp.where(iota((3 * LANES, width), 1) // HEADDIM == row, 1.0, 0.0).astype(BF16)

    dt = softplus(bm_ref[:, 2 * STATE :] + hp_ref[0:1, :])
    tri = jnp.where(iota((q, q), 0) >= iota((q, q), 1), 1.0, 0.0).astype(BF16)
    cum = sums_of(tri, dt * (hp_ref[1:2, :] * LOG2E))
    cumt_ref[...] = cum.T[: cumt_ref.shape[0], :]
    cume_ref[...] = dot_nn(jnp.concatenate(thirds(cum), axis=1), spread[...])
    dte_ref[...] = dot_nn(jnp.concatenate(thirds(dt), axis=1), spread[...])
    end = cume_ref[q - 1 : q, :]

    bpre = conv_rows(
        bm_ref[:, : 2 * STATE], bt_ref[:, : 2 * STATE], bcpar_ref[0:CONV, :], bcpar_ref[CONV : CONV + 1, :]
    )
    bc_ref[...] = bpre * sigmoid(bpre)

    block = 2 * LANES

    def body(i, carry):
        sl = pl.ds(pl.multiple_of(i * block, block), block)
        pre = conv_rows(
            xm_ref[:, sl], xt_ref[:, sl], par_ref[0:CONV, sl], par_ref[CONV : CONV + 1, sl]
        )
        sig = sigmoid(pre)
        xs = pre * sig
        u = xs * dte_ref[:, sl]
        xs_ref[:, sl] = xs
        dsil_ref[:, sl] = sig * (1.0 + pre * (1.0 - sig))
        u_ref[:, sl] = u.astype(BF16)
        cume = cume_ref[:, sl]
        ue[:, sl] = (u * jnp.exp2(cume[q - 1 : q, :] - cume)).astype(BF16)
        return carry

    lax.fori_loop(0, width // block, body, 0)
    sloc_ref[0] = state[...]
    dec_ref[0] = jnp.exp2(dsum[...])
    state[...] = jnp.exp2(end) * state[...] + dot_nn(bc_ref[:, :STATE].T.astype(BF16), ue[...])
    dsum[...] = dsum[...] + end
    fin_ref[...] = state[...].astype(BF16)


def main_kernel(
    xs_ref, u_ref, cume_ref, cumt_ref, bc_ref, sloc_ref, sin_ref, dec_ref, z_ref, gyn_ref, par_ref,
    y_ref, stat_ref,
    gram, ya, acc_sq, acc_in,
):
    q, width = xs_ref.shape
    bmat = bc_ref[:, :STATE].astype(BF16)
    cmat = bc_ref[:, STATE:].astype(BF16)
    lower = iota((q, q), 0) >= iota((q, q), 1)
    gram[...] = jnp.where(lower, dot_nt(cmat, bmat), 0.0)
    entering = sloc_ref[0] + dec_ref[0, 0:1, :] * sin_ref[...].astype(F32)
    ya[...] = dot_nn(cmat, entering.astype(BF16))
    acc_sq[...] = jnp.zeros_like(acc_sq)
    acc_in[...] = jnp.zeros_like(acc_in)
    first = iota((q, LANES), 1) < HEADDIM
    hq = q // 2

    def body(p, carry):
        sl = pl.ds(pl.multiple_of(p * LANES, LANES), LANES)
        cume = cume_ref[:, sl]
        u = u_ref[:, sl]
        y = jnp.exp2(cume) * ya[:, sl] + par_ref[CONV + 2 : CONV + 3, sl] * xs_ref[:, sl]
        low_y, high_y = y[:hq], y[hq:]
        for s in range(2):
            column = cume[:, HEADDIM * s : HEADDIM * s + 1]
            row = cumt_ref[pl.ds(2 * p + s, 1), :]
            mine = jnp.where(first == (s == 0), u, jnp.zeros_like(u))
            gap = column[:hq] - row[:, :hq]
            pairs = (gram[:hq, :hq] * jnp.exp2(jnp.minimum(gap, 0.0))).astype(BF16)
            low_y = low_y + dot_nn(pairs, mine[:hq])
            gap = column[hq:] - row
            pairs = (gram[hq:, :] * jnp.exp2(jnp.minimum(gap, 0.0))).astype(BF16)
            high_y = high_y + dot_nn(pairs, mine)
        y = jnp.concatenate([low_y, high_y], axis=0)
        y_ref[:, sl] = y
        z = z_ref[:, sl]
        gated = y * z * sigmoid(z)
        acc_sq[...] += gated * gated
        acc_in[...] += gated * gyn_ref[:, sl] * par_ref[CONV + 1 : CONV + 2, sl]
        return carry

    lax.fori_loop(0, width // LANES, body, 0)
    ones = jnp.ones((8, LANES), F32)
    sums_sq = dot_nt(ones, acc_sq[...], HIGHEST)
    sums_in = dot_nt(ones, acc_in[...], HIGHEST)
    stat_ref[...] = jnp.where(iota(sums_sq.shape, 0) == 0, sums_sq, sums_in)


def gate_kernel(
    y_ref, z_ref, gyn_ref, cume_ref, bc_ref, stat_ref, par_ref,
    yn_ref, gy_ref, dz_ref, gloc_ref, gin_ref, dec_ref, acc_ref,
    adj, dsum, ge,
):
    q, width = y_ref.shape

    @pl.when(pl.program_id(0) == 0)
    def _():
        adj[...] = jnp.zeros_like(adj)
        dsum[...] = jnp.zeros_like(dsum)
        acc_ref[...] = jnp.zeros_like(acc_ref)

    end = cume_ref[q - 1 : q, :]
    inv = jnp.broadcast_to(stat_ref[:, 0:1], (q, LANES))
    back = jnp.broadcast_to(stat_ref[:, 1:2], (q, LANES))

    def body(p, carry):
        sl = pl.ds(pl.multiple_of(p * LANES, LANES), LANES)
        y, z, gyn = y_ref[:, sl], z_ref[:, sl], gyn_ref[:, sl]
        sig = sigmoid(z)
        sil = z * sig
        gated = y * sil
        gain = par_ref[CONV + 1 : CONV + 2, sl]
        unit = gated * inv
        yn_ref[:, sl] = (unit * gain).astype(BF16)
        d_gated = inv * gyn * gain - gated * back
        gy = d_gated * sil
        gy_ref[:, sl] = gy.astype(BF16)
        dz_ref[:, sl] = (d_gated * y * (sig * (1.0 + z * (1.0 - sig)))).astype(BF16)
        ge[:, sl] = (gy * jnp.exp2(cume_ref[:, sl])).astype(BF16)
        acc_ref[0:1, sl] += jnp.sum(gyn * unit, axis=0, keepdims=True)
        return carry

    lax.fori_loop(0, width // LANES, body, 0)
    gloc_ref[0] = adj[...]
    dec_ref[0] = jnp.exp2(dsum[...])
    adj[...] = jnp.exp2(end) * adj[...] + dot_nn(bc_ref[:, STATE:].T.astype(BF16), ge[...])
    dsum[...] = dsum[...] + end
    gin_ref[...] = adj[...].astype(BF16)


def back_kernel(
    tok_bits, row_bits,
    xm_ref, xt_ref, bm_ref, bt_ref, par_ref, bcpar_ref, hp_ref,
    cume_ref, dte_ref, xs, dsil, u, cumt_ref, gy_ref, sloc_ref, sin_ref, sdec_ref, gloc_ref, gout_ref, gdec_ref,
    gz_ref, go_ref,
    dx_ref, ds_ref, accx_ref, accb_ref, acch_ref, oz_ref, oo_ref,
    ue, ge, dus, ya, qx, qb, gram, dgram, da, acc_x, acc_w, acc_g, acc_k, kept,
    kz, ko, rz, ro, fz, send_sem, recv_sem, local_sem,
):
    step = pl.program_id(0)
    q, width = xm_ref.shape
    tokens = dx_ref.shape[0] - HALO
    steps = tokens // q
    links = Links(send_sem, recv_sem, local_sem, tok_bits, row_bits)
    up = [0] + links.tok_bits[1:]
    down = [0] + links.tok_bits[1:][::-1]
    groups = [
        [Sum(links, gz_ref, kz, rz, fz, oz_ref, p, 2, (down, up)[p]) for p in range(2)],
        [Sum(links, go_ref, ko, ro, None, oo_ref, p, 2, (down, up)[p]) for p in range(2)],
    ]
    plans = [[(0, 0), (0, 2), (1, 2), (2, 3)], [(0, 0), (0, 3), (2, 2)]]

    def go_on(point):
        for when in range(steps):

            @pl.when(step == when)
            def _():
                if (when, point) == (0, 0):
                    links.enter()
                for group, plan in zip(groups, plans):
                    for k, (number, place) in enumerate(plan):
                        if (min(number, steps - 1), place) == (when, point):
                            for each in group:
                                each.step(k)
                if (when, point) == (steps - 1, 3):
                    for group, plan in list(zip(groups, plans))[::-1]:
                        for k in range(len(plan), group[0].last + 1):
                            for each in group:
                                each.step(k)
                    for group in groups:
                        for each in group:
                            each.close()
                    links.leave()

    go_on(0)
    c = tokens // q - 1 - step
    block = 2 * LANES

    @pl.when(step == 0)
    def _():
        accx_ref[...] = jnp.zeros_like(accx_ref)
        accb_ref[...] = jnp.zeros_like(accb_ref)
        acch_ref[...] = jnp.zeros_like(acch_ref)
        qx[q:, :] = jnp.zeros((8, width), F32)
        qb[q:, :] = jnp.zeros((8, 2 * STATE), F32)
        da[...] = jnp.zeros_like(da)
        ds_ref[...] = jnp.zeros_like(ds_ref)

    bpre = conv_rows(
        bm_ref[:, : 2 * STATE], bt_ref[:, : 2 * STATE], bcpar_ref[0:CONV, :], bcpar_ref[CONV : CONV + 1, :]
    )
    bsig = sigmoid(bpre)
    bc = bpre * bsig
    qb[0:q, :] = bsig * (1.0 + bpre * (1.0 - bsig))
    bmat, cmat = bc[:, :STATE].astype(BF16), bc[:, STATE:].astype(BF16)

    def conv_body(i, carry):
        sl = pl.ds(pl.multiple_of(i * block, block), block)
        x = xs[:, sl]
        uu = x * dte_ref[:, sl]
        cume = cume_ref[:, sl]
        ue[:, sl] = (uu * jnp.exp2(cume[q - 1 : q, :] - cume)).astype(BF16)
        gy = gy_ref[:, sl].astype(F32)
        ge[:, sl] = (gy * jnp.exp2(cume)).astype(BF16)
        accx_ref[CONV + 1 : CONV + 2, sl] += jnp.sum(gy * x, axis=0, keepdims=True)
        return carry

    lax.fori_loop(0, width // block, conv_body, 0)
    go_on(1)

    last = cume_ref[q - 1 : q, :]
    adj = gloc_ref[0] + gdec_ref[0, 0:1, :] * gout_ref[...].astype(F32)
    entering = sloc_ref[0] + sdec_ref[0, 0:1, :] * sin_ref[...].astype(F32)
    kept_parts = thirds(jnp.exp2(last) * jnp.sum(adj * entering, axis=0, keepdims=True))
    kept[...] = jnp.concatenate(list(kept_parts) + [jnp.zeros((13, width), BF16)], axis=0)
    adj_low, ent_low = adj.astype(BF16), entering.astype(BF16)
    dus[...] = dot_nn(bmat, adj_low)
    ya[...] = dot_nn(cmat, ent_low)
    db = dot_nt(ue[...], adj_low)
    dc = dot_nt(ge[...], ent_low)
    upper = iota((q, q), 1) >= iota((q, q), 0)
    gram[...] = jnp.where(upper, dot_nt(bmat, cmat), 0.0)
    dgram[...] = jnp.zeros_like(dgram)
    acc_x[...] = jnp.zeros_like(acc_x)
    acc_k[...] = jnp.zeros_like(acc_k)
    acc_w[...] = jnp.zeros_like(acc_w)
    acc_g[...] = jnp.zeros_like(acc_g)
    later = jnp.where(iota((q, q), 0) >= iota((q, q), 1), 1.0, 0.0).astype(BF16)
    first = iota((q, LANES), 1) < HEADDIM
    hq = q // 2
    before_top = iota((hq, q), 0) < iota((hq, q), 1)
    before_low = iota((hq, hq), 0) < iota((hq, hq), 1)

    def pair_body(p, carry):
        sl = pl.ds(pl.multiple_of(p * LANES, LANES), LANES)
        cume = cume_ref[:, sl]
        ul = u[:, sl]
        gl = gy_ref[:, sl]
        gy = gl.astype(F32)
        low_du = jnp.zeros((hq, LANES), F32)
        high_du = jnp.zeros((hq, LANES), F32)
        for s in range(2):
            mine = first == (s == 0)
            row = pl.ds(2 * p + s, 1)
            column = cume[:, HEADDIM * s : HEADDIM * s + 1]
            later_row = cumt_ref[row, :]
            um = jnp.where(mine, ul, jnp.zeros_like(ul))
            gm = jnp.where(mine, gl, jnp.zeros_like(gl))
            decay = jnp.exp2(jnp.minimum(later_row - column[:hq], 0.0))
            pairs = gram[:hq, :] * decay
            dpairs = dot_nt(um[:hq], gl)
            dgram[:hq, :] += dpairs * decay
            through = dot_nn((dpairs * pairs).astype(BF16), later)
            total = jnp.sum(jnp.where(before_top, through, 0.0), axis=0, keepdims=True)
            low_du = low_du + dot_nn(pairs.astype(BF16), gm)
            decay = jnp.exp2(jnp.minimum(later_row[:, hq:] - column[hq:], 0.0))
            pairs = gram[hq:, hq:] * decay
            dpairs = dot_nt(um[hq:], gl[hq:])
            dgram[hq:, hq:] += dpairs * decay
            through = dot_nn((dpairs * pairs).astype(BF16), later[hq:, hq:])
            more = jnp.sum(jnp.where(before_low, through, 0.0), axis=0, keepdims=True)
            da[row, :] = total + jnp.concatenate([jnp.zeros((1, hq), F32), more], axis=1)
            high_du = high_du + dot_nn(pairs.astype(BF16), gm[hq:])
        du = jnp.concatenate([low_du, high_du], axis=0)
        x = xs[:, sl]
        wide = dus[:, sl] * jnp.exp2(cume[q - 1 : q, :] - cume)
        du = du + wide
        to_head = (iota((LANES, LANES), 1) == 2 * p + iota((LANES, LANES), 0) // HEADDIM).astype(BF16)
        dte = dte_ref[:, sl]
        acc_x[...] += dot_nn((x * du).astype(BF16), to_head)
        acc_w[...] += dot_nn((x * dte * wide).astype(BF16), to_head)
        acc_g[...] += dot_nn((gy * jnp.exp2(cume) * ya[:, sl]).astype(BF16), to_head)
        acc_k[...] += dot_nn(kept[:, sl], to_head)
        qx[0:q, sl] = (dte * du + par_ref[CONV + 2 : CONV + 3, sl] * gy) * dsil[:, sl]
        return carry

    lax.fori_loop(0, width // LANES, pair_body, 0)
    go_on(2)

    def unconv_body(i, carry):
        sl = pl.ds(pl.multiple_of(i * block, block), block)
        weight = par_ref[0:CONV, sl]
        ext = qx[:, sl]
        cur = ext[0:q]
        dpre = weight[CONV - 1 : CONV] * cur
        for k in range(CONV - 1):
            dpre = dpre + weight[k : k + 1] * ext[CONV - 1 - k : CONV - 1 - k + q]
        dx_ref[pl.ds(pl.multiple_of(c * q, q), q), sl] = dpre.astype(BF16)
        past = jnp.concatenate([xt_ref[:, sl], xm_ref[:, sl]], axis=0)
        for k in range(CONV):
            start = 8 - (CONV - 1) + k
            accx_ref[k : k + 1, sl] += jnp.sum(cur * past[start : start + q], axis=0, keepdims=True)
        accx_ref[CONV : CONV + 1, sl] += jnp.sum(cur, axis=0, keepdims=True)
        head_rows = jnp.concatenate([jnp.zeros((HALO, block), F32), cur[0:8]], axis=0)
        before = jnp.zeros((HALO, block), F32)
        for k in range(CONV - 1):
            before = before + weight[k : k + 1] * head_rows[CONV - 1 - k : CONV - 1 - k + HALO]
        dx_ref[pl.ds(tokens, HALO), sl] = before.astype(BF16)
        qx[q:, sl] = cur[0:8]
        return carry

    lax.fori_loop(0, width // block, unconv_body, 0)

    dg = jnp.where(upper, dgram[...], 0.0)
    db = db + dot_split(dg, bc[:, STATE:])
    dc = dc + dot_split(dg.T, bc[:, :STATE])
    qb[0:q, 0:STATE] = qb[0:q, 0:STATE] * db
    qb[0:q, STATE:] = qb[0:q, STATE:] * dc
    weight = bcpar_ref[0:CONV, :]
    ext = qb[...]
    cur = ext[0:q]
    dpre = weight[CONV - 1 : CONV] * cur
    for k in range(CONV - 1):
        dpre = dpre + weight[k : k + 1] * ext[CONV - 1 - k : CONV - 1 - k + q]
    ds_ref[pl.ds(pl.multiple_of(c * q, q), q), 0 : 2 * STATE] = dpre.astype(BF16)
    past = jnp.concatenate([bt_ref[:, 0 : 2 * STATE], bm_ref[:, 0 : 2 * STATE]], axis=0)
    for k in range(CONV):
        start = 8 - (CONV - 1) + k
        accb_ref[k : k + 1, :] += jnp.sum(cur * past[start : start + q], axis=0, keepdims=True)
    accb_ref[CONV : CONV + 1, :] += jnp.sum(cur, axis=0, keepdims=True)
    head_rows = jnp.concatenate([jnp.zeros((HALO, 2 * STATE), F32), cur[0:8]], axis=0)
    before = jnp.zeros((HALO, 2 * STATE), F32)
    for k in range(CONV - 1):
        before = before + weight[k : k + 1] * head_rows[CONV - 1 - k : CONV - 1 - k + HALO]
    ds_ref[pl.ds(tokens, HALO), 0 : 2 * STATE] = before.astype(BF16)
    qb[q:, :] = cur[0:8]

    raw = bm_ref[:, 2 * STATE :] + hp_ref[0:1, :]
    dt = softplus(raw)
    rate = hp_ref[1:2, :]
    from_here = jnp.where(iota((q, q), 1) >= iota((q, q), 0), 1.0, 0.0).astype(BF16)
    up_to_here = jnp.where(iota((q, q), 1) < iota((q, q), 0), 1.0, 0.0).astype(BF16)
    total = (
        da[...].T
        + sums_of(from_here, acc_g[...])
        + sums_of(up_to_here, acc_w[...])
        + jnp.sum(acc_k[0:3, :], axis=0, keepdims=True)
    )
    d_raw = (acc_x[...] + rate * total) * sigmoid(raw)
    ds_ref[pl.ds(pl.multiple_of(c * q, q), q), 2 * STATE :] = d_raw.astype(BF16)
    acch_ref[0:1, :] += jnp.sum(d_raw, axis=0, keepdims=True)
    acch_ref[1:2, :] += rate * jnp.sum(dt * total, axis=0, keepdims=True)
    go_on(3)


def shape(dims, dtype):
    return jax.ShapeDtypeStruct(dims, dtype)


def whole(dims):
    return pl.BlockSpec(dims, lambda c: (0,) * len(dims))


def run(kernel, name, grid, in_specs, out_specs, out_shape, scratch, args, flops, collective_id=None):
    return pl.pallas_call(
        kernel,
        grid=(grid,),
        in_specs=in_specs,
        out_specs=out_specs,
        out_shape=out_shape,
        scratch_shapes=scratch,
        name=name,
        compiler_params=pltpu.CompilerParams(
            dimension_semantics=("arbitrary",),
            vmem_limit_bytes=62 * 1024 * 1024,
            collective_id=collective_id,
            has_side_effects=collective_id is not None,
        ),
        cost_estimate=pl.CostEstimate(
            flops=flops, bytes_accessed=sum(a.size * a.dtype.itemsize for a in args), transcendentals=0
        ),
    )(*args)


def mixer_forward_state(x_ext, s_ext, par, bcpar, hp, tokens):
    width = x_ext.shape[1]
    small = s_ext.shape[1]
    n = tokens // CHUNK
    q = CHUNK
    tail = q // 8
    last = (tokens + HALO) // 8 - 1
    tail_map = lambda c: (jnp.where(c == 0, last, c * tail - 1), 0)
    heads_pad = -(-(width // HEADDIM) // 8) * 8
    return run(
        state_kernel,
        "scan_states",
        n,
        [
            pl.BlockSpec((q, width), lambda c: (c, 0)),
            pl.BlockSpec((8, width), tail_map),
            pl.BlockSpec((q, small), lambda c: (c, 0)),
            pl.BlockSpec((8, small), tail_map),
            whole(par.shape),
            whole(bcpar.shape),
            whole(hp.shape),
        ],
        [
            pl.BlockSpec((q, width), lambda c: (c, 0)),
            pl.BlockSpec((q, width), lambda c: (c, 0)),
            pl.BlockSpec((q, width), lambda c: (c, 0)),
            pl.BlockSpec((q, width), lambda c: (c, 0)),
            pl.BlockSpec((q, width), lambda c: (c, 0)),
            pl.BlockSpec((q, 2 * STATE), lambda c: (c, 0)),
            pl.BlockSpec((heads_pad, q), lambda c: (0, c)),
            pl.BlockSpec((1, STATE, width), lambda c: (c, 0, 0)),
            whole((STATE, width)),
            pl.BlockSpec((1, 1, width), lambda c: (c, 0, 0)),
        ],
        [
            shape((tokens, width), F32),
            shape((tokens, width), BF16),
            shape((tokens, width), F32),
            shape((tokens, width), F32),
            shape((tokens, width), F32),
            shape((tokens, 2 * STATE), F32),
            shape((heads_pad, tokens), F32),
            shape((n, STATE, width), F32),
            shape((STATE, width), BF16),
            shape((n, 1, width), F32),
        ],
        [
            pltpu.VMEM((STATE, width), F32),
            pltpu.VMEM((1, width), F32),
            pltpu.VMEM((q, width), BF16),
            pltpu.VMEM((3 * LANES, width), BF16),
        ],
        (x_ext, x_ext, s_ext, s_ext, par, bcpar, hp),
        int(3e9),
    )


def mixer_forward_main(xs, u, cume, cumt, bc, sloc, sin, dec, z, gyn, par):
    tokens, width = xs.shape
    q = CHUNK
    n = tokens // q
    rows = pl.BlockSpec((q, width), lambda c: (c, 0))
    return run(
        main_kernel,
        "scan_outputs",
        n,
        [
            rows,
            rows,
            rows,
            pl.BlockSpec((cumt.shape[0], q), lambda c: (0, c)),
            pl.BlockSpec((q, 2 * STATE), lambda c: (c, 0)),
            pl.BlockSpec((1, STATE, width), lambda c: (c, 0, 0)),
            whole(sin.shape),
            pl.BlockSpec((1, 1, width), lambda c: (c, 0, 0)),
            rows,
            rows,
            whole(par.shape),
        ],
        [rows, pl.BlockSpec((8, q), lambda c: (0, c))],
        [shape((tokens, width), F32), shape((8, tokens), F32)],
        [
            pltpu.VMEM((q, q), F32),
            pltpu.VMEM((q, width), F32),
            pltpu.VMEM((q, LANES), F32),
            pltpu.VMEM((q, LANES), F32),
        ],
        (xs, u, cume, cumt, bc, sloc, sin, dec, z, gyn, par),
        int(10e9),
    )


def mixer_backward_gate(y, z, gyn, cume, bc, stat, par):
    tokens, width = y.shape
    q = CHUNK
    n = tokens // q
    rows = pl.BlockSpec((q, width), lambda c: (n - 1 - c, 0))
    return run(
        gate_kernel,
        "gate_back",
        n,
        [
            rows,
            rows,
            rows,
            rows,
            pl.BlockSpec((q, 2 * STATE), lambda c: (n - 1 - c, 0)),
            pl.BlockSpec((q, 8), lambda c: (n - 1 - c, 0)),
            whole(par.shape),
        ],
        [
            rows,
            rows,
            rows,
            pl.BlockSpec((1, STATE, width), lambda c: (n - 1 - c, 0, 0)),
            whole((STATE, width)),
            pl.BlockSpec((1, 1, width), lambda c: (n - 1 - c, 0, 0)),
            whole((8, width)),
        ],
        [
            shape((tokens, width), BF16),
            shape((tokens, width), BF16),
            shape((tokens, width), BF16),
            shape((n, STATE, width), F32),
            shape((STATE, width), BF16),
            shape((n, 1, width), F32),
            shape((8, width), F32),
        ],
        [
            pltpu.VMEM((STATE, width), F32),
            pltpu.VMEM((1, width), F32),
            pltpu.VMEM((q, width), BF16),
        ],
        (y, z, gyn, cume, bc, stat, par),
        int(5e9),
    )


def mixer_backward_main(
    x_ext, s_ext, par, bcpar, hp, cume, dte, xs, dsil, u, cumt, gy, sloc, sin, sdec, gloc, gout, gdec, gz, go
):
    tok_size, head_size = lax.axis_size("tok"), lax.axis_size("head")
    tok_bits = range(tok_size.bit_length() - 1)
    row_bits = range((head_size // HALVES).bit_length() - 1)
    share = gz.shape[1]
    copies = 16 * len(tok_bits)
    tokens, width = cume.shape
    small = s_ext.shape[1]
    q = CHUNK
    n = tokens // q
    tail = q // 8
    last = (tokens + HALO) // 8 - 1
    rows = pl.BlockSpec((q, width), lambda c: (n - 1 - c, 0))
    tail_map = lambda c: (jnp.where(c == n - 1, last, (n - 1 - c) * tail - 1), 0)
    states = pl.BlockSpec((1, STATE, width), lambda c: (n - 1 - c, 0, 0))
    decays = pl.BlockSpec((1, 1, width), lambda c: (n - 1 - c, 0, 0))
    anywhere = pl.BlockSpec(memory_space=pl.ANY)
    return run(
        functools.partial(back_kernel, tok_bits, row_bits),
        "scan_back",
        n,
        [
            rows,
            pl.BlockSpec((8, width), tail_map),
            pl.BlockSpec((q, small), lambda c: (n - 1 - c, 0)),
            pl.BlockSpec((8, small), tail_map),
            whole(par.shape),
            whole(bcpar.shape),
            whole(hp.shape),
            rows,
            rows,
            rows,
            rows,
            rows,
            pl.BlockSpec((cumt.shape[0], q), lambda c: (0, n - 1 - c)),
            rows,
            states,
            whole(sin.shape),
            decays,
            states,
            whole(gout.shape),
            decays,
            anywhere,
            anywhere,
        ],
        [
            whole((tokens + HALO, width)),
            whole((tokens + HALO, small)),
            whole((8, width)),
            whole((8, 2 * STATE)),
            whole((8, LANES)),
            anywhere,
            anywhere,
        ],
        [
            shape((tokens + HALO, width), BF16),
            shape((tokens + HALO, small), BF16),
            shape((8, width), F32),
            shape((8, 2 * STATE), F32),
            shape((8, LANES), F32),
            shape((share, width // HALVES), F32),
            shape((share, width), BF16),
        ],
        [
            pltpu.VMEM((q, width), BF16),
            pltpu.VMEM((q, width), BF16),
            pltpu.VMEM((q, width), F32),
            pltpu.VMEM((q, width), F32),
            pltpu.VMEM((q + 8, width), F32),
            pltpu.VMEM((q + 8, 2 * STATE), F32),
            pltpu.VMEM((q, q), F32),
            pltpu.VMEM((q, q), F32),
            pltpu.VMEM((LANES, q), F32),
            pltpu.VMEM((q, LANES), F32),
            pltpu.VMEM((q, LANES), F32),
            pltpu.VMEM((q, LANES), F32),
            pltpu.VMEM((16, LANES), F32),
            pltpu.VMEM((16, width), BF16),
        ]
        + [pltpu.VMEM((tok_size // 2, share, width), BF16)] * 2
        + [pltpu.VMEM((tok_size, share, width), BF16)] * 2
        + [pltpu.VMEM((share, width // HALVES), F32)]
        + [pltpu.SemaphoreType.DMA((copies,))] * 3,
        (x_ext, x_ext, s_ext, s_ext, par, bcpar, hp, cume, dte, xs, dsil, u, cumt, gy, sloc, sin, sdec, gloc, gout, gdec, gz, go),
        int(30e9),
        collective_id=2,
    )


def gather_kernel(
    tok_bits, row_bits, half_bit,
    in_ref, gain_ref, par_ref, small_ref, wx_ref, wz_ref, wo_ref,
    x_out, s_out, normed_out, ws_out, wx_out, wz_out, wo_out, gains_out, pars_out,
    ws, wx, wz, wo, joined, rows, halo, normed, gains, gain_all, pars, stage,
    send_sem, recv_sem, local_sem, stage_sem,
):
    tok, head = lax.axis_index("tok"), lax.axis_index("head")
    sets = 1 << len(row_bits)
    heads = 2 * sets
    half, mine = head // sets, head % sets
    own_rows, model = in_ref.shape
    share, own_width = wx_ref.shape
    tokens = own_rows * sets
    partners = [{"tok": flip(tok, b)} for b in tok_bits]
    partners += [{"head": flip_all(head, p)} for p in range(1, heads)]

    barrier = pltpu.get_barrier_semaphore()
    for partner in partners:
        pl.semaphore_signal(barrier, inc=1, device_id=partner, device_id_type=MESH)
    pl.semaphore_wait(barrier, len(partners))

    sent, stored, open_local = [], [], []

    def send(src, dst, device):
        k = len(sent)
        copy = pltpu.make_async_remote_copy(
            src_ref=src, dst_ref=dst, send_sem=send_sem.at[k], recv_sem=recv_sem.at[k],
            device_id=device, device_id_type=MESH,
        )
        copy.start()
        sent.append(copy)
        return copy

    def local(src, dst):
        copy = pltpu.make_async_copy(src, dst, local_sem.at[len(stored)])
        copy.start()
        stored.append(copy)
        open_local.append(copy)
        return copy

    def settle(copy):
        if any(copy is other for other in open_local):
            open_local[:] = [other for other in open_local if other is not copy]
            copy.wait()

    def arrive(copies):
        for copy in copies:
            copy.wait_recv()

    other_half = {"head": flip(head, half_bit)}
    lanes = pl.ds(pl.multiple_of(half * own_width, LANES), own_width)

    class Own:
        def __init__(self, src, dst, rows_at, src_lanes, dst_lanes, order):
            self.rows, self.lanes = rows_at, dst_lanes
            self.dst, self.order = dst, list(order)
            slot = dst.at[tok, self.rows, self.lanes]
            bit = self.order.pop(0)
            self.flight = [send(src.at[self.rows, src_lanes], slot, {"tok": flip(tok, bit)})]
            self.kept = local(src.at[self.rows, src_lanes], slot)
            self.held = [0, 1 << bit]

        def advance(self):
            arrive(self.flight)
            settle(self.kept)
            self.flight = []
            if self.order:
                bit = self.order.pop(0)
                for offset in self.held:
                    slot = self.dst.at[flip_all(tok, offset), self.rows, self.lanes]
                    self.flight.append(send(slot, slot, {"tok": flip(tok, bit)}))
                self.held = self.held + [offset ^ (1 << bit) for offset in self.held]

        def finish(self):
            while self.flight:
                self.advance()

    class Other(Own):
        def __init__(self, src, dst, rows_at, src_lanes, sent_lanes, dst_lanes, order):
            self.rows, self.lanes = rows_at, dst_lanes
            self.dst, self.order, self.held, self.kept = dst, list(order), [0], None
            self.flight = [send(src.at[self.rows, src_lanes], dst.at[tok, self.rows, sent_lanes], other_half)]

    class Rows:
        def __init__(self, src, dst):
            self.dst, self.order, self.held = dst, list(row_bits), [0]
            self.src = src
            self.kept = local(src, dst.at[mine])
            self.flight = []
            if self.order:
                bit = self.order.pop(0)
                self.flight.append(send(src, dst.at[mine], {"head": flip(head, bit)}))
                self.held = [0, 1 << bit]

        def advance(self):
            arrive(self.flight)
            settle(self.kept)
            self.flight = []
            if self.order:
                bit = self.order.pop(0)
                for offset in self.held:
                    slot = self.dst.at[flip_all(mine, offset)]
                    self.flight.append(send(slot, slot, {"head": flip(head, bit)}))
                self.held = self.held + [offset ^ (1 << bit) for offset in self.held]

        def finish(self):
            settle(self.kept)
            while self.flight:
                self.advance()

    up = list(tok_bits)[1:] + [0]
    down = list(tok_bits)[1:][::-1] + [0]
    gain_copies = [
        send(gain_ref, gains.at[head], {"head": flip_all(head, p)}) for p in range(1, heads)
    ]
    gain_kept = local(gain_ref, gains.at[head])
    par_slot = pars.at[:, lanes]
    par_copy = send(par_ref, par_slot, other_half)
    par_kept = local(par_ref, par_slot)
    own_all = pl.ds(0, own_width)
    there = pl.ds(pl.multiple_of((1 - half) * own_width, LANES), own_width)
    parts = [pl.ds(n * (share // 2), share // 2) for n in range(2)]

    def own_pieces(src, dst):
        return [Own(src, dst, parts[n], own_all, lanes, (up, down)[n]) for n in range(2)]

    def other_pieces(src, dst):
        return [Other(src, dst, parts[n], own_all, lanes, there, (up, down)[n]) for n in range(2)]

    def step_lanes(which):
        return pl.ds(pl.multiple_of(2 * STATE + which * LANES, LANES), LANES)

    every, bc_lanes, own_steps = pl.ds(0, share), pl.ds(0, 2 * STATE), pl.ds(2 * STATE, LANES)
    x_other = other_pieces(wx_ref, wx)
    x_other.append(Other(small_ref, ws, every, own_steps, step_lanes(half), step_lanes(1 - half), down))
    x_own = own_pieces(wx_ref, wx)
    x_own.append(Own(small_ref, ws, every, bc_lanes, bc_lanes, up))
    x_own.append(Own(small_ref, ws, every, own_steps, step_lanes(half), down))
    z_own = own_pieces(wz_ref, wz)
    z_other = other_pieces(wz_ref, wz)
    r_in = Rows(in_ref, rows)
    o_own = own_pieces(wo_ref, wo)
    o_other = other_pieces(wo_ref, wo)

    def advance(pieces):
        for piece in pieces:
            piece.advance()

    def normalise(src, start, count, scale):
        def body(i, carry):
            at = pl.ds(pl.multiple_of(start + i * 16, 16), 16)
            wide = src[pl.ds(pl.multiple_of(i * 16, 16), 16), :].astype(F32)
            inv = lax.rsqrt(jnp.sum(wide * wide, axis=1, keepdims=True) / model + EPS)
            normed[at, :] = (wide * inv * scale).astype(BF16)
            return carry

        lax.fori_loop(0, count // 16, body, 0, unroll=4 if count >= 64 else 1)

    def project(lhs, count, weight, out, width):
        tile = 256 if width % 256 == 0 else 3 * LANES
        steps = width // tile

        def out_copy(i):
            at = pl.ds(pl.multiple_of(i * tile, tile), tile)
            return pltpu.make_async_copy(
                stage.at[i % 2, pl.ds(0, count), pl.ds(0, tile)], out.at[:, at], stage_sem.at[i % 2]
            )

        def body(i, carry):
            @pl.when(i >= 2)
            def _():
                out_copy(i - 2).wait()

            at = pl.ds(pl.multiple_of(i * tile, tile), tile)
            block = weight[:, :, at].reshape(model, tile)
            stage[i % 2, 0:count, 0:tile] = dot_nn(lhs[...].reshape(count, model), block)
            out_copy(i).start()
            return carry

        lax.fori_loop(0, steps, body, 0)
        for i in range(max(steps - 2, 0), steps):
            out_copy(i).wait()

    def finish(pieces):
        for piece in pieces:
            piece.finish()

    def join_heads():
        def body(i, carry):
            low = ws[i, :, 2 * STATE : 2 * STATE + LANES].astype(F32)
            high = ws[i, :, 2 * STATE + LANES :].astype(F32)
            joined[i, :, : 2 * STATE] = ws[i, :, : 2 * STATE]
            joined[i, :, 2 * STATE :] = (low + pltpu.roll(high, own_width // HEADDIM, 1)).astype(BF16)
            return carry

        lax.fori_loop(0, ws.shape[0], body, 0)

    advance(x_own)
    arrive(gain_copies)
    settle(gain_kept)
    gain_share = model // heads
    scale = jnp.concatenate([gains[g, 0:1, 0:gain_share] for g in range(heads)], axis=1)
    gain_all[...] = jnp.broadcast_to(scale, (8, model))
    advance(x_other)
    advance(x_own)
    settle(r_in.kept)
    normalise(rows.at[mine], mine * own_rows, own_rows, scale)
    advance(x_other)
    advance(z_own)
    advance(z_other)
    advance(x_other)
    advance(z_own)
    advance(o_own)
    advance(z_other)
    finish(x_own)
    finish(x_other)
    join_heads()
    local(joined, ws_out)
    local(wx, wx_out)
    r_in.finish()
    tail = rows.at[sets - 1, pl.ds(own_rows - HALO, HALO), :]
    tail_copy = send(tail, halo, other_half)
    for i in range(1, sets):
        other = flip_all(mine, i)
        normalise(rows.at[other], other * own_rows, own_rows, scale)
    advance(o_other)
    advance(o_own)
    advance(z_other)
    tail_copy.wait_recv()
    normalise(halo, tokens, HALO, scale * half.astype(F32))
    local(normed, normed_out)
    project(normed, tokens + HALO, joined, s_out, s_out.shape[1])
    advance(o_other)
    project(normed, tokens + HALO, wx, x_out, wx.shape[2])
    finish(z_own)
    finish(z_other)
    local(wz, wz_out)
    advance(o_other)
    finish(o_own)
    finish(o_other)
    local(wo, wo_out)
    arrive([par_copy])
    settle(par_kept)
    local(pars, pars_out)
    local(gain_all, gains_out)
    for copy in list(open_local):
        settle(copy)
    for copy in sent:
        copy.wait_send()


def gather_and_project(block_in, gain, par, small, wx, wz, wo):
    tok_size, head_size = lax.axis_size("tok"), lax.axis_size("head")
    sets = head_size // HALVES
    tok_bits = range(tok_size.bit_length() - 1)
    row_bits = range(sets.bit_length() - 1)
    own_rows, model = block_in.shape
    share, own_width = wx.shape
    width = HALVES * own_width
    tokens = own_rows * sets
    lanes = 2 * STATE + HALVES * LANES
    anywhere = pl.BlockSpec(memory_space=pl.ANY)
    slots = (tok_size, share)
    copies = 16 * tok_size
    outs = [
        shape((tokens + HALO, width), F32),
        shape((tokens + HALO, 2 * STATE + LANES), F32),
        shape((tokens + HALO, model), BF16),
        shape(slots + (2 * STATE + LANES,), BF16),
        shape(slots + (width,), BF16),
        shape(slots + (width,), BF16),
        shape(slots + (width,), BF16),
        shape((8, model), F32),
        shape((8, width), F32),
    ]
    return pl.pallas_call(
        functools.partial(gather_kernel, tok_bits, row_bits, sets.bit_length() - 1),
        in_specs=[anywhere] * 7,
        out_specs=[anywhere] * len(outs),
        out_shape=outs,
        scratch_shapes=[
            pltpu.VMEM(slots + (lanes,), BF16),
            pltpu.VMEM(slots + (width,), BF16),
            pltpu.VMEM(slots + (width,), BF16),
            pltpu.VMEM(slots + (width,), BF16),
            pltpu.VMEM(slots + (2 * STATE + LANES,), BF16),
            pltpu.VMEM((sets, own_rows, model), BF16),
            pltpu.VMEM((HALO, model), BF16),
            pltpu.VMEM((tokens + HALO, model), BF16),
            pltpu.VMEM((head_size,) + gain.shape, F32),
            pltpu.VMEM((8, model), F32),
            pltpu.VMEM((8, width), F32),
            pltpu.VMEM((2, tokens + HALO, 3 * LANES), F32),
            pltpu.SemaphoreType.DMA((copies,)),
            pltpu.SemaphoreType.DMA((copies,)),
            pltpu.SemaphoreType.DMA((32,)),
            pltpu.SemaphoreType.DMA((2,)),
        ],
        name="gather",
        compiler_params=pltpu.CompilerParams(
            collective_id=0, has_side_effects=True, vmem_limit_bytes=60 * 1024 * 1024
        ),
        cost_estimate=pl.CostEstimate(flops=int(12e9), bytes_accessed=int(60e6), transcendentals=0),
    )(block_in, gain, par, small, wx, wz, wo)


def reduce_kernel(
    tok_bits, row_bits,
    gx_ref, to_ref, dx_ref, ds_ref, dz_ref, norm_ref, in_ref, wx_ref, wz_ref, ws_ref, cot_ref, gain_ref, per_ref, bc_ref,
    ox_ref, oo_ref, os_ref, dblock_ref, gain_out, rest_out,
    kx, ks, rx, rs, fx, ls, gs, gl, own_o, got_o, fo,
    dx, ds, dz, wx, wz, ws, norms, own_in, cots, dnorm, low, got, halo_out, halo_in, sums, sums_got, per_got, bc_got, bc_own,
    send_sem, recv_sem, local_sem,
):
    links = Links(send_sem, recv_sem, local_sem, tok_bits, row_bits)
    half, mine, sets = links.half, links.mine, links.sets
    own_rows, model = cot_ref.shape
    own_width = ox_ref.shape[1]
    tokens = own_rows * sets
    chunk = min(CHUNK, own_rows)
    loads = [
        links.local(src, dst)
        for src, dst in ((dx_ref, dx), (ds_ref, ds), (dz_ref, dz), (wx_ref, wx), (wz_ref, wz), (ws_ref, ws))
    ]
    links.enter()

    up = [0] + links.tok_bits[1:]
    down = [0] + links.tok_bits[1:][::-1]
    s_x = [Sum(links, gx_ref, kx, rx, fx, ox_ref, p, 2, (down, up)[p]) for p in range(2)]

    def advance(group):
        for each in group:
            each.advance()

    advance(s_x)
    late_loads = [
        links.local(norm_ref, norms), links.local(in_ref, own_in), links.local(cot_ref, cots)
    ]

    def project_back(at):
        lhs_x, lhs_s = dx[at, :], ds[at, :]
        return dot_nt(lhs_x, wx[...].reshape(model, wx.shape[2])) + dot_nt(lhs_s, ws[...].reshape(model, ws.shape[2]))

    def slot_rows(slot, first=0, count=None):
        def body(i, carry):
            here = pl.ds(pl.multiple_of(i * chunk, chunk), chunk)
            at = pl.ds(pl.multiple_of(slot * own_rows + i * chunk, chunk), chunk)
            gates = dot_nt(dz[at, :], wz[...].reshape(model, wz.shape[2]))
            dnorm[slot, here, :] = project_back(at) + gates
            return carry

        lax.fori_loop(first, own_rows // chunk if count is None else first + count, body, 0)

    def fold(slot):
        keep = jnp.where(half == 0, 1.0, 0.0) * jnp.where(slot == sets - 1, 1.0, 0.0)
        tail = pl.ds(own_rows - HALO, HALO)
        dnorm[slot, tail, :] = dnorm[slot, tail, :] + keep * halo_in[...]

    def rows_at(i, count):
        return pl.ds(pl.multiple_of(i * count, count), count)

    def gain_part(slot, start):
        def body(i, total):
            normed = norms[pl.ds(pl.multiple_of(slot * own_rows + i * 16, 16), 16), :].astype(F32)
            part = dnorm[slot, rows_at(i, 16), :] * normed
            return total + part[0:8] + part[8:16]

        return lax.fori_loop(0, own_rows // 16, body, start, unroll=2)

    everywhere, rest, owned = pl.ds(0, model), pl.ds(model, own_width + bc_ref.shape[1]), pl.ds(model, own_width)
    bc_lanes = pl.ds(model + own_width, bc_ref.shape[1])

    def channel_lanes(which):
        return pl.ds(pl.multiple_of(which * own_width, LANES), own_width)

    o_load = links.local(to_ref.at[:, channel_lanes(half)], own_o)
    early = [
        links.send(per_ref.at[:, channel_lanes(1 - half)], per_got, links.head_peer(links.half_bit)),
        links.send(bc_ref, bc_got.at[0], links.head_peer(links.half_bit)),
    ]

    o_tail = links.send(to_ref.at[:, channel_lanes(1 - half)], got_o, links.head_peer(links.half_bit))

    links.settle(loads + late_loads[:1])
    small_grad = dot_tn(norms[...], ds[...])
    gs[...] = small_grad.reshape(gs.shape)
    gl[...] = small_grad.astype(BF16).reshape(gl.shape)
    away = list(range(1, sets))[::-1]
    slots = [flip_all(mine, o) for o in away]
    early_rows = sets == 2 and own_rows > chunk
    pieces = own_rows // chunk
    row_pieces = []

    def lower(piece, slot):
        def body(i, carry):
            at = pl.ds(pl.multiple_of(piece * chunk + i * 32, 32), 32)
            low[0, at, :] = dnorm[slot, at, :].astype(BF16)
            return carry

        lax.fori_loop(0, chunk // 32, body, 0)

    def send_piece(piece):
        at = pl.ds(piece * chunk, chunk)
        row_pieces.append(links.send(low.at[0, at], got.at[0, at], links.head_peer(0)))

    if early_rows:
        slot_rows(slots[0], 0, 1)
        lower(0, slots[0])
    elif slots:
        slot_rows(slots[0])
    for copy in early:
        copy.wait_recv()
    sums[0, :, owned] = per_ref[:, channel_lanes(half)] + per_got[...]
    bc_total = bc_ref[...] + bc_got[0]
    for n, bit in enumerate(links.row_bits):
        bc_own[n] = bc_total
        bc_copy = links.send(bc_own.at[n], bc_got.at[n + 1], links.head_peer(bit))
        if not early_rows:
            bc_copy.wait_recv()
            bc_total = bc_total + bc_got[n + 1]
    halo_out[...] = project_back(pl.ds(tokens, HALO))
    s_small = SmallSum(links, gs, gl, ks, ls, rs, up)
    if early_rows:
        send_piece(0)
    halo_copy = links.send(halo_out, halo_in, links.head_peer(links.half_bit))
    if early_rows:
        advance(s_x)
        advance([s_small])
        slot_rows(slots[0], 1, pieces - 1)
        bc_copy.wait_recv()
        bc_total = bc_ref[...] + bc_got[0] + bc_got[1]
    sums[0, :, bc_lanes] = bc_total
    for slot in slots[1:]:
        slot_rows(slot)
    halo_copy.wait_recv()
    for slot in slots:
        fold(slot)

    row_order = list(row_bits)[::-1]
    held = list(range(sets))
    places = 0

    def send_rows():
        nonlocal held, places
        bit = row_order.pop(0)
        stay = [o for o in held if not (o >> bit) & 1]
        copies = []
        for o in stay:
            slot = flip_all(mine, o ^ (1 << bit))

            def body(i, carry, slot=slot, place=places):
                low[place, rows_at(i, 32), :] = dnorm[slot, rows_at(i, 32), :].astype(BF16)
                return carry

            lax.fori_loop(0, own_rows // 32, body, 0)
            copies.append((o, places, bit))
            places += 1
        held = stay
        return copies

    def start_rows(copies):
        return [(o, p, links.send(low.at[p], got.at[p], links.head_peer(bit))) for o, p, bit in copies]

    def take_rows(copies):
        for o, place, copy in copies:
            copy.wait_recv()
            slot = flip_all(mine, o)

            def body(i, carry, slot=slot, place=place):
                at = rows_at(i, 32)
                dnorm[slot, at, :] = dnorm[slot, at, :] + got[place, at, :].astype(F32)
                return carry

            lax.fori_loop(0, own_rows // 32, body, 0)

    if early_rows:
        for piece in range(1, pieces):
            lower(piece, slots[0])
        row_order, row_copies = [], [(0, 0, None)]
        for piece in range(1, pieces):
            send_piece(piece)
    else:
        prepared = send_rows() if row_order else []
        advance([s_small])
        row_copies = start_rows(prepared)
    if not early_rows:
        advance(s_x)
    slot_rows(mine)
    if early_rows:
        advance(s_x)
    fold(mine)
    links.settle(late_loads)
    gain_sum = jnp.zeros((8, model), F32)
    for slot in slots + [mine]:
        gain_sum = gain_part(slot, gain_sum)
    gain = gain_ref[0:1, :]
    gain_row = jnp.sum(gain_sum, axis=0, keepdims=True) / gain

    sums[0, :, everywhere] = jnp.concatenate([gain_row, jnp.zeros((7, model), F32)], axis=0)
    advance([s_small])
    between = {0: s_x, 2: [s_small]} if not early_rows else {2: [s_small]}
    for n, bit in enumerate(tok_bits):
        copy = links.send(sums.at[n], sums_got.at[n], links.tok_peer(bit))
        advance(between.get(n, []))
        copy.wait_recv()
        sums[n + 1] = sums[n] + sums_got[n]
    n = len(tok_bits)
    links.local(sums.at[n, :, rest], rest_out)
    while not s_small.done:
        s_small.advance()

    def exchange_gain(bit):
        return links.send(sums.at[n, :, everywhere], sums_got.at[n, :, everywhere], links.head_peer(bit))

    def take_gain(copy):
        copy.wait_recv()
        sums[n + 1, :, everywhere] = sums[n, :, everywhere] + sums_got[n, :, everywhere]

    gain_copy = exchange_gain(links.half_bit)
    for each in s_x:
        while each.next < each.last:
            each.advance()

    while row_copies:
        if not row_order:
            break
        take_rows(row_copies)
        row_copies = start_rows(send_rows())
    for copy in row_pieces if early_rows else [copy for _, _, copy in row_copies]:
        copy.wait_recv()

    def block_rows(i, carry):
        at = rows_at(i, 32)
        wide = own_in[at, :].astype(F32)
        inv = lax.rsqrt(jnp.sum(wide * wide, axis=1, keepdims=True) / model + EPS)
        total = dnorm[mine, at, :]
        for _, place, _ in row_copies:
            total = total + got[place, at, :].astype(F32)
        scaled = total * gain
        inner = jnp.sum(scaled * wide, axis=1, keepdims=True) / model
        dnorm[mine, at, :] = cots[at, :].astype(F32) + inv * scaled - wide * (inv * inv * inv * inner)
        return carry

    lax.fori_loop(0, own_rows // 32, block_rows, 0)
    links.local(dnorm.at[mine], dblock_ref)
    take_gain(gain_copy)
    n += 1
    for bit in links.row_bits:
        gain_copy = exchange_gain(bit)
        if bit == links.row_bits[0]:
            s_small.finish()
        take_gain(gain_copy)
        n += 1
    if not links.row_bits:
        s_small.finish()
    links.local(sums.at[n, :, everywhere], gain_out)
    links.local(ks.at[0], os_ref)
    o_tail.wait_recv()
    links.settle([o_load])

    def o_rows(i, carry):
        at = rows_at(i, 32)
        fo[at, :] = own_o[at, :].astype(F32) + got_o[at, :].astype(F32)
        return carry

    lax.fori_loop(0, fo.shape[0] // 32, o_rows, 0)
    links.local(fo, oo_ref)
    for each in s_x:
        each.finish()
    for each in s_x:
        each.close()
    links.leave()


def reduce_sums(gx, to, dx, ds, dz, normed, block_in, wx, wz, ws, cot, gain, per, bc):
    tok_size, head_size = lax.axis_size("tok"), lax.axis_size("head")
    sets = head_size // HALVES
    tok_bits = range(tok_size.bit_length() - 1)
    row_bits = range(sets.bit_length() - 1)
    own_rows, model = cot.shape
    share, width = gx.shape[1:]
    lanes = ws.shape[2]
    own_width = width // HALVES
    anywhere = pl.BlockSpec(memory_space=pl.ANY)
    inside = pl.BlockSpec(memory_space=pltpu.VMEM)
    keep, slots = tok_size // 2, tok_size + len(row_bits)
    stages = len(tok_bits) + len(row_bits) + 1
    away = max(sets - 1, 1)
    copies = 32 * len(tok_bits)
    outs = [
        shape((share, own_width), F32),
        shape((share, own_width), F32),
        shape((share, lanes), F32),
        shape((own_rows, model), F32),
        shape((8, model), F32),
        shape((8, own_width + bc.shape[1]), F32),
    ]
    return pl.pallas_call(
        functools.partial(reduce_kernel, tok_bits, row_bits),
        in_specs=[anywhere] * 11 + [inside] * 3,
        out_specs=[anywhere] * len(outs),
        out_shape=outs,
        scratch_shapes=[pltpu.VMEM((keep, share, width), BF16)]
        + [pltpu.VMEM((keep, share, lanes), F32)]
        + [pltpu.VMEM((slots, share, width), BF16)]
        + [pltpu.VMEM((slots, share, lanes), BF16)]
        + [pltpu.VMEM((share, own_width), F32)]
        + [pltpu.VMEM((slots, share, lanes), BF16)]
        + [pltpu.VMEM((tok_size, share, lanes), F32)]
        + [pltpu.VMEM((tok_size, share, lanes), BF16)]
        + [pltpu.VMEM((share, own_width), BF16)] * 2
        + [pltpu.VMEM((share, own_width), F32)]
        + [
            pltpu.VMEM(dx.shape, BF16),
            pltpu.VMEM(ds.shape, BF16),
            pltpu.VMEM(dz.shape, BF16),
            pltpu.VMEM(wx.shape, BF16),
            pltpu.VMEM(wz.shape, BF16),
            pltpu.VMEM(ws.shape, BF16),
            pltpu.VMEM(normed.shape, BF16),
            pltpu.VMEM(cot.shape, BF16),
            pltpu.VMEM(cot.shape, BF16),
            pltpu.VMEM((sets, own_rows, model), F32),
            pltpu.VMEM((away, own_rows, model), BF16),
            pltpu.VMEM((away, own_rows, model), BF16),
            pltpu.VMEM((HALO, model), F32),
            pltpu.VMEM((HALO, model), F32),
            pltpu.VMEM((stages + 1, 8, model + own_width + bc.shape[1]), F32),
            pltpu.VMEM((stages, 8, model + own_width + bc.shape[1]), F32),
            pltpu.VMEM((8, own_width), F32),
            pltpu.VMEM((len(row_bits) + 1,) + bc.shape, F32),
            pltpu.VMEM((max(len(row_bits), 1),) + bc.shape, F32),
            pltpu.SemaphoreType.DMA((copies,)),
            pltpu.SemaphoreType.DMA((copies,)),
            pltpu.SemaphoreType.DMA((copies,)),
        ],
        name="reduce",
        compiler_params=pltpu.CompilerParams(
            collective_id=1, has_side_effects=True, vmem_limit_bytes=62 * 1024 * 1024
        ),
        cost_estimate=pl.CostEstimate(flops=int(12e9), bytes_accessed=int(60e6), transcendentals=0),
    )(gx, to, dx, ds, dz, normed, block_in, wx, wz, ws, cot, gain, per, bc)


def per_device(
    block_in,
    norm_gain,
    w_zx,
    w_bc,
    w_dt,
    conv_x_w,
    conv_x_b,
    conv_bc_w,
    conv_bc_b,
    dt_bias,
    a_log,
    d_skip,
    gate_gain,
    w_out,
    cotangent,
):
    head_size = lax.axis_size("head")
    tok_size = lax.axis_size("tok")
    sets = head_size // HALVES
    row_bits = range(sets.bit_length() - 1)
    half_bit = sets.bit_length() - 1
    half = bit_of("head", half_bit)
    own_rows, model = block_in.shape
    share, _, own_width = w_zx.shape
    own_heads = w_dt.shape[1]
    tokens = own_rows * sets

    def all_rows(value):
        for bit in row_bits:
            value = grow(value, "head", bit, 0)
        return value

    def lane_pad(v):
        return jnp.pad(v, (0, LANES - v.shape[0]))

    heads_row = jnp.concatenate([lane_pad(dt_bias), lane_pad(a_log), lane_pad(d_skip)])
    own_par = jnp.concatenate(
        [
            conv_x_w,
            conv_x_b[None],
            gate_gain[None],
            jnp.repeat(d_skip, HEADDIM)[None],
            jnp.pad(heads_row, (0, own_width - heads_row.shape[0]))[None],
        ]
    )
    gain_share = norm_gain.shape[0]
    own_gain = jnp.broadcast_to(
        jnp.pad(norm_gain.astype(F32), (0, -gain_share % LANES))[None], (8, gain_share + -gain_share % LANES)
    )
    small = jnp.concatenate([w_bc, jnp.pad(w_dt, ((0, 0), (0, LANES - own_heads)))], axis=1)
    x_ext, s_ext, normed_ext, w_small, w_x, w_z, w_o, gain, par = gather_and_project(
        block_in, own_gain, own_par, small, w_zx[:, 1], w_zx[:, 0], w_out.T
    )
    later_cot, x_ext = lax.optimization_barrier((cotangent, x_ext))
    cot = all_rows(later_cot)
    gain = gain[0:1]
    normed = normed_ext[:tokens]
    slots_small, slots_x, slots_z, gain_rows = w_small, w_x, w_z, gain
    w_z, w_o = w_z.reshape(model, w_z.shape[2]), w_o.reshape(model, w_o.shape[2])

    def of_heads(start):
        pieces = [
            par[CONV + 3, i * own_width + start : i * own_width + start + own_heads] for i in range(HALVES)
        ]
        return jnp.concatenate(pieces)

    rate = -jnp.exp(of_heads(LANES))
    hp = jnp.stack([lane_pad(of_heads(0)), lane_pad(rate)] + [jnp.zeros((LANES,), F32)] * 6)
    bcpar = jnp.concatenate([conv_bc_w, conv_bc_b[None], jnp.zeros((3, 2 * STATE), F32)])

    xs, u, cume, dte, dsil, bc, cumt, sloc, fin, sdec = mixer_forward_state(x_ext, s_ext, par, bcpar, hp, tokens)
    to_next = [(i, i + sets) for i in range(sets)]
    to_prev = [(i + sets, i) for i in range(sets)]
    sin = lax.ppermute(fin, "head", to_next)
    z = dot_nn(normed, w_z)
    gyn = dot_nn(cot, w_o)
    y, stat = mixer_forward_main(xs, u, cume, cumt, bc, sloc, sin, sdec, z, gyn, par)
    stat = add_pairs(stat, "head", row_bits).T
    inv_gate = lax.rsqrt(stat[:, 0:1] / INNER + EPS)
    stat = jnp.concatenate(
        [inv_gate, inv_gate * inv_gate * inv_gate * stat[:, 1:2] / INNER, stat[:, 2:]], axis=1
    )
    yn, gy, dz, gloc, gin, gdec, acc_gate = mixer_backward_gate(y, z, gyn, cume, bc, stat, par)
    gout = lax.ppermute(gin, "head", to_prev)

    def own_row_sum(value):
        for bit in list(row_bits)[::-1]:
            value = halve(value, "head", bit, 0)
        return value

    def slots_of(grad):
        return grad.astype(BF16).reshape(tok_size, share, grad.shape[1])

    branch = dot_nt(yn, w_o)
    block_out = block_in.astype(F32) + own_row_sum(branch)
    grad_o = slots_of(dot_tn(cot, yn))
    grad_z = slots_of(dot_tn(normed, dz))
    dx, ds, acc_x, acc_b, acc_h, d_w_z, tail_o = mixer_backward_main(
        x_ext, s_ext, par, bcpar, hp, cume, dte, xs, dsil, u, cumt, gy, sloc, sin, sdec, gloc, gout, gdec, grad_z, grad_o
    )
    grad_x = slots_of(dot_tn(normed_ext, dx))

    per_channel = jnp.concatenate(
        [
            acc_x[: CONV + 1],
            acc_gate[0:1],
            jnp.concatenate(
                [
                    jnp.pad(
                        jnp.concatenate(
                            [
                                lane_pad(acc_h[0, i * own_heads : (i + 1) * own_heads]),
                                lane_pad(acc_h[1, i * own_heads : (i + 1) * own_heads]),
                                lane_pad(
                                    jnp.sum(
                                        acc_x[CONV + 1, i * own_width : (i + 1) * own_width].reshape(own_heads, HEADDIM),
                                        axis=1,
                                    )
                                ),
                            ]
                        ),
                        (0, own_width - 3 * LANES),
                    )
                    for i in range(HALVES)
                ]
            )[None],
            jnp.zeros((1, HALVES * own_width), F32),
        ]
    )

    d_w_x, d_w_o, d_small, d_block_in, gain_sums, own_sums = reduce_sums(
        grad_x, tail_o, dx, ds, dz, normed_ext, block_in, slots_x, slots_z, slots_small, cotangent,
        gain_rows, per_channel, acc_b,
    )
    all_gain, bc_sums = gain_sums[0], own_sums[:, own_width:]
    own_sums = own_sums[:, :own_width]
    d_w_bc = d_small[:, : 2 * STATE]
    d_w_dt = jnp.where(
        half == 0,
        d_small[:, 2 * STATE : 2 * STATE + own_heads],
        d_small[:, 2 * STATE + own_heads : 2 * STATE + 2 * own_heads],
    )
    d_norm_gain = lax.dynamic_slice_in_dim(all_gain, lax.axis_index("head") * gain_share, gain_share, 0)
    return (
        block_out,
        d_block_in,
        d_norm_gain,
        jnp.stack([d_w_z, d_w_x], axis=1),
        d_w_bc,
        d_w_dt,
        own_sums[:CONV],
        own_sums[CONV],
        bc_sums[:CONV],
        bc_sums[CONV],
        own_sums[CONV + 2, :own_heads],
        own_sums[CONV + 2, LANES : LANES + own_heads],
        own_sums[CONV + 2, 2 * LANES : 2 * LANES + own_heads],
        own_sums[CONV + 1],
        d_w_o.T,
    )


def solution(mesh):
    placed = (
        P(("tok", "head"), None),
        P("head"),
        P("tok", None, "head"),
        P("tok", None),
        P("tok", "head"),
        P(None, "head"),
        P("head"),
        P(),
        P(),
        P("head"),
        P("head"),
        P("head"),
        P("head"),
        P("head", "tok"),
        P(("tok", "head"), None),
    )
    return jax.shard_map(
        per_device,
        mesh=mesh,
        in_specs=placed,
        out_specs=(
            P(("tok", "head"), None),
            P(("tok", "head"), None),
            P("head"),
            P("tok", None, "head"),
            P("tok", None),
            P("tok", "head"),
            P(None, "head"),
            P("head"),
            P(),
            P(),
            P("head"),
            P("head"),
            P("head"),
            P("head"),
            P("head", "tok"),
        ),
        check_vma=False,
    )
```
